32 devices in a mesh: fsdp: 16 (over z, y, x), tensor: 2 (over core).
Axes of the slice: x: 2, y: 2, z: 4, core: 2. Of those that a mesh axis runs over, the one named last changes fastest.
Arguments:
- inputs: bfloat16 [4, 2048, 1024], P(None, ('fsdp', 'tensor')), may hold values from -6 to 6
- encoder_out: bfloat16 [4, 512, 1024], P(None, ('fsdp', 'tensor')), may hold values from -6 to 6
- out_cotangent: bfloat16 [4, 2048, 1024], P(None, ('fsdp', 'tensor')), may hold values from -6 to 6
- bucket_ids: int32 [2048], replicated, may hold values from 0 to 31, as said below
- position_table: float32 [16, 32], replicated, may hold values from -4 to 4
- self_gain: float32 [1024], replicated, may hold values from 0.5 to 1.5
- self_query: bfloat16 [1024, 1024], P('fsdp', 'tensor'), may hold values from -0.1875 to 0.1875
- self_key: bfloat16 [1024, 512], P('fsdp', 'tensor'), may hold values from -0.1875 to 0.1875
- self_value: bfloat16 [1024, 512], P('fsdp', 'tensor'), may hold values from -0.1875 to 0.1875
- self_output: bfloat16 [1024, 1024], P('tensor', 'fsdp'), may hold values from -4 to 4
- cross_gain: float32 [1024], replicated, may hold values from 0.5 to 1.5
- cross_query: bfloat16 [1024, 1024], P('fsdp', 'tensor'), may hold values from -0.1875 to 0.1875
- cross_key: bfloat16 [1024, 512], P('fsdp', 'tensor'), may hold values from -0.1875 to 0.1875
- cross_value: bfloat16 [1024, 512], P('fsdp', 'tensor'), may hold values from -0.1875 to 0.1875
- cross_output: bfloat16 [1024, 1024], P('tensor', 'fsdp'), may hold values from -2 to 2
- feed_gain: float32 [1024], replicated, may hold values from 0.5 to 1.5
- gate_weight: bfloat16 [1024, 2816], P('fsdp', 'tensor'), may hold values from -0.1875 to 0.1875
- up_weight: bfloat16 [1024, 2816], P('fsdp', 'tensor'), may hold values from -0.1875 to 0.1875
- down_weight: bfloat16 [2816, 1024], P('tensor', 'fsdp'), may hold values from -0.109375 to 0.109375
Outputs:
- layer_out: bfloat16 [4, 2048, 1024], P(None, ('fsdp', 'tensor'))
- input_grad: float32 [4, 2048, 1024], P(None, ('fsdp', 'tensor'))
- encoder_grad: float32 [4, 512, 1024], P(None, ('fsdp', 'tensor'))
- table_grad: float32 [16, 32], replicated
- self_gain_grad: float32 [1024], replicated
- self_query_grad: float32 [1024, 1024], P('fsdp', 'tensor')
- self_key_grad: float32 [1024, 512], P('fsdp', 'tensor')
- self_value_grad: float32 [1024, 512], P('fsdp', 'tensor')
- self_output_grad: float32 [1024, 1024], P('tensor', 'fsdp')
- cross_gain_grad: float32 [1024], replicated
- cross_query_grad: float32 [1024, 1024], P('fsdp', 'tensor')
- cross_key_grad: float32 [1024, 512], P('fsdp', 'tensor')
- cross_value_grad: float32 [1024, 512], P('fsdp', 'tensor')
- cross_output_grad: float32 [1024, 1024], P('tensor', 'fsdp')
- feed_gain_grad: float32 [1024], replicated
- gate_grad: float32 [1024, 2816], P('fsdp', 'tensor')
- up_grad: float32 [1024, 2816], P('fsdp', 'tensor')
- down_grad: float32 [2816, 1024], P('tensor', 'fsdp')
The draws below stay inside these ranges and needn't reach their ends.
Inputs may be any that keep to these rules, and one draw needn't show every extreme that they name: bucket_ids[o] is the bucket of a key o positions before its query; it never falls as o grows, equals o for o < 16, and is 31 at o = 2047.
All inputs are finite; a program needn't handle non-finite values.
Results may differ from the reference program's by a relative error of at most 0.03.
Values may be sent and summed in bfloat16 or wider, within the bound.
A program may use at most 256 MiB of HBM per device.

```python
import math
import jax
import jax.numpy as jnp
from jax import lax

D = 1024
HEADS = 16
KV = 8
HEAD = 64
FF = 2816
NB = 32
E = 512
MB = 4
L = 2048


def draw_bucket_ids(key, part):
    exact_count = NB // 2
    near_bounds = jnp.arange(1, exact_count, dtype=jnp.int32)
    far_bounds = exact_count + jax.random.randint(key, (NB - exact_count,), 0, L - exact_count, dtype=jnp.int32)
    all_bounds = jnp.concatenate([near_bounds, far_bounds])
    offsets = jnp.arange(L, dtype=jnp.int32)
    return jnp.sum((offsets[:, None] >= all_bounds[None, :]).astype(jnp.int32), axis=1)


def raised(drawn, rng, source, target, blocks, factor):
    owner, partner = [(jnp.arange(drawn.shape[dim]) // (drawn.shape[dim] // blocks)).reshape([-1 if axis == dim else 1 for axis in range(drawn.ndim)]) for dim in (source, target)]
    chosen = jax.random.permutation(rng, blocks)[partner]
    strong = (owner == chosen) | (owner == (partner + blocks // 2) % blocks)
    return jnp.where(strong, factor * drawn, drawn)


def block_scale(stream_key, shape, cuts, low, high):
    factor_of = 1.0
    for axis_at, parts in cuts:
        draws = jax.random.uniform(jax.random.fold_in(jax.random.fold_in(stream_key, 6), axis_at), (parts,), jnp.float32, low / len(cuts), high / len(cuts))
        factor_of = factor_of * jnp.repeat(jnp.exp(draws), shape[axis_at] // parts).reshape((-1,) + (1,) * (len(shape) - 1 - axis_at))
    return factor_of


def gaussian(stream_key, extent, scale, limit, shards=(), held_as=jnp.bfloat16):
    entries = scale * jax.random.normal(stream_key, extent, jnp.float32)
    if shards:
        entries = entries * block_scale(stream_key, extent, shards, -0.22, 0.18)
    return jnp.clip(entries, -limit, limit).astype(held_as)


def noise_with(stream_key, dims, scale, reach, cuts, heavy, kind=jnp.bfloat16):
    values = scale * jax.random.normal(stream_key, dims, jnp.float32)
    if cuts:
        values = values * block_scale(stream_key, dims, cuts, -0.22, 0.18)
    return jnp.clip(raised(values, jax.random.fold_in(stream_key, 3), *heavy), -reach, reach).astype(kind)


def setup_inputs(seed: int = 0) -> dict:
    splits = jax.random.split(jax.random.key(seed), 20)
    inputs = gaussian(splits[0], (MB, L, D), 1.0, 6.0, ((1, 32),))
    encoder_out = gaussian(splits[1], (MB, E, D), 1.0, 6.0, ((1, 32),))
    out_cotangent = noise_with(splits[2], (MB, L, D), 1.0, 6.0, ((1, 32),), (1, 2, 32, 2.75))
    bucket_ids = draw_bucket_ids(jax.random.fold_in(splits[19], 71), 0)
    position_table = gaussian(splits[4], (HEADS, NB), 1.0, 4.0, (), jnp.float32)
    self_gain = jnp.clip(1.0 + 0.1 * jax.random.normal(splits[5], (D,), jnp.float32), 0.5, 1.5)
    self_query = gaussian(splits[6], (D, HEADS * HEAD), D ** -0.5, 0.1875, ((0, 16), (1, 2)))
    self_key = gaussian(splits[7], (D, KV * HEAD), D ** -0.5, 0.1875, ((0, 16), (1, 2)))
    self_value = gaussian(splits[8], (D, KV * HEAD), D ** -0.5, 0.1875, ((0, 16), (1, 2)))
    self_output = gaussian(splits[9], (HEADS * HEAD, D), (max(1, HEADS * HEAD // 512)) ** -0.5, 4.0, ((0, 2), (1, 16)))
    cross_gain = jnp.clip(1.0 + 0.1 * jax.random.normal(splits[10], (D,), jnp.float32), 0.5, 1.5)
    cross_query = gaussian(splits[11], (D, HEADS * HEAD), D ** -0.5, 0.1875, ((0, 16), (1, 2)))
    cross_key = gaussian(splits[12], (D, KV * HEAD), D ** -0.5, 0.1875, ((0, 16), (1, 2)))
    cross_value = gaussian(splits[13], (D, KV * HEAD), D ** -0.5, 0.1875, ((0, 16), (1, 2)))
    cross_output = gaussian(splits[14], (HEADS * HEAD, D), (max(1, HEADS * HEAD // 128)) ** -0.5, 2.0, ((0, 2), (1, 16)))
    feed_gain = jnp.clip(1.0 + 0.1 * jax.random.normal(splits[15], (D,), jnp.float32), 0.5, 1.5)
    gate_weight = gaussian(splits[16], (D, FF), D ** -0.5, 0.1875, ((0, 16), (1, 2)))
    up_weight = gaussian(splits[17], (D, FF), D ** -0.5, 0.1875, ((0, 16), (1, 2)))
    down_weight = gaussian(splits[18], (FF, D), FF ** -0.5, 0.109375, ((0, 2), (1, 16)))
    return {"inputs": inputs, "encoder_out": encoder_out, "out_cotangent": out_cotangent, "bucket_ids": bucket_ids, "position_table": position_table, "self_gain": self_gain, "self_query": self_query, "self_key": self_key, "self_value": self_value, "self_output": self_output, "cross_gain": cross_gain, "cross_query": cross_query, "cross_key": cross_key, "cross_value": cross_value, "cross_output": cross_output, "feed_gain": feed_gain, "gate_weight": gate_weight, "up_weight": up_weight, "down_weight": down_weight}


norm_eps = 1e-06
masked_score = -1e+30
highest = lax.Precision.HIGHEST

@jax.custom_vjp
def low(v):
    return lax.optimization_barrier(v.astype(jnp.bfloat16)).astype(jnp.float32)

@jax.custom_vjp
def low_back(v):
    return v

def low_keep(v):
    return (low(v), None)

def low_pass(kept, grad):
    return (grad,)

def back_keep(v):
    return (v, None)

def back_low(kept, grad):
    return (low(grad),)
low.defvjp(low_keep, low_pass)
low_back.defvjp(back_keep, back_low)

def matmul(left, right):
    return jnp.dot(left, right, precision=highest)

def norm_rows(row_values, gain):
    return row_values * lax.rsqrt(lax.optimization_barrier(jnp.mean(row_values * row_values, axis=-1, keepdims=True)) + norm_eps) * gain

def self_attend(queries, keys, values, bias_rows):
    length = queries.shape[0]
    block_rows = math.gcd(length, 512)
    group_size = HEADS // KV
    score_scale = HEAD ** (-0.5)
    query_heads = queries.reshape(length, KV, group_size, HEAD)
    key_heads = keys.reshape(length, KV, HEAD)
    value_heads = values.reshape(length, KV, HEAD)
    columns = jnp.arange(length, dtype=jnp.int32)

    def one_block(block_start):
        query_block = lax.dynamic_slice_in_dim(query_heads, block_start, block_rows, 0)
        raw_scores = jnp.einsum('ikgd,jkd->kgij', query_block, key_heads, precision=highest)
        offsets = block_start + jnp.arange(block_rows, dtype=jnp.int32)[:, None] - columns[None, :]
        bias_values = jnp.take(bias_rows, jnp.clip(offsets, 0, length - 1), axis=1).reshape(KV, group_size, block_rows, length)
        scores = jnp.where(offsets >= 0, low_back(score_scale * raw_scores) + bias_values, masked_score)
        attention = low(jax.nn.softmax(scores, axis=-1))
        return jnp.einsum('kgij,jkd->ikgd', attention, value_heads, precision=highest).reshape(block_rows, HEADS * HEAD)
    starts = jnp.arange(0, length, block_rows, dtype=jnp.int32)
    return lax.map(jax.checkpoint(one_block), starts).reshape(length, HEADS * HEAD)

def cross_attend(queries, keys, values):
    length = queries.shape[0]
    rows_enc = keys.shape[0]
    group_size = HEADS // KV
    score_scale = HEAD ** (-0.5)
    query_heads = queries.reshape(length, KV, group_size, HEAD)
    key_heads = keys.reshape(rows_enc, KV, HEAD)
    value_heads = values.reshape(rows_enc, KV, HEAD)
    raw_scores = jnp.einsum('ikgd,jkd->kgij', query_heads, key_heads, precision=highest)
    attention = low(jax.nn.softmax(low_back(score_scale * raw_scores), axis=-1))
    return jnp.einsum('kgij,jkd->ikgd', attention, value_heads, precision=highest).reshape(length, HEADS * HEAD)

def layer(inputs, encoded, bucket_ids, position_table, self_gain, self_query, self_key, self_value, self_output, cross_gain, cross_query, cross_key, cross_value, cross_output, feed_gain, gate_weight, up_weight, down_weight):
    normed_self = low(norm_rows(inputs, self_gain))
    queries = low(low_back(matmul(normed_self, self_query)))
    keys = low(low_back(matmul(normed_self, self_key)))
    values = low(low_back(matmul(normed_self, self_value)))
    context = low(low_back(self_attend(queries, keys, values, position_table[:, bucket_ids])))
    after_self = inputs + low_back(matmul(context, self_output))
    normed_cross = low(norm_rows(after_self, cross_gain))
    cross_queries = low(low_back(matmul(normed_cross, cross_query)))
    cross_keys = low(low_back(matmul(encoded, cross_key)))
    cross_values = low(low_back(matmul(encoded, cross_value)))
    cross_context = low(low_back(cross_attend(cross_queries, cross_keys, cross_values)))
    after_cross = after_self + low_back(matmul(cross_context, cross_output))
    normed_feed = low(norm_rows(after_cross, feed_gain))
    gate_values = low_back(matmul(normed_feed, gate_weight))
    up_values = low_back(matmul(normed_feed, up_weight))
    hidden = low(jax.nn.gelu(gate_values, approximate=True) * up_values)
    return after_cross + low_back(matmul(hidden, down_weight))

def reference(inputs, encoder_out, out_cotangent, bucket_ids, position_table, self_gain, self_query, self_key, self_value, self_output, cross_gain, cross_query, cross_key, cross_value, cross_output, feed_gain, gate_weight, up_weight, down_weight):
    weights = tuple((weight.astype(jnp.float32) for weight in (position_table, self_gain, self_query, self_key, self_value, self_output, cross_gain, cross_query, cross_key, cross_value, cross_output, feed_gain, gate_weight, up_weight, down_weight)))

    def apply_layer(seq_rows, encoded, *params):
        return layer(seq_rows, encoded, bucket_ids, *params)

    def one_batch(totals, batch_data):
        seq_rows, encoded, cotangent = batch_data
        result, pullback = jax.vjp(apply_layer, seq_rows, encoded, *weights)
        all_grads = pullback(cotangent)
        totals = tuple((summed + fresh for summed, fresh in zip(totals, all_grads[2:])))
        return (totals, (result.astype(jnp.bfloat16), all_grads[0], all_grads[1]))
    initial = tuple((jnp.zeros_like(weight) for weight in weights))
    totals, stacked = lax.scan(one_batch, initial, (inputs.astype(jnp.float32), encoder_out.astype(jnp.float32), out_cotangent.astype(jnp.float32)))
    return (stacked[0], stacked[1], stacked[2], totals[0], totals[1], totals[2], totals[3], totals[4], totals[5], totals[6], totals[7], totals[8], totals[9], totals[10], totals[11], totals[12], totals[13], totals[14])
```

```python
import functools
import math
import types

import jax
import jax.numpy as jnp
from jax import lax
from jax.experimental import pallas as pl
from jax.experimental.pallas import tpu as pltpu
from jax.sharding import PartitionSpec as P

norm_eps = 1e-06
masked_score = -1e30
highest = lax.Precision.HIGHEST
key_block_width = 256
tile = 256
fsdp_axis, tensor_axis = "fsdp", "tensor"


def matmul(left, right):
    return jnp.dot(left, right, preferred_element_type=jnp.float32)


def norm_rows(row_block, gain):
    return (
        row_block
        * lax.rsqrt(jnp.mean(row_block * row_block, axis=-1, keepdims=True) + norm_eps)
        * gain
    )


def gather_rows(row_block):
    return lax.all_gather(row_block, tensor_axis, axis=0, tiled=True)


def sum_rows(row_block):
    return lax.psum_scatter(
        row_block.astype(jnp.bfloat16), tensor_axis, scatter_dimension=0, tiled=True
    ).astype(jnp.float32)


def gather_weights(shards):
    (
        self_query,
        self_key,
        self_value,
        self_output,
        cross_query,
        cross_key,
        cross_value,
        cross_output,
        gate_weight,
        up_weight,
        down_weight,
    ) = shards
    inner = (
        lax.all_gather(self_query, fsdp_axis, axis=0, tiled=True),
        lax.all_gather(self_key, fsdp_axis, axis=0, tiled=True),
        lax.all_gather(self_value, fsdp_axis, axis=0, tiled=True),
        lax.all_gather(cross_query, fsdp_axis, axis=0, tiled=True),
        lax.all_gather(cross_key, fsdp_axis, axis=0, tiled=True),
        lax.all_gather(cross_value, fsdp_axis, axis=0, tiled=True),
        lax.all_gather(gate_weight, fsdp_axis, axis=0, tiled=True),
        lax.all_gather(up_weight, fsdp_axis, axis=0, tiled=True),
    )
    outer = (
        lax.all_gather(self_output, fsdp_axis, axis=1, tiled=True),
        lax.all_gather(cross_output, fsdp_axis, axis=1, tiled=True),
        lax.all_gather(down_weight, fsdp_axis, axis=1, tiled=True),
    )
    return (
        inner[0],
        inner[1],
        inner[2],
        outer[0],
        inner[3],
        inner[4],
        inner[5],
        outer[1],
        inner[6],
        inner[7],
        outer[2],
    )


def scatter_grads(grads_full):
    (
        self_query,
        self_key,
        self_value,
        self_output,
        cross_query,
        cross_key,
        cross_value,
        cross_output,
        gate_weight,
        up_weight,
        down_weight,
    ) = grads_full
    inner = (
        lax.psum_scatter(self_query, fsdp_axis, scatter_dimension=0, tiled=True),
        lax.psum_scatter(self_key, fsdp_axis, scatter_dimension=0, tiled=True),
        lax.psum_scatter(self_value, fsdp_axis, scatter_dimension=0, tiled=True),
        lax.psum_scatter(cross_query, fsdp_axis, scatter_dimension=0, tiled=True),
        lax.psum_scatter(cross_key, fsdp_axis, scatter_dimension=0, tiled=True),
        lax.psum_scatter(cross_value, fsdp_axis, scatter_dimension=0, tiled=True),
        lax.psum_scatter(gate_weight, fsdp_axis, scatter_dimension=0, tiled=True),
        lax.psum_scatter(up_weight, fsdp_axis, scatter_dimension=0, tiled=True),
    )
    outer = (
        lax.psum_scatter(self_output, fsdp_axis, scatter_dimension=1, tiled=True),
        lax.psum_scatter(cross_output, fsdp_axis, scatter_dimension=1, tiled=True),
        lax.psum_scatter(down_weight, fsdp_axis, scatter_dimension=1, tiled=True),
    )
    return (
        inner[0],
        inner[1],
        inner[2],
        outer[0],
        inner[3],
        inner[4],
        inner[5],
        outer[1],
        inner[6],
        inner[7],
        outer[2],
    )


def add_all(first, second):
    return tuple((left_item + right_item for left_item, right_item in zip(first, second)))


def fold_keys(key_rows, value_rows, step_fn, initial):
    return step_fn(
        initial,
        (
            lax.all_gather(key_rows, fsdp_axis, axis=0, tiled=True),
            lax.all_gather(value_rows, fsdp_axis, axis=0, tiled=True),
        ),
        jnp.int32(0),
    )


def on_device(
    inputs,
    encoder_out,
    out_cotangent,
    bucket_ids,
    position_table,
    self_gain,
    self_query,
    self_key,
    self_value,
    self_output,
    cross_gain,
    cross_query,
    cross_key,
    cross_value,
    cross_output,
    feed_gain,
    gate_weight,
    up_weight,
    down_weight,
):
    shards = (
        self_query,
        self_key,
        self_value,
        self_output,
        cross_query,
        cross_key,
        cross_value,
        cross_output,
        gate_weight,
        up_weight,
        down_weight,
    )
    batches = inputs.shape[0]
    tensor_size = lax.axis_size(tensor_axis)
    piece_rows = inputs.shape[1] * tensor_size
    length = bucket_ids.shape[0]
    heads_all = position_table.shape[0]
    buckets = position_table.shape[1]
    local_heads = heads_all // tensor_size
    head_size = self_query.shape[1] // local_heads
    kv_local = self_key.shape[1] // head_size
    group_size = local_heads // kv_local
    score_scale = head_size ** (-0.5)
    fsdp_rank = lax.axis_index(fsdp_axis)
    tensor_rank = lax.axis_index(tensor_axis)
    query_start = fsdp_rank * piece_rows
    encoder_rows = encoder_out.shape[1] * tensor_size
    table_local = lax.dynamic_slice_in_dim(
        position_table, tensor_rank * local_heads, local_heads, 0
    )
    bucket_range = jnp.arange(buckets, dtype=jnp.int32)
    lower_bounds = jnp.sum((bucket_ids[None, :] < bucket_range[:, None]).astype(jnp.int32), axis=1)
    upper_bounds = jnp.concatenate([lower_bounds[1:], jnp.full((1,), length, jnp.int32)])

    def position_bias(row_start, col_start, row_count, col_count):
        offsets = (
            row_start
            - col_start
            + jnp.arange(row_count, dtype=jnp.int32)[:, None]
            - jnp.arange(col_count, dtype=jnp.int32)[None, :]
        )
        indicator = (
            (offsets[None] >= lower_bounds[:, None, None])
            & (offsets[None] < upper_bounds[:, None, None])
        ).astype(jnp.float32)
        bias_values = jnp.einsum("hb,bij->hij", table_local, indicator, precision=highest).reshape(
            kv_local, group_size, row_count, col_count
        )
        return (bias_values, offsets >= 0, indicator)

    def split_heads(row_block):
        return row_block.reshape(row_block.shape[0], kv_local, group_size, head_size)

    def split_kv(row_block):
        return row_block.reshape(row_block.shape[0], kv_local, head_size)

    def backward(batch_index, saved_state, weights):
        (
            query_full,
            key_full,
            value_full,
            output_full,
            cross_query_full,
            cross_key_full,
            cross_value_full,
            cross_output_full,
            gate_full,
            up_full,
            down_full,
        ) = weights
        cotangent = out_cotangent[batch_index].astype(jnp.float32)
        grad_feed = gather_rows(out_cotangent[batch_index])
        hidden = saved_state.hidden
        normed_feed = saved_state.normed_feed
        down_grad = jnp.einsum("tf,td->fd", hidden, grad_feed, preferred_element_type=jnp.float32)
        grad_hidden = jnp.einsum(
            "td,fd->tf", grad_feed, down_full, preferred_element_type=jnp.float32
        )
        gelu_pull = jax.vjp(
            lambda gate_in, up_in: jax.nn.gelu(gate_in, approximate=True) * up_in,
            saved_state.gate_values,
            saved_state.up_values,
        )[1]
        grad_gate, grad_up = gelu_pull(grad_hidden)
        grad_gate = grad_gate.astype(jnp.bfloat16)
        grad_up = grad_up.astype(jnp.bfloat16)
        gate_grad = jnp.einsum(
            "td,tf->df", normed_feed, grad_gate, preferred_element_type=jnp.float32
        )
        up_grad = jnp.einsum("td,tf->df", normed_feed, grad_up, preferred_element_type=jnp.float32)
        feed_rows = sum_rows(
            jnp.einsum("tf,df->td", grad_gate, gate_full, preferred_element_type=jnp.float32)
            + jnp.einsum("tf,df->td", grad_up, up_full, preferred_element_type=jnp.float32)
        )
        grad_norm_feed, feed_gain_grad = jax.vjp(norm_rows, saved_state.after_cross, feed_gain)[
            1
        ](feed_rows)
        grad_after_cross = cotangent + grad_norm_feed
        cross_context = saved_state.cross_context
        cross_weights = saved_state.cross_weights
        encoded = saved_state.encoded
        grad_cross_branch = gather_rows(grad_after_cross.astype(jnp.bfloat16))
        cross_output_grad = jnp.einsum(
            "te,td->ed", cross_context, grad_cross_branch, preferred_element_type=jnp.float32
        )
        grad_cross_context = split_heads(
            jnp.einsum(
                "td,ed->te",
                grad_cross_branch,
                cross_output_full,
                preferred_element_type=jnp.float32,
            ).astype(jnp.bfloat16)
        )
        grad_cross_weights = jnp.einsum(
            "ikgd,jkd->kgij",
            grad_cross_context,
            split_kv(saved_state.cross_values),
            preferred_element_type=jnp.float32,
        )
        grad_cross_scores = (
            cross_weights
            * (
                grad_cross_weights
                - jnp.sum(cross_weights * grad_cross_weights, axis=-1, keepdims=True)
            )
        ).astype(jnp.bfloat16)
        grad_cross_queries = (
            (
                jnp.einsum(
                    "kgij,jkd->ikgd",
                    grad_cross_scores,
                    split_kv(saved_state.cross_keys),
                    preferred_element_type=jnp.float32,
                )
                * score_scale
            )
            .reshape(piece_rows, local_heads * head_size)
            .astype(jnp.bfloat16)
        )
        key_part = (
            jnp.einsum(
                "kgij,ikgd->jkd",
                grad_cross_scores,
                split_heads(saved_state.cross_queries),
                preferred_element_type=jnp.float32,
            )
            * score_scale
        ).reshape(encoded.shape[0], kv_local * head_size)
        value_part = jnp.einsum(
            "kgij,ikgd->jkd",
            saved_state.cross_low,
            grad_cross_context,
            preferred_element_type=jnp.float32,
        ).reshape(encoded.shape[0], kv_local * head_size)
        key_sum, value_sum = (
            lax.psum_scatter(key_part, fsdp_axis, scatter_dimension=0, tiled=True),
            lax.psum_scatter(value_part, fsdp_axis, scatter_dimension=0, tiled=True),
        )
        key_low = key_sum.astype(jnp.bfloat16)
        value_low = value_sum.astype(jnp.bfloat16)
        encoded_own = lax.dynamic_slice_in_dim(encoded, fsdp_rank * encoder_rows, encoder_rows, 0)
        cross_key_grad = jnp.einsum(
            "ed,ec->dc", encoded_own, key_low, preferred_element_type=jnp.float32
        )
        cross_value_grad = jnp.einsum(
            "ed,ec->dc", encoded_own, value_low, preferred_element_type=jnp.float32
        )
        encoder_grad = sum_rows(
            jnp.einsum("ec,dc->ed", key_low, cross_key_full, preferred_element_type=jnp.float32)
            + jnp.einsum(
                "ec,dc->ed", value_low, cross_value_full, preferred_element_type=jnp.float32
            )
        )
        cross_query_grad = jnp.einsum(
            "td,tc->dc",
            saved_state.normed_cross,
            grad_cross_queries,
            preferred_element_type=jnp.float32,
        )
        cross_rows = sum_rows(
            jnp.einsum(
                "tc,dc->td",
                grad_cross_queries,
                cross_query_full,
                preferred_element_type=jnp.float32,
            )
        )
        grad_norm_cross, cross_gain_grad = jax.vjp(
            norm_rows, saved_state.after_self, cross_gain
        )[1](cross_rows)
        grad_after_self = grad_after_cross + grad_norm_cross
        queries = saved_state.queries
        keys_own = saved_state.keys_own
        values_own = saved_state.values_own
        context = saved_state.context
        log_total = saved_state.log_total
        normed_self = saved_state.normed_self
        query_heads = split_heads(queries)
        grad_self_branch = gather_rows(grad_after_self.astype(jnp.bfloat16))
        self_output_grad = jnp.einsum(
            "te,td->ed",
            saved_state.context_low,
            grad_self_branch,
            preferred_element_type=jnp.float32,
        )
        grad_context = jnp.einsum(
            "td,ed->te", grad_self_branch, output_full, preferred_element_type=jnp.float32
        ).astype(jnp.bfloat16)
        grad_context_heads = split_heads(grad_context)
        row_delta = jnp.transpose(
            jnp.sum(grad_context_heads.astype(jnp.float32) * context, axis=-1), (1, 2, 0)
        )

        def query_step():

            def step(carried, pieces, piece_start):
                key_piece, value_piece = pieces
                piece_length = key_piece.shape[0]
                block_width = math.gcd(piece_length, key_block_width)
                block_count = piece_length // block_width
                key_blocks = key_piece.reshape(block_count, block_width, kv_local, head_size)
                value_blocks = value_piece.reshape(block_count, block_width, kv_local, head_size)
                block_starts = block_width * jnp.arange(block_count, dtype=jnp.int32)

                def step_one_block(current, block_data):
                    key_block, value_block, block_start = block_data
                    bias_values, allowed, indicator = position_bias(
                        query_start, block_start, piece_rows, block_width
                    )
                    scores = (
                        jnp.einsum(
                            "ikgd,jkd->kgij",
                            query_heads,
                            key_block,
                            preferred_element_type=jnp.float32,
                        )
                        * score_scale
                        + bias_values
                    )
                    shares = jnp.where(allowed, jnp.exp(scores - log_total[..., None]), 0.0)
                    grad_shares = jnp.einsum(
                        "ikgd,jkd->kgij",
                        grad_context_heads,
                        value_block,
                        preferred_element_type=jnp.float32,
                    )
                    grad_scores = shares * (grad_shares - row_delta[..., None])
                    bias_grad = current[1] + jnp.einsum(
                        "hij,bij->hb",
                        grad_scores.reshape(local_heads, piece_rows, block_width),
                        indicator,
                        precision=highest,
                    )
                    scores_low = grad_scores.astype(jnp.bfloat16)
                    query_grad = (
                        current[0]
                        + jnp.einsum(
                            "kgij,jkd->ikgd",
                            scores_low,
                            key_block,
                            preferred_element_type=jnp.float32,
                        )
                        * score_scale
                    )
                    key_block_grad = (
                        jnp.einsum(
                            "kgij,ikgd->jkd",
                            scores_low,
                            query_heads,
                            preferred_element_type=jnp.float32,
                        ).reshape(block_width, kv_local * head_size)
                        * score_scale
                    )
                    value_block_grad = jnp.einsum(
                        "kgij,ikgd->jkd",
                        shares.astype(jnp.bfloat16),
                        grad_context_heads,
                        preferred_element_type=jnp.float32,
                    ).reshape(block_width, kv_local * head_size)
                    keys_all = lax.dynamic_update_slice_in_dim(
                        current[2],
                        lax.dynamic_slice_in_dim(current[2], block_start, block_width, 0)
                        + key_block_grad,
                        block_start,
                        0,
                    )
                    values_all = lax.dynamic_update_slice_in_dim(
                        current[3],
                        lax.dynamic_slice_in_dim(current[3], block_start, block_width, 0)
                        + value_block_grad,
                        block_start,
                        0,
                    )
                    return ((query_grad, bias_grad, keys_all, values_all), None)

                carried, unused = lax.scan(
                    step_one_block, carried, (key_blocks, value_blocks, block_starts)
                )
                return carried

            return step

        query_zero = jnp.zeros((piece_rows, kv_local, group_size, head_size), jnp.float32)
        bias_zero = jnp.zeros((local_heads, buckets), jnp.float32)
        all_zero = jnp.zeros((length, kv_local * head_size), jnp.float32)
        query_grad, bias_grad, keys_all, values_all = fold_keys(
            keys_own, values_own, query_step(), (query_zero, bias_zero, all_zero, all_zero)
        )
        key_sum_self, value_sum_self = (
            lax.psum_scatter(keys_all, fsdp_axis, scatter_dimension=0, tiled=True),
            lax.psum_scatter(values_all, fsdp_axis, scatter_dimension=0, tiled=True),
        )
        key_grad_low = key_sum_self.astype(jnp.bfloat16)
        value_grad_low = value_sum_self.astype(jnp.bfloat16)
        query_grad_low = query_grad.reshape(piece_rows, local_heads * head_size).astype(
            jnp.bfloat16
        )
        self_query_grad = jnp.einsum(
            "td,tc->dc", normed_self, query_grad_low, preferred_element_type=jnp.float32
        )
        self_key_grad = jnp.einsum(
            "td,tc->dc", normed_self, key_grad_low, preferred_element_type=jnp.float32
        )
        self_value_grad = jnp.einsum(
            "td,tc->dc", normed_self, value_grad_low, preferred_element_type=jnp.float32
        )
        self_rows = sum_rows(
            jnp.einsum("tc,dc->td", query_grad_low, query_full, preferred_element_type=jnp.float32)
            + jnp.einsum("tc,dc->td", key_grad_low, key_full, preferred_element_type=jnp.float32)
            + jnp.einsum(
                "tc,dc->td", value_grad_low, value_full, preferred_element_type=jnp.float32
            )
        )
        grad_norm_self, self_gain_grad = jax.vjp(norm_rows, saved_state.own_rows, self_gain)[1](
            self_rows
        )
        input_grad = grad_after_self + grad_norm_self
        grads_full = (
            self_query_grad,
            self_key_grad,
            self_value_grad,
            self_output_grad,
            cross_query_grad,
            cross_key_grad,
            cross_value_grad,
            cross_output_grad,
            gate_grad,
            up_grad,
            down_grad,
        )
        extras = (bias_grad, self_gain_grad, cross_gain_grad, feed_gain_grad)
        return (grads_full, extras, input_grad, encoder_grad)

    layer_list = []
    input_list = []
    encoder_list = []
    small_sums = None
    shard_grads = None
    for batch_index in range(batches):
        weights_forward = gather_weights(shards)
        (
            forward_query_full,
            forward_key_full,
            forward_value_full,
            forward_output_full,
            forward_cross_query_full,
            forward_cross_key_full,
            forward_cross_value_full,
            forward_cross_output_full,
            forward_gate_full,
            forward_up_full,
            forward_down_full,
        ) = weights_forward
        own_rows = inputs[batch_index].astype(jnp.float32)
        forward_normed_self = gather_rows(norm_rows(own_rows, self_gain).astype(jnp.bfloat16))
        forward_queries = matmul(forward_normed_self, forward_query_full).astype(jnp.bfloat16)
        forward_keys_own = matmul(forward_normed_self, forward_key_full).astype(jnp.bfloat16)
        forward_values_own = matmul(forward_normed_self, forward_value_full).astype(jnp.bfloat16)
        forward_query_heads = split_heads(forward_queries)

        def forward_step(carried, pieces, piece_start):
            key_piece, value_piece = pieces
            piece_length = key_piece.shape[0]
            block_width = math.gcd(piece_length, key_block_width)
            block_count = piece_length // block_width
            key_blocks = key_piece.reshape(block_count, block_width, kv_local, head_size)
            value_blocks = value_piece.reshape(block_count, block_width, kv_local, head_size)
            block_starts = block_width * jnp.arange(block_count, dtype=jnp.int32)

            def forward_one_block(current, block_data):
                running_max, running_total, accumulated = current
                key_block, value_block, block_start = block_data
                bias_values, allowed, indicator = position_bias(
                    query_start, block_start, piece_rows, block_width
                )
                scores = (
                    jnp.einsum(
                        "ikgd,jkd->kgij",
                        forward_query_heads,
                        key_block,
                        preferred_element_type=jnp.float32,
                    )
                    * score_scale
                    + bias_values
                )
                scores = jnp.where(allowed, scores, masked_score)
                new_max = jnp.maximum(running_max, jnp.max(scores, axis=-1))
                factor = jnp.exp(running_max - new_max)
                shares = jnp.where(allowed, jnp.exp(scores - new_max[..., None]), 0.0)
                running_total = running_total * factor + jnp.sum(shares, axis=-1)
                update = jnp.einsum(
                    "kgij,jkd->ikgd",
                    shares.astype(jnp.bfloat16),
                    value_block,
                    preferred_element_type=jnp.float32,
                )
                accumulated = accumulated * jnp.transpose(factor, (2, 0, 1))[..., None] + update
                return ((new_max, running_total, accumulated), None)

            carried, unused = lax.scan(
                forward_one_block, carried, (key_blocks, value_blocks, block_starts)
            )
            return carried

        stat_shape = (kv_local, group_size, piece_rows)
        initial = (
            jnp.full(stat_shape, masked_score, jnp.float32),
            jnp.zeros(stat_shape, jnp.float32),
            jnp.zeros((piece_rows, kv_local, group_size, head_size), jnp.float32),
        )
        running_max, running_total, accumulated = fold_keys(
            forward_keys_own, forward_values_own, forward_step, initial
        )
        forward_context = accumulated / jnp.transpose(running_total, (2, 0, 1))[..., None]
        forward_log_total = running_max + jnp.log(running_total)
        context_low = forward_context.reshape(piece_rows, local_heads * head_size).astype(
            jnp.bfloat16
        )
        after_self = own_rows + sum_rows(matmul(context_low, forward_output_full))
        normed_cross = gather_rows(norm_rows(after_self, cross_gain).astype(jnp.bfloat16))
        cross_queries = matmul(normed_cross, forward_cross_query_full).astype(jnp.bfloat16)
        forward_encoded = lax.all_gather(
            encoder_out[batch_index], (fsdp_axis, tensor_axis), axis=0, tiled=True
        )
        cross_keys = matmul(forward_encoded, forward_cross_key_full).astype(jnp.bfloat16)
        cross_values = matmul(forward_encoded, forward_cross_value_full).astype(jnp.bfloat16)
        cross_scores = (
            jnp.einsum(
                "ikgd,jkd->kgij",
                split_heads(cross_queries),
                split_kv(cross_keys),
                preferred_element_type=jnp.float32,
            )
            * score_scale
        )
        forward_cross_weights = jax.nn.softmax(cross_scores, axis=-1)
        cross_low = forward_cross_weights.astype(jnp.bfloat16)
        forward_cross_context = (
            jnp.einsum(
                "kgij,jkd->ikgd",
                cross_low,
                split_kv(cross_values),
                preferred_element_type=jnp.float32,
            )
            .reshape(piece_rows, local_heads * head_size)
            .astype(jnp.bfloat16)
        )
        after_cross = after_self + sum_rows(
            matmul(forward_cross_context, forward_cross_output_full)
        )
        forward_normed_feed = gather_rows(norm_rows(after_cross, feed_gain).astype(jnp.bfloat16))
        gate_values = matmul(forward_normed_feed, forward_gate_full)
        up_values = matmul(forward_normed_feed, forward_up_full)
        forward_hidden = (jax.nn.gelu(gate_values, approximate=True) * up_values).astype(
            jnp.bfloat16
        )
        layer_rows = after_cross + sum_rows(matmul(forward_hidden, forward_down_full))
        forward_saved_state = types.SimpleNamespace(
            own_rows=own_rows,
            normed_self=forward_normed_self,
            queries=forward_queries,
            keys_own=forward_keys_own,
            values_own=forward_values_own,
            context=forward_context,
            log_total=forward_log_total,
            context_low=context_low,
            after_self=after_self,
            normed_cross=normed_cross,
            cross_queries=cross_queries,
            encoded=forward_encoded,
            cross_keys=cross_keys,
            cross_values=cross_values,
            cross_weights=forward_cross_weights,
            cross_low=cross_low,
            cross_context=forward_cross_context,
            after_cross=after_cross,
            normed_feed=forward_normed_feed,
            gate_values=gate_values,
            up_values=up_values,
            hidden=forward_hidden,
        )
        layer_rows, saved_state = (layer_rows.astype(jnp.bfloat16), forward_saved_state)
        weights_backward = gather_weights(shards)
        grads_full, extras, input_grad, encoder_grad = backward(
            batch_index, saved_state, weights_backward
        )
        reduced = scatter_grads(grads_full)
        shard_grads = reduced if shard_grads is None else add_all(shard_grads, reduced)
        small_sums = extras if small_sums is None else add_all(small_sums, extras)
        layer_list.append(layer_rows)
        input_list.append(input_grad)
        encoder_list.append(encoder_grad)
    table_full = lax.dynamic_update_slice_in_dim(
        jnp.zeros((heads_all, buckets), jnp.float32), small_sums[0], tensor_rank * local_heads, 0
    )
    table_sum, self_gain_sum, cross_gain_sum, feed_gain_sum = lax.psum(
        (table_full, small_sums[1], small_sums[2], small_sums[3]), (fsdp_axis, tensor_axis)
    )
    return (
        jnp.stack(layer_list),
        jnp.stack(input_list),
        jnp.stack(encoder_list),
        table_sum,
        self_gain_sum,
        shard_grads[0],
        shard_grads[1],
        shard_grads[2],
        shard_grads[3],
        cross_gain_sum,
        shard_grads[4],
        shard_grads[5],
        shard_grads[6],
        shard_grads[7],
        feed_gain_sum,
        shard_grads[8],
        shard_grads[9],
        shard_grads[10],
    )


def to_chip(fsdp):
    return dict(device_id={fsdp_axis: fsdp}, device_id_type=pl.DeviceIdType.MESH)


def chip_place(layers):
    rank = lax.axis_index(fsdp_axis)
    return rank, rank // 4, rank // 2 % 2, rank % 2


def greet_neighbours(layers):
    rank, z, y, x = chip_place(layers)
    barrier = pltpu.get_barrier_semaphore()
    pl.semaphore_signal(barrier, inc=1, **to_chip(rank + 1 - 2 * x))
    pl.semaphore_signal(barrier, inc=1, **to_chip(rank + 2 - 4 * y))

    @pl.when(z > 0)
    def _():
        pl.semaphore_signal(barrier, inc=1, **to_chip(rank - 4))

    @pl.when(z < layers - 1)
    def _():
        pl.semaphore_signal(barrier, inc=1, **to_chip(rank + 4))

    pl.semaphore_wait(barrier, 2 + (z > 0).astype(jnp.int32) + (z < layers - 1).astype(jnp.int32))


def sum_scratch(layers, cols):
    steps = 2 * layers
    bf16, dma = jnp.bfloat16, pltpu.SemaphoreType.DMA
    return [
        pltpu.VMEM((layers, 2, 2, 2, 2, 16, cols), bf16),
        pltpu.VMEM((steps, 2, 2, 16, cols), bf16),
        pltpu.VMEM((steps, 2, 16, cols), bf16),
        pltpu.VMEM((steps, 2, 16, cols), bf16),
        pltpu.VMEM((steps, 2, 16, cols), bf16),
        dma((layers,)),
        dma((2, steps, 2, 2)),
        dma((2, steps, 2)),
        dma((2, steps)),
        dma((2, steps)),
    ]


def sum_steps(layers):
    return 2 * layers + layers + 3


class GradSum:
    def __init__(self, layers, whole, out, own, first, second, below, above, load, s1, s2, su, sd):
        self.layers, self.whole, self.out, self.own = layers, whole, out, own
        self.first, self.second, self.below, self.above = first, second, below, above
        self.load, self.s1, self.s2, self.su, self.sd = load, s1, s2, su, sd
        self.rank, self.z, self.y, self.x = chip_place(layers)
        self.x_chip = self.rank + 1 - 2 * self.x
        self.y_chip = self.rank + 2 - 4 * self.y
        self.steps = 2 * layers

    def layer_of(self, n):
        turn = n // 2
        return jnp.where(turn % 2 == 1, turn // 2, self.layers - 1 - turn // 2)

    def loads(self, turn):
        layer = self.layer_of(2 * turn)
        return pltpu.make_async_copy(self.whole.at[layer], self.own.at[layer], self.load.at[turn])

    def hop_one(self, n, colour, which):
        layer, chunk = self.layer_of(n), n % 2
        if colour == 0:
            source, chip = self.own.at[layer, which, 1 - self.x, 0, chunk], self.x_chip
        else:
            source, chip = self.own.at[layer, 1 - self.y, which, 1, chunk], self.y_chip
        return pltpu.make_async_remote_copy(
            src_ref=source,
            dst_ref=self.first.at[n, colour, which],
            send_sem=self.s1.at[0, n, colour, which],
            recv_sem=self.s1.at[1, n, colour, which],
            **to_chip(chip),
        )

    def hop_two(self, n, colour):
        layer, chunk = self.layer_of(n), n % 2
        if colour == 0:
            source, chip = self.own.at[layer, 1 - self.y, self.x, 0, chunk], self.y_chip
        else:
            source, chip = self.own.at[layer, self.y, 1 - self.x, 1, chunk], self.x_chip
        return pltpu.make_async_remote_copy(
            src_ref=source,
            dst_ref=self.second.at[n, colour],
            send_sem=self.s2.at[0, n, colour],
            recv_sem=self.s2.at[1, n, colour],
            **to_chip(chip),
        )

    def hop_z(self, n, up):
        layer, chunk = self.layer_of(n), n % 2
        sems = self.su if up else self.sd
        return pltpu.make_async_remote_copy(
            src_ref=self.own.at[layer, self.y, self.x, :, chunk],
            dst_ref=(self.below if up else self.above).at[n],
            send_sem=sems.at[0, n],
            recv_sem=sems.at[1, n],
            **to_chip(self.rank + (4 if up else -4)),
        )

    def start(self):
        for turn in range(self.layers):
            self.loads(turn).start()

    def send_first(self, n):
        @pl.when(n < self.steps)
        def _():
            @pl.when(n % 2 == 0)
            def _():
                self.loads(n // 2).wait()

            for which in range(2):
                for colour in range(2):
                    self.hop_one(n, colour, which).start()

    def advance(self, m):
        steps, layers = self.steps, self.layers
        n = m - 1

        @pl.when((n >= 0) & (n < steps))
        def _():
            layer, chunk = self.layer_of(n), n % 2
            for colour in range(2):
                for other in range(2):
                    if colour == 0:
                        which = (1 - self.y) if other == 0 else self.y
                        place = (layer, which, self.x, 0, chunk)
                    else:
                        which = (1 - self.x) if other == 0 else self.x
                        place = (layer, self.y, which, 1, chunk)
                    self.hop_one_dynamic(n, colour, which).wait_recv()
                    self.own[place] = self.own[place] + self.first[n, colour, which]
                    if other == 0:
                        self.hop_two(n, colour).start()

        n2 = m - 2

        @pl.when((n2 >= 0) & (n2 < steps))
        def _():
            layer, chunk = self.layer_of(n2), n2 % 2
            for colour in range(2):
                self.hop_two(n2, colour).wait_recv()
                place = (layer, self.y, self.x, colour, chunk)
                self.own[place] = self.own[place] + self.second[n2, colour]

        for up in (True, False):
            chain = self.z if up else layers - 1 - self.z
            nz = m - 2 - chain
            layer = self.layer_of(nz)
            beyond = (layer > self.z) if up else (layer < self.z)

            @pl.when((nz >= 0) & (nz < steps) & beyond)
            def _():
                @pl.when(chain > 0)
                def _():
                    self.hop_z(nz, up).wait_recv()
                    came = self.below if up else self.above
                    for colour in range(2):
                        place = (layer, self.y, self.x, colour, nz % 2)
                        self.own[place] = self.own[place] + came[nz, colour]

                self.hop_z(nz, up).start()

        nf = m - 2 - layers

        @pl.when((nf >= 0) & (nf < steps) & (self.layer_of(nf) == self.z))
        def _():
            layer, chunk = self.layer_of(nf), nf % 2
            for colour in range(2):
                self.out[colour, chunk] = self.own[layer, self.y, self.x, colour, chunk].astype(
                    jnp.float32
                )
            for up in (True, False):
                chain = self.z if up else layers - 1 - self.z

                @pl.when(chain > 0)
                def _():
                    self.hop_z(nf, up).wait_recv()
                    came = self.below if up else self.above
                    for colour in range(2):
                        self.out[colour, chunk] += came[nf, colour].astype(jnp.float32)

    def hop_one_dynamic(self, n, colour, which):
        return self.hop_one(n, colour, which)

    def finish(self):
        def one(n, carry):
            for colour in range(2):
                for which in range(2):
                    self.hop_one(n, colour, which).wait_send()
                self.hop_two(n, colour).wait_send()
            layer = self.layer_of(n)
            for up in (True, False):

                @pl.when((layer > self.z) if up else (layer < self.z))
                def _():
                    self.hop_z(n, up).wait_send()

            return carry

        lax.fori_loop(0, self.steps, one, 0)


def rs_kernel(layers, whole, out, *scratch):
    s = GradSum(layers, whole, out, *scratch)
    s.start()
    greet_neighbours(layers)

    def body(m, c):
        s.send_first(m)
        s.advance(m)
        return c

    lax.fori_loop(0, sum_steps(layers), body, 0)
    s.finish()


def rs(g, layers=4):
    cols = g.shape[1]
    out = pl.pallas_call(
        functools.partial(rs_kernel, layers),
        name="grad_sum",
        out_shape=jax.ShapeDtypeStruct((2, 2, 16, cols), jnp.float32),
        in_specs=[pl.BlockSpec(memory_space=pl.ANY)],
        out_specs=pl.BlockSpec(memory_space=pltpu.VMEM),
        scratch_shapes=sum_scratch(layers, cols),
        compiler_params=pltpu.CompilerParams(collective_id=3, has_side_effects=True, vmem_limit_bytes=60 << 20),
    )(g.reshape(layers, 2, 2, 2, 2, 16, cols))
    return out.reshape(64, cols)

def swap_cores(block):
    return lax.ppermute(block, tensor_axis, [(0, 1), (1, 0)])


def pair_rows(block):
    other = swap_cores(block)
    first = lax.axis_index(tensor_axis) == 0
    low_rows = jnp.where(first, block, other)
    high_rows = jnp.where(first, other, block)
    return jnp.concatenate([low_rows, high_rows], axis=1)


def dot_t(left, right):
    return lax.dot_general(
        left, right, (((1,), (1,)), ((), ())), preferred_element_type=jnp.float32
    )


def dot_first(left, right):
    return lax.dot_general(
        left, right, (((0,), (0,)), ((), ())), preferred_element_type=jnp.float32
    )


def unpack_pair(qkv_ref, q_s, k_s, v_s, score_scale):
    sources, rows, _ = qkv_ref.shape
    blocks = rows // 128 * sources
    head = k_s.shape[1]
    for block in range(blocks):
        source, turn = block % sources, block // sources
        tile = qkv_ref[source, turn * 128 : (turn + 1) * 128, :]
        at = slice(block * 128, (block + 1) * 128)
        q_s[0, at, :] = (tile[:, :head] * score_scale).astype(jnp.bfloat16)
        q_s[1, at, :] = (tile[:, head : 2 * head] * score_scale).astype(jnp.bfloat16)
        k_s[at, :] = tile[:, 2 * head : 3 * head]
        v_s[at, :] = tile[:, 3 * head :]


def attend_forward_kernel(
    score_scale, qkv_ref, bias_ref, low_ref, full_ref, total_ref, q_s, k_s, v_s, bias_s, score_s
):
    blocks = bias_s.shape[1]
    sources = qkv_ref.shape[0]
    head = k_s.shape[1]
    unpack_pair(qkv_ref, q_s, k_s, v_s, score_scale)

    def make_bias(n, carry):
        row = jnp.broadcast_to(bias_ref[pl.ds(n, 1), :], (tile, 2 * tile))
        turned = pltpu.roll(row, tile + 1, 1, stride=1, stride_axis=0)
        bias_s[n // blocks, n % blocks] = turned[:, :tile]
        return carry

    lax.fori_loop(0, 2 * blocks, make_bias, 0)

    def row_block(i, carry):
        at = pl.ds(pl.multiple_of(i * tile, tile), tile)
        found = []
        for h in range(2):
            query = q_s[h, at, :]

            def score_step(j, top):
                key = k_s[pl.ds(pl.multiple_of(j * tile, tile), tile), :]
                score = dot_t(query, key) + bias_s[h, i - j]
                score_s[j] = score
                return jnp.maximum(top, jnp.maximum(score[:, :128], score[:, 128:]))

            top = lax.fori_loop(
                0, i + 1, score_step, jnp.full((tile, 128), masked_score, jnp.float32)
            )
            top = jnp.max(top, axis=1, keepdims=True)

            def share_step(j, state):
                total, summed = state
                share = jnp.exp(score_s[j] - top)
                value = v_s[pl.ds(pl.multiple_of(j * tile, tile), tile), :]
                summed = summed + jnp.dot(
                    share.astype(jnp.bfloat16), value, preferred_element_type=jnp.float32
                )
                return (total + share[:, :128] + share[:, 128:], summed)

            total, summed = lax.fori_loop(
                0,
                i + 1,
                share_step,
                (jnp.zeros((tile, 128), jnp.float32), jnp.zeros((tile, head), jnp.float32)),
            )
            total = jnp.sum(total, axis=1, keepdims=True)
            found.append(summed / total)
            log_total = jnp.broadcast_to(top + jnp.log(total), (tile, 128))
            total_ref[pl.ds(h * blocks + i, 1), :] = jnp.transpose(log_total)[0:1, :]
        both = jnp.concatenate(found, axis=1)
        full_ref[at, :] = both
        both = both.astype(jnp.bfloat16)
        for part in range(tile // 128):
            block = i * (tile // 128) + part
            low_ref[
                block % sources, pl.ds(pl.multiple_of(block // sources * 128, 128), 128), :
            ] = both[part * 128 : (part + 1) * 128]
        return carry

    lax.fori_loop(0, blocks, row_block, 0)


def attend_backward_kernel(
    score_scale,
    qkv_ref,
    grad_ref,
    full_ref,
    total_ref,
    bias_ref,
    out_ref,
    sums_ref,
    q_s,
    k_s,
    v_s,
    g_s,
    bias_s,
    sum_s,
    delta_s,
    dq_s,
    dk_s,
    dv_s,
):
    blocks = bias_s.shape[1]
    sources, rows, _ = qkv_ref.shape
    head = k_s.shape[1]
    unpack_pair(qkv_ref, q_s, k_s, v_s, score_scale)
    for block in range(rows // 128 * sources):
        source, turn = block % sources, block // sources
        part = grad_ref[source, turn * 128 : (turn + 1) * 128, :]
        at = slice(block * 128, (block + 1) * 128)
        g_s[0, at, :] = part[:, :head]
        g_s[1, at, :] = part[:, head:]

    def make_bias(n, carry):
        row = jnp.broadcast_to(bias_ref[pl.ds(n, 1), :], (tile, 2 * tile))
        turned = pltpu.roll(row, 0, 1, stride=1, stride_axis=0)
        bias_s[n // blocks, n % blocks] = turned[:, tile:]
        return carry

    lax.fori_loop(0, 2 * blocks, make_bias, 0)
    sum_s[...] = jnp.zeros_like(sum_s)
    dq_s[...] = jnp.zeros_like(dq_s)
    dk_s[...] = jnp.zeros_like(dk_s)
    dv_s[...] = jnp.zeros_like(dv_s)

    def make_delta(i, carry):
        at = pl.ds(pl.multiple_of(i * tile, tile), tile)
        for h in range(2):
            product = g_s[h, at, :].astype(jnp.float32) * full_ref[at, h * head : (h + 1) * head]
            column = jnp.broadcast_to(jnp.sum(product, axis=1, keepdims=True), (tile, 128))
            delta_s[pl.ds(h * blocks + i, 1), :] = jnp.transpose(column)[0:1, :]
        return carry

    lax.fori_loop(0, blocks, make_delta, 0)

    def diagonal(d, carry):
        def one(i, inner):
            j = i - d
            at_q = pl.ds(pl.multiple_of(i * tile, tile), tile)
            at_k = pl.ds(pl.multiple_of(j * tile, tile), tile)
            key, value = k_s[at_k, :], v_s[at_k, :]
            for h in range(2):
                query, grad = q_s[h, at_q, :], g_s[h, at_q, :]
                score = dot_t(key, query) + bias_s[h, d]
                share = jnp.exp(score - total_ref[pl.ds(h * blocks + i, 1), :])
                pull = dot_t(value, grad)
                grad_score = share * (pull - delta_s[pl.ds(h * blocks + i, 1), :])
                sum_s[h, d] += grad_score
                share_low = share.astype(jnp.bfloat16)
                grad_low = grad_score.astype(jnp.bfloat16)
                dv_s[at_k, :] += jnp.dot(share_low, grad, preferred_element_type=jnp.float32)
                dk_s[at_k, :] += jnp.dot(grad_low, query, preferred_element_type=jnp.float32)
                dq_s[h, at_q, :] += dot_first(grad_low, key)
            return inner

        return lax.fori_loop(d, blocks, one, carry)

    lax.fori_loop(0, blocks, diagonal, 0)

    for block in range(rows // 128 * sources):
        source, turn = block % sources, block // sources
        at = slice(block * 128, (block + 1) * 128)
        out_ref[source, turn * 128 : (turn + 1) * 128, :] = jnp.concatenate(
            [dq_s[0, at, :] * score_scale, dq_s[1, at, :] * score_scale, dk_s[at, :], dv_s[at, :]],
            axis=1,
        ).astype(jnp.bfloat16)

    row_at = lax.broadcasted_iota(jnp.int32, (tile, tile), 0)
    col_at = lax.broadcasted_iota(jnp.int32, (tile, tile), 1)
    turn_rows = (row_at + col_at == tile - 1).astype(jnp.float32)

    def make_sums(n, carry):
        turned = jnp.dot(
            turn_rows,
            sum_s[n // blocks, n % blocks],
            precision=highest,
            preferred_element_type=jnp.float32,
        )
        wide = jnp.concatenate([turned, jnp.zeros_like(turned)], axis=1)
        wide = pltpu.roll(wide, 0, 1, stride=1, stride_axis=0)
        sums_ref[pl.ds(n, 1), :] = jnp.sum(wide, axis=0, keepdims=True)
        return carry

    lax.fori_loop(0, 2 * blocks, make_sums, 0)


def cross_forward_kernel(score_scale, q_ref, k_ref, v_ref, out_ref):
    head = k_ref.shape[1] // 2
    for kv in range(2):
        key = k_ref[:, kv * head : (kv + 1) * head]
        value = v_ref[:, kv * head : (kv + 1) * head]
        found = []
        for h in range(2):
            at = (2 * kv + h) * head
            query = (q_ref[:, at : at + head] * score_scale).astype(jnp.bfloat16)
            score = dot_t(query, key)
            share = jnp.exp(score - jnp.max(score, axis=1, keepdims=True))
            total = jnp.sum(share, axis=1, keepdims=True)
            summed = jnp.dot(share.astype(jnp.bfloat16), value, preferred_element_type=jnp.float32)
            found.append(summed / total)
        out_ref[:, 2 * kv * head : 2 * (kv + 1) * head] = jnp.concatenate(found, axis=1).astype(
            jnp.bfloat16
        )


def cross_backward_kernel(score_scale, q_ref, k_ref, v_ref, g_ref, dq_ref, dk_ref, dv_ref):
    head = k_ref.shape[1] // 2
    key_grads, value_grads = [], []
    for kv in range(2):
        key = k_ref[:, kv * head : (kv + 1) * head]
        value = v_ref[:, kv * head : (kv + 1) * head]
        query_grads = []
        key_grad = value_grad = None
        for h in range(2):
            at = (2 * kv + h) * head
            query = (q_ref[:, at : at + head] * score_scale).astype(jnp.bfloat16)
            grad = g_ref[:, at : at + head]
            score = dot_t(key, query)
            share = jnp.exp(score - jnp.max(score, axis=0, keepdims=True))
            share = share / jnp.sum(share, axis=0, keepdims=True)
            pull = dot_t(value, grad)
            delta = jnp.sum(share * pull, axis=0, keepdims=True)
            grad_low = (share * (pull - delta)).astype(jnp.bfloat16)
            query_grads.append(dot_first(grad_low, key) * score_scale)
            more_key = jnp.dot(grad_low, query, preferred_element_type=jnp.float32)
            more_value = jnp.dot(
                share.astype(jnp.bfloat16), grad, preferred_element_type=jnp.float32
            )
            key_grad = more_key if key_grad is None else key_grad + more_key
            value_grad = more_value if value_grad is None else value_grad + more_value
        dq_ref[:, 2 * kv * head : 2 * (kv + 1) * head] = jnp.concatenate(
            query_grads, axis=1
        ).astype(jnp.bfloat16)
        key_grads.append(key_grad)
        value_grads.append(value_grad)
    dk_ref[...] = jnp.concatenate(key_grads, axis=1).astype(jnp.bfloat16)
    dv_ref[...] = jnp.concatenate(value_grads, axis=1).astype(jnp.bfloat16)


def by_heads(
    inputs,
    encoder_out,
    out_cotangent,
    bucket_ids,
    position_table,
    self_gain,
    self_query,
    self_key,
    self_value,
    self_output,
    cross_gain,
    cross_query,
    cross_key,
    cross_value,
    cross_output,
    feed_gain,
    gate_weight,
    up_weight,
    down_weight,
):
    f32, bf16 = jnp.float32, jnp.bfloat16
    batches, own, width = inputs.shape
    enc_own = encoder_out.shape[1]
    length = bucket_ids.shape[0]
    heads_all, buckets = position_table.shape
    fsdp = lax.axis_size(fsdp_axis)
    plane = fsdp // batches
    rank, core = lax.axis_index(fsdp_axis), lax.axis_index(tensor_axis)
    head = self_query.shape[1] // (heads_all // 2)
    kv_local = self_key.shape[1] // head
    scale = head ** (-0.5)
    blocks = length // tile
    rows = batches * 2 * own
    enc_rows = batches * 2 * enc_own
    feed = gate_weight.shape[1]
    across = [[z * plane + q for z in range(batches)] for q in range(plane)]
    within = [[z * plane + q for q in range(plane)] for z in range(batches)]

    def exchange(x, groups):
        return lax.all_to_all(
            x, fsdp_axis, split_axis=0, concat_axis=0, axis_index_groups=groups, tiled=True
        )

    def by_kv(weight):
        return weight.reshape(weight.shape[0], kv_local, -1)

    self_in = jnp.concatenate([by_kv(self_query), by_kv(self_key), by_kv(self_value)], axis=2)
    self_in = self_in.reshape(self_in.shape[0], -1)
    wide_self = self_in.shape[1]
    first_shard = jnp.concatenate([self_in, self_output.T], axis=1)
    rest_shard = jnp.concatenate(
        [cross_query, cross_key, cross_value, cross_output.T, gate_weight, up_weight, down_weight.T],
        axis=1,
    )
    first_full = lax.all_gather(first_shard, fsdp_axis, axis=0, tiled=True)
    rest_full = lax.all_gather(rest_shard, fsdp_axis, axis=0, tiled=True)
    in_full, out_full = first_full[:, :wide_self], first_full[:, wide_self:]
    cuts = [
        cross_query.shape[1],
        cross_key.shape[1],
        cross_value.shape[1],
        cross_output.shape[0],
        feed,
        feed,
        feed,
    ]

    def split(x):
        pieces, at = [], 0
        for cut in cuts:
            pieces.append(x[:, at : at + cut])
            at += cut
        return pieces

    cq_full, ck_full, cv_full, co_full, gate_full, up_full, down_full = split(rest_full)

    started = jnp.concatenate([inputs, out_cotangent, encoder_out], axis=1)
    started = pair_rows(exchange(started, across))
    half = started.reshape(batches, 2, 2 * own + enc_own, width)
    x_rows = half[:, :, :own].reshape(rows, width).astype(f32)
    cot_low = half[:, :, own : 2 * own].reshape(rows, width)
    enc_here = half[:, :, 2 * own :].reshape(enc_rows, width)

    kv_index = core * kv_local + rank % plane
    table_here = lax.dynamic_slice_in_dim(position_table, 2 * kv_index, 2, 0)
    bucket_range = jnp.arange(buckets, dtype=jnp.int32)
    lower = jnp.sum((bucket_ids[None, :] < bucket_range[:, None]).astype(jnp.int32), axis=1)
    upper = jnp.concatenate([lower[1:], jnp.full((1,), length, jnp.int32)])
    offsets = (
        tile * jnp.arange(blocks, dtype=jnp.int32)[:, None]
        + jnp.arange(2 * tile, dtype=jnp.int32)[None, :]
    ).reshape(-1)

    def bias_of(offset):
        hit = (offset[None] >= lower[:, None]) & (offset[None] < upper[:, None])
        value = jnp.dot(table_here, hit.astype(f32), precision=highest)
        return jnp.where(offset[None] >= 0, value, masked_score).reshape(2 * blocks, 2 * tile)

    down_steps = (
        tile * jnp.arange(blocks, dtype=jnp.int32)[:, None]
        + (tile - 1)
        - jnp.arange(2 * tile, dtype=jnp.int32)[None, :]
    ).reshape(-1)
    bias_down = bias_of(down_steps)
    bias_up = bias_of(offsets - tile)

    def norm_low(v, gain):
        return norm_rows(v, gain).astype(bf16)

    def swap_add(partial):
        low = partial.astype(bf16)
        return low.astype(f32) + swap_cores(low).astype(f32)

    normed_self = norm_low(x_rows, self_gain)
    qkv = jnp.einsum(
        "rd,dkc->krc",
        normed_self,
        in_full.reshape(width, kv_local, -1),
        preferred_element_type=f32,
    ).astype(bf16)
    qkv_here = exchange(qkv, within)
    params = pltpu.CompilerParams(vmem_limit_bytes=58 << 20)
    context_out, context_full, log_total = pl.pallas_call(
        functools.partial(attend_forward_kernel, scale),
        name="attend_forward",
        out_shape=(
            jax.ShapeDtypeStruct((plane, rows, 2 * head), bf16),
            jax.ShapeDtypeStruct((length, 2 * head), f32),
            jax.ShapeDtypeStruct((2 * blocks, tile), f32),
        ),
        scratch_shapes=[
            pltpu.VMEM((2, length, head), bf16),
            pltpu.VMEM((length, head), bf16),
            pltpu.VMEM((length, head), bf16),
            pltpu.VMEM((2, blocks, tile, tile), f32),
            pltpu.VMEM((blocks, tile, tile), f32),
        ],
        compiler_params=params,
        cost_estimate=pl.CostEstimate(
            flops=4 * length * length * head, bytes_accessed=4 << 20, transcendentals=0
        ),
    )(qkv_here, bias_down)

    def heads_last(x):
        return jnp.transpose(x, (1, 0, 2)).reshape(rows, -1)

    context_low = heads_last(exchange(context_out, within))
    after_self = x_rows + swap_add(dot_t(context_low, out_full))

    enc_all = lax.all_gather(enc_here, fsdp_axis, axis=0, axis_index_groups=within, tiled=True)
    cross_k = matmul(enc_all, ck_full).astype(bf16)
    cross_v = matmul(enc_all, cv_full).astype(bf16)
    normed_cross = norm_low(after_self, cross_gain)
    cross_q = matmul(normed_cross, cq_full).astype(bf16)
    q_cols = cross_q.shape[1]
    halves = kv_local // 2
    q_spec = pl.BlockSpec((rows, q_cols // halves), lambda i: (0, i))
    k_spec = pl.BlockSpec((cross_k.shape[0], 2 * head), lambda i: (0, i))
    cross_flops = 4 * rows * cross_k.shape[0] * head * 2 * kv_local
    cross_context = pl.pallas_call(
        functools.partial(cross_forward_kernel, scale),
        name="cross_forward",
        grid=(halves,),
        in_specs=[q_spec, k_spec, k_spec],
        out_specs=q_spec,
        out_shape=jax.ShapeDtypeStruct(cross_q.shape, bf16),
        compiler_params=params,
        cost_estimate=pl.CostEstimate(
            flops=cross_flops, bytes_accessed=2 << 20, transcendentals=0
        ),
    )(cross_q, cross_k, cross_v)
    after_cross = after_self + swap_add(dot_t(cross_context, co_full))

    normed_feed = norm_low(after_cross, feed_gain)
    gate_values = matmul(normed_feed, gate_full)
    up_values = matmul(normed_feed, up_full)

    def gated(gate_in, up_in):
        return jax.nn.gelu(gate_in, approximate=True) * up_in

    hidden_value, gelu_pull = jax.vjp(gated, gate_values, up_values)
    hidden = hidden_value.astype(bf16)
    down_part = dot_t(hidden, down_full).astype(bf16).reshape(batches, 2, own, width)

    def own_half(x):
        return lax.dynamic_index_in_dim(x, core, 1, keepdims=False)

    def other_half(x):
        return lax.dynamic_index_in_dim(x, 1 - core, 1, keepdims=False)

    def keep_half(part):
        return own_half(part).astype(f32) + swap_cores(other_half(part)).astype(f32)

    after_cross_own = own_half(after_cross.reshape(batches, 2, own, width))
    layer_rows = (after_cross_own + keep_half(down_part)).astype(bf16)
    layer_out = exchange(layer_rows, across)

    down_grad = dot_first(cot_low, hidden)
    grad_hidden = matmul(cot_low, down_full)
    grad_gate, grad_up = gelu_pull(grad_hidden)
    grad_gate, grad_up = grad_gate.astype(bf16), grad_up.astype(bf16)
    gate_grad = dot_first(normed_feed, grad_gate)
    up_grad = dot_first(normed_feed, grad_up)
    feed_rows = swap_add(dot_t(grad_gate, gate_full) + dot_t(grad_up, up_full))
    grad_feed, feed_gain_grad = jax.vjp(norm_rows, after_cross, feed_gain)[1](feed_rows)
    grad_after_cross = cot_low.astype(f32) + grad_feed

    grad_cross_low = grad_after_cross.astype(bf16)
    co_grad = dot_first(grad_cross_low, cross_context)
    grad_cross_context = matmul(grad_cross_low, co_full).astype(bf16)
    cross_dq, cross_dk, cross_dv = pl.pallas_call(
        functools.partial(cross_backward_kernel, scale),
        name="cross_backward",
        grid=(halves,),
        in_specs=[q_spec, k_spec, k_spec, q_spec],
        out_specs=(q_spec, k_spec, k_spec),
        out_shape=(
            jax.ShapeDtypeStruct(cross_q.shape, bf16),
            jax.ShapeDtypeStruct(cross_k.shape, bf16),
            jax.ShapeDtypeStruct(cross_v.shape, bf16),
        ),
        compiler_params=params,
        cost_estimate=pl.CostEstimate(
            flops=cross_flops * 5 // 2, bytes_accessed=4 << 20, transcendentals=0
        ),
    )(cross_q, cross_k, cross_v, grad_cross_context)
    cq_grad = dot_first(normed_cross, cross_dq)
    cross_rows = swap_add(dot_t(cross_dq, cq_full))
    grad_cross, cross_gain_grad = jax.vjp(norm_rows, after_self, cross_gain)[1](cross_rows)
    grad_after_self = grad_after_cross + grad_cross
    both = jnp.concatenate([cross_dk, cross_dv], axis=1).reshape(plane, enc_rows, -1)
    both = jnp.sum(exchange(both, within).astype(f32), axis=0).astype(bf16)
    dk_sum, dv_sum = both[:, : cross_dk.shape[1]], both[:, cross_dk.shape[1] :]
    ck_grad = dot_first(enc_here, dk_sum)
    cv_grad = dot_first(enc_here, dv_sum)
    enc_part = (dot_t(dk_sum, ck_full) + dot_t(dv_sum, cv_full)).astype(bf16)
    enc_grad_rows = keep_half(enc_part.reshape(batches, 2, enc_own, width)).astype(bf16)

    grad_self_low = grad_after_self.astype(bf16)
    out_grad = dot_first(grad_self_low, context_low)
    grad_context = (
        jnp.einsum(
            "rd,dkc->krc",
            grad_self_low,
            out_full.reshape(width, kv_local, -1),
            preferred_element_type=f32,
        )
    ).astype(bf16)
    grad_context_here = exchange(grad_context, within)
    grad_qkv, diagonal_sums = pl.pallas_call(
        functools.partial(attend_backward_kernel, scale),
        name="attend_backward",
        out_shape=(
            jax.ShapeDtypeStruct(qkv_here.shape, bf16),
            jax.ShapeDtypeStruct((2 * blocks, 2 * tile), f32),
        ),
        scratch_shapes=[
            pltpu.VMEM((2, length, head), bf16),
            pltpu.VMEM((length, head), bf16),
            pltpu.VMEM((length, head), bf16),
            pltpu.VMEM((2, length, head), bf16),
            pltpu.VMEM((2, blocks, tile, tile), f32),
            pltpu.VMEM((2, blocks, tile, tile), f32),
            pltpu.VMEM((2 * blocks, tile), f32),
            pltpu.VMEM((2, length, head), f32),
            pltpu.VMEM((length, head), f32),
            pltpu.VMEM((length, head), f32),
        ],
        compiler_params=params,
        cost_estimate=pl.CostEstimate(
            flops=10 * length * length * head, bytes_accessed=8 << 20, transcendentals=0
        ),
    )(qkv_here, grad_context_here, context_full, log_total, bias_up)
    grad_qkv = heads_last(exchange(grad_qkv, within))
    in_grad = dot_first(normed_self, grad_qkv)
    self_part = dot_t(grad_qkv, in_full)
    self_rows = swap_add(self_part)
    grad_self, self_gain_grad = jax.vjp(norm_rows, x_rows, self_gain)[1](self_rows)
    input_rows = own_half((grad_after_self + grad_self).reshape(batches, 2, own, width))
    ended = exchange(
        jnp.concatenate([input_rows.astype(bf16), enc_grad_rows], axis=1), across
    ).astype(f32)
    input_grad, encoder_grad = ended[:, :own], ended[:, own:]
    parts = [in_grad, out_grad, cq_grad, ck_grad, cv_grad, co_grad, gate_grad, up_grad, down_grad]
    sums = rs(jnp.concatenate([part.astype(bf16) for part in parts], axis=1), batches)

    spread = offsets - (tile - 1)
    hit = ((spread[None] >= lower[:, None]) & (spread[None] < upper[:, None])).astype(f32)
    by_offset = diagonal_sums.reshape(2, -1)
    table_here_grad = jnp.dot(by_offset, hit.T, precision=highest)
    table_full = lax.dynamic_update_slice_in_dim(
        jnp.zeros((heads_all, buckets), f32), table_here_grad, 2 * kv_index, 0
    )
    once = (core == 0).astype(f32)
    table_sum, gain_sums = lax.psum(
        (table_full, once * jnp.stack([self_gain_grad, cross_gain_grad, feed_gain_grad])),
        (fsdp_axis, tensor_axis),
    )

    q_wide = self_query.shape[1] // kv_local
    k_wide = self_key.shape[1] // kv_local
    in_sum = sums[:, :wide_self].reshape(sums.shape[0], kv_local, -1)

    def flat(x):
        return x.reshape(x.shape[0], -1)

    out_sum = sums[:, wide_self : wide_self + self_output.shape[0]]
    pieces = split(sums[:, wide_self + self_output.shape[0] :])
    return (
        layer_out,
        input_grad,
        encoder_grad,
        table_sum,
        gain_sums[0],
        flat(in_sum[:, :, :q_wide]),
        flat(in_sum[:, :, q_wide : q_wide + k_wide]),
        flat(in_sum[:, :, q_wide + k_wide :]),
        out_sum.T,
        gain_sums[1],
        pieces[0],
        pieces[1],
        pieces[2],
        pieces[3].T,
        gain_sums[2],
        pieces[4],
        pieces[5],
        pieces[6].T,
    )


def on_either(*args):
    batches, kv_heads = args[0].shape[0], args[7].shape[1] * lax.axis_size(tensor_axis)
    head_size = args[6].shape[1] * lax.axis_size(tensor_axis) // args[4].shape[0]
    devices = lax.axis_size(fsdp_axis) * lax.axis_size(tensor_axis)
    if devices == batches * (kv_heads // head_size):
        return by_heads(*args)
    return on_device(*args)


def solution(mesh):
    placed = (
        P(None, (fsdp_axis, tensor_axis), None),
        P(None, (fsdp_axis, tensor_axis), None),
        P(None, (fsdp_axis, tensor_axis), None),
        P(),
        P(),
        P(),
        P(fsdp_axis, tensor_axis),
        P(fsdp_axis, tensor_axis),
        P(fsdp_axis, tensor_axis),
        P(tensor_axis, fsdp_axis),
        P(),
        P(fsdp_axis, tensor_axis),
        P(fsdp_axis, tensor_axis),
        P(fsdp_axis, tensor_axis),
        P(tensor_axis, fsdp_axis),
        P(),
        P(fsdp_axis, tensor_axis),
        P(fsdp_axis, tensor_axis),
        P(tensor_axis, fsdp_axis),
    )
    return jax.shard_map(
        on_either,
        mesh=mesh,
        in_specs=placed,
        out_specs=(
            P(None, (fsdp_axis, tensor_axis), None),
            P(None, (fsdp_axis, tensor_axis), None),
            P(None, (fsdp_axis, tensor_axis), None),
            P(),
            P(),
            P(fsdp_axis, tensor_axis),
            P(fsdp_axis, tensor_axis),
            P(fsdp_axis, tensor_axis),
            P(tensor_axis, fsdp_axis),
            P(),
            P(fsdp_axis, tensor_axis),
            P(fsdp_axis, tensor_axis),
            P(fsdp_axis, tensor_axis),
            P(tensor_axis, fsdp_axis),
            P(),
            P(fsdp_axis, tensor_axis),
            P(fsdp_axis, tensor_axis),
            P(tensor_axis, fsdp_axis),
        ),
        check_vma=False,
    )
```

```python
import functools
import math
import types

import jax
import jax.numpy as jnp
from jax import lax
from jax.experimental import pallas as pl
from jax.experimental.pallas import tpu as pltpu
from jax.sharding import PartitionSpec as P

norm_eps = 1e-06
masked_score = -1e30
highest = lax.Precision.HIGHEST
key_block_width = 256
tile = 256
fsdp_axis, tensor_axis = "fsdp", "tensor"


def matmul(left, right):
    return jnp.dot(left, right, preferred_element_type=jnp.float32)


def norm_rows(row_block, gain):
    return (
        row_block
        * lax.rsqrt(jnp.mean(row_block * row_block, axis=-1, keepdims=True) + norm_eps)
        * gain
    )


def gather_rows(row_block):
    return lax.all_gather(row_block, tensor_axis, axis=0, tiled=True)


def sum_rows(row_block):
    return lax.psum_scatter(
        row_block.astype(jnp.bfloat16), tensor_axis, scatter_dimension=0, tiled=True
    ).astype(jnp.float32)


def gather_weights(shards):
    (
        self_query,
        self_key,
        self_value,
        self_output,
        cross_query,
        cross_key,
        cross_value,
        cross_output,
        gate_weight,
        up_weight,
        down_weight,
    ) = shards
    inner = (
        lax.all_gather(self_query, fsdp_axis, axis=0, tiled=True),
        lax.all_gather(self_key, fsdp_axis, axis=0, tiled=True),
        lax.all_gather(self_value, fsdp_axis, axis=0, tiled=True),
        lax.all_gather(cross_query, fsdp_axis, axis=0, tiled=True),
        lax.all_gather(cross_key, fsdp_axis, axis=0, tiled=True),
        lax.all_gather(cross_value, fsdp_axis, axis=0, tiled=True),
        lax.all_gather(gate_weight, fsdp_axis, axis=0, tiled=True),
        lax.all_gather(up_weight, fsdp_axis, axis=0, tiled=True),
    )
    outer = (
        lax.all_gather(self_output, fsdp_axis, axis=1, tiled=True),
        lax.all_gather(cross_output, fsdp_axis, axis=1, tiled=True),
        lax.all_gather(down_weight, fsdp_axis, axis=1, tiled=True),
    )
    return (
        inner[0],
        inner[1],
        inner[2],
        outer[0],
        inner[3],
        inner[4],
        inner[5],
        outer[1],
        inner[6],
        inner[7],
        outer[2],
    )


def scatter_grads(grads_full):
    (
        self_query,
        self_key,
        self_value,
        self_output,
        cross_query,
        cross_key,
        cross_value,
        cross_output,
        gate_weight,
        up_weight,
        down_weight,
    ) = grads_full
    inner = (
        lax.psum_scatter(self_query, fsdp_axis, scatter_dimension=0, tiled=True),
        lax.psum_scatter(self_key, fsdp_axis, scatter_dimension=0, tiled=True),
        lax.psum_scatter(self_value, fsdp_axis, scatter_dimension=0, tiled=True),
        lax.psum_scatter(cross_query, fsdp_axis, scatter_dimension=0, tiled=True),
        lax.psum_scatter(cross_key, fsdp_axis, scatter_dimension=0, tiled=True),
        lax.psum_scatter(cross_value, fsdp_axis, scatter_dimension=0, tiled=True),
        lax.psum_scatter(gate_weight, fsdp_axis, scatter_dimension=0, tiled=True),
        lax.psum_scatter(up_weight, fsdp_axis, scatter_dimension=0, tiled=True),
    )
    outer = (
        lax.psum_scatter(self_output, fsdp_axis, scatter_dimension=1, tiled=True),
        lax.psum_scatter(cross_output, fsdp_axis, scatter_dimension=1, tiled=True),
        lax.psum_scatter(down_weight, fsdp_axis, scatter_dimension=1, tiled=True),
    )
    return (
        inner[0],
        inner[1],
        inner[2],
        outer[0],
        inner[3],
        inner[4],
        inner[5],
        outer[1],
        inner[6],
        inner[7],
        outer[2],
    )


def add_all(first, second):
    return tuple((left_item + right_item for left_item, right_item in zip(first, second)))


def fold_keys(key_rows, value_rows, step_fn, initial):
    return step_fn(
        initial,
        (
            lax.all_gather(key_rows, fsdp_axis, axis=0, tiled=True),
            lax.all_gather(value_rows, fsdp_axis, axis=0, tiled=True),
        ),
        jnp.int32(0),
    )


def on_device(
    inputs,
    encoder_out,
    out_cotangent,
    bucket_ids,
    position_table,
    self_gain,
    self_query,
    self_key,
    self_value,
    self_output,
    cross_gain,
    cross_query,
    cross_key,
    cross_value,
    cross_output,
    feed_gain,
    gate_weight,
    up_weight,
    down_weight,
):
    shards = (
        self_query,
        self_key,
        self_value,
        self_output,
        cross_query,
        cross_key,
        cross_value,
        cross_output,
        gate_weight,
        up_weight,
        down_weight,
    )
    batches = inputs.shape[0]
    tensor_size = lax.axis_size(tensor_axis)
    piece_rows = inputs.shape[1] * tensor_size
    length = bucket_ids.shape[0]
    heads_all = position_table.shape[0]
    buckets = position_table.shape[1]
    local_heads = heads_all // tensor_size
    head_size = self_query.shape[1] // local_heads
    kv_local = self_key.shape[1] // head_size
    group_size = local_heads // kv_local
    score_scale = head_size ** (-0.5)
    fsdp_rank = lax.axis_index(fsdp_axis)
    tensor_rank = lax.axis_index(tensor_axis)
    query_start = fsdp_rank * piece_rows
    encoder_rows = encoder_out.shape[1] * tensor_size
    table_local = lax.dynamic_slice_in_dim(
        position_table, tensor_rank * local_heads, local_heads, 0
    )
    bucket_range = jnp.arange(buckets, dtype=jnp.int32)
    lower_bounds = jnp.sum((bucket_ids[None, :] < bucket_range[:, None]).astype(jnp.int32), axis=1)
    upper_bounds = jnp.concatenate([lower_bounds[1:], jnp.full((1,), length, jnp.int32)])

    def position_bias(row_start, col_start, row_count, col_count):
        offsets = (
            row_start
            - col_start
            + jnp.arange(row_count, dtype=jnp.int32)[:, None]
            - jnp.arange(col_count, dtype=jnp.int32)[None, :]
        )
        indicator = (
            (offsets[None] >= lower_bounds[:, None, None])
            & (offsets[None] < upper_bounds[:, None, None])
        ).astype(jnp.float32)
        bias_values = jnp.einsum("hb,bij->hij", table_local, indicator, precision=highest).reshape(
            kv_local, group_size, row_count, col_count
        )
        return (bias_values, offsets >= 0, indicator)

    def split_heads(row_block):
        return row_block.reshape(row_block.shape[0], kv_local, group_size, head_size)

    def split_kv(row_block):
        return row_block.reshape(row_block.shape[0], kv_local, head_size)

    def backward(batch_index, saved_state, weights):
        (
            query_full,
            key_full,
            value_full,
            output_full,
            cross_query_full,
            cross_key_full,
            cross_value_full,
            cross_output_full,
            gate_full,
            up_full,
            down_full,
        ) = weights
        cotangent = out_cotangent[batch_index].astype(jnp.float32)
        grad_feed = gather_rows(out_cotangent[batch_index])
        hidden = saved_state.hidden
        normed_feed = saved_state.normed_feed
        down_grad = jnp.einsum("tf,td->fd", hidden, grad_feed, preferred_element_type=jnp.float32)
        grad_hidden = jnp.einsum(
            "td,fd->tf", grad_feed, down_full, preferred_element_type=jnp.float32
        )
        gelu_pull = jax.vjp(
            lambda gate_in, up_in: jax.nn.gelu(gate_in, approximate=True) * up_in,
            saved_state.gate_values,
            saved_state.up_values,
        )[1]
        grad_gate, grad_up = gelu_pull(grad_hidden)
        grad_gate = grad_gate.astype(jnp.bfloat16)
        grad_up = grad_up.astype(jnp.bfloat16)
        gate_grad = jnp.einsum(
            "td,tf->df", normed_feed, grad_gate, preferred_element_type=jnp.float32
        )
        up_grad = jnp.einsum("td,tf->df", normed_feed, grad_up, preferred_element_type=jnp.float32)
        feed_rows = sum_rows(
            jnp.einsum("tf,df->td", grad_gate, gate_full, preferred_element_type=jnp.float32)
            + jnp.einsum("tf,df->td", grad_up, up_full, preferred_element_type=jnp.float32)
        )
        grad_norm_feed, feed_gain_grad = jax.vjp(norm_rows, saved_state.after_cross, feed_gain)[
            1
        ](feed_rows)
        grad_after_cross = cotangent + grad_norm_feed
        cross_context = saved_state.cross_context
        cross_weights = saved_state.cross_weights
        encoded = saved_state.encoded
        grad_cross_branch = gather_rows(grad_after_cross.astype(jnp.bfloat16))
        cross_output_grad = jnp.einsum(
            "te,td->ed", cross_context, grad_cross_branch, preferred_element_type=jnp.float32
        )
        grad_cross_context = split_heads(
            jnp.einsum(
                "td,ed->te",
                grad_cross_branch,
                cross_output_full,
                preferred_element_type=jnp.float32,
            ).astype(jnp.bfloat16)
        )
        grad_cross_weights = jnp.einsum(
            "ikgd,jkd->kgij",
            grad_cross_context,
            split_kv(saved_state.cross_values),
            preferred_element_type=jnp.float32,
        )
        grad_cross_scores = (
            cross_weights
            * (
                grad_cross_weights
                - jnp.sum(cross_weights * grad_cross_weights, axis=-1, keepdims=True)
            )
        ).astype(jnp.bfloat16)
        grad_cross_queries = (
            (
                jnp.einsum(
                    "kgij,jkd->ikgd",
                    grad_cross_scores,
                    split_kv(saved_state.cross_keys),
                    preferred_element_type=jnp.float32,
                )
                * score_scale
            )
            .reshape(piece_rows, local_heads * head_size)
            .astype(jnp.bfloat16)
        )
        key_part = (
            jnp.einsum(
                "kgij,ikgd->jkd",
                grad_cross_scores,
                split_heads(saved_state.cross_queries),
                preferred_element_type=jnp.float32,
            )
            * score_scale
        ).reshape(encoded.shape[0], kv_local * head_size)
        value_part = jnp.einsum(
            "kgij,ikgd->jkd",
            saved_state.cross_low,
            grad_cross_context,
            preferred_element_type=jnp.float32,
        ).reshape(encoded.shape[0], kv_local * head_size)
        key_sum, value_sum = (
            lax.psum_scatter(key_part, fsdp_axis, scatter_dimension=0, tiled=True),
            lax.psum_scatter(value_part, fsdp_axis, scatter_dimension=0, tiled=True),
        )
        key_low = key_sum.astype(jnp.bfloat16)
        value_low = value_sum.astype(jnp.bfloat16)
        encoded_own = lax.dynamic_slice_in_dim(encoded, fsdp_rank * encoder_rows, encoder_rows, 0)
        cross_key_grad = jnp.einsum(
            "ed,ec->dc", encoded_own, key_low, preferred_element_type=jnp.float32
        )
        cross_value_grad = jnp.einsum(
            "ed,ec->dc", encoded_own, value_low, preferred_element_type=jnp.float32
        )
        encoder_grad = sum_rows(
            jnp.einsum("ec,dc->ed", key_low, cross_key_full, preferred_element_type=jnp.float32)
            + jnp.einsum(
                "ec,dc->ed", value_low, cross_value_full, preferred_element_type=jnp.float32
            )
        )
        cross_query_grad = jnp.einsum(
            "td,tc->dc",
            saved_state.normed_cross,
            grad_cross_queries,
            preferred_element_type=jnp.float32,
        )
        cross_rows = sum_rows(
            jnp.einsum(
                "tc,dc->td",
                grad_cross_queries,
                cross_query_full,
                preferred_element_type=jnp.float32,
            )
        )
        grad_norm_cross, cross_gain_grad = jax.vjp(
            norm_rows, saved_state.after_self, cross_gain
        )[1](cross_rows)
        grad_after_self = grad_after_cross + grad_norm_cross
        queries = saved_state.queries
        keys_own = saved_state.keys_own
        values_own = saved_state.values_own
        context = saved_state.context
        log_total = saved_state.log_total
        normed_self = saved_state.normed_self
        query_heads = split_heads(queries)
        grad_self_branch = gather_rows(grad_after_self.astype(jnp.bfloat16))
        self_output_grad = jnp.einsum(
            "te,td->ed",
            saved_state.context_low,
            grad_self_branch,
            preferred_element_type=jnp.float32,
        )
        grad_context = jnp.einsum(
            "td,ed->te", grad_self_branch, output_full, preferred_element_type=jnp.float32
        ).astype(jnp.bfloat16)
        grad_context_heads = split_heads(grad_context)
        row_delta = jnp.transpose(
            jnp.sum(grad_context_heads.astype(jnp.float32) * context, axis=-1), (1, 2, 0)
        )

        def query_step():

            def step(carried, pieces, piece_start):
                key_piece, value_piece = pieces
                piece_length = key_piece.shape[0]
                block_width = math.gcd(piece_length, key_block_width)
                block_count = piece_length // block_width
                key_blocks = key_piece.reshape(block_count, block_width, kv_local, head_size)
                value_blocks = value_piece.reshape(block_count, block_width, kv_local, head_size)
                block_starts = block_width * jnp.arange(block_count, dtype=jnp.int32)

                def step_one_block(current, block_data):
                    key_block, value_block, block_start = block_data
                    bias_values, allowed, indicator = position_bias(
                        query_start, block_start, piece_rows, block_width
                    )
                    scores = (
                        jnp.einsum(
                            "ikgd,jkd->kgij",
                            query_heads,
                            key_block,
                            preferred_element_type=jnp.float32,
                        )
                        * score_scale
                        + bias_values
                    )
                    shares = jnp.where(allowed, jnp.exp(scores - log_total[..., None]), 0.0)
                    grad_shares = jnp.einsum(
                        "ikgd,jkd->kgij",
                        grad_context_heads,
                        value_block,
                        preferred_element_type=jnp.float32,
                    )
                    grad_scores = shares * (grad_shares - row_delta[..., None])
                    bias_grad = current[1] + jnp.einsum(
                        "hij,bij->hb",
                        grad_scores.reshape(local_heads, piece_rows, block_width),
                        indicator,
                        precision=highest,
                    )
                    scores_low = grad_scores.astype(jnp.bfloat16)
                    query_grad = (
                        current[0]
                        + jnp.einsum(
                            "kgij,jkd->ikgd",
                            scores_low,
                            key_block,
                            preferred_element_type=jnp.float32,
                        )
                        * score_scale
                    )
                    key_block_grad = (
                        jnp.einsum(
                            "kgij,ikgd->jkd",
                            scores_low,
                            query_heads,
                            preferred_element_type=jnp.float32,
                        ).reshape(block_width, kv_local * head_size)
                        * score_scale
                    )
                    value_block_grad = jnp.einsum(
                        "kgij,ikgd->jkd",
                        shares.astype(jnp.bfloat16),
                        grad_context_heads,
                        preferred_element_type=jnp.float32,
                    ).reshape(block_width, kv_local * head_size)
                    keys_all = lax.dynamic_update_slice_in_dim(
                        current[2],
                        lax.dynamic_slice_in_dim(current[2], block_start, block_width, 0)
                        + key_block_grad,
                        block_start,
                        0,
                    )
                    values_all = lax.dynamic_update_slice_in_dim(
                        current[3],
                        lax.dynamic_slice_in_dim(current[3], block_start, block_width, 0)
                        + value_block_grad,
                        block_start,
                        0,
                    )
                    return ((query_grad, bias_grad, keys_all, values_all), None)

                carried, unused = lax.scan(
                    step_one_block, carried, (key_blocks, value_blocks, block_starts)
                )
                return carried

            return step

        query_zero = jnp.zeros((piece_rows, kv_local, group_size, head_size), jnp.float32)
        bias_zero = jnp.zeros((local_heads, buckets), jnp.float32)
        all_zero = jnp.zeros((length, kv_local * head_size), jnp.float32)
        query_grad, bias_grad, keys_all, values_all = fold_keys(
            keys_own, values_own, query_step(), (query_zero, bias_zero, all_zero, all_zero)
        )
        key_sum_self, value_sum_self = (
            lax.psum_scatter(keys_all, fsdp_axis, scatter_dimension=0, tiled=True),
            lax.psum_scatter(values_all, fsdp_axis, scatter_dimension=0, tiled=True),
        )
        key_grad_low = key_sum_self.astype(jnp.bfloat16)
        value_grad_low = value_sum_self.astype(jnp.bfloat16)
        query_grad_low = query_grad.reshape(piece_rows, local_heads * head_size).astype(
            jnp.bfloat16
        )
        self_query_grad = jnp.einsum(
            "td,tc->dc", normed_self, query_grad_low, preferred_element_type=jnp.float32
        )
        self_key_grad = jnp.einsum(
            "td,tc->dc", normed_self, key_grad_low, preferred_element_type=jnp.float32
        )
        self_value_grad = jnp.einsum(
            "td,tc->dc", normed_self, value_grad_low, preferred_element_type=jnp.float32
        )
        self_rows = sum_rows(
            jnp.einsum("tc,dc->td", query_grad_low, query_full, preferred_element_type=jnp.float32)
            + jnp.einsum("tc,dc->td", key_grad_low, key_full, preferred_element_type=jnp.float32)
            + jnp.einsum(
                "tc,dc->td", value_grad_low, value_full, preferred_element_type=jnp.float32
            )
        )
        grad_norm_self, self_gain_grad = jax.vjp(norm_rows, saved_state.own_rows, self_gain)[1](
            self_rows
        )
        input_grad = grad_after_self + grad_norm_self
        grads_full = (
            self_query_grad,
            self_key_grad,
            self_value_grad,
            self_output_grad,
            cross_query_grad,
            cross_key_grad,
            cross_value_grad,
            cross_output_grad,
            gate_grad,
            up_grad,
            down_grad,
        )
        extras = (bias_grad, self_gain_grad, cross_gain_grad, feed_gain_grad)
        return (grads_full, extras, input_grad, encoder_grad)

    layer_list = []
    input_list = []
    encoder_list = []
    small_sums = None
    shard_grads = None
    for batch_index in range(batches):
        weights_forward = gather_weights(shards)
        (
            forward_query_full,
            forward_key_full,
            forward_value_full,
            forward_output_full,
            forward_cross_query_full,
            forward_cross_key_full,
            forward_cross_value_full,
            forward_cross_output_full,
            forward_gate_full,
            forward_up_full,
            forward_down_full,
        ) = weights_forward
        own_rows = inputs[batch_index].astype(jnp.float32)
        forward_normed_self = gather_rows(norm_rows(own_rows, self_gain).astype(jnp.bfloat16))
        forward_queries = matmul(forward_normed_self, forward_query_full).astype(jnp.bfloat16)
        forward_keys_own = matmul(forward_normed_self, forward_key_full).astype(jnp.bfloat16)
        forward_values_own = matmul(forward_normed_self, forward_value_full).astype(jnp.bfloat16)
        forward_query_heads = split_heads(forward_queries)

        def forward_step(carried, pieces, piece_start):
            key_piece, value_piece = pieces
            piece_length = key_piece.shape[0]
            block_width = math.gcd(piece_length, key_block_width)
            block_count = piece_length // block_width
            key_blocks = key_piece.reshape(block_count, block_width, kv_local, head_size)
            value_blocks = value_piece.reshape(block_count, block_width, kv_local, head_size)
            block_starts = block_width * jnp.arange(block_count, dtype=jnp.int32)

            def forward_one_block(current, block_data):
                running_max, running_total, accumulated = current
                key_block, value_block, block_start = block_data
                bias_values, allowed, indicator = position_bias(
                    query_start, block_start, piece_rows, block_width
                )
                scores = (
                    jnp.einsum(
                        "ikgd,jkd->kgij",
                        forward_query_heads,
                        key_block,
                        preferred_element_type=jnp.float32,
                    )
                    * score_scale
                    + bias_values
                )
                scores = jnp.where(allowed, scores, masked_score)
                new_max = jnp.maximum(running_max, jnp.max(scores, axis=-1))
                factor = jnp.exp(running_max - new_max)
                shares = jnp.where(allowed, jnp.exp(scores - new_max[..., None]), 0.0)
                running_total = running_total * factor + jnp.sum(shares, axis=-1)
                update = jnp.einsum(
                    "kgij,jkd->ikgd",
                    shares.astype(jnp.bfloat16),
                    value_block,
                    preferred_element_type=jnp.float32,
                )
                accumulated = accumulated * jnp.transpose(factor, (2, 0, 1))[..., None] + update
                return ((new_max, running_total, accumulated), None)

            carried, unused = lax.scan(
                forward_one_block, carried, (key_blocks, value_blocks, block_starts)
            )
            return carried

        stat_shape = (kv_local, group_size, piece_rows)
        initial = (
            jnp.full(stat_shape, masked_score, jnp.float32),
            jnp.zeros(stat_shape, jnp.float32),
            jnp.zeros((piece_rows, kv_local, group_size, head_size), jnp.float32),
        )
        running_max, running_total, accumulated = fold_keys(
            forward_keys_own, forward_values_own, forward_step, initial
        )
        forward_context = accumulated / jnp.transpose(running_total, (2, 0, 1))[..., None]
        forward_log_total = running_max + jnp.log(running_total)
        context_low = forward_context.reshape(piece_rows, local_heads * head_size).astype(
            jnp.bfloat16
        )
        after_self = own_rows + sum_rows(matmul(context_low, forward_output_full))
        normed_cross = gather_rows(norm_rows(after_self, cross_gain).astype(jnp.bfloat16))
        cross_queries = matmul(normed_cross, forward_cross_query_full).astype(jnp.bfloat16)
        forward_encoded = lax.all_gather(
            encoder_out[batch_index], (fsdp_axis, tensor_axis), axis=0, tiled=True
        )
        cross_keys = matmul(forward_encoded, forward_cross_key_full).astype(jnp.bfloat16)
        cross_values = matmul(forward_encoded, forward_cross_value_full).astype(jnp.bfloat16)
        cross_scores = (
            jnp.einsum(
                "ikgd,jkd->kgij",
                split_heads(cross_queries),
                split_kv(cross_keys),
                preferred_element_type=jnp.float32,
            )
            * score_scale
        )
        forward_cross_weights = jax.nn.softmax(cross_scores, axis=-1)
        cross_low = forward_cross_weights.astype(jnp.bfloat16)
        forward_cross_context = (
            jnp.einsum(
                "kgij,jkd->ikgd",
                cross_low,
                split_kv(cross_values),
                preferred_element_type=jnp.float32,
            )
            .reshape(piece_rows, local_heads * head_size)
            .astype(jnp.bfloat16)
        )
        after_cross = after_self + sum_rows(
            matmul(forward_cross_context, forward_cross_output_full)
        )
        forward_normed_feed = gather_rows(norm_rows(after_cross, feed_gain).astype(jnp.bfloat16))
        gate_values = matmul(forward_normed_feed, forward_gate_full)
        up_values = matmul(forward_normed_feed, forward_up_full)
        forward_hidden = (jax.nn.gelu(gate_values, approximate=True) * up_values).astype(
            jnp.bfloat16
        )
        layer_rows = after_cross + sum_rows(matmul(forward_hidden, forward_down_full))
        forward_saved_state = types.SimpleNamespace(
            own_rows=own_rows,
            normed_self=forward_normed_self,
            queries=forward_queries,
            keys_own=forward_keys_own,
            values_own=forward_values_own,
            context=forward_context,
            log_total=forward_log_total,
            context_low=context_low,
            after_self=after_self,
            normed_cross=normed_cross,
            cross_queries=cross_queries,
            encoded=forward_encoded,
            cross_keys=cross_keys,
            cross_values=cross_values,
            cross_weights=forward_cross_weights,
            cross_low=cross_low,
            cross_context=forward_cross_context,
            after_cross=after_cross,
            normed_feed=forward_normed_feed,
            gate_values=gate_values,
            up_values=up_values,
            hidden=forward_hidden,
        )
        layer_rows, saved_state = (layer_rows.astype(jnp.bfloat16), forward_saved_state)
        weights_backward = gather_weights(shards)
        grads_full, extras, input_grad, encoder_grad = backward(
            batch_index, saved_state, weights_backward
        )
        reduced = scatter_grads(grads_full)
        shard_grads = reduced if shard_grads is None else add_all(shard_grads, reduced)
        small_sums = extras if small_sums is None else add_all(small_sums, extras)
        layer_list.append(layer_rows)
        input_list.append(input_grad)
        encoder_list.append(encoder_grad)
    table_full = lax.dynamic_update_slice_in_dim(
        jnp.zeros((heads_all, buckets), jnp.float32), small_sums[0], tensor_rank * local_heads, 0
    )
    table_sum, self_gain_sum, cross_gain_sum, feed_gain_sum = lax.psum(
        (table_full, small_sums[1], small_sums[2], small_sums[3]), (fsdp_axis, tensor_axis)
    )
    return (
        jnp.stack(layer_list),
        jnp.stack(input_list),
        jnp.stack(encoder_list),
        table_sum,
        self_gain_sum,
        shard_grads[0],
        shard_grads[1],
        shard_grads[2],
        shard_grads[3],
        cross_gain_sum,
        shard_grads[4],
        shard_grads[5],
        shard_grads[6],
        shard_grads[7],
        feed_gain_sum,
        shard_grads[8],
        shard_grads[9],
        shard_grads[10],
    )


def to_chip(fsdp):
    return dict(device_id={fsdp_axis: fsdp}, device_id_type=pl.DeviceIdType.MESH)


def to_core(core):
    return dict(device_id={tensor_axis: core}, device_id_type=pl.DeviceIdType.MESH)


def chip_place(layers):
    rank = lax.axis_index(fsdp_axis)
    return rank, rank // 4, rank // 2 % 2, rank % 2


def peers_of(rank, y, x):
    found = []
    for o in (1, 2, 3):
        other_y = 1 - y if o & 2 else y
        other_x = 1 - x if o & 1 else x
        spot = 2 * other_y + other_x
        found.append((rank - 2 * y - x + spot, spot))
    return found


def greet(layers):
    rank, z, y, x = chip_place(layers)
    barrier = pltpu.get_barrier_semaphore()
    for chip, spot in peers_of(rank, y, x):
        pl.semaphore_signal(barrier, inc=1, **to_chip(chip))
    for o in range(1, layers):
        pl.semaphore_signal(barrier, inc=1, **to_chip(rank - 4 * z + 4 * ((z + o) % layers)))
    pl.semaphore_signal(barrier, inc=1, **to_core(1 - lax.axis_index(tensor_axis)))
    pl.semaphore_wait(barrier, 3 + layers)


dma = pltpu.SemaphoreType.DMA


class Column:
    def __init__(self, layers, source, land, z_sem, core_sem=None):
        self.layers, self.source, self.land = layers, source, land
        self.z_sem, self.core_sem = z_sem, core_sem
        self.rank, self.z, self.y, self.x = chip_place(layers)
        self.core = lax.axis_index(tensor_axis)

    def place(self, layer):
        return (layer,) if self.core_sem is None else (layer, self.core)

    def hop(self, o):
        there = (self.z + o) % self.layers
        return pltpu.make_async_remote_copy(
            src_ref=self.source.at[there],
            dst_ref=self.land.at[self.place(self.z)],
            send_sem=self.z_sem.at[0, o],
            recv_sem=self.z_sem.at[1, self.z],
            **to_chip(self.rank + 4 * (there - self.z)),
        )

    def arrival(self, layer):
        return pltpu.make_async_remote_copy(
            src_ref=self.source.at[0],
            dst_ref=self.land.at[self.place(layer)],
            send_sem=self.z_sem.at[0, 0],
            recv_sem=self.z_sem.at[1, layer],
            **to_chip(self.rank + 4 - 8 * (self.z // 2)),
        )

    def over(self, layer):
        return pltpu.make_async_remote_copy(
            src_ref=self.land.at[layer, self.core],
            dst_ref=self.land.at[layer, self.core],
            send_sem=self.core_sem.at[0, layer],
            recv_sem=self.core_sem.at[1, layer],
            **to_core(1 - self.core),
        )

    def start(self):
        for o in range(1, self.layers):
            self.hop(o).start()
        self.land[self.place(self.z)] = self.source[self.z]

    def arrive(self):
        for o in range(1, self.layers):
            self.arrival((self.z + o) % self.layers).wait_recv()
        if self.core_sem is not None:
            for layer in range(self.layers):
                self.over(layer).start()

    def finish(self):
        for o in range(1, self.layers):
            self.hop(o).wait_send()
        if self.core_sem is not None:
            for layer in range(self.layers):
                self.over(layer).wait()


class PlaneSwap:
    def __init__(self, layers, source, land, sem):
        self.source, self.land, self.sem = source, land, sem
        self.rank, self.z, self.y, self.x = chip_place(layers)
        self.spot = 2 * self.y + self.x
        self.peers = peers_of(self.rank, self.y, self.x)

    def hop(self, o):
        chip, there = self.peers[o]
        return pltpu.make_async_remote_copy(
            src_ref=self.source.at[there],
            dst_ref=self.land.at[self.spot],
            send_sem=self.sem.at[0, o],
            recv_sem=self.sem.at[1, o],
            **to_chip(chip),
        )

    def start(self):
        for o in range(3):
            self.hop(o).start()
        self.land[self.spot] = self.source[self.spot]

    def arrival(self, o):
        chip, there = self.peers[o]
        return pltpu.make_async_remote_copy(
            src_ref=self.source.at[there],
            dst_ref=self.land.at[there],
            send_sem=self.sem.at[0, o],
            recv_sem=self.sem.at[1, o],
            **to_chip(chip),
        )

    def arrive(self):
        for o in range(3):
            self.arrival(o).wait_recv()

    def finish(self):
        for o in range(3):
            self.hop(o).wait_send()


class PlaneGather:
    def __init__(self, layers, source, land, sem, core_sem):
        self.source, self.land, self.sem, self.core_sem = source, land, sem, core_sem
        self.rank, self.z, self.y, self.x = chip_place(layers)
        self.core = lax.axis_index(tensor_axis)
        self.spot = 2 * self.y + self.x
        self.peers = peers_of(self.rank, self.y, self.x)

    def hop(self, o, spot):
        return pltpu.make_async_remote_copy(
            src_ref=self.source,
            dst_ref=self.land.at[spot, self.core],
            send_sem=self.sem.at[0, o],
            recv_sem=self.sem.at[1, o],
            **to_chip(self.peers[o][0]),
        )

    def over(self, spot):
        return pltpu.make_async_remote_copy(
            src_ref=self.land.at[spot, self.core],
            dst_ref=self.land.at[spot, self.core],
            send_sem=self.core_sem.at[0, spot],
            recv_sem=self.core_sem.at[1, spot],
            **to_core(1 - self.core),
        )

    def start(self):
        for o in range(3):
            self.hop(o, self.spot).start()
        self.land[self.spot, self.core] = self.source[...]

    def arrive(self):
        for o in range(3):
            self.hop(o, self.peers[o][1]).wait_recv()
        for spot in range(4):
            self.over(spot).start()

    def finish(self):
        for o in range(3):
            self.hop(o, self.spot).wait_send()
        for spot in range(4):
            self.over(spot).wait()


def open_kernel(
    layers,
    rows_ref,
    enc_ref,
    shard_ref,
    rows_out,
    enc_out,
    whole_ref,
    rows_land,
    enc_land,
    enc_all,
    rows_z,
    rows_core,
    enc_z,
    plane_sem,
    plane_core,
    *gather_refs,
):
    gather = RowGather(layers, shard_ref, whole_ref, *gather_refs)
    rows = Column(layers, rows_ref, rows_land, rows_z, rows_core)
    enc = Column(layers, enc_ref, enc_land, enc_z)
    plane = PlaneGather(layers, enc_land, enc_all, plane_sem, plane_core)
    gather.begin()
    greet(layers)
    rows.start()
    enc.start()
    gather.send_own()
    rows.arrive()
    enc.arrive()
    plane.start()

    def one(m, carry):
        gather.step(m)
        return carry

    lax.fori_loop(0, 2 * layers - 4, one, 0)
    plane.arrive()
    lax.fori_loop(2 * layers - 4, 2 * layers, one, 0)
    rows.finish()
    rows_out[...] = rows_land[...]
    enc.finish()
    plane.finish()
    enc_out[...] = enc_all[...]
    gather.finish()


def open_rows(layers, inputs, encoder, shard):
    bf16 = jnp.bfloat16
    own, width = inputs.shape[1:]
    enc_own = encoder.shape[1]
    cols = shard.shape[1]
    vmem, anywhere = pl.BlockSpec(memory_space=pltpu.VMEM), pl.BlockSpec(memory_space=pl.ANY)
    rows_shape, enc_shape = (layers, 2, own, width), (4, 2, layers, enc_own, width)
    rows, enc, whole = pl.pallas_call(
        functools.partial(open_kernel, layers),
        name="open_rows",
        out_shape=(
            jax.ShapeDtypeStruct(rows_shape, bf16),
            jax.ShapeDtypeStruct(enc_shape, bf16),
            jax.ShapeDtypeStruct((layers, 2, 2, 2, 2, 16, cols), bf16),
        ),
        in_specs=[vmem, vmem, anywhere],
        out_specs=(vmem, vmem, anywhere),
        scratch_shapes=[
            pltpu.VMEM(rows_shape, bf16),
            pltpu.VMEM((layers, enc_own, width), bf16),
            pltpu.VMEM(enc_shape, bf16),
            dma((2, layers)),
            dma((2, layers)),
            dma((2, layers)),
            dma((2, 3)),
            dma((2, 4)),
            *gather_scratch(layers, cols),
        ],
        compiler_params=pltpu.CompilerParams(collective_id=5, has_side_effects=True),
    )(inputs, encoder, shard.reshape(2, 2, 16, cols))
    return rows, enc, whole.reshape(layers * 256, cols)


def close_kernel(
    layers,
    grads_ref,
    rows_ref,
    small_ref,
    sum_ref,
    rows_out,
    small_out,
    rows_land,
    small_x,
    small_y,
    small_z,
    small_c,
    small_s,
    rows_z,
    small_sem,
    z_sem,
    *sum_refs,
):
    grads = GradSum(layers, grads_ref, sum_ref, *sum_refs)
    rows = Column(layers, rows_ref, rows_land, rows_z)
    rank, z, y, x = chip_place(layers)
    core = lax.axis_index(tensor_axis)
    grads.start()
    greet(layers)
    grads.send_first(0)
    rows.start()

    def swap(source, land, n, where):
        return pltpu.make_async_remote_copy(
            src_ref=source,
            dst_ref=land,
            send_sem=small_sem.at[0, n],
            recv_sem=small_sem.at[1, n],
            **where,
        )

    across_x = swap(small_ref, small_x, 0, to_chip(rank + 1 - 2 * x))
    across_y = swap(small_s.at[0], small_y, 1, to_chip(rank + 2 - 4 * y))
    across_core = swap(small_s.at[2], small_c, 2, to_core(1 - core))

    def across_z(o, layer):
        there = (z + o) % layers
        return pltpu.make_async_remote_copy(
            src_ref=small_s.at[1],
            dst_ref=small_z.at[layer],
            send_sem=z_sem.at[0, o],
            recv_sem=z_sem.at[1, layer],
            **to_chip(rank + 4 * (there - z)),
        )

    across_x.start()
    across_x.wait()
    small_s[0] = small_ref[...] + small_x[...]
    grads.send_first(1)
    grads.advance(1)
    across_y.start()
    across_y.wait()
    small_s[1] = small_s[0] + small_y[...]
    small_z[z] = small_s[1]
    for o in range(1, layers):
        across_z(o, z).start()
    grads.send_first(2)
    grads.advance(2)
    for o in range(1, layers):
        across_z(o, (z + o) % layers).wait_recv()
        across_z(o, z).wait_send()
    total = small_z[0]
    for layer in range(1, layers):
        total = total + small_z[layer]
    small_s[2] = total
    across_core.start()

    def one(m, carry):
        grads.send_first(m)
        grads.advance(m)
        return carry

    lax.fori_loop(3, sum_steps(layers), one, 0)
    across_core.wait()
    low = jnp.where(core == 0, small_s[2], small_c[...])
    row = lax.broadcasted_iota(jnp.int32, low.shape, 0)
    small_out[...] = jnp.where(row == 3, small_s[2] + small_c[...], low)
    rows.arrive()
    rows_out[...] = rows_land[...].astype(jnp.float32)
    rows.finish()
    grads.finish()


def close_rows(layers, grads, rows, small):
    f32, bf16 = jnp.float32, jnp.bfloat16
    cols = grads.shape[1]
    vmem, anywhere = pl.BlockSpec(memory_space=pltpu.VMEM), pl.BlockSpec(memory_space=pl.ANY)
    sums, rows_full, small_full = pl.pallas_call(
        functools.partial(close_kernel, layers),
        name="close_rows",
        out_shape=(
            jax.ShapeDtypeStruct((2, 2, 16, cols), f32),
            jax.ShapeDtypeStruct(rows.shape, f32),
            jax.ShapeDtypeStruct(small.shape, f32),
        ),
        in_specs=[anywhere, vmem, vmem],
        out_specs=(vmem, vmem, vmem),
        scratch_shapes=[
            pltpu.VMEM(rows.shape, bf16),
            pltpu.VMEM(small.shape, f32),
            pltpu.VMEM(small.shape, f32),
            pltpu.VMEM((layers, *small.shape), f32),
            pltpu.VMEM(small.shape, f32),
            pltpu.VMEM((3, *small.shape), f32),
            dma((2, layers)),
            dma((2, 3)),
            dma((2, layers)),
            *sum_scratch(layers, cols),
        ],
        compiler_params=pltpu.CompilerParams(
            collective_id=7, has_side_effects=True, vmem_limit_bytes=40 << 20
        ),
    )(grads.reshape(layers, 2, 2, 2, 2, 16, cols), rows, small)
    return sums.reshape(-1, cols), rows_full, small_full

def sum_scratch(layers, cols):
    steps = 2 * layers
    bf16 = jnp.bfloat16
    return [
        pltpu.VMEM((layers, 2, 2, 2, 2, 16, cols), bf16),
        pltpu.VMEM((steps, 2, 2, 16, cols), bf16),
        pltpu.VMEM((steps, 2, 16, cols), bf16),
        pltpu.VMEM((steps, 2, 16, cols), bf16),
        pltpu.VMEM((steps, 2, 16, cols), bf16),
        dma((layers,)),
        dma((2, steps, 2, 2)),
        dma((2, steps, 2)),
        dma((2, steps)),
        dma((2, steps)),
    ]


def sum_steps(layers):
    return 2 * layers + layers + 3


class GradSum:
    def __init__(self, layers, whole, out, own, first, second, below, above, load, s1, s2, su, sd):
        self.layers, self.whole, self.out, self.own = layers, whole, out, own
        self.first, self.second, self.below, self.above = first, second, below, above
        self.load, self.s1, self.s2, self.su, self.sd = load, s1, s2, su, sd
        self.rank, self.z, self.y, self.x = chip_place(layers)
        self.x_chip = self.rank + 1 - 2 * self.x
        self.y_chip = self.rank + 2 - 4 * self.y
        self.steps = 2 * layers

    def layer_of(self, n):
        turn = n // 2
        return jnp.where(turn % 2 == 1, turn // 2, self.layers - 1 - turn // 2)

    def loads(self, turn):
        layer = self.layer_of(2 * turn)
        return pltpu.make_async_copy(self.whole.at[layer], self.own.at[layer], self.load.at[turn])

    def hop_one(self, n, colour, which):
        layer, chunk = self.layer_of(n), n % 2
        if colour == 0:
            source, chip = self.own.at[layer, which, 1 - self.x, 0, chunk], self.x_chip
        else:
            source, chip = self.own.at[layer, 1 - self.y, which, 1, chunk], self.y_chip
        return pltpu.make_async_remote_copy(
            src_ref=source,
            dst_ref=self.first.at[n, colour, which],
            send_sem=self.s1.at[0, n, colour, which],
            recv_sem=self.s1.at[1, n, colour, which],
            **to_chip(chip),
        )

    def hop_two(self, n, colour):
        layer, chunk = self.layer_of(n), n % 2
        if colour == 0:
            source, chip = self.own.at[layer, 1 - self.y, self.x, 0, chunk], self.y_chip
        else:
            source, chip = self.own.at[layer, self.y, 1 - self.x, 1, chunk], self.x_chip
        return pltpu.make_async_remote_copy(
            src_ref=source,
            dst_ref=self.second.at[n, colour],
            send_sem=self.s2.at[0, n, colour],
            recv_sem=self.s2.at[1, n, colour],
            **to_chip(chip),
        )

    def hop_z(self, n, up):
        layer, chunk = self.layer_of(n), n % 2
        sems = self.su if up else self.sd
        return pltpu.make_async_remote_copy(
            src_ref=self.own.at[layer, self.y, self.x, :, chunk],
            dst_ref=(self.below if up else self.above).at[n],
            send_sem=sems.at[0, n],
            recv_sem=sems.at[1, n],
            **to_chip(self.rank + (4 if up else -4)),
        )

    def start(self):
        for turn in range(self.layers):
            self.loads(turn).start()

    def send_first(self, n):
        @pl.when(n < self.steps)
        def _():
            @pl.when(n % 2 == 0)
            def _():
                self.loads(n // 2).wait()

            for which in range(2):
                for colour in range(2):
                    self.hop_one(n, colour, which).start()

    def advance(self, m):
        steps, layers = self.steps, self.layers
        n = m - 1

        @pl.when((n >= 0) & (n < steps))
        def _():
            layer, chunk = self.layer_of(n), n % 2
            for colour in range(2):
                for other in range(2):
                    if colour == 0:
                        which = (1 - self.y) if other == 0 else self.y
                        place = (layer, which, self.x, 0, chunk)
                    else:
                        which = (1 - self.x) if other == 0 else self.x
                        place = (layer, self.y, which, 1, chunk)
                    self.hop_one(n, colour, which).wait_recv()
                    self.own[place] = self.own[place] + self.first[n, colour, which]
                    if other == 0:
                        self.hop_two(n, colour).start()

        n2 = m - 2

        @pl.when((n2 >= 0) & (n2 < steps))
        def _():
            layer, chunk = self.layer_of(n2), n2 % 2
            for colour in range(2):
                self.hop_two(n2, colour).wait_recv()
                place = (layer, self.y, self.x, colour, chunk)
                self.own[place] = self.own[place] + self.second[n2, colour]

        for up in (True, False):
            chain = self.z if up else layers - 1 - self.z
            nz = m - 2 - chain
            layer = self.layer_of(nz)
            beyond = (layer > self.z) if up else (layer < self.z)

            @pl.when((nz >= 0) & (nz < steps) & beyond)
            def _():
                @pl.when(chain > 0)
                def _():
                    self.hop_z(nz, up).wait_recv()
                    came = self.below if up else self.above
                    for colour in range(2):
                        place = (layer, self.y, self.x, colour, nz % 2)
                        self.own[place] = self.own[place] + came[nz, colour]

                self.hop_z(nz, up).start()

        nf = m - 2 - layers

        @pl.when((nf >= 0) & (nf < steps) & (self.layer_of(nf) == self.z))
        def _():
            layer, chunk = self.layer_of(nf), nf % 2
            for colour in range(2):
                self.out[colour, chunk] = self.own[layer, self.y, self.x, colour, chunk].astype(
                    jnp.float32
                )
            for up in (True, False):
                chain = self.z if up else layers - 1 - self.z

                @pl.when(chain > 0)
                def _():
                    self.hop_z(nf, up).wait_recv()
                    came = self.below if up else self.above
                    for colour in range(2):
                        self.out[colour, chunk] += came[nf, colour].astype(jnp.float32)

    def finish(self):
        def one(n, carry):
            for colour in range(2):
                for which in range(2):
                    self.hop_one(n, colour, which).wait_send()
                self.hop_two(n, colour).wait_send()
            layer = self.layer_of(n)
            for up in (True, False):

                @pl.when((layer > self.z) if up else (layer < self.z))
                def _():
                    self.hop_z(n, up).wait_send()

            return carry

        lax.fori_loop(0, self.steps, one, 0)

def gather_scratch(layers, cols):
    return [
        pltpu.VMEM((2, 2, 16, cols), jnp.bfloat16),
        dma((2,)),
        dma((2, 2, layers, 2)),
        dma((2, layers, 2)),
        dma((2, layers, 2)),
        dma((2, layers, 2)),
        dma((2, layers, 2)),
    ]


class RowGather:
    def __init__(self, layers, shard, whole, here, local, sz, sx, sy, sfx, sfy):
        self.layers, self.shard, self.whole, self.here = layers, shard, whole, here
        self.local, self.sz, self.sx, self.sy, self.sfx, self.sfy = local, sz, sx, sy, sfx, sfy
        self.rank, self.z, self.y, self.x = chip_place(layers)
        self.x_chip = self.rank + 1 - 2 * self.x
        self.y_chip = self.rank + 2 - 4 * self.y

    def take(self):
        return pltpu.make_async_copy(self.shard, self.here, self.local.at[0])

    def put(self):
        place = self.whole.at[self.z, self.y, self.x]
        return pltpu.make_async_copy(self.here, place, self.local.at[1])

    def source(self, layer, chunk, own):
        if own:
            return self.shard.at[:, chunk]
        return self.whole.at[layer, self.y, self.x, :, chunk]

    def along_z(self, layer, chunk, up, own=False):
        return pltpu.make_async_remote_copy(
            src_ref=self.source(layer, chunk, own),
            dst_ref=self.whole.at[layer, self.y, self.x, :, chunk],
            send_sem=self.sz.at[0, int(up), layer, chunk],
            recv_sem=self.sz.at[1, int(up), layer, chunk],
            **to_chip(self.rank + (4 if up else -4)),
        )

    def in_plane(self, layer, chunk, along_x, own=False):
        sems = self.sx if along_x else self.sy
        return pltpu.make_async_remote_copy(
            src_ref=self.source(layer, chunk, own),
            dst_ref=self.whole.at[layer, self.y, self.x, :, chunk],
            send_sem=sems.at[0, layer, chunk],
            recv_sem=sems.at[1, layer, chunk],
            **to_chip(self.x_chip if along_x else self.y_chip),
        )

    def onward(self, layer, chunk, along_x):
        if along_x:
            place = (layer, 1 - self.y, self.x, 1, chunk)
            sems, chip = self.sfx, self.x_chip
        else:
            place = (layer, self.y, 1 - self.x, 0, chunk)
            sems, chip = self.sfy, self.y_chip
        return pltpu.make_async_remote_copy(
            src_ref=self.whole.at[place],
            dst_ref=self.whole.at[place],
            send_sem=sems.at[0, layer, chunk],
            recv_sem=sems.at[1, layer, chunk],
            **to_chip(chip),
        )

    def begin(self):
        self.take().start()

    def send_own(self):
        for chunk in range(2):

            @pl.when(self.z < self.layers - 1)
            def _():
                self.along_z(self.z, chunk, True, own=True).start()

            @pl.when(self.z > 0)
            def _():
                self.along_z(self.z, chunk, False, own=True).start()

            for along_x in (True, False):
                self.in_plane(self.z, chunk, along_x, own=True).start()
        self.take().wait()
        self.put().start()

    def pass_on(self, m):
        far, chunk = m // 2, m % 2
        for up in (True, False):
            layer = self.z - far if up else self.z + far
            near = (layer >= 0) if up else (layer < self.layers)

            @pl.when((far > 0) & near)
            def _():
                self.along_z(layer, chunk, up).wait_recv()

                @pl.when((self.z < self.layers - 1) if up else (self.z > 0))
                def _():
                    self.along_z(layer, chunk, up).start()

                for along_x in (True, False):
                    self.in_plane(layer, chunk, along_x).start()

    def turn(self, m):
        far, chunk = m // 2, m % 2
        for up in (True, False):
            layer = self.z - far if up else self.z + far
            near = (layer >= 0) if up else ((layer < self.layers) & (far > 0))

            @pl.when(near)
            def _():
                for along_x in (True, False):
                    self.in_plane(layer, chunk, along_x).wait_recv()
                    self.onward(layer, chunk, not along_x).start()

    def step(self, m):
        @pl.when(m + 2 < 2 * self.layers)
        def _():
            self.pass_on(m + 2)

        self.turn(m)

    def finish(self):
        self.put().wait()

        def one(n, carry):
            layer, chunk = n // 2, n % 2
            for along_x in (True, False):
                self.onward(layer, chunk, along_x).wait()
                self.in_plane(layer, chunk, along_x).wait_send()

            @pl.when((self.z < self.layers - 1) & (layer <= self.z))
            def _():
                self.along_z(layer, chunk, True).wait_send()

            @pl.when((self.z > 0) & (layer >= self.z))
            def _():
                self.along_z(layer, chunk, False).wait_send()

            return carry

        lax.fori_loop(0, 2 * self.layers, one, 0)

def attend_forward_kernel(
    score_scale,
    layers,
    qkv_ref,
    bias_ref,
    cot_ref,
    shard_ref,
    kept_ref,
    low_ref,
    full_ref,
    total_ref,
    cot_out,
    whole_ref,
    came,
    landed,
    low_s,
    cot_land,
    q_s,
    k_s,
    v_s,
    bias_s,
    score_s,
    in_sem,
    out_send,
    out_recv,
    cot_z,
    cot_core,
    *gather_refs,
):
    blocks = bias_s.shape[1]
    sources = qkv_ref.shape[0]
    head = k_s.shape[1]
    gather = RowGather(layers, shard_ref, whole_ref, *gather_refs)
    rank, z, y, x = chip_place(layers)
    spot = 2 * y + x
    peers = peers_of(rank, y, x)
    heads = PlaneSwap(layers, qkv_ref, came, in_sem)
    cot = Column(layers, cot_ref, cot_land, cot_z, cot_core)
    gather.begin()
    greet(layers)
    heads.start()
    gather.send_own()
    cot.start()

    def make_bias(n, carry):
        row = jnp.broadcast_to(bias_ref[pl.ds(n, 1), :], (tile, 2 * tile))
        turned = pltpu.roll(row, tile + 1, 1, stride=1, stride_axis=0)
        bias_s[n // blocks, n % blocks] = turned[:, :tile]
        return carry

    lax.fori_loop(0, 2 * blocks, make_bias, 0)
    heads.arrive()
    unpack_pair(came, q_s, k_s, v_s, score_scale)
    kept_ref[...] = came[...]

    def row_block(turn, carry):
        i = blocks - 1 - turn
        at = pl.ds(pl.multiple_of(i * tile, tile), tile)
        found = []
        for h in range(2):
            query = q_s[h, at, :]

            def score_step(j, top):
                key = k_s[pl.ds(pl.multiple_of(j * tile, tile), tile), :]
                score = dot_t(query, key) + bias_s[h, i - j]
                score_s[j] = score
                return jnp.maximum(top, jnp.maximum(score[:, :128], score[:, 128:]))

            top = lax.fori_loop(
                0, i + 1, score_step, jnp.full((tile, 128), masked_score, jnp.float32)
            )
            top = jnp.max(top, axis=1, keepdims=True)

            def share_step(j, state):
                total, summed = state
                share = jnp.exp(score_s[j] - top)
                value = v_s[pl.ds(pl.multiple_of(j * tile, tile), tile), :]
                summed = summed + jnp.dot(
                    share.astype(jnp.bfloat16), value, preferred_element_type=jnp.float32
                )
                return (total + share[:, :128] + share[:, 128:], summed)

            total, summed = lax.fori_loop(
                0,
                i + 1,
                share_step,
                (jnp.zeros((tile, 128), jnp.float32), jnp.zeros((tile, head), jnp.float32)),
            )
            total = jnp.sum(total, axis=1, keepdims=True)
            found.append(summed / total)
            log_total = jnp.broadcast_to(top + jnp.log(total), (tile, 128))
            total_ref[pl.ds(h * blocks + i, 1), :] = jnp.transpose(log_total)[0:1, :]
        both = jnp.concatenate(found, axis=1)
        full_ref[at, :] = both
        both = both.astype(jnp.bfloat16)
        for part in range(tile // 128):
            block = i * (tile // 128) + part
            low_s[block] = both[part * 128 : (part + 1) * 128]

        gather.step(turn)
        for part in range(tile // 128):
            block = i * (tile // 128) + part

            @pl.when(block % sources == spot)
            def _():
                landed[spot, block // sources] = low_s[block]

            @pl.when(block % sources != spot)
            def _():
                hand_back(block).start()

        return carry

    def hand_back(block):
        return pltpu.make_async_remote_copy(
            src_ref=low_s.at[block],
            dst_ref=landed.at[spot, block // sources],
            send_sem=out_send.at[block],
            recv_sem=out_recv.at[spot, block // sources],
            **to_chip(rank - spot + block % sources),
        )

    lax.fori_loop(0, blocks // 2, row_block, 0)
    cot.arrive()
    lax.fori_loop(blocks // 2, blocks, row_block, 0)
    for o in range(3):
        chip, there = peers[o]
        for turn in range(layers):
            pltpu.make_async_remote_copy(
                src_ref=low_s.at[0],
                dst_ref=landed.at[there, turn],
                send_sem=out_send.at[0],
                recv_sem=out_recv.at[there, turn],
                **to_chip(chip),
            ).wait_recv()
    for source in range(sources):
        for turn in range(layers):
            low_ref[turn * 128 : (turn + 1) * 128, source * 128 : (source + 1) * 128] = landed[
                source, turn
            ]
    heads.finish()
    cot.finish()
    cot_out[...] = cot_land[...]
    for block in range(sources * layers):

        @pl.when(block % sources != spot)
        def _():
            hand_back(block).wait_send()

    gather.finish()


def attend_forward(scale, layers, qkv, bias, cotangent, shard):
    f32, bf16 = jnp.float32, jnp.bfloat16
    sources, rows, wide = qkv.shape
    head = wide // 4
    length = sources * rows
    blocks = length // tile
    cols = shard.shape[1]
    cot_shape = (layers, 2, *cotangent.shape[1:])
    vmem, anywhere = pl.BlockSpec(memory_space=pltpu.VMEM), pl.BlockSpec(memory_space=pl.ANY)
    kept, low, full, total, cot, whole = pl.pallas_call(
        functools.partial(attend_forward_kernel, scale, layers),
        name="attend_forward",
        out_shape=(
            jax.ShapeDtypeStruct(qkv.shape, bf16),
            jax.ShapeDtypeStruct((rows, sources * 2 * head), bf16),
            jax.ShapeDtypeStruct((length, 2 * head), f32),
            jax.ShapeDtypeStruct((2 * blocks, tile), f32),
            jax.ShapeDtypeStruct(cot_shape, bf16),
            jax.ShapeDtypeStruct((layers, 2, 2, 2, 2, 16, cols), bf16),
        ),
        in_specs=[vmem, vmem, vmem, anywhere],
        out_specs=(vmem, vmem, vmem, vmem, vmem, anywhere),
        scratch_shapes=[
            pltpu.VMEM(qkv.shape, bf16),
            pltpu.VMEM((sources, layers, 128, 2 * head), bf16),
            pltpu.VMEM((length // 128, 128, 2 * head), bf16),
            pltpu.VMEM(cot_shape, bf16),
            pltpu.VMEM((2, length, head), bf16),
            pltpu.VMEM((length, head), bf16),
            pltpu.VMEM((length, head), bf16),
            pltpu.VMEM((2, blocks, tile, tile), f32),
            pltpu.VMEM((blocks, tile, tile), f32),
            dma((2, 3)),
            dma((length // 128,)),
            dma((sources, layers)),
            dma((2, layers)),
            dma((2, layers)),
            *gather_scratch(layers, cols),
        ],
        compiler_params=pltpu.CompilerParams(
            collective_id=6, has_side_effects=True, vmem_limit_bytes=56 << 20
        ),
    )(qkv, bias, cotangent, shard.reshape(2, 2, 16, cols))
    return kept, low, full, total, cot, whole.reshape(layers * 256, cols)

def attend_backward_kernel(
    score_scale,
    layers,
    kept_ref,
    ctx_ref,
    full_ref,
    total_ref,
    bias_ref,
    kv_ref,
    rows_ref,
    grads_ref,
    out_ref,
    sums_ref,
    kv_out,
    rows_out,
    grad_sum_ref,
    ctx_land,
    kv_land,
    rows_land,
    out_s,
    out_land,
    q_s,
    k_s,
    v_s,
    g_s,
    bias_s,
    sum_s,
    delta_s,
    dq_s,
    dk_s,
    dv_s,
    ctx_sem,
    kv_sem,
    rows_z,
    out_sem,
    *sum_refs,
):
    blocks = bias_s.shape[1]
    sources, rows, _ = kept_ref.shape
    head = k_s.shape[1]
    grads = GradSum(layers, grads_ref, grad_sum_ref, *sum_refs)
    context = PlaneSwap(layers, ctx_ref, ctx_land, ctx_sem)
    cross = PlaneSwap(layers, kv_ref, kv_land, kv_sem)
    ended = Column(layers, rows_ref, rows_land, rows_z)
    back = PlaneSwap(layers, out_s, out_land, out_sem)
    grads.start()
    greet(layers)
    context.start()
    grads.send_first(0)
    cross.start()
    ended.start()
    unpack_pair(kept_ref, q_s, k_s, v_s, score_scale)

    def make_bias(n, carry):
        row = jnp.broadcast_to(bias_ref[pl.ds(n, 1), :], (tile, 2 * tile))
        turned = pltpu.roll(row, 0, 1, stride=1, stride_axis=0)
        bias_s[n // blocks, n % blocks] = turned[:, tile:]
        return carry

    lax.fori_loop(0, 2 * blocks, make_bias, 0)
    sum_s[...] = jnp.zeros_like(sum_s)
    dq_s[...] = jnp.zeros_like(dq_s)
    dk_s[...] = jnp.zeros_like(dk_s)
    dv_s[...] = jnp.zeros_like(dv_s)
    context.arrive()
    for block in range(rows // 128 * sources):
        source, turn = block % sources, block // sources
        part = ctx_land[source, turn * 128 : (turn + 1) * 128, :]
        at = slice(block * 128, (block + 1) * 128)
        g_s[0, at, :] = part[:, :head]
        g_s[1, at, :] = part[:, head:]

    def make_delta(i, carry):
        at = pl.ds(pl.multiple_of(i * tile, tile), tile)
        for h in range(2):
            product = g_s[h, at, :].astype(jnp.float32) * full_ref[at, h * head : (h + 1) * head]
            column = jnp.broadcast_to(jnp.sum(product, axis=1, keepdims=True), (tile, 128))
            delta_s[pl.ds(h * blocks + i, 1), :] = jnp.transpose(column)[0:1, :]
        return carry

    lax.fori_loop(0, blocks, make_delta, 0)

    def one_tile(n, carry):
        line, at = n // blocks, n % blocks
        first = at < blocks - line
        d = jnp.where(first, line, blocks - line)
        i = jnp.where(first, at + line, at)
        at_q = pl.ds(pl.multiple_of(i * tile, tile), tile)
        at_k = pl.ds(pl.multiple_of((i - d) * tile, tile), tile)
        key, value = k_s[at_k, :], v_s[at_k, :]
        for h in range(2):
            query, grad = q_s[h, at_q, :], g_s[h, at_q, :]
            score = dot_t(key, query) + bias_s[h, d]
            share = jnp.exp(score - total_ref[pl.ds(h * blocks + i, 1), :])
            pull = dot_t(value, grad)
            grad_score = share * (pull - delta_s[pl.ds(h * blocks + i, 1), :])
            sum_s[h, d] += grad_score
            share_low = share.astype(jnp.bfloat16)
            grad_low = grad_score.astype(jnp.bfloat16)
            dv_s[at_k, :] += jnp.dot(share_low, grad, preferred_element_type=jnp.float32)
            dk_s[at_k, :] += jnp.dot(grad_low, query, preferred_element_type=jnp.float32)
            dq_s[h, at_q, :] += dot_first(grad_low, key)
        return carry

    tiles = blocks * (blocks + 1) // 2
    busy = 6

    def work(m, carry):
        grads.send_first(m)
        low = (m - 1) * tiles // busy
        lax.fori_loop(low, m * tiles // busy, one_tile, 0)
        grads.advance(m)
        return carry

    lax.fori_loop(1, 1 + busy, work, 0)

    for block in range(rows // 128 * sources):
        source, turn = block % sources, block // sources
        at = slice(block * 128, (block + 1) * 128)
        out_s[source, turn * 128 : (turn + 1) * 128, :] = jnp.concatenate(
            [dq_s[0, at, :] * score_scale, dq_s[1, at, :] * score_scale, dk_s[at, :], dv_s[at, :]],
            axis=1,
        ).astype(jnp.bfloat16)
    back.start()

    row_at = lax.broadcasted_iota(jnp.int32, (tile, tile), 0)
    col_at = lax.broadcasted_iota(jnp.int32, (tile, tile), 1)
    turn_rows = (row_at + col_at == tile - 1).astype(jnp.float32)

    def make_sums(n, carry):
        turned = jnp.dot(
            turn_rows,
            sum_s[n // blocks, n % blocks],
            precision=highest,
            preferred_element_type=jnp.float32,
        )
        wide = jnp.concatenate([turned, jnp.zeros_like(turned)], axis=1)
        wide = pltpu.roll(wide, 0, 1, stride=1, stride_axis=0)
        sums_ref[pl.ds(n, 1), :] = jnp.sum(wide, axis=0, keepdims=True)
        return carry

    lax.fori_loop(0, 2 * blocks, make_sums, 0)
    cross.arrive()
    both = kv_land[0].astype(jnp.float32)
    for source in range(1, sources):
        both = both + kv_land[source].astype(jnp.float32)
    kv_out[...] = both.astype(jnp.bfloat16)
    ended.arrive()
    rows_out[...] = rows_land[...]

    def rest(m, carry):
        grads.send_first(m)
        grads.advance(m)
        return carry

    lax.fori_loop(1 + busy, sum_steps(layers), rest, 0)
    back.arrive()
    wide = 4 * head
    for source in range(sources):
        out_ref[:, source * wide : (source + 1) * wide] = out_land[source]
    context.finish()
    cross.finish()
    ended.finish()
    back.finish()
    grads.finish()


def attend_backward(scale, layers, kept, ctx_grad, full, total, bias, kv, layer_rows, grads):
    f32, bf16 = jnp.float32, jnp.bfloat16
    sources, rows, wide = kept.shape
    head = wide // 4
    length = sources * rows
    blocks = length // tile
    cols = grads.shape[1]
    vmem, anywhere = pl.BlockSpec(memory_space=pltpu.VMEM), pl.BlockSpec(memory_space=pl.ANY)
    grad_qkv, sums, kv_sum, layer_out, grad_sum = pl.pallas_call(
        functools.partial(attend_backward_kernel, scale, layers),
        name="attend_backward",
        out_shape=(
            jax.ShapeDtypeStruct((rows, sources * wide), bf16),
            jax.ShapeDtypeStruct((2 * blocks, 2 * tile), f32),
            jax.ShapeDtypeStruct(kv.shape[1:], bf16),
            jax.ShapeDtypeStruct(layer_rows.shape, bf16),
            jax.ShapeDtypeStruct((2, 2, 16, cols), f32),
        ),
        in_specs=[vmem] * 7 + [anywhere],
        out_specs=(vmem,) * 5,
        scratch_shapes=[
            pltpu.VMEM(ctx_grad.shape, bf16),
            pltpu.VMEM(kv.shape, bf16),
            pltpu.VMEM(layer_rows.shape, bf16),
            pltpu.VMEM(kept.shape, bf16),
            pltpu.VMEM(kept.shape, bf16),
            pltpu.VMEM((2, length, head), bf16),
            pltpu.VMEM((length, head), bf16),
            pltpu.VMEM((length, head), bf16),
            pltpu.VMEM((2, length, head), bf16),
            pltpu.VMEM((2, blocks, tile, tile), f32),
            pltpu.VMEM((2, blocks, tile, tile), f32),
            pltpu.VMEM((2 * blocks, tile), f32),
            pltpu.VMEM((2, length, head), f32),
            pltpu.VMEM((length, head), f32),
            pltpu.VMEM((length, head), f32),
            dma((2, 3)),
            dma((2, 3)),
            dma((2, layers)),
            dma((2, 3)),
            *sum_scratch(layers, cols),
        ],
        compiler_params=pltpu.CompilerParams(
            collective_id=8, has_side_effects=True, vmem_limit_bytes=62 << 20
        ),
    )(kept, ctx_grad, full, total, bias, kv, layer_rows, grads.reshape(layers, 2, 2, 2, 2, 16, cols))
    return grad_qkv, sums, kv_sum, layer_out, grad_sum.reshape(-1, cols)

def swap_cores(block):
    return lax.ppermute(block, tensor_axis, [(0, 1), (1, 0)])


def dot_t(left, right):
    return lax.dot_general(
        left, right, (((1,), (1,)), ((), ())), preferred_element_type=jnp.float32
    )


def dot_first(left, right):
    return lax.dot_general(
        left, right, (((0,), (0,)), ((), ())), preferred_element_type=jnp.float32
    )


def unpack_pair(qkv_ref, q_s, k_s, v_s, score_scale):
    sources, rows, _ = qkv_ref.shape
    blocks = rows // 128 * sources
    head = k_s.shape[1]
    for block in range(blocks):
        source, turn = block % sources, block // sources
        tile = qkv_ref[source, turn * 128 : (turn + 1) * 128, :]
        at = slice(block * 128, (block + 1) * 128)
        q_s[0, at, :] = (tile[:, :head] * score_scale).astype(jnp.bfloat16)
        q_s[1, at, :] = (tile[:, head : 2 * head] * score_scale).astype(jnp.bfloat16)
        k_s[at, :] = tile[:, 2 * head : 3 * head]
        v_s[at, :] = tile[:, 3 * head :]


def cross_forward_kernel(score_scale, q_ref, k_ref, v_ref, out_ref):
    head = k_ref.shape[1] // 2
    for kv in range(2):
        key = k_ref[:, kv * head : (kv + 1) * head]
        value = v_ref[:, kv * head : (kv + 1) * head]
        found = []
        for h in range(2):
            at = (2 * kv + h) * head
            query = (q_ref[:, at : at + head] * score_scale).astype(jnp.bfloat16)
            score = dot_t(query, key)
            share = jnp.exp(score - jnp.max(score, axis=1, keepdims=True))
            total = jnp.sum(share, axis=1, keepdims=True)
            summed = jnp.dot(share.astype(jnp.bfloat16), value, preferred_element_type=jnp.float32)
            found.append(summed / total)
        out_ref[:, 2 * kv * head : 2 * (kv + 1) * head] = jnp.concatenate(found, axis=1).astype(
            jnp.bfloat16
        )


def cross_backward_kernel(score_scale, q_ref, k_ref, v_ref, g_ref, dq_ref, dk_ref, dv_ref):
    head = k_ref.shape[1] // 2
    key_grads, value_grads = [], []
    for kv in range(2):
        key = k_ref[:, kv * head : (kv + 1) * head]
        value = v_ref[:, kv * head : (kv + 1) * head]
        query_grads = []
        key_grad = value_grad = None
        for h in range(2):
            at = (2 * kv + h) * head
            query = (q_ref[:, at : at + head] * score_scale).astype(jnp.bfloat16)
            grad = g_ref[:, at : at + head]
            score = dot_t(key, query)
            share = jnp.exp(score - jnp.max(score, axis=0, keepdims=True))
            share = share / jnp.sum(share, axis=0, keepdims=True)
            pull = dot_t(value, grad)
            delta = jnp.sum(share * pull, axis=0, keepdims=True)
            grad_low = (share * (pull - delta)).astype(jnp.bfloat16)
            query_grads.append(dot_first(grad_low, key) * score_scale)
            more_key = jnp.dot(grad_low, query, preferred_element_type=jnp.float32)
            more_value = jnp.dot(
                share.astype(jnp.bfloat16), grad, preferred_element_type=jnp.float32
            )
            key_grad = more_key if key_grad is None else key_grad + more_key
            value_grad = more_value if value_grad is None else value_grad + more_value
        dq_ref[:, 2 * kv * head : 2 * (kv + 1) * head] = jnp.concatenate(
            query_grads, axis=1
        ).astype(jnp.bfloat16)
        key_grads.append(key_grad)
        value_grads.append(value_grad)
    dk_ref[...] = jnp.concatenate(key_grads, axis=1).astype(jnp.bfloat16)
    dv_ref[...] = jnp.concatenate(value_grads, axis=1).astype(jnp.bfloat16)


def by_heads(
    inputs,
    encoder_out,
    out_cotangent,
    bucket_ids,
    position_table,
    self_gain,
    self_query,
    self_key,
    self_value,
    self_output,
    cross_gain,
    cross_query,
    cross_key,
    cross_value,
    cross_output,
    feed_gain,
    gate_weight,
    up_weight,
    down_weight,
):
    f32, bf16 = jnp.float32, jnp.bfloat16
    batches, own, width = inputs.shape
    enc_own = encoder_out.shape[1]
    length = bucket_ids.shape[0]
    heads_all, buckets = position_table.shape
    fsdp = lax.axis_size(fsdp_axis)
    plane = fsdp // batches
    rank, core = lax.axis_index(fsdp_axis), lax.axis_index(tensor_axis)
    head = self_query.shape[1] // (heads_all // 2)
    kv_local = self_key.shape[1] // head
    scale = head ** (-0.5)
    blocks = length // tile
    rows = batches * 2 * own
    enc_rows = batches * 2 * enc_own
    feed = gate_weight.shape[1]
    def by_kv(weight):
        return weight.reshape(weight.shape[0], kv_local, -1)

    self_in = jnp.concatenate([by_kv(self_query), by_kv(self_key), by_kv(self_value)], axis=2)
    self_in = self_in.reshape(self_in.shape[0], -1)
    wide_self = self_in.shape[1]
    first_shard = jnp.concatenate([self_in, self_output.T], axis=1)
    rest_shard = jnp.concatenate(
        [cross_query, cross_key, cross_value, cross_output.T, gate_weight, up_weight, down_weight.T],
        axis=1,
    )
    started, enc_all, first_full = open_rows(batches, inputs, encoder_out, first_shard)
    in_full, out_full = first_full[:, :wide_self], first_full[:, wide_self:]
    cuts = [
        cross_query.shape[1],
        cross_key.shape[1],
        cross_value.shape[1],
        cross_output.shape[0],
        feed,
        feed,
        feed,
    ]

    def split(x):
        pieces, at = [], 0
        for cut in cuts:
            pieces.append(x[:, at : at + cut])
            at += cut
        return pieces


    x_rows = started.reshape(rows, width).astype(f32)
    enc_all = enc_all.reshape(-1, width)

    kv_index = core * kv_local + rank % plane
    table_here = lax.dynamic_slice_in_dim(position_table, 2 * kv_index, 2, 0)
    bucket_range = jnp.arange(buckets, dtype=jnp.int32)
    lower = jnp.sum((bucket_ids[None, :] < bucket_range[:, None]).astype(jnp.int32), axis=1)
    upper = jnp.concatenate([lower[1:], jnp.full((1,), length, jnp.int32)])
    offsets = (
        tile * jnp.arange(blocks, dtype=jnp.int32)[:, None]
        + jnp.arange(2 * tile, dtype=jnp.int32)[None, :]
    ).reshape(-1)

    def bias_of(offset):
        hit = (offset[None] >= lower[:, None]) & (offset[None] < upper[:, None])
        value = jnp.dot(table_here, hit.astype(f32), precision=highest)
        return jnp.where(offset[None] >= 0, value, masked_score).reshape(2 * blocks, 2 * tile)

    down_steps = (
        tile * jnp.arange(blocks, dtype=jnp.int32)[:, None]
        + (tile - 1)
        - jnp.arange(2 * tile, dtype=jnp.int32)[None, :]
    ).reshape(-1)
    bias_down = bias_of(down_steps)
    bias_up = bias_of(offsets - tile)

    def norm_low(v, gain):
        return norm_rows(v, gain).astype(bf16)

    def swap_add(partial):
        low = partial.astype(bf16)
        return low.astype(f32) + swap_cores(low).astype(f32)

    normed_self = norm_low(x_rows, self_gain)
    qkv = jnp.einsum(
        "rd,dkc->krc",
        normed_self,
        in_full.reshape(width, kv_local, -1),
        preferred_element_type=f32,
    ).astype(bf16)
    params = pltpu.CompilerParams(vmem_limit_bytes=58 << 20)
    qkv_here, context_low, context_full, log_total, cot_low, rest_full = attend_forward(
        scale, batches, qkv, bias_down, out_cotangent, rest_shard
    )
    cot_low = cot_low.reshape(rows, width)
    cq_full, ck_full, cv_full, co_full, gate_full, up_full, down_full = split(rest_full)

    after_self = x_rows + swap_add(dot_t(context_low, out_full))

    cross_k = matmul(enc_all, ck_full).astype(bf16)
    cross_v = matmul(enc_all, cv_full).astype(bf16)
    normed_cross = norm_low(after_self, cross_gain)
    cross_q = matmul(normed_cross, cq_full).astype(bf16)
    q_cols = cross_q.shape[1]
    halves = kv_local // 2
    q_spec = pl.BlockSpec((rows, q_cols // halves), lambda i: (0, i))
    k_spec = pl.BlockSpec((cross_k.shape[0], 2 * head), lambda i: (0, i))
    cross_flops = 4 * rows * cross_k.shape[0] * head * 2 * kv_local
    cross_context = pl.pallas_call(
        functools.partial(cross_forward_kernel, scale),
        name="cross_forward",
        grid=(halves,),
        in_specs=[q_spec, k_spec, k_spec],
        out_specs=q_spec,
        out_shape=jax.ShapeDtypeStruct(cross_q.shape, bf16),
        compiler_params=params,
        cost_estimate=pl.CostEstimate(
            flops=cross_flops, bytes_accessed=2 << 20, transcendentals=0
        ),
    )(cross_q, cross_k, cross_v)
    after_cross = after_self + swap_add(dot_t(cross_context, co_full))

    normed_feed = norm_low(after_cross, feed_gain)
    gate_values = matmul(normed_feed, gate_full)
    up_values = matmul(normed_feed, up_full)

    def gated(gate_in, up_in):
        return jax.nn.gelu(gate_in, approximate=True) * up_in

    hidden_value, gelu_pull = jax.vjp(gated, gate_values, up_values)
    hidden = hidden_value.astype(bf16)
    down_part = dot_t(hidden, down_full).astype(bf16).reshape(batches, 2, own, width)

    def keep_half(part, axis):
        mine = lax.dynamic_index_in_dim(part, core, axis, keepdims=False)
        other = lax.dynamic_index_in_dim(part, 1 - core, axis, keepdims=False)
        return mine.astype(f32) + swap_cores(other).astype(f32)

    def own_half(x):
        x = x.reshape(batches, 2, own, width)
        return lax.dynamic_index_in_dim(x, core, 1, keepdims=False)

    layer_rows = (own_half(after_cross) + keep_half(down_part, 1)).astype(bf16)

    down_grad = dot_first(cot_low, hidden)
    grad_hidden = matmul(cot_low, down_full)
    grad_gate, grad_up = gelu_pull(grad_hidden)
    grad_gate, grad_up = grad_gate.astype(bf16), grad_up.astype(bf16)
    gate_grad = dot_first(normed_feed, grad_gate)
    up_grad = dot_first(normed_feed, grad_up)
    feed_rows = swap_add(dot_t(grad_gate, gate_full) + dot_t(grad_up, up_full))
    grad_feed, feed_gain_grad = jax.vjp(norm_rows, after_cross, feed_gain)[1](feed_rows)
    grad_after_cross = cot_low.astype(f32) + grad_feed

    grad_cross_low = grad_after_cross.astype(bf16)
    co_grad = dot_first(grad_cross_low, cross_context)
    grad_cross_context = matmul(grad_cross_low, co_full).astype(bf16)
    cross_dq, cross_dk, cross_dv = pl.pallas_call(
        functools.partial(cross_backward_kernel, scale),
        name="cross_backward",
        grid=(halves,),
        in_specs=[q_spec, k_spec, k_spec, q_spec],
        out_specs=(q_spec, k_spec, k_spec),
        out_shape=(
            jax.ShapeDtypeStruct(cross_q.shape, bf16),
            jax.ShapeDtypeStruct(cross_k.shape, bf16),
            jax.ShapeDtypeStruct(cross_v.shape, bf16),
        ),
        compiler_params=params,
        cost_estimate=pl.CostEstimate(
            flops=cross_flops * 5 // 2, bytes_accessed=4 << 20, transcendentals=0
        ),
    )(cross_q, cross_k, cross_v, grad_cross_context)
    cq_grad = dot_first(normed_cross, cross_dq)
    cross_rows = swap_add(dot_t(cross_dq, cq_full))
    grad_cross, cross_gain_grad = jax.vjp(norm_rows, after_self, cross_gain)[1](cross_rows)
    grad_after_self = grad_after_cross + grad_cross
    ck_grad = dot_first(enc_all, cross_dk)
    cv_grad = dot_first(enc_all, cross_dv)
    cross_kv = jnp.concatenate([cross_dk, cross_dv], axis=1).reshape(plane, enc_rows, -1)

    grad_self_low = grad_after_self.astype(bf16)
    out_grad = dot_first(grad_self_low, context_low)
    grad_context = (
        jnp.einsum(
            "rd,dkc->krc",
            grad_self_low,
            out_full.reshape(width, kv_local, -1),
            preferred_element_type=f32,
        )
    ).astype(bf16)
    parts = [out_grad, cq_grad, ck_grad, cv_grad, co_grad, gate_grad, up_grad, down_grad]
    grads = jnp.concatenate([part.astype(bf16) for part in parts], axis=1)
    grad_qkv, diagonal_sums, kv_sum, layer_out, sums = attend_backward(
        scale,
        batches,
        qkv_here,
        grad_context,
        context_full,
        log_total,
        bias_up,
        cross_kv,
        layer_rows,
        grads,
    )
    enc_part = dot_t(kv_sum[:, : cross_k.shape[1]], ck_full)
    enc_part = enc_part + dot_t(kv_sum[:, cross_k.shape[1] :], cv_full)
    enc_grad = keep_half(enc_part.astype(bf16).reshape(2, batches, enc_own, width), 0)
    in_grad = dot_first(normed_self, grad_qkv)
    self_part = dot_t(grad_qkv, in_full)
    self_rows = swap_add(self_part)
    grad_self, self_gain_grad = jax.vjp(norm_rows, x_rows, self_gain)[1](self_rows)
    input_rows = own_half(grad_after_self + grad_self)

    spread = offsets - (tile - 1)
    hit = ((spread[None] >= lower[:, None]) & (spread[None] < upper[:, None])).astype(f32)
    by_offset = diagonal_sums.reshape(2, -1)
    table_here_grad = jnp.dot(by_offset, hit.T, precision=highest)
    table_full = lax.dynamic_update_slice_in_dim(
        jnp.zeros((heads_all, buckets), f32), table_here_grad, 2 * kv_index, 0
    )
    table_row = jnp.pad(table_full.reshape(1, -1), ((0, 0), (0, width - heads_all * buckets)))
    small = jnp.concatenate(
        [self_gain_grad[None], cross_gain_grad[None], feed_gain_grad[None], table_row]
    )
    in_sum, ended, small_sum = close_rows(
        batches,
        in_grad.astype(bf16),
        jnp.concatenate([input_rows, enc_grad], axis=1).astype(bf16),
        jnp.concatenate([small, jnp.zeros_like(small)]),
    )
    table_sum = small_sum[3, : heads_all * buckets].reshape(heads_all, buckets)
    q_wide = self_query.shape[1] // kv_local
    k_wide = self_key.shape[1] // kv_local
    in_sum = in_sum.reshape(in_sum.shape[0], kv_local, -1)

    def flat(x):
        return x.reshape(x.shape[0], -1)

    out_sum = sums[:, : self_output.shape[0]]
    pieces = split(sums[:, self_output.shape[0] :])
    return (
        layer_out,
        ended[:, :own],
        ended[:, own:],
        table_sum,
        small_sum[0],
        flat(in_sum[:, :, :q_wide]),
        flat(in_sum[:, :, q_wide : q_wide + k_wide]),
        flat(in_sum[:, :, q_wide + k_wide :]),
        out_sum.T,
        small_sum[1],
        pieces[0],
        pieces[1],
        pieces[2],
        pieces[3].T,
        small_sum[2],
        pieces[4],
        pieces[5],
        pieces[6].T,
    )


def on_either(*args):
    batches, kv_heads = args[0].shape[0], args[7].shape[1] * lax.axis_size(tensor_axis)
    head_size = args[6].shape[1] * lax.axis_size(tensor_axis) // args[4].shape[0]
    devices = lax.axis_size(fsdp_axis) * lax.axis_size(tensor_axis)
    if devices == batches * (kv_heads // head_size):
        return by_heads(*args)
    return on_device(*args)


def solution(mesh):
    placed = (
        P(None, (fsdp_axis, tensor_axis), None),
        P(None, (fsdp_axis, tensor_axis), None),
        P(None, (fsdp_axis, tensor_axis), None),
        P(),
        P(),
        P(),
        P(fsdp_axis, tensor_axis),
        P(fsdp_axis, tensor_axis),
        P(fsdp_axis, tensor_axis),
        P(tensor_axis, fsdp_axis),
        P(),
        P(fsdp_axis, tensor_axis),
        P(fsdp_axis, tensor_axis),
        P(fsdp_axis, tensor_axis),
        P(tensor_axis, fsdp_axis),
        P(),
        P(fsdp_axis, tensor_axis),
        P(fsdp_axis, tensor_axis),
        P(tensor_axis, fsdp_axis),
    )
    return jax.shard_map(
        on_either,
        mesh=mesh,
        in_specs=placed,
        out_specs=(
            P(None, (fsdp_axis, tensor_axis), None),
            P(None, (fsdp_axis, tensor_axis), None),
            P(None, (fsdp_axis, tensor_axis), None),
            P(),
            P(),
            P(fsdp_axis, tensor_axis),
            P(fsdp_axis, tensor_axis),
            P(fsdp_axis, tensor_axis),
            P(tensor_axis, fsdp_axis),
            P(),
            P(fsdp_axis, tensor_axis),
            P(fsdp_axis, tensor_axis),
            P(fsdp_axis, tensor_axis),
            P(tensor_axis, fsdp_axis),
            P(),
            P(fsdp_axis, tensor_axis),
            P(fsdp_axis, tensor_axis),
            P(tensor_axis, fsdp_axis),
        ),
        check_vma=False,
    )
```

```python
import functools
import math
import types

import jax
import jax.numpy as jnp
from jax import lax
from jax.experimental import pallas as pl
from jax.experimental.pallas import tpu as pltpu
from jax.sharding import PartitionSpec as P

norm_eps = 1e-06
masked_score = -1e30
highest = lax.Precision.HIGHEST
key_block_width = 256
tile = 256
fsdp_axis, tensor_axis = "fsdp", "tensor"


def matmul(left, right):
    return jnp.dot(left, right, preferred_element_type=jnp.float32)


def norm_rows(row_block, gain):
    return (
        row_block
        * lax.rsqrt(jnp.mean(row_block * row_block, axis=-1, keepdims=True) + norm_eps)
        * gain
    )


def gather_rows(row_block):
    return lax.all_gather(row_block, tensor_axis, axis=0, tiled=True)


def sum_rows(row_block):
    return lax.psum_scatter(
        row_block.astype(jnp.bfloat16), tensor_axis, scatter_dimension=0, tiled=True
    ).astype(jnp.float32)


def gather_weights(shards):
    (
        self_query,
        self_key,
        self_value,
        self_output,
        cross_query,
        cross_key,
        cross_value,
        cross_output,
        gate_weight,
        up_weight,
        down_weight,
    ) = shards
    inner = (
        lax.all_gather(self_query, fsdp_axis, axis=0, tiled=True),
        lax.all_gather(self_key, fsdp_axis, axis=0, tiled=True),
        lax.all_gather(self_value, fsdp_axis, axis=0, tiled=True),
        lax.all_gather(cross_query, fsdp_axis, axis=0, tiled=True),
        lax.all_gather(cross_key, fsdp_axis, axis=0, tiled=True),
        lax.all_gather(cross_value, fsdp_axis, axis=0, tiled=True),
        lax.all_gather(gate_weight, fsdp_axis, axis=0, tiled=True),
        lax.all_gather(up_weight, fsdp_axis, axis=0, tiled=True),
    )
    outer = (
        lax.all_gather(self_output, fsdp_axis, axis=1, tiled=True),
        lax.all_gather(cross_output, fsdp_axis, axis=1, tiled=True),
        lax.all_gather(down_weight, fsdp_axis, axis=1, tiled=True),
    )
    return (
        inner[0],
        inner[1],
        inner[2],
        outer[0],
        inner[3],
        inner[4],
        inner[5],
        outer[1],
        inner[6],
        inner[7],
        outer[2],
    )


def scatter_grads(grads_full):
    (
        self_query,
        self_key,
        self_value,
        self_output,
        cross_query,
        cross_key,
        cross_value,
        cross_output,
        gate_weight,
        up_weight,
        down_weight,
    ) = grads_full
    inner = (
        lax.psum_scatter(self_query, fsdp_axis, scatter_dimension=0, tiled=True),
        lax.psum_scatter(self_key, fsdp_axis, scatter_dimension=0, tiled=True),
        lax.psum_scatter(self_value, fsdp_axis, scatter_dimension=0, tiled=True),
        lax.psum_scatter(cross_query, fsdp_axis, scatter_dimension=0, tiled=True),
        lax.psum_scatter(cross_key, fsdp_axis, scatter_dimension=0, tiled=True),
        lax.psum_scatter(cross_value, fsdp_axis, scatter_dimension=0, tiled=True),
        lax.psum_scatter(gate_weight, fsdp_axis, scatter_dimension=0, tiled=True),
        lax.psum_scatter(up_weight, fsdp_axis, scatter_dimension=0, tiled=True),
    )
    outer = (
        lax.psum_scatter(self_output, fsdp_axis, scatter_dimension=1, tiled=True),
        lax.psum_scatter(cross_output, fsdp_axis, scatter_dimension=1, tiled=True),
        lax.psum_scatter(down_weight, fsdp_axis, scatter_dimension=1, tiled=True),
    )
    return (
        inner[0],
        inner[1],
        inner[2],
        outer[0],
        inner[3],
        inner[4],
        inner[5],
        outer[1],
        inner[6],
        inner[7],
        outer[2],
    )


def add_all(first, second):
    return tuple((left_item + right_item for left_item, right_item in zip(first, second)))


def fold_keys(key_rows, value_rows, step_fn, initial):
    return step_fn(
        initial,
        (
            lax.all_gather(key_rows, fsdp_axis, axis=0, tiled=True),
            lax.all_gather(value_rows, fsdp_axis, axis=0, tiled=True),
        ),
        jnp.int32(0),
    )


def on_device(
    inputs,
    encoder_out,
    out_cotangent,
    bucket_ids,
    position_table,
    self_gain,
    self_query,
    self_key,
    self_value,
    self_output,
    cross_gain,
    cross_query,
    cross_key,
    cross_value,
    cross_output,
    feed_gain,
    gate_weight,
    up_weight,
    down_weight,
):
    shards = (
        self_query,
        self_key,
        self_value,
        self_output,
        cross_query,
        cross_key,
        cross_value,
        cross_output,
        gate_weight,
        up_weight,
        down_weight,
    )
    batches = inputs.shape[0]
    tensor_size = lax.axis_size(tensor_axis)
    piece_rows = inputs.shape[1] * tensor_size
    length = bucket_ids.shape[0]
    heads_all = position_table.shape[0]
    buckets = position_table.shape[1]
    local_heads = heads_all // tensor_size
    head_size = self_query.shape[1] // local_heads
    kv_local = self_key.shape[1] // head_size
    group_size = local_heads // kv_local
    score_scale = head_size ** (-0.5)
    fsdp_rank = lax.axis_index(fsdp_axis)
    tensor_rank = lax.axis_index(tensor_axis)
    query_start = fsdp_rank * piece_rows
    encoder_rows = encoder_out.shape[1] * tensor_size
    table_local = lax.dynamic_slice_in_dim(
        position_table, tensor_rank * local_heads, local_heads, 0
    )
    bucket_range = jnp.arange(buckets, dtype=jnp.int32)
    lower_bounds = jnp.sum((bucket_ids[None, :] < bucket_range[:, None]).astype(jnp.int32), axis=1)
    upper_bounds = jnp.concatenate([lower_bounds[1:], jnp.full((1,), length, jnp.int32)])

    def position_bias(row_start, col_start, row_count, col_count):
        offsets = (
            row_start
            - col_start
            + jnp.arange(row_count, dtype=jnp.int32)[:, None]
            - jnp.arange(col_count, dtype=jnp.int32)[None, :]
        )
        indicator = (
            (offsets[None] >= lower_bounds[:, None, None])
            & (offsets[None] < upper_bounds[:, None, None])
        ).astype(jnp.float32)
        bias_values = jnp.einsum("hb,bij->hij", table_local, indicator, precision=highest).reshape(
            kv_local, group_size, row_count, col_count
        )
        return (bias_values, offsets >= 0, indicator)

    def split_heads(row_block):
        return row_block.reshape(row_block.shape[0], kv_local, group_size, head_size)

    def split_kv(row_block):
        return row_block.reshape(row_block.shape[0], kv_local, head_size)

    def backward(batch_index, saved_state, weights):
        (
            query_full,
            key_full,
            value_full,
            output_full,
            cross_query_full,
            cross_key_full,
            cross_value_full,
            cross_output_full,
            gate_full,
            up_full,
            down_full,
        ) = weights
        cotangent = out_cotangent[batch_index].astype(jnp.float32)
        grad_feed = gather_rows(out_cotangent[batch_index])
        hidden = saved_state.hidden
        normed_feed = saved_state.normed_feed
        down_grad = jnp.einsum("tf,td->fd", hidden, grad_feed, preferred_element_type=jnp.float32)
        grad_hidden = jnp.einsum(
            "td,fd->tf", grad_feed, down_full, preferred_element_type=jnp.float32
        )
        gelu_pull = jax.vjp(
            lambda gate_in, up_in: jax.nn.gelu(gate_in, approximate=True) * up_in,
            saved_state.gate_values,
            saved_state.up_values,
        )[1]
        grad_gate, grad_up = gelu_pull(grad_hidden)
        grad_gate = grad_gate.astype(jnp.bfloat16)
        grad_up = grad_up.astype(jnp.bfloat16)
        gate_grad = jnp.einsum(
            "td,tf->df", normed_feed, grad_gate, preferred_element_type=jnp.float32
        )
        up_grad = jnp.einsum("td,tf->df", normed_feed, grad_up, preferred_element_type=jnp.float32)
        feed_rows = sum_rows(
            jnp.einsum("tf,df->td", grad_gate, gate_full, preferred_element_type=jnp.float32)
            + jnp.einsum("tf,df->td", grad_up, up_full, preferred_element_type=jnp.float32)
        )
        grad_norm_feed, feed_gain_grad = jax.vjp(norm_rows, saved_state.after_cross, feed_gain)[
            1
        ](feed_rows)
        grad_after_cross = cotangent + grad_norm_feed
        cross_context = saved_state.cross_context
        cross_weights = saved_state.cross_weights
        encoded = saved_state.encoded
        grad_cross_branch = gather_rows(grad_after_cross.astype(jnp.bfloat16))
        cross_output_grad = jnp.einsum(
            "te,td->ed", cross_context, grad_cross_branch, preferred_element_type=jnp.float32
        )
        grad_cross_context = split_heads(
            jnp.einsum(
                "td,ed->te",
                grad_cross_branch,
                cross_output_full,
                preferred_element_type=jnp.float32,
            ).astype(jnp.bfloat16)
        )
        grad_cross_weights = jnp.einsum(
            "ikgd,jkd->kgij",
            grad_cross_context,
            split_kv(saved_state.cross_values),
            preferred_element_type=jnp.float32,
        )
        grad_cross_scores = (
            cross_weights
            * (
                grad_cross_weights
                - jnp.sum(cross_weights * grad_cross_weights, axis=-1, keepdims=True)
            )
        ).astype(jnp.bfloat16)
        grad_cross_queries = (
            (
                jnp.einsum(
                    "kgij,jkd->ikgd",
                    grad_cross_scores,
                    split_kv(saved_state.cross_keys),
                    preferred_element_type=jnp.float32,
                )
                * score_scale
            )
            .reshape(piece_rows, local_heads * head_size)
            .astype(jnp.bfloat16)
        )
        key_part = (
            jnp.einsum(
                "kgij,ikgd->jkd",
                grad_cross_scores,
                split_heads(saved_state.cross_queries),
                preferred_element_type=jnp.float32,
            )
            * score_scale
        ).reshape(encoded.shape[0], kv_local * head_size)
        value_part = jnp.einsum(
            "kgij,ikgd->jkd",
            saved_state.cross_low,
            grad_cross_context,
            preferred_element_type=jnp.float32,
        ).reshape(encoded.shape[0], kv_local * head_size)
        key_sum, value_sum = (
            lax.psum_scatter(key_part, fsdp_axis, scatter_dimension=0, tiled=True),
            lax.psum_scatter(value_part, fsdp_axis, scatter_dimension=0, tiled=True),
        )
        key_low = key_sum.astype(jnp.bfloat16)
        value_low = value_sum.astype(jnp.bfloat16)
        encoded_own = lax.dynamic_slice_in_dim(encoded, fsdp_rank * encoder_rows, encoder_rows, 0)
        cross_key_grad = jnp.einsum(
            "ed,ec->dc", encoded_own, key_low, preferred_element_type=jnp.float32
        )
        cross_value_grad = jnp.einsum(
            "ed,ec->dc", encoded_own, value_low, preferred_element_type=jnp.float32
        )
        encoder_grad = sum_rows(
            jnp.einsum("ec,dc->ed", key_low, cross_key_full, preferred_element_type=jnp.float32)
            + jnp.einsum(
                "ec,dc->ed", value_low, cross_value_full, preferred_element_type=jnp.float32
            )
        )
        cross_query_grad = jnp.einsum(
            "td,tc->dc",
            saved_state.normed_cross,
            grad_cross_queries,
            preferred_element_type=jnp.float32,
        )
        cross_rows = sum_rows(
            jnp.einsum(
                "tc,dc->td",
                grad_cross_queries,
                cross_query_full,
                preferred_element_type=jnp.float32,
            )
        )
        grad_norm_cross, cross_gain_grad = jax.vjp(
            norm_rows, saved_state.after_self, cross_gain
        )[1](cross_rows)
        grad_after_self = grad_after_cross + grad_norm_cross
        queries = saved_state.queries
        keys_own = saved_state.keys_own
        values_own = saved_state.values_own
        context = saved_state.context
        log_total = saved_state.log_total
        normed_self = saved_state.normed_self
        query_heads = split_heads(queries)
        grad_self_branch = gather_rows(grad_after_self.astype(jnp.bfloat16))
        self_output_grad = jnp.einsum(
            "te,td->ed",
            saved_state.context_low,
            grad_self_branch,
            preferred_element_type=jnp.float32,
        )
        grad_context = jnp.einsum(
            "td,ed->te", grad_self_branch, output_full, preferred_element_type=jnp.float32
        ).astype(jnp.bfloat16)
        grad_context_heads = split_heads(grad_context)
        row_delta = jnp.transpose(
            jnp.sum(grad_context_heads.astype(jnp.float32) * context, axis=-1), (1, 2, 0)
        )

        def query_step():

            def step(carried, pieces, piece_start):
                key_piece, value_piece = pieces
                piece_length = key_piece.shape[0]
                block_width = math.gcd(piece_length, key_block_width)
                block_count = piece_length // block_width
                key_blocks = key_piece.reshape(block_count, block_width, kv_local, head_size)
                value_blocks = value_piece.reshape(block_count, block_width, kv_local, head_size)
                block_starts = block_width * jnp.arange(block_count, dtype=jnp.int32)

                def step_one_block(current, block_data):
                    key_block, value_block, block_start = block_data
                    bias_values, allowed, indicator = position_bias(
                        query_start, block_start, piece_rows, block_width
                    )
                    scores = (
                        jnp.einsum(
                            "ikgd,jkd->kgij",
                            query_heads,
                            key_block,
                            preferred_element_type=jnp.float32,
                        )
                        * score_scale
                        + bias_values
                    )
                    shares = jnp.where(allowed, jnp.exp(scores - log_total[..., None]), 0.0)
                    grad_shares = jnp.einsum(
                        "ikgd,jkd->kgij",
                        grad_context_heads,
                        value_block,
                        preferred_element_type=jnp.float32,
                    )
                    grad_scores = shares * (grad_shares - row_delta[..., None])
                    bias_grad = current[1] + jnp.einsum(
                        "hij,bij->hb",
                        grad_scores.reshape(local_heads, piece_rows, block_width),
                        indicator,
                        precision=highest,
                    )
                    scores_low = grad_scores.astype(jnp.bfloat16)
                    query_grad = (
                        current[0]
                        + jnp.einsum(
                            "kgij,jkd->ikgd",
                            scores_low,
                            key_block,
                            preferred_element_type=jnp.float32,
                        )
                        * score_scale
                    )
                    key_block_grad = (
                        jnp.einsum(
                            "kgij,ikgd->jkd",
                            scores_low,
                            query_heads,
                            preferred_element_type=jnp.float32,
                        ).reshape(block_width, kv_local * head_size)
                        * score_scale
                    )
                    value_block_grad = jnp.einsum(
                        "kgij,ikgd->jkd",
                        shares.astype(jnp.bfloat16),
                        grad_context_heads,
                        preferred_element_type=jnp.float32,
                    ).reshape(block_width, kv_local * head_size)
                    keys_all = lax.dynamic_update_slice_in_dim(
                        current[2],
                        lax.dynamic_slice_in_dim(current[2], block_start, block_width, 0)
                        + key_block_grad,
                        block_start,
                        0,
                    )
                    values_all = lax.dynamic_update_slice_in_dim(
                        current[3],
                        lax.dynamic_slice_in_dim(current[3], block_start, block_width, 0)
                        + value_block_grad,
                        block_start,
                        0,
                    )
                    return ((query_grad, bias_grad, keys_all, values_all), None)

                carried, unused = lax.scan(
                    step_one_block, carried, (key_blocks, value_blocks, block_starts)
                )
                return carried

            return step

        query_zero = jnp.zeros((piece_rows, kv_local, group_size, head_size), jnp.float32)
        bias_zero = jnp.zeros((local_heads, buckets), jnp.float32)
        all_zero = jnp.zeros((length, kv_local * head_size), jnp.float32)
        query_grad, bias_grad, keys_all, values_all = fold_keys(
            keys_own, values_own, query_step(), (query_zero, bias_zero, all_zero, all_zero)
        )
        key_sum_self, value_sum_self = (
            lax.psum_scatter(keys_all, fsdp_axis, scatter_dimension=0, tiled=True),
            lax.psum_scatter(values_all, fsdp_axis, scatter_dimension=0, tiled=True),
        )
        key_grad_low = key_sum_self.astype(jnp.bfloat16)
        value_grad_low = value_sum_self.astype(jnp.bfloat16)
        query_grad_low = query_grad.reshape(piece_rows, local_heads * head_size).astype(
            jnp.bfloat16
        )
        self_query_grad = jnp.einsum(
            "td,tc->dc", normed_self, query_grad_low, preferred_element_type=jnp.float32
        )
        self_key_grad = jnp.einsum(
            "td,tc->dc", normed_self, key_grad_low, preferred_element_type=jnp.float32
        )
        self_value_grad = jnp.einsum(
            "td,tc->dc", normed_self, value_grad_low, preferred_element_type=jnp.float32
        )
        self_rows = sum_rows(
            jnp.einsum("tc,dc->td", query_grad_low, query_full, preferred_element_type=jnp.float32)
            + jnp.einsum("tc,dc->td", key_grad_low, key_full, preferred_element_type=jnp.float32)
            + jnp.einsum(
                "tc,dc->td", value_grad_low, value_full, preferred_element_type=jnp.float32
            )
        )
        grad_norm_self, self_gain_grad = jax.vjp(norm_rows, saved_state.own_rows, self_gain)[1](
            self_rows
        )
        input_grad = grad_after_self + grad_norm_self
        grads_full = (
            self_query_grad,
            self_key_grad,
            self_value_grad,
            self_output_grad,
            cross_query_grad,
            cross_key_grad,
            cross_value_grad,
            cross_output_grad,
            gate_grad,
            up_grad,
            down_grad,
        )
        extras = (bias_grad, self_gain_grad, cross_gain_grad, feed_gain_grad)
        return (grads_full, extras, input_grad, encoder_grad)

    layer_list = []
    input_list = []
    encoder_list = []
    small_sums = None
    shard_grads = None
    for batch_index in range(batches):
        weights_forward = gather_weights(shards)
        (
            forward_query_full,
            forward_key_full,
            forward_value_full,
            forward_output_full,
            forward_cross_query_full,
            forward_cross_key_full,
            forward_cross_value_full,
            forward_cross_output_full,
            forward_gate_full,
            forward_up_full,
            forward_down_full,
        ) = weights_forward
        own_rows = inputs[batch_index].astype(jnp.float32)
        forward_normed_self = gather_rows(norm_rows(own_rows, self_gain).astype(jnp.bfloat16))
        forward_queries = matmul(forward_normed_self, forward_query_full).astype(jnp.bfloat16)
        forward_keys_own = matmul(forward_normed_self, forward_key_full).astype(jnp.bfloat16)
        forward_values_own = matmul(forward_normed_self, forward_value_full).astype(jnp.bfloat16)
        forward_query_heads = split_heads(forward_queries)

        def forward_step(carried, pieces, piece_start):
            key_piece, value_piece = pieces
            piece_length = key_piece.shape[0]
            block_width = math.gcd(piece_length, key_block_width)
            block_count = piece_length // block_width
            key_blocks = key_piece.reshape(block_count, block_width, kv_local, head_size)
            value_blocks = value_piece.reshape(block_count, block_width, kv_local, head_size)
            block_starts = block_width * jnp.arange(block_count, dtype=jnp.int32)

            def forward_one_block(current, block_data):
                running_max, running_total, accumulated = current
                key_block, value_block, block_start = block_data
                bias_values, allowed, indicator = position_bias(
                    query_start, block_start, piece_rows, block_width
                )
                scores = (
                    jnp.einsum(
                        "ikgd,jkd->kgij",
                        forward_query_heads,
                        key_block,
                        preferred_element_type=jnp.float32,
                    )
                    * score_scale
                    + bias_values
                )
                scores = jnp.where(allowed, scores, masked_score)
                new_max = jnp.maximum(running_max, jnp.max(scores, axis=-1))
                factor = jnp.exp(running_max - new_max)
                shares = jnp.where(allowed, jnp.exp(scores - new_max[..., None]), 0.0)
                running_total = running_total * factor + jnp.sum(shares, axis=-1)
                update = jnp.einsum(
                    "kgij,jkd->ikgd",
                    shares.astype(jnp.bfloat16),
                    value_block,
                    preferred_element_type=jnp.float32,
                )
                accumulated = accumulated * jnp.transpose(factor, (2, 0, 1))[..., None] + update
                return ((new_max, running_total, accumulated), None)

            carried, unused = lax.scan(
                forward_one_block, carried, (key_blocks, value_blocks, block_starts)
            )
            return carried

        stat_shape = (kv_local, group_size, piece_rows)
        initial = (
            jnp.full(stat_shape, masked_score, jnp.float32),
            jnp.zeros(stat_shape, jnp.float32),
            jnp.zeros((piece_rows, kv_local, group_size, head_size), jnp.float32),
        )
        running_max, running_total, accumulated = fold_keys(
            forward_keys_own, forward_values_own, forward_step, initial
        )
        forward_context = accumulated / jnp.transpose(running_total, (2, 0, 1))[..., None]
        forward_log_total = running_max + jnp.log(running_total)
        context_low = forward_context.reshape(piece_rows, local_heads * head_size).astype(
            jnp.bfloat16
        )
        after_self = own_rows + sum_rows(matmul(context_low, forward_output_full))
        normed_cross = gather_rows(norm_rows(after_self, cross_gain).astype(jnp.bfloat16))
        cross_queries = matmul(normed_cross, forward_cross_query_full).astype(jnp.bfloat16)
        forward_encoded = lax.all_gather(
            encoder_out[batch_index], (fsdp_axis, tensor_axis), axis=0, tiled=True
        )
        cross_keys = matmul(forward_encoded, forward_cross_key_full).astype(jnp.bfloat16)
        cross_values = matmul(forward_encoded, forward_cross_value_full).astype(jnp.bfloat16)
        cross_scores = (
            jnp.einsum(
                "ikgd,jkd->kgij",
                split_heads(cross_queries),
                split_kv(cross_keys),
                preferred_element_type=jnp.float32,
            )
            * score_scale
        )
        forward_cross_weights = jax.nn.softmax(cross_scores, axis=-1)
        cross_low = forward_cross_weights.astype(jnp.bfloat16)
        forward_cross_context = (
            jnp.einsum(
                "kgij,jkd->ikgd",
                cross_low,
                split_kv(cross_values),
                preferred_element_type=jnp.float32,
            )
            .reshape(piece_rows, local_heads * head_size)
            .astype(jnp.bfloat16)
        )
        after_cross = after_self + sum_rows(
            matmul(forward_cross_context, forward_cross_output_full)
        )
        forward_normed_feed = gather_rows(norm_rows(after_cross, feed_gain).astype(jnp.bfloat16))
        gate_values = matmul(forward_normed_feed, forward_gate_full)
        up_values = matmul(forward_normed_feed, forward_up_full)
        forward_hidden = (jax.nn.gelu(gate_values, approximate=True) * up_values).astype(
            jnp.bfloat16
        )
        layer_rows = after_cross + sum_rows(matmul(forward_hidden, forward_down_full))
        forward_saved_state = types.SimpleNamespace(
            own_rows=own_rows,
            normed_self=forward_normed_self,
            queries=forward_queries,
            keys_own=forward_keys_own,
            values_own=forward_values_own,
            context=forward_context,
            log_total=forward_log_total,
            context_low=context_low,
            after_self=after_self,
            normed_cross=normed_cross,
            cross_queries=cross_queries,
            encoded=forward_encoded,
            cross_keys=cross_keys,
            cross_values=cross_values,
            cross_weights=forward_cross_weights,
            cross_low=cross_low,
            cross_context=forward_cross_context,
            after_cross=after_cross,
            normed_feed=forward_normed_feed,
            gate_values=gate_values,
            up_values=up_values,
            hidden=forward_hidden,
        )
        layer_rows, saved_state = (layer_rows.astype(jnp.bfloat16), forward_saved_state)
        weights_backward = gather_weights(shards)
        grads_full, extras, input_grad, encoder_grad = backward(
            batch_index, saved_state, weights_backward
        )
        reduced = scatter_grads(grads_full)
        shard_grads = reduced if shard_grads is None else add_all(shard_grads, reduced)
        small_sums = extras if small_sums is None else add_all(small_sums, extras)
        layer_list.append(layer_rows)
        input_list.append(input_grad)
        encoder_list.append(encoder_grad)
    table_full = lax.dynamic_update_slice_in_dim(
        jnp.zeros((heads_all, buckets), jnp.float32), small_sums[0], tensor_rank * local_heads, 0
    )
    table_sum, self_gain_sum, cross_gain_sum, feed_gain_sum = lax.psum(
        (table_full, small_sums[1], small_sums[2], small_sums[3]), (fsdp_axis, tensor_axis)
    )
    return (
        jnp.stack(layer_list),
        jnp.stack(input_list),
        jnp.stack(encoder_list),
        table_sum,
        self_gain_sum,
        shard_grads[0],
        shard_grads[1],
        shard_grads[2],
        shard_grads[3],
        cross_gain_sum,
        shard_grads[4],
        shard_grads[5],
        shard_grads[6],
        shard_grads[7],
        feed_gain_sum,
        shard_grads[8],
        shard_grads[9],
        shard_grads[10],
    )


def to_chip(fsdp):
    return dict(device_id={fsdp_axis: fsdp}, device_id_type=pl.DeviceIdType.MESH)


def to_core(core):
    return dict(device_id={tensor_axis: core}, device_id_type=pl.DeviceIdType.MESH)


def chip_place(layers):
    rank = lax.axis_index(fsdp_axis)
    return rank, rank // 4, rank // 2 % 2, rank % 2


def peers_of(rank, y, x):
    found = []
    for o in (1, 2, 3):
        other_y = 1 - y if o & 2 else y
        other_x = 1 - x if o & 1 else x
        spot = 2 * other_y + other_x
        found.append((rank - 2 * y - x + spot, spot))
    return found


def greet(layers):
    rank, z, y, x = chip_place(layers)
    barrier = pltpu.get_barrier_semaphore()
    for chip, spot in peers_of(rank, y, x):
        pl.semaphore_signal(barrier, inc=1, **to_chip(chip))
    for o in range(1, layers):
        pl.semaphore_signal(barrier, inc=1, **to_chip(rank - 4 * z + 4 * ((z + o) % layers)))
    pl.semaphore_signal(barrier, inc=1, **to_core(1 - lax.axis_index(tensor_axis)))
    pl.semaphore_wait(barrier, 3 + layers)


dma = pltpu.SemaphoreType.DMA


class Column:
    def __init__(self, layers, source, land, z_sem, core_sem=None):
        self.layers, self.source, self.land = layers, source, land
        self.z_sem, self.core_sem = z_sem, core_sem
        self.rank, self.z, self.y, self.x = chip_place(layers)
        self.core = lax.axis_index(tensor_axis)

    def place(self, layer):
        return (layer,) if self.core_sem is None else (layer, self.core)

    def hop(self, o):
        there = (self.z + o) % self.layers
        return pltpu.make_async_remote_copy(
            src_ref=self.source.at[there],
            dst_ref=self.land.at[self.place(self.z)],
            send_sem=self.z_sem.at[0, o],
            recv_sem=self.z_sem.at[1, self.z],
            **to_chip(self.rank + 4 * (there - self.z)),
        )

    def arrival(self, layer):
        return pltpu.make_async_remote_copy(
            src_ref=self.source.at[0],
            dst_ref=self.land.at[self.place(layer)],
            send_sem=self.z_sem.at[0, 0],
            recv_sem=self.z_sem.at[1, layer],
            **to_chip(self.rank + 4 - 8 * (self.z // 2)),
        )

    def over(self, layer):
        return pltpu.make_async_remote_copy(
            src_ref=self.land.at[layer, self.core],
            dst_ref=self.land.at[layer, self.core],
            send_sem=self.core_sem.at[0, layer],
            recv_sem=self.core_sem.at[1, layer],
            **to_core(1 - self.core),
        )

    def start(self):
        for o in range(1, self.layers):
            self.hop(o).start()
        self.land[self.place(self.z)] = self.source[self.z]

    def arrive(self):
        for o in range(1, self.layers):
            self.arrival((self.z + o) % self.layers).wait_recv()
        if self.core_sem is not None:
            for layer in range(self.layers):
                self.over(layer).start()

    def finish(self):
        for o in range(1, self.layers):
            self.hop(o).wait_send()
        if self.core_sem is not None:
            for layer in range(self.layers):
                self.over(layer).wait()


class PlaneSwap:
    def __init__(self, layers, source, land, sem):
        self.source, self.land, self.sem = source, land, sem
        self.rank, self.z, self.y, self.x = chip_place(layers)
        self.spot = 2 * self.y + self.x
        self.peers = peers_of(self.rank, self.y, self.x)

    def hop(self, o):
        chip, there = self.peers[o]
        return pltpu.make_async_remote_copy(
            src_ref=self.source.at[there],
            dst_ref=self.land.at[self.spot],
            send_sem=self.sem.at[0, o],
            recv_sem=self.sem.at[1, o],
            **to_chip(chip),
        )

    def start(self):
        for o in range(3):
            self.hop(o).start()
        self.land[self.spot] = self.source[self.spot]

    def arrival(self, o):
        chip, there = self.peers[o]
        return pltpu.make_async_remote_copy(
            src_ref=self.source.at[there],
            dst_ref=self.land.at[there],
            send_sem=self.sem.at[0, o],
            recv_sem=self.sem.at[1, o],
            **to_chip(chip),
        )

    def arrive(self):
        for o in range(3):
            self.arrival(o).wait_recv()

    def finish(self):
        for o in range(3):
            self.hop(o).wait_send()


class PlaneGather:
    def __init__(self, layers, source, land, sem, core_sem):
        self.source, self.land, self.sem, self.core_sem = source, land, sem, core_sem
        self.rank, self.z, self.y, self.x = chip_place(layers)
        self.core = lax.axis_index(tensor_axis)
        self.spot = 2 * self.y + self.x
        self.peers = peers_of(self.rank, self.y, self.x)

    def hop(self, o, spot):
        return pltpu.make_async_remote_copy(
            src_ref=self.source,
            dst_ref=self.land.at[spot, self.core],
            send_sem=self.sem.at[0, o],
            recv_sem=self.sem.at[1, o],
            **to_chip(self.peers[o][0]),
        )

    def over(self, spot):
        return pltpu.make_async_remote_copy(
            src_ref=self.land.at[spot, self.core],
            dst_ref=self.land.at[spot, self.core],
            send_sem=self.core_sem.at[0, spot],
            recv_sem=self.core_sem.at[1, spot],
            **to_core(1 - self.core),
        )

    def start(self):
        for o in range(3):
            self.hop(o, self.spot).start()
        self.land[self.spot, self.core] = self.source[...]

    def arrive(self):
        for o in range(3):
            self.hop(o, self.peers[o][1]).wait_recv()
        for spot in range(4):
            self.over(spot).start()

    def finish(self):
        for o in range(3):
            self.hop(o, self.spot).wait_send()
        for spot in range(4):
            self.over(spot).wait()


def open_kernel(
    layers,
    rows_ref,
    enc_ref,
    shard_ref,
    rows_out,
    enc_out,
    whole_ref,
    rows_land,
    enc_land,
    enc_all,
    rows_z,
    rows_core,
    enc_z,
    plane_sem,
    plane_core,
    *gather_refs,
):
    gather = RowGather(layers, False, shard_ref, whole_ref, *gather_refs)
    rows = Column(layers, rows_ref, rows_land, rows_z, rows_core)
    enc = Column(layers, enc_ref, enc_land, enc_z)
    plane = PlaneGather(layers, enc_land, enc_all, plane_sem, plane_core)
    gather.begin()
    greet(layers)
    rows.start()
    enc.start()
    gather.send_own()
    rows.arrive()
    enc.arrive()
    plane.start()

    def one(m, carry):
        gather.step(m)
        return carry

    lax.fori_loop(0, 2 * layers - 4, one, 0)
    plane.arrive()
    lax.fori_loop(2 * layers - 4, 2 * layers, one, 0)
    rows.finish()
    rows_out[...] = rows_land[...]
    enc.finish()
    plane.finish()
    enc_out[...] = enc_all[...]
    gather.finish()


def open_rows(layers, inputs, encoder, shard):
    bf16 = jnp.bfloat16
    own, width = inputs.shape[1:]
    enc_own = encoder.shape[1]
    cols = shard.shape[1]
    vmem, anywhere = pl.BlockSpec(memory_space=pltpu.VMEM), pl.BlockSpec(memory_space=pl.ANY)
    rows_shape, enc_shape = (layers, 2, own, width), (4, 2, layers, enc_own, width)
    rows, enc, whole = pl.pallas_call(
        functools.partial(open_kernel, layers),
        name="open_rows",
        out_shape=(
            jax.ShapeDtypeStruct(rows_shape, bf16),
            jax.ShapeDtypeStruct(enc_shape, bf16),
            jax.ShapeDtypeStruct((layers, 2, 2, 2, 2, 16, cols), bf16),
        ),
        in_specs=[vmem, vmem, anywhere],
        out_specs=(vmem, vmem, anywhere),
        scratch_shapes=[
            pltpu.VMEM(rows_shape, bf16),
            pltpu.VMEM((layers, enc_own, width), bf16),
            pltpu.VMEM(enc_shape, bf16),
            dma((2, layers)),
            dma((2, layers)),
            dma((2, layers)),
            dma((2, 3)),
            dma((2, 4)),
            *gather_scratch(layers, cols),
        ],
        compiler_params=pltpu.CompilerParams(collective_id=5, has_side_effects=True),
    )(inputs, encoder, shard.reshape(2, 2, 16, cols))
    return rows, enc, whole.reshape(layers * 256, cols)


def close_kernel(
    layers,
    grads_ref,
    got_x,
    got_y,
    rows_ref,
    small_ref,
    sum_ref,
    rows_out,
    small_out,
    rows_land,
    small_x,
    small_y,
    small_z,
    small_c,
    small_s,
    rows_z,
    small_sem,
    z_sem,
    *sum_refs,
):
    grads = GradSum(layers, grads_ref, (got_x, got_y), sum_ref, *sum_refs)
    rows = Column(layers, rows_ref, rows_land, rows_z)
    rank, z, y, x = chip_place(layers)
    core = lax.axis_index(tensor_axis)
    grads.start()
    greet(layers)
    grads.send_first(0)
    rows.start()

    def swap(source, land, n, where):
        return pltpu.make_async_remote_copy(
            src_ref=source,
            dst_ref=land,
            send_sem=small_sem.at[0, n],
            recv_sem=small_sem.at[1, n],
            **where,
        )

    across_x = swap(small_ref, small_x, 0, to_chip(rank + 1 - 2 * x))
    across_y = swap(small_s.at[0], small_y, 1, to_chip(rank + 2 - 4 * y))
    across_core = swap(small_s.at[2], small_c, 2, to_core(1 - core))

    def across_z(o, layer):
        there = (z + o) % layers
        return pltpu.make_async_remote_copy(
            src_ref=small_s.at[1],
            dst_ref=small_z.at[layer],
            send_sem=z_sem.at[0, o],
            recv_sem=z_sem.at[1, layer],
            **to_chip(rank + 4 * (there - z)),
        )

    across_x.start()
    across_x.wait()
    small_s[0] = small_ref[...] + small_x[...]
    grads.send_first(1)
    grads.advance(1)
    across_y.start()
    across_y.wait()
    small_s[1] = small_s[0] + small_y[...]
    small_z[z] = small_s[1]
    for o in range(1, layers):
        across_z(o, z).start()
    grads.send_first(2)
    grads.advance(2)
    for o in range(1, layers):
        across_z(o, (z + o) % layers).wait_recv()
        across_z(o, z).wait_send()
    total = small_z[0]
    for layer in range(1, layers):
        total = total + small_z[layer]
    small_s[2] = total
    across_core.start()

    def one(m, carry):
        grads.send_first(m)
        grads.advance(m)
        return carry

    lax.fori_loop(3, sum_steps(layers), one, 0)
    across_core.wait()
    low = jnp.where(core == 0, small_s[2], small_c[...])
    row = lax.broadcasted_iota(jnp.int32, low.shape, 0)
    small_out[...] = jnp.where(row == 3, small_s[2] + small_c[...], low)
    rows.arrive()
    rows_out[...] = rows_land[...].astype(jnp.float32)
    rows.finish()
    grads.finish()


def close_rows(layers, grads, got, rows, small):
    f32, bf16 = jnp.float32, jnp.bfloat16
    cols = grads.shape[1]
    vmem, anywhere = pl.BlockSpec(memory_space=pltpu.VMEM), pl.BlockSpec(memory_space=pl.ANY)
    sums, rows_full, small_full = pl.pallas_call(
        functools.partial(close_kernel, layers),
        name="close_rows",
        out_shape=(
            jax.ShapeDtypeStruct((2, 2, 16, cols), f32),
            jax.ShapeDtypeStruct(rows.shape, f32),
            jax.ShapeDtypeStruct(small.shape, f32),
        ),
        in_specs=[anywhere] * 3 + [vmem, vmem],
        out_specs=(vmem, vmem, vmem),
        scratch_shapes=[
            pltpu.VMEM(rows.shape, bf16),
            pltpu.VMEM(small.shape, f32),
            pltpu.VMEM(small.shape, f32),
            pltpu.VMEM((layers, *small.shape), f32),
            pltpu.VMEM(small.shape, f32),
            pltpu.VMEM((3, *small.shape), f32),
            dma((2, layers)),
            dma((2, 3)),
            dma((2, layers)),
            *sum_scratch(layers, cols),
        ],
        compiler_params=pltpu.CompilerParams(
            collective_id=7, has_side_effects=True, vmem_limit_bytes=40 << 20
        ),
    )(grads.reshape(layers, 2, 2, 2, 2, 16, cols), *got, rows, small)
    return sums.reshape(-1, cols), rows_full, small_full


def first_hop(layers, grads):
    rank = lax.axis_index(fsdp_axis)
    chips = range(4 * layers)
    whole = grads.reshape(layers, 2, 2, 2, 2, 16, grads.shape[1])
    to_x = lax.dynamic_index_in_dim(whole[:, :, :, 0], 1 - rank % 2, 2, keepdims=False)
    to_y = lax.dynamic_index_in_dim(whole[:, :, :, 1], 1 - rank // 2 % 2, 1, keepdims=False)
    return (
        lax.ppermute(to_x, fsdp_axis, [(chip, chip ^ 1) for chip in chips]),
        lax.ppermute(to_y, fsdp_axis, [(chip, chip ^ 2) for chip in chips]),
    )


def last_hop(layers, whole):
    rank = lax.axis_index(fsdp_axis)
    chips = range(4 * layers)
    x, y = rank % 2, rank // 2 % 2
    to_y = lax.dynamic_index_in_dim(whole[:, :, :, 0], y, 1, keepdims=False)
    to_x = lax.dynamic_index_in_dim(whole[:, :, :, 1], x, 2, keepdims=False)
    from_y = lax.ppermute(to_y, fsdp_axis, [(chip, chip ^ 2) for chip in chips])
    from_x = lax.ppermute(to_x, fsdp_axis, [(chip, chip ^ 1) for chip in chips])
    zero = jnp.int32(0)
    whole = lax.dynamic_update_slice(
        whole, from_y[:, None, :, None], (zero, 1 - y, zero, zero, zero, zero, zero)
    )
    return lax.dynamic_update_slice(
        whole, from_x[:, :, None, None], (zero, zero, 1 - x, 1 + zero, zero, zero, zero)
    )

def sum_scratch(layers, cols):
    steps = 2 * layers
    bf16 = jnp.bfloat16
    return [
        pltpu.VMEM((layers, 2, 2, 2, 2, 16, cols), bf16),
        pltpu.VMEM((layers, 2, 2, 2, 16, cols), bf16),
        pltpu.VMEM((steps, 2, 16, cols), bf16),
        pltpu.VMEM((steps, 2, 16, cols), bf16),
        pltpu.VMEM((steps, 2, 16, cols), bf16),
        dma((3, layers)),
        dma((2, steps, 2, 2)),
        dma((2, steps, 2)),
        dma((2, steps)),
        dma((2, steps)),
    ]


def sum_steps(layers):
    return 2 * layers + layers + 3


class GradSum:
    def __init__(self, layers, whole, got, out, own, first, second, below, above, load, s1, s2, su, sd):
        self.got = got
        self.layers, self.whole, self.out, self.own = layers, whole, out, own
        self.first, self.second, self.below, self.above = first, second, below, above
        self.load, self.s1, self.s2, self.su, self.sd = load, s1, s2, su, sd
        self.rank, self.z, self.y, self.x = chip_place(layers)
        self.x_chip = self.rank + 1 - 2 * self.x
        self.y_chip = self.rank + 2 - 4 * self.y
        self.steps = 2 * layers

    def layer_of(self, n):
        turn = n // 2
        return jnp.where(turn % 2 == 1, turn // 2, self.layers - 1 - turn // 2)

    def loads(self, turn):
        layer = self.layer_of(2 * turn)
        copies = [
            pltpu.make_async_copy(self.whole.at[layer], self.own.at[layer], self.load.at[0, turn])
        ]
        for colour, came in enumerate(self.got):
            copies.append(
                pltpu.make_async_copy(
                    came.at[layer], self.first.at[layer, colour], self.load.at[1 + colour, turn]
                )
            )
        return copies

    def hop_one(self, n, colour, which):
        layer, chunk = self.layer_of(n), n % 2
        if colour == 0:
            source, chip = self.own.at[layer, which, 1 - self.x, 0, chunk], self.x_chip
        else:
            source, chip = self.own.at[layer, 1 - self.y, which, 1, chunk], self.y_chip
        return pltpu.make_async_remote_copy(
            src_ref=source,
            dst_ref=self.first.at[layer, colour, which, chunk],
            send_sem=self.s1.at[0, n, colour, which],
            recv_sem=self.s1.at[1, n, colour, which],
            **to_chip(chip),
        )

    def hop_two(self, n, colour):
        layer, chunk = self.layer_of(n), n % 2
        if colour == 0:
            source, chip = self.own.at[layer, 1 - self.y, self.x, 0, chunk], self.y_chip
        else:
            source, chip = self.own.at[layer, self.y, 1 - self.x, 1, chunk], self.x_chip
        return pltpu.make_async_remote_copy(
            src_ref=source,
            dst_ref=self.second.at[n, colour],
            send_sem=self.s2.at[0, n, colour],
            recv_sem=self.s2.at[1, n, colour],
            **to_chip(chip),
        )

    def hop_z(self, n, up):
        layer, chunk = self.layer_of(n), n % 2
        sems = self.su if up else self.sd
        return pltpu.make_async_remote_copy(
            src_ref=self.own.at[layer, self.y, self.x, :, chunk],
            dst_ref=(self.below if up else self.above).at[n],
            send_sem=sems.at[0, n],
            recv_sem=sems.at[1, n],
            **to_chip(self.rank + (4 if up else -4)),
        )

    def start(self):
        for turn in range(self.layers):
            for copy in self.loads(turn):
                copy.start()

    def send_first(self, n):
        @pl.when(n < self.steps)
        def _():
            @pl.when(n % 2 == 0)
            def _():
                for copy in self.loads(n // 2):
                    copy.wait()

            if not self.got:
                for which in range(2):
                    for colour in range(2):
                        self.hop_one(n, colour, which).start()

    def advance(self, m):
        steps, layers = self.steps, self.layers
        n = m - 1

        @pl.when((n >= 0) & (n < steps))
        def _():
            layer, chunk = self.layer_of(n), n % 2
            for colour in range(2):
                for other in range(2):
                    if colour == 0:
                        which = (1 - self.y) if other == 0 else self.y
                        place = (layer, which, self.x, 0, chunk)
                    else:
                        which = (1 - self.x) if other == 0 else self.x
                        place = (layer, self.y, which, 1, chunk)
                    if not self.got:
                        self.hop_one(n, colour, which).wait_recv()
                    self.own[place] = self.own[place] + self.first[layer, colour, which, chunk]
                    if other == 0:
                        self.hop_two(n, colour).start()

        n2 = m - 2

        @pl.when((n2 >= 0) & (n2 < steps))
        def _():
            layer, chunk = self.layer_of(n2), n2 % 2
            for colour in range(2):
                self.hop_two(n2, colour).wait_recv()
                place = (layer, self.y, self.x, colour, chunk)
                self.own[place] = self.own[place] + self.second[n2, colour]

        for up in (True, False):
            chain = self.z if up else layers - 1 - self.z
            nz = m - 2 - chain
            layer = self.layer_of(nz)
            beyond = (layer > self.z) if up else (layer < self.z)

            @pl.when((nz >= 0) & (nz < steps) & beyond)
            def _():
                @pl.when(chain > 0)
                def _():
                    self.hop_z(nz, up).wait_recv()
                    came = self.below if up else self.above
                    for colour in range(2):
                        place = (layer, self.y, self.x, colour, nz % 2)
                        self.own[place] = self.own[place] + came[nz, colour]

                self.hop_z(nz, up).start()

        nf = m - 2 - layers

        @pl.when((nf >= 0) & (nf < steps) & (self.layer_of(nf) == self.z))
        def _():
            layer, chunk = self.layer_of(nf), nf % 2
            for colour in range(2):
                self.out[colour, chunk] = self.own[layer, self.y, self.x, colour, chunk].astype(
                    jnp.float32
                )
            for up in (True, False):
                chain = self.z if up else layers - 1 - self.z

                @pl.when(chain > 0)
                def _():
                    self.hop_z(nf, up).wait_recv()
                    came = self.below if up else self.above
                    for colour in range(2):
                        self.out[colour, chunk] += came[nf, colour].astype(jnp.float32)

    def finish(self):
        def one(n, carry):
            for colour in range(2):
                if not self.got:
                    for which in range(2):
                        self.hop_one(n, colour, which).wait_send()
                self.hop_two(n, colour).wait_send()
            layer = self.layer_of(n)
            for up in (True, False):

                @pl.when((layer > self.z) if up else (layer < self.z))
                def _():
                    self.hop_z(n, up).wait_send()

            return carry

        lax.fori_loop(0, self.steps, one, 0)

def gather_scratch(layers, cols):
    return [
        pltpu.VMEM((2, 2, 16, cols), jnp.bfloat16),
        dma((2,)),
        dma((2, 2, layers, 2)),
        dma((2, layers, 2)),
        dma((2, layers, 2)),
        dma((2, layers, 2)),
        dma((2, layers, 2)),
    ]


class RowGather:
    def __init__(self, layers, short, shard, whole, here, local, sz, sx, sy, sfx, sfy):
        self.short = short
        self.layers, self.shard, self.whole, self.here = layers, shard, whole, here
        self.local, self.sz, self.sx, self.sy, self.sfx, self.sfy = local, sz, sx, sy, sfx, sfy
        self.rank, self.z, self.y, self.x = chip_place(layers)
        self.x_chip = self.rank + 1 - 2 * self.x
        self.y_chip = self.rank + 2 - 4 * self.y

    def take(self):
        return pltpu.make_async_copy(self.shard, self.here, self.local.at[0])

    def put(self):
        place = self.whole.at[self.z, self.y, self.x]
        return pltpu.make_async_copy(self.here, place, self.local.at[1])

    def source(self, layer, chunk, own, colours=slice(None)):
        if own:
            return self.shard.at[colours, chunk]
        return self.whole.at[layer, self.y, self.x, colours, chunk]

    def along_z(self, layer, chunk, up, own=False):
        return pltpu.make_async_remote_copy(
            src_ref=self.source(layer, chunk, own),
            dst_ref=self.whole.at[layer, self.y, self.x, :, chunk],
            send_sem=self.sz.at[0, int(up), layer, chunk],
            recv_sem=self.sz.at[1, int(up), layer, chunk],
            **to_chip(self.rank + (4 if up else -4)),
        )

    def in_plane(self, layer, chunk, along_x, own=False):
        sems = self.sx if along_x else self.sy
        colours = slice(None)
        if self.short:
            colours = 0 if along_x else 1
        return pltpu.make_async_remote_copy(
            src_ref=self.source(layer, chunk, own, colours),
            dst_ref=self.whole.at[layer, self.y, self.x, colours, chunk],
            send_sem=sems.at[0, layer, chunk],
            recv_sem=sems.at[1, layer, chunk],
            **to_chip(self.x_chip if along_x else self.y_chip),
        )

    def onward(self, layer, chunk, along_x):
        if along_x:
            place = (layer, 1 - self.y, self.x, 1, chunk)
            sems, chip = self.sfx, self.x_chip
        else:
            place = (layer, self.y, 1 - self.x, 0, chunk)
            sems, chip = self.sfy, self.y_chip
        return pltpu.make_async_remote_copy(
            src_ref=self.whole.at[place],
            dst_ref=self.whole.at[place],
            send_sem=sems.at[0, layer, chunk],
            recv_sem=sems.at[1, layer, chunk],
            **to_chip(chip),
        )

    def begin(self):
        self.take().start()

    def send_own(self):
        for chunk in range(2):

            @pl.when(self.z < self.layers - 1)
            def _():
                self.along_z(self.z, chunk, True, own=True).start()

            @pl.when(self.z > 0)
            def _():
                self.along_z(self.z, chunk, False, own=True).start()

            for along_x in (True, False):
                self.in_plane(self.z, chunk, along_x, own=True).start()
        self.take().wait()
        self.put().start()

    def pass_on(self, m):
        far, chunk = m // 2, m % 2
        for up in (True, False):
            layer = self.z - far if up else self.z + far
            near = (layer >= 0) if up else (layer < self.layers)

            @pl.when((far > 0) & near)
            def _():
                self.along_z(layer, chunk, up).wait_recv()

                @pl.when((self.z < self.layers - 1) if up else (self.z > 0))
                def _():
                    self.along_z(layer, chunk, up).start()

                for along_x in (True, False):
                    self.in_plane(layer, chunk, along_x).start()

    def turn(self, m):
        far, chunk = m // 2, m % 2
        for up in (True, False):
            layer = self.z - far if up else self.z + far
            near = (layer >= 0) if up else ((layer < self.layers) & (far > 0))

            @pl.when(near)
            def _():
                for along_x in (True, False):
                    self.in_plane(layer, chunk, along_x).wait_recv()
                    self.onward(layer, chunk, not along_x).start()

    def step(self, m):
        @pl.when(m + 2 < 2 * self.layers)
        def _():
            self.pass_on(m + 2)

        if not self.short:
            self.turn(m)

    def finish(self):
        self.put().wait()

        def one(n, carry):
            layer, chunk = n // 2, n % 2
            for along_x in (True, False):
                if self.short:
                    self.in_plane(layer, chunk, along_x).wait_recv()
                else:
                    self.onward(layer, chunk, along_x).wait()
                self.in_plane(layer, chunk, along_x).wait_send()

            @pl.when((self.z < self.layers - 1) & (layer <= self.z))
            def _():
                self.along_z(layer, chunk, True).wait_send()

            @pl.when((self.z > 0) & (layer >= self.z))
            def _():
                self.along_z(layer, chunk, False).wait_send()

            return carry

        lax.fori_loop(0, 2 * self.layers, one, 0)

def attend_forward_kernel(
    score_scale,
    layers,
    qkv_ref,
    bias_ref,
    cot_ref,
    shard_ref,
    feed_ref,
    kept_ref,
    low_ref,
    full_ref,
    total_ref,
    cot_out,
    whole_ref,
    feed_whole,
    came,
    landed,
    low_s,
    cot_land,
    q_s,
    k_s,
    v_s,
    bias_s,
    score_s,
    in_sem,
    out_send,
    out_recv,
    cot_z,
    cot_core,
    *gather_refs,
):
    blocks = bias_s.shape[1]
    sources = qkv_ref.shape[0]
    head = k_s.shape[1]
    half = len(gather_refs) // 2
    gathers = (
        RowGather(layers, True, feed_ref, feed_whole, *gather_refs[half:]),
        RowGather(layers, False, shard_ref, whole_ref, *gather_refs[:half]),
    )
    rank, z, y, x = chip_place(layers)
    spot = 2 * y + x
    peers = peers_of(rank, y, x)
    heads = PlaneSwap(layers, qkv_ref, came, in_sem)
    cot = Column(layers, cot_ref, cot_land, cot_z, cot_core)
    for gather in gathers:
        gather.begin()
    greet(layers)
    heads.start()
    for gather in gathers:
        gather.send_own()
    cot.start()

    def make_bias(n, carry):
        row = jnp.broadcast_to(bias_ref[pl.ds(n, 1), :], (tile, 2 * tile))
        turned = pltpu.roll(row, tile + 1, 1, stride=1, stride_axis=0)
        bias_s[n // blocks, n % blocks] = turned[:, :tile]
        return carry

    lax.fori_loop(0, 2 * blocks, make_bias, 0)
    heads.arrive()
    unpack_pair(came, q_s, k_s, v_s, score_scale)
    kept_ref[...] = came[...]

    def row_block(turn, carry):
        i = blocks - 1 - turn
        at = pl.ds(pl.multiple_of(i * tile, tile), tile)
        found = []
        for h in range(2):
            query = q_s[h, at, :]

            def score_step(j, top):
                key = k_s[pl.ds(pl.multiple_of(j * tile, tile), tile), :]
                score = dot_t(query, key) + bias_s[h, i - j]
                score_s[j] = score
                return jnp.maximum(top, jnp.maximum(score[:, :128], score[:, 128:]))

            top = lax.fori_loop(
                0, i + 1, score_step, jnp.full((tile, 128), masked_score, jnp.float32)
            )
            top = jnp.max(top, axis=1, keepdims=True)

            def share_step(j, state):
                total, summed = state
                share = jnp.exp(score_s[j] - top)
                value = v_s[pl.ds(pl.multiple_of(j * tile, tile), tile), :]
                summed = summed + jnp.dot(
                    share.astype(jnp.bfloat16), value, preferred_element_type=jnp.float32
                )
                return (total + share[:, :128] + share[:, 128:], summed)

            total, summed = lax.fori_loop(
                0,
                i + 1,
                share_step,
                (jnp.zeros((tile, 128), jnp.float32), jnp.zeros((tile, head), jnp.float32)),
            )
            total = jnp.sum(total, axis=1, keepdims=True)
            found.append(summed / total)
            log_total = jnp.broadcast_to(top + jnp.log(total), (tile, 128))
            total_ref[pl.ds(h * blocks + i, 1), :] = jnp.transpose(log_total)[0:1, :]
        both = jnp.concatenate(found, axis=1)
        full_ref[at, :] = both
        both = both.astype(jnp.bfloat16)
        for part in range(tile // 128):
            block = i * (tile // 128) + part
            low_s[block] = both[part * 128 : (part + 1) * 128]

        for gather in gathers:
            gather.step(turn)
        for part in range(tile // 128):
            block = i * (tile // 128) + part

            @pl.when(block % sources == spot)
            def _():
                landed[spot, block // sources] = low_s[block]

            @pl.when(block % sources != spot)
            def _():
                hand_back(block).start()

        return carry

    def hand_back(block):
        return pltpu.make_async_remote_copy(
            src_ref=low_s.at[block],
            dst_ref=landed.at[spot, block // sources],
            send_sem=out_send.at[block],
            recv_sem=out_recv.at[spot, block // sources],
            **to_chip(rank - spot + block % sources),
        )

    lax.fori_loop(0, blocks // 2, row_block, 0)
    cot.arrive()
    lax.fori_loop(blocks // 2, blocks, row_block, 0)
    for o in range(3):
        chip, there = peers[o]
        for turn in range(layers):
            pltpu.make_async_remote_copy(
                src_ref=low_s.at[0],
                dst_ref=landed.at[there, turn],
                send_sem=out_send.at[0],
                recv_sem=out_recv.at[there, turn],
                **to_chip(chip),
            ).wait_recv()
    for source in range(sources):
        for turn in range(layers):
            low_ref[turn * 128 : (turn + 1) * 128, source * 128 : (source + 1) * 128] = landed[
                source, turn
            ]
    heads.finish()
    cot.finish()
    cot_out[...] = cot_land[...]
    for block in range(sources * layers):

        @pl.when(block % sources != spot)
        def _():
            hand_back(block).wait_send()

    for gather in gathers:
        gather.finish()


def attend_forward(scale, layers, qkv, bias, cotangent, shard, feed_shard):
    f32, bf16 = jnp.float32, jnp.bfloat16
    sources, rows, wide = qkv.shape
    head = wide // 4
    length = sources * rows
    blocks = length // tile
    cols, feed_cols = shard.shape[1], feed_shard.shape[1]
    chips = (layers, 2, 2, 2, 2, 16)
    cot_shape = (layers, 2, *cotangent.shape[1:])
    vmem, anywhere = pl.BlockSpec(memory_space=pltpu.VMEM), pl.BlockSpec(memory_space=pl.ANY)
    kept, low, full, total, cot, whole, feed_whole = pl.pallas_call(
        functools.partial(attend_forward_kernel, scale, layers),
        name="attend_forward",
        out_shape=(
            jax.ShapeDtypeStruct(qkv.shape, bf16),
            jax.ShapeDtypeStruct((rows, sources * 2 * head), bf16),
            jax.ShapeDtypeStruct((length, 2 * head), f32),
            jax.ShapeDtypeStruct((2 * blocks, tile), f32),
            jax.ShapeDtypeStruct(cot_shape, bf16),
            jax.ShapeDtypeStruct((*chips, cols), bf16),
            jax.ShapeDtypeStruct((*chips, feed_cols), bf16),
        ),
        in_specs=[vmem, vmem, vmem, anywhere, anywhere],
        out_specs=(vmem, vmem, vmem, vmem, vmem, anywhere, anywhere),
        scratch_shapes=[
            pltpu.VMEM(qkv.shape, bf16),
            pltpu.VMEM((sources, layers, 128, 2 * head), bf16),
            pltpu.VMEM((length // 128, 128, 2 * head), bf16),
            pltpu.VMEM(cot_shape, bf16),
            pltpu.VMEM((2, length, head), bf16),
            pltpu.VMEM((length, head), bf16),
            pltpu.VMEM((length, head), bf16),
            pltpu.VMEM((2, blocks, tile, tile), f32),
            pltpu.VMEM((blocks, tile, tile), f32),
            dma((2, 3)),
            dma((length // 128,)),
            dma((sources, layers)),
            dma((2, layers)),
            dma((2, layers)),
            *gather_scratch(layers, cols),
            *gather_scratch(layers, feed_cols),
        ],
        compiler_params=pltpu.CompilerParams(
            collective_id=6, has_side_effects=True, vmem_limit_bytes=56 << 20
        ),
    )(
        qkv,
        bias,
        cotangent,
        shard.reshape(2, 2, 16, cols),
        feed_shard.reshape(2, 2, 16, feed_cols),
    )
    return kept, low, full, total, cot, whole.reshape(layers * 256, cols), feed_whole

def attend_backward_kernel(
    score_scale,
    layers,
    kept_ref,
    ctx_ref,
    full_ref,
    total_ref,
    bias_ref,
    kv_ref,
    rows_ref,
    grads_ref,
    feed_ref,
    got_x,
    got_y,
    out_ref,
    sums_ref,
    kv_out,
    rows_out,
    grad_sum_ref,
    feed_sum_ref,
    ctx_land,
    kv_land,
    rows_land,
    out_s,
    out_land,
    q_s,
    k_s,
    v_s,
    g_s,
    bias_s,
    sum_s,
    delta_s,
    dq_s,
    dk_s,
    dv_s,
    ctx_sem,
    kv_sem,
    rows_z,
    out_sem,
    *sum_refs,
):
    blocks = bias_s.shape[1]
    sources, rows, _ = kept_ref.shape
    head = k_s.shape[1]
    half = len(sum_refs) // 2
    sums = (
        GradSum(layers, feed_ref, (got_x, got_y), feed_sum_ref, *sum_refs[half:]),
        GradSum(layers, grads_ref, (), grad_sum_ref, *sum_refs[:half]),
    )
    context = PlaneSwap(layers, ctx_ref, ctx_land, ctx_sem)
    cross = PlaneSwap(layers, kv_ref, kv_land, kv_sem)
    ended = Column(layers, rows_ref, rows_land, rows_z)
    back = PlaneSwap(layers, out_s, out_land, out_sem)
    for grads in sums:
        grads.start()
    greet(layers)
    context.start()
    for grads in sums:
        grads.send_first(0)
    cross.start()
    ended.start()
    unpack_pair(kept_ref, q_s, k_s, v_s, score_scale)

    def make_bias(n, carry):
        row = jnp.broadcast_to(bias_ref[pl.ds(n, 1), :], (tile, 2 * tile))
        turned = pltpu.roll(row, 0, 1, stride=1, stride_axis=0)
        bias_s[n // blocks, n % blocks] = turned[:, tile:]
        return carry

    lax.fori_loop(0, 2 * blocks, make_bias, 0)
    sum_s[...] = jnp.zeros_like(sum_s)
    dq_s[...] = jnp.zeros_like(dq_s)
    dk_s[...] = jnp.zeros_like(dk_s)
    dv_s[...] = jnp.zeros_like(dv_s)
    context.arrive()
    for block in range(rows // 128 * sources):
        source, turn = block % sources, block // sources
        part = ctx_land[source, turn * 128 : (turn + 1) * 128, :]
        at = slice(block * 128, (block + 1) * 128)
        g_s[0, at, :] = part[:, :head]
        g_s[1, at, :] = part[:, head:]

    def make_delta(i, carry):
        at = pl.ds(pl.multiple_of(i * tile, tile), tile)
        for h in range(2):
            product = g_s[h, at, :].astype(jnp.float32) * full_ref[at, h * head : (h + 1) * head]
            column = jnp.broadcast_to(jnp.sum(product, axis=1, keepdims=True), (tile, 128))
            delta_s[pl.ds(h * blocks + i, 1), :] = jnp.transpose(column)[0:1, :]
        return carry

    lax.fori_loop(0, blocks, make_delta, 0)

    def one_tile(n, carry):
        line, at = n // blocks, n % blocks
        first = at < blocks - line
        d = jnp.where(first, line, blocks - line)
        i = jnp.where(first, at + line, at)
        at_q = pl.ds(pl.multiple_of(i * tile, tile), tile)
        at_k = pl.ds(pl.multiple_of((i - d) * tile, tile), tile)
        key, value = k_s[at_k, :], v_s[at_k, :]
        for h in range(2):
            query, grad = q_s[h, at_q, :], g_s[h, at_q, :]
            score = dot_t(key, query) + bias_s[h, d]
            share = jnp.exp(score - total_ref[pl.ds(h * blocks + i, 1), :])
            pull = dot_t(value, grad)
            grad_score = share * (pull - delta_s[pl.ds(h * blocks + i, 1), :])
            sum_s[h, d] += grad_score
            share_low = share.astype(jnp.bfloat16)
            grad_low = grad_score.astype(jnp.bfloat16)
            dv_s[at_k, :] += jnp.dot(share_low, grad, preferred_element_type=jnp.float32)
            dk_s[at_k, :] += jnp.dot(grad_low, query, preferred_element_type=jnp.float32)
            dq_s[h, at_q, :] += dot_first(grad_low, key)
        return carry

    tiles = blocks * (blocks + 1) // 2
    busy = 6

    def work(m, carry):
        for grads in sums:
            grads.send_first(m)
        low = (m - 1) * tiles // busy
        lax.fori_loop(low, m * tiles // busy, one_tile, 0)
        for grads in sums:
            grads.advance(m)
        return carry

    lax.fori_loop(1, 1 + busy, work, 0)

    for block in range(rows // 128 * sources):
        source, turn = block % sources, block // sources
        at = slice(block * 128, (block + 1) * 128)
        out_s[source, turn * 128 : (turn + 1) * 128, :] = jnp.concatenate(
            [dq_s[0, at, :] * score_scale, dq_s[1, at, :] * score_scale, dk_s[at, :], dv_s[at, :]],
            axis=1,
        ).astype(jnp.bfloat16)
    back.start()

    row_at = lax.broadcasted_iota(jnp.int32, (tile, tile), 0)
    col_at = lax.broadcasted_iota(jnp.int32, (tile, tile), 1)
    turn_rows = (row_at + col_at == tile - 1).astype(jnp.float32)

    def make_sums(n, carry):
        turned = jnp.dot(
            turn_rows,
            sum_s[n // blocks, n % blocks],
            precision=highest,
            preferred_element_type=jnp.float32,
        )
        wide = jnp.concatenate([turned, jnp.zeros_like(turned)], axis=1)
        wide = pltpu.roll(wide, 0, 1, stride=1, stride_axis=0)
        sums_ref[pl.ds(n, 1), :] = jnp.sum(wide, axis=0, keepdims=True)
        return carry

    lax.fori_loop(0, 2 * blocks, make_sums, 0)
    cross.arrive()
    both = kv_land[0].astype(jnp.float32)
    for source in range(1, sources):
        both = both + kv_land[source].astype(jnp.float32)
    kv_out[...] = both.astype(jnp.bfloat16)
    ended.arrive()
    rows_out[...] = rows_land[...]

    def rest(m, carry):
        for grads in sums:
            grads.send_first(m)
        for grads in sums:
            grads.advance(m)
        return carry

    lax.fori_loop(1 + busy, sum_steps(layers), rest, 0)
    back.arrive()
    wide = 4 * head
    for source in range(sources):
        out_ref[:, source * wide : (source + 1) * wide] = out_land[source]
    context.finish()
    cross.finish()
    ended.finish()
    back.finish()
    for grads in sums:
        grads.finish()


def attend_backward(
    scale, layers, kept, ctx_grad, full, total, bias, kv, layer_rows, grads, feed_grads, got
):
    f32, bf16 = jnp.float32, jnp.bfloat16
    sources, rows, wide = kept.shape
    head = wide // 4
    length = sources * rows
    blocks = length // tile
    cols, feed_cols = grads.shape[1], feed_grads.shape[1]
    chips = (layers, 2, 2, 2, 2, 16)
    vmem, anywhere = pl.BlockSpec(memory_space=pltpu.VMEM), pl.BlockSpec(memory_space=pl.ANY)
    grad_qkv, sums, kv_sum, layer_out, grad_sum, feed_sum = pl.pallas_call(
        functools.partial(attend_backward_kernel, scale, layers),
        name="attend_backward",
        out_shape=(
            jax.ShapeDtypeStruct((rows, sources * wide), bf16),
            jax.ShapeDtypeStruct((2 * blocks, 2 * tile), f32),
            jax.ShapeDtypeStruct(kv.shape[1:], bf16),
            jax.ShapeDtypeStruct(layer_rows.shape, bf16),
            jax.ShapeDtypeStruct((2, 2, 16, cols), f32),
            jax.ShapeDtypeStruct((2, 2, 16, feed_cols), f32),
        ),
        in_specs=[vmem] * 7 + [anywhere] * 4,
        out_specs=(vmem,) * 6,
        scratch_shapes=[
            pltpu.VMEM(ctx_grad.shape, bf16),
            pltpu.VMEM(kv.shape, bf16),
            pltpu.VMEM(layer_rows.shape, bf16),
            pltpu.VMEM(kept.shape, bf16),
            pltpu.VMEM(kept.shape, bf16),
            pltpu.VMEM((2, length, head), bf16),
            pltpu.VMEM((length, head), bf16),
            pltpu.VMEM((length, head), bf16),
            pltpu.VMEM((2, length, head), bf16),
            pltpu.VMEM((2, blocks, tile, tile), f32),
            pltpu.VMEM((2, blocks, tile, tile), f32),
            pltpu.VMEM((2 * blocks, tile), f32),
            pltpu.VMEM((2, length, head), f32),
            pltpu.VMEM((length, head), f32),
            pltpu.VMEM((length, head), f32),
            dma((2, 3)),
            dma((2, 3)),
            dma((2, layers)),
            dma((2, 3)),
            *sum_scratch(layers, cols),
            *sum_scratch(layers, feed_cols),
        ],
        compiler_params=pltpu.CompilerParams(
            collective_id=8, has_side_effects=True, vmem_limit_bytes=62 << 20
        ),
    )(
        kept,
        ctx_grad,
        full,
        total,
        bias,
        kv,
        layer_rows,
        grads.reshape(*chips, cols),
        feed_grads.reshape(*chips, feed_cols),
        *got,
    )
    grad_sum, feed_sum = grad_sum.reshape(-1, cols), feed_sum.reshape(-1, feed_cols)
    return grad_qkv, sums, kv_sum, layer_out, grad_sum, feed_sum

def norm_scale(v):
    return lax.rsqrt(jnp.mean(v * v, axis=-1, keepdims=True) + norm_eps)


def norm_pull(v, gain, grad):
    scale = norm_scale(v)
    turned = v * scale
    pulled = grad * gain
    mean = jnp.mean(pulled * turned, axis=-1, keepdims=True)
    return scale * (pulled - turned * mean), jnp.sum(grad * turned, axis=0, keepdims=True)


def middle_kernel(
    score_scale,
    layers,
    feed,
    ctx_ref,
    x_ref,
    cot_ref,
    enc_ref,
    wa_ref,
    gains_ref,
    wf_ref,
    layer_out,
    grad_out,
    gctx_out,
    kv_out,
    ga_out,
    gain_out,
    gb_out,
    got_x,
    got_y,
    w_s,
    gb_s,
    after_self,
    after_cross,
    nc_s,
    nf_s,
    nft_s,
    cott_s,
    down_s,
    dx_s,
    send_s,
    land_s,
    half_s,
    q_s,
    k_s,
    v_s,
    g_s,
    pair_s,
    cc_s,
    dq_s,
    dk_s,
    low_s,
    w_load,
    w_send,
    w_recv,
    g_send,
    g_recv,
    g_store,
    swap_sem,
):
    f32, bf16 = jnp.float32, jnp.bfloat16
    rank, z, y, x = chip_place(layers)
    core = lax.axis_index(tensor_axis)
    x_chip, y_chip = rank + 1 - 2 * x, rank + 2 - 4 * y
    rows, width = x_ref.shape
    heads, _, head = q_s.shape
    kv_heads = heads // 2
    wide = heads * head
    enc_rows = enc_ref.shape[0]
    block = send_s.shape[2]
    chunks = rows // block
    at_out, at_cq, at_ck = 0, wide, 2 * wide
    at_cv, at_co = at_ck + wide // 2, at_ck + wide
    row_chip = 64

    def row_of(layer, at_y, at_x, colour=0):
        return pl.multiple_of(((layer * 2 + at_y) * 2 + at_x) * row_chip + 32 * colour, 32)

    def loads():
        copies = []
        for layer in range(layers):
            for n, (start, count) in enumerate(
                (
                    (row_of(layer, y, x), 64),
                    (row_of(layer, y, 1 - x, 0), 32),
                    (row_of(layer, 1 - y, x, 1), 32),
                )
            ):
                at = pl.ds(start, count)
                copies.append(
                    pltpu.make_async_copy(wf_ref.at[at], w_s.at[at], w_load.at[layer, n])
                )
        return copies

    def weights_hop(layer, along_y, which):
        spot = row_of(layer, y, which, 0) if along_y else row_of(layer, which, x, 1)
        at = pl.ds(spot, 32)
        return pltpu.make_async_remote_copy(
            src_ref=wf_ref.at[at],
            dst_ref=w_s.at[at],
            send_sem=w_send.at[int(along_y), layer, which],
            recv_sem=w_recv.at[int(along_y), layer, which],
            **to_chip(y_chip if along_y else x_chip),
        )

    def grads_hop(layer, along_y, which):
        spot = row_of(layer, 1 - y, which, 1) if along_y else row_of(layer, which, 1 - x, 0)
        return pltpu.make_async_remote_copy(
            src_ref=gb_s.at[pl.ds(spot, 32)],
            dst_ref=(got_y if along_y else got_x).at[layer, which],
            send_sem=g_send.at[int(along_y), layer, which],
            recv_sem=g_recv.at[int(along_y), layer, which],
            **to_chip(y_chip if along_y else x_chip),
        )

    hops = [(layer, a, w) for layer in range(layers) for w in range(2) for a in (True, False)]
    greet(layers)
    for hop in hops:
        weights_hop(*hop).start()
    for copy in loads():
        copy.start()

    def swap(n, chunk):
        half = n == 3
        return pltpu.make_async_remote_copy(
            src_ref=half_s.at[0] if half else send_s.at[slots[n], chunk],
            dst_ref=half_s.at[1] if half else land_s.at[slots[n], chunk],
            send_sem=swap_sem.at[0, n, chunk],
            recv_sem=swap_sem.at[1, n, chunk],
            **to_core(1 - core),
        )

    slots = (0, 1, 0, None, 1)

    def span(chunk):
        return pl.ds(pl.multiple_of(chunk * block, block), block)

    def send_parts(n, part_of):
        def one(chunk, carry):
            send_s[slots[n], chunk] = part_of(span(chunk)).astype(bf16)
            swap(n, chunk).start()
            return carry

        lax.fori_loop(0, chunks, one, 0)

    def take_parts(n, use):
        def one(chunk, carry):
            swap(n, chunk).wait()
            both = send_s[slots[n], chunk].astype(f32) + land_s[slots[n], chunk].astype(f32)
            use(span(chunk), both)
            return carry

        lax.fori_loop(0, chunks, one, 0)

    cross_gain, feed_gain = gains_ref[0:1, :], gains_ref[1:2, :]

    send_parts(0, lambda at: dot_t(ctx_ref[at, :], wa_ref[:, at_out : at_out + wide]))
    key_value = matmul(enc_ref[...], wa_ref[:, at_ck : at_ck + wide]).astype(bf16)
    for kv in range(kv_heads):
        k_s[kv] = key_value[:, kv * head : (kv + 1) * head]
        v_s[kv] = key_value[:, wide // 2 + kv * head : wide // 2 + (kv + 1) * head]
    cott_s[...] = jnp.transpose(cot_ref[...])

    def enter_cross(at, both):
        v = x_ref[at, :].astype(f32) + both
        after_self[at, :] = v
        nc_s[at, :] = (v * norm_scale(v) * cross_gain).astype(bf16)
        query = matmul(nc_s[at, :], wa_ref[:, at_cq : at_cq + wide]).astype(bf16)
        for h in range(heads):
            q_s[h, at, :] = (query[:, h * head : (h + 1) * head] * score_scale).astype(bf16)

    take_parts(0, enter_cross)

    def attend(kv, carry):
        key, value = k_s[kv], v_s[kv]
        for chunk in range(chunks):
            at = slice(chunk * block, (chunk + 1) * block)
            found = []
            for h in range(2):
                score = dot_t(q_s[2 * kv + h, at, :], key)
                share = jnp.exp(score - jnp.max(score, axis=1, keepdims=True))
                total = jnp.sum(share, axis=1, keepdims=True)
                found.append(matmul(share.astype(bf16), value) / total)
            pair_s[kv, at, :] = jnp.concatenate(found, axis=1).astype(bf16)
        return carry

    lax.fori_loop(0, kv_heads, attend, 0)
    for kv in range(kv_heads):
        cc_s[:, 2 * kv * head : 2 * (kv + 1) * head] = pair_s[kv]
    send_parts(1, lambda at: dot_t(cc_s[at, :], wa_ref[:, at_co : at_co + wide]))

    def enter_feed(at, both):
        v = after_self[at, :] + both
        after_cross[at, :] = v
        nf_s[at, :] = (v * norm_scale(v) * feed_gain).astype(bf16)

    take_parts(1, enter_feed)
    nft_s[...] = jnp.transpose(nf_s[...])
    for copy in loads():
        copy.wait()
    for hop in hops:
        weights_hop(*hop).wait_recv()

    down_s[...] = jnp.zeros_like(down_s)
    dx_s[...] = jnp.zeros_like(dx_s)
    slope = math.sqrt(2.0 / math.pi)

    def feed_block(at_gu, at_down, units):
        pair = w_s[:, pl.ds(at_gu, 2 * units)]
        down = w_s[:, pl.ds(at_down, units)]
        both = matmul(nf_s[...], pair)
        gate, up = both[:, :units], both[:, units:]
        square = gate * gate
        bend = jnp.tanh(slope * (gate + 0.044715 * square * gate))
        bent = 0.5 * gate * (1.0 + bend)
        pull = 0.5 * (1.0 + bend) + 0.5 * gate * (1.0 - bend * bend) * slope * (
            1.0 + 3.0 * 0.044715 * square
        )
        hidden = (bent * up).astype(bf16)
        down_s[...] += dot_t(hidden, down)
        grad = matmul(cot_ref[...], down)
        grads = jnp.concatenate([grad * up * pull, grad * bent], axis=1).astype(bf16)
        dx_s[...] += dot_t(grads, pair)
        gb_s[:, pl.ds(at_gu, 2 * units)] = matmul(nft_s[...], grads).astype(bf16)
        gb_s[:, pl.ds(at_down, units)] = matmul(cott_s[...], hidden).astype(bf16)

    full_blocks = feed // tile

    def one_block(n, carry):
        feed_block(
            pl.multiple_of(n * 2 * tile, 2 * tile),
            pl.multiple_of(2 * feed + n * tile, 128),
            tile,
        )
        return carry

    lax.fori_loop(0, full_blocks, one_block, 0)
    if feed % tile:
        feed_block(full_blocks * 2 * tile, 2 * feed + full_blocks * tile, feed % tile)

    send_parts(2, lambda at: dx_s[at, :])
    store = pltpu.make_async_copy(gb_s, gb_out, g_store.at[0])
    store.start()
    for hop in hops:
        grads_hop(*hop).start()
    own = rows // (2 * layers)

    def halves(ref, which):
        return [ref[pl.ds((2 * layer + which) * own, own), :] for layer in range(layers)]

    low = jnp.concatenate(halves(down_s, 1 - core), axis=0).astype(bf16)
    half_s[0] = low
    swap(3, 0).start()

    def leave_feed(at, both):
        grad, gain = norm_pull(after_cross[at, :], feed_gain, both)
        dx_s[at, :] = cot_ref[at, :].astype(f32) + grad
        low = dx_s[at, :].astype(bf16)
        low_s[at, :] = low
        gain_out[1:2, :] += gain
        context = matmul(low, wa_ref[:, at_co : at_co + wide]).astype(bf16)
        for h in range(heads):
            g_s[h, at, :] = context[:, h * head : (h + 1) * head]

    gain_out[...] = jnp.zeros_like(gain_out)
    take_parts(2, leave_feed)
    swap(3, 0).wait()
    mine = halves(after_cross, core)
    down = halves(down_s, core)
    for layer in range(layers):
        came = half_s[1, layer * own : (layer + 1) * own, :].astype(f32)
        layer_out[layer] = (mine[layer] + (down[layer].astype(bf16).astype(f32) + came)).astype(bf16)

    ga_out[:, at_co : at_co + wide] = dot_first(low_s[...], cc_s[...]).astype(bf16)

    def attend_back(kv, carry):
        key, value = k_s[kv], v_s[kv]
        key_grad = jnp.zeros((enc_rows, head), f32)
        value_grad = jnp.zeros((enc_rows, head), f32)
        for chunk in range(chunks):
            at = slice(chunk * block, (chunk + 1) * block)
            found = []
            for h in range(2):
                query, grad = q_s[2 * kv + h, at, :], g_s[2 * kv + h, at, :]
                score = dot_t(key, query)
                share = jnp.exp(score - jnp.max(score, axis=0, keepdims=True))
                share = share * (1.0 / jnp.sum(share, axis=0, keepdims=True))
                pull = dot_t(value, grad)
                delta = jnp.sum(share * pull, axis=0, keepdims=True)
                grad_low = (share * (pull - delta)).astype(bf16)
                found.append(dot_first(grad_low, key) * score_scale)
                key_grad = key_grad + matmul(grad_low, query)
                value_grad = value_grad + matmul(share.astype(bf16), grad)
            pair_s[kv, at, :] = jnp.concatenate(found, axis=1).astype(bf16)
        dk_s[0, kv] = key_grad.astype(bf16)
        dk_s[1, kv] = value_grad.astype(bf16)
        return carry

    lax.fori_loop(0, kv_heads, attend_back, 0)
    for kv in range(kv_heads):
        dq_s[:, 2 * kv * head : 2 * (kv + 1) * head] = pair_s[kv]
    send_parts(4, lambda at: dot_t(dq_s[at, :], wa_ref[:, at_cq : at_cq + wide]))
    for n in range(2):
        kv_out[:, n * wide // 2 : (n + 1) * wide // 2] = jnp.concatenate(
            [dk_s[n, kv] for kv in range(kv_heads)], axis=1
        )
    ga_out[:, at_cq : at_cq + wide] = dot_first(nc_s[...], dq_s[...]).astype(bf16)
    ga_out[:, at_ck : at_ck + wide] = dot_first(enc_ref[...], kv_out[...]).astype(bf16)

    def leave_cross(at, both):
        grad, gain = norm_pull(after_self[at, :], cross_gain, both)
        dx_s[at, :] += grad
        low = dx_s[at, :].astype(bf16)
        low_s[at, :] = low
        gain_out[0:1, :] += gain
        context = matmul(low, wa_ref[:, at_out : at_out + wide]).astype(bf16)
        for q in range(4):
            gctx_out[q, at, :] = context[:, q * wide // 4 : (q + 1) * wide // 4]

    take_parts(4, leave_cross)
    ga_out[:, at_out : at_out + wide] = dot_first(low_s[...], ctx_ref[...]).astype(bf16)
    mine = halves(dx_s, core)
    for layer in range(layers):
        grad_out[layer] = mine[layer]

    store.wait()
    for hop in hops:
        weights_hop(*hop).wait_send()
        grads_hop(*hop).wait()


def middle(scale, layers, feed, context, x_low, cot, enc, weights, gains, feed_whole):
    f32, bf16 = jnp.float32, jnp.bfloat16
    rows, width = x_low.shape
    wide = context.shape[1]
    head = round(scale**-2)
    heads = wide // head
    own = rows // (2 * layers)
    cols = feed_whole.shape[1]
    block = rows // 2
    vmem, anywhere = pl.BlockSpec(memory_space=pltpu.VMEM), pl.BlockSpec(memory_space=pl.ANY)
    got = jax.ShapeDtypeStruct((layers, 2, 32, cols), bf16)
    return pl.pallas_call(
        functools.partial(middle_kernel, scale, layers, feed),
        name="middle",
        out_shape=(
            jax.ShapeDtypeStruct((layers, own, width), bf16),
            jax.ShapeDtypeStruct((layers, own, width), f32),
            jax.ShapeDtypeStruct((4, rows, wide // 4), bf16),
            jax.ShapeDtypeStruct((enc.shape[0], wide), bf16),
            jax.ShapeDtypeStruct((width, weights.shape[1]), bf16),
            jax.ShapeDtypeStruct((2, width), f32),
            jax.ShapeDtypeStruct((width, cols), bf16),
            got,
            got,
        ),
        in_specs=[vmem] * 6 + [anywhere],
        out_specs=(vmem,) * 6 + (anywhere,) * 3,
        scratch_shapes=[
            pltpu.VMEM((width, cols), bf16),
            pltpu.VMEM((width, cols), bf16),
            pltpu.VMEM((rows, width), f32),
            pltpu.VMEM((rows, width), f32),
            pltpu.VMEM((rows, width), bf16),
            pltpu.VMEM((rows, width), bf16),
            pltpu.VMEM((width, rows), bf16),
            pltpu.VMEM((width, rows), bf16),
            pltpu.VMEM((rows, width), f32),
            pltpu.VMEM((rows, width), f32),
            pltpu.VMEM((2, 2, block, width), bf16),
            pltpu.VMEM((2, 2, block, width), bf16),
            pltpu.VMEM((2, rows // 2, width), bf16),
            pltpu.VMEM((heads, rows, head), bf16),
            pltpu.VMEM((heads // 2, enc.shape[0], head), bf16),
            pltpu.VMEM((heads // 2, enc.shape[0], head), bf16),
            pltpu.VMEM((heads, rows, head), bf16),
            pltpu.VMEM((heads // 2, rows, 2 * head), bf16),
            pltpu.VMEM((rows, wide), bf16),
            pltpu.VMEM((rows, wide), bf16),
            pltpu.VMEM((2, heads // 2, enc.shape[0], head), bf16),
            pltpu.VMEM((rows, width), bf16),
            dma((layers, 3)),
            dma((2, layers, 2)),
            dma((2, layers, 2)),
            dma((2, layers, 2)),
            dma((2, layers, 2)),
            dma((1,)),
            dma((2, 5, 2)),
        ],
        compiler_params=pltpu.CompilerParams(
            collective_id=9, has_side_effects=True, vmem_limit_bytes=67043328
        ),
    )(context, x_low, cot, enc, weights, gains, feed_whole)

def swap_cores(block):
    return lax.ppermute(block, tensor_axis, [(0, 1), (1, 0)])


def dot_t(left, right):
    return lax.dot_general(
        left, right, (((1,), (1,)), ((), ())), preferred_element_type=jnp.float32
    )


def dot_first(left, right):
    return lax.dot_general(
        left, right, (((0,), (0,)), ((), ())), preferred_element_type=jnp.float32
    )


def unpack_pair(qkv_ref, q_s, k_s, v_s, score_scale):
    sources, rows, _ = qkv_ref.shape
    blocks = rows // 128 * sources
    head = k_s.shape[1]
    for block in range(blocks):
        source, turn = block % sources, block // sources
        tile = qkv_ref[source, turn * 128 : (turn + 1) * 128, :]
        at = slice(block * 128, (block + 1) * 128)
        q_s[0, at, :] = (tile[:, :head] * score_scale).astype(jnp.bfloat16)
        q_s[1, at, :] = (tile[:, head : 2 * head] * score_scale).astype(jnp.bfloat16)
        k_s[at, :] = tile[:, 2 * head : 3 * head]
        v_s[at, :] = tile[:, 3 * head :]


def by_heads(
    inputs,
    encoder_out,
    out_cotangent,
    bucket_ids,
    position_table,
    self_gain,
    self_query,
    self_key,
    self_value,
    self_output,
    cross_gain,
    cross_query,
    cross_key,
    cross_value,
    cross_output,
    feed_gain,
    gate_weight,
    up_weight,
    down_weight,
):
    f32, bf16 = jnp.float32, jnp.bfloat16
    batches, own, width = inputs.shape
    enc_own = encoder_out.shape[1]
    length = bucket_ids.shape[0]
    heads_all, buckets = position_table.shape
    fsdp = lax.axis_size(fsdp_axis)
    plane = fsdp // batches
    rank, core = lax.axis_index(fsdp_axis), lax.axis_index(tensor_axis)
    head = self_query.shape[1] // (heads_all // 2)
    kv_local = self_key.shape[1] // head
    scale = head ** (-0.5)
    blocks = length // tile
    rows = batches * 2 * own
    enc_rows = batches * 2 * enc_own
    feed = gate_weight.shape[1]
    def by_kv(weight):
        return weight.reshape(weight.shape[0], kv_local, -1)

    self_in = jnp.concatenate([by_kv(self_query), by_kv(self_key), by_kv(self_value)], axis=2)
    self_in = self_in.reshape(self_in.shape[0], -1)
    rest_shard = jnp.concatenate(
        [self_output.T, cross_query, cross_key, cross_value, cross_output.T], axis=1
    )
    spans = [(at, min(at + tile, feed)) for at in range(0, feed, tile)]
    paired = [side[:, at:end] for at, end in spans for side in (gate_weight, up_weight)]
    feed_shard = jnp.concatenate([*paired, down_weight.T], axis=1)
    started, enc_all, in_full = open_rows(batches, inputs, encoder_out, self_in)
    cuts = [
        self_output.shape[0],
        cross_query.shape[1],
        cross_key.shape[1],
        cross_value.shape[1],
        cross_output.shape[0],
    ]

    def split(x, cuts):
        pieces, at = [], 0
        for cut in cuts:
            pieces.append(x[:, at : at + cut])
            at += cut
        return pieces

    x_low = started.reshape(rows, width)
    x_rows = x_low.astype(f32)
    enc_all = enc_all.reshape(-1, width)

    kv_index = core * kv_local + rank % plane
    table_here = lax.dynamic_slice_in_dim(position_table, 2 * kv_index, 2, 0)
    bucket_range = jnp.arange(buckets, dtype=jnp.int32)
    lower = jnp.sum((bucket_ids[None, :] < bucket_range[:, None]).astype(jnp.int32), axis=1)
    upper = jnp.concatenate([lower[1:], jnp.full((1,), length, jnp.int32)])
    offsets = (
        tile * jnp.arange(blocks, dtype=jnp.int32)[:, None]
        + jnp.arange(2 * tile, dtype=jnp.int32)[None, :]
    ).reshape(-1)

    def bias_of(offset):
        hit = (offset[None] >= lower[:, None]) & (offset[None] < upper[:, None])
        value = jnp.dot(table_here, hit.astype(f32), precision=highest)
        return jnp.where(offset[None] >= 0, value, masked_score).reshape(2 * blocks, 2 * tile)

    down_steps = (
        tile * jnp.arange(blocks, dtype=jnp.int32)[:, None]
        + (tile - 1)
        - jnp.arange(2 * tile, dtype=jnp.int32)[None, :]
    ).reshape(-1)
    bias_down = bias_of(down_steps)
    bias_up = bias_of(offsets - tile)

    def swap_add(partial):
        low = partial.astype(bf16)
        return low.astype(f32) + swap_cores(low).astype(f32)

    normed_self = norm_rows(x_rows, self_gain).astype(bf16)
    qkv = jnp.einsum(
        "rd,dkc->krc",
        normed_self,
        in_full.reshape(width, kv_local, -1),
        preferred_element_type=f32,
    ).astype(bf16)
    qkv_here, context_low, context_full, log_total, cot_low, rest_full, feed_full = attend_forward(
        scale, batches, qkv, bias_down, out_cotangent, rest_shard, feed_shard
    )
    ck_full, cv_full = split(rest_full, cuts)[2:4]

    def keep_half(part, axis):
        mine = lax.dynamic_index_in_dim(part, core, axis, keepdims=False)
        other = lax.dynamic_index_in_dim(part, 1 - core, axis, keepdims=False)
        return mine.astype(f32) + swap_cores(other).astype(f32)

    def own_half(x):
        x = x.reshape(batches, 2, own, width)
        return lax.dynamic_index_in_dim(x, core, 1, keepdims=False)

    layer_rows, grad_after_self, grad_context, cross_kv, grads, mid_gains, feed_grads, *feed_got = (
        middle(
            scale,
            batches,
            feed,
            context_low,
            x_low,
            cot_low.reshape(rows, width),
            enc_all,
            rest_full,
            jnp.stack([cross_gain, feed_gain]),
            feed_full.reshape(width, -1),
        )
    )
    feed_got = [came.reshape(batches, 2, 2, 16, -1) for came in feed_got]

    grad_qkv, diagonal_sums, kv_sum, layer_out, sums, feed_sums = attend_backward(
        scale,
        batches,
        qkv_here,
        grad_context,
        context_full,
        log_total,
        bias_up,
        cross_kv.reshape(plane, enc_rows, -1),
        layer_rows,
        grads,
        feed_grads,
        feed_got,
    )
    enc_part = dot_t(kv_sum[:, : cuts[2]], ck_full) + dot_t(kv_sum[:, cuts[2] :], cv_full)
    enc_grad = keep_half(enc_part.astype(bf16).reshape(2, batches, enc_own, width), 0)
    in_grad = dot_first(normed_self, grad_qkv).astype(bf16)
    in_got = first_hop(batches, in_grad)
    self_part = dot_t(grad_qkv, in_full)
    self_rows = swap_add(self_part)
    grad_self, self_gain_grad = jax.vjp(norm_rows, x_rows, self_gain)[1](self_rows)
    input_rows = grad_after_self + own_half(grad_self)

    spread = offsets - (tile - 1)
    hit = ((spread[None] >= lower[:, None]) & (spread[None] < upper[:, None])).astype(f32)
    by_offset = diagonal_sums.reshape(2, -1)
    table_here_grad = jnp.dot(by_offset, hit.T, precision=highest)
    table_full = lax.dynamic_update_slice_in_dim(
        jnp.zeros((heads_all, buckets), f32), table_here_grad, 2 * kv_index, 0
    )
    table_row = jnp.pad(table_full.reshape(1, -1), ((0, 0), (0, width - heads_all * buckets)))
    small = jnp.concatenate([self_gain_grad[None], mid_gains, table_row])
    in_sum, ended, small_sum = close_rows(
        batches,
        in_grad,
        in_got,
        jnp.concatenate([input_rows, enc_grad], axis=1).astype(bf16),
        jnp.concatenate([small, jnp.zeros_like(small)]),
    )
    table_sum = small_sum[3, : heads_all * buckets].reshape(heads_all, buckets)
    q_wide = self_query.shape[1] // kv_local
    k_wide = self_key.shape[1] // kv_local
    in_sum = in_sum.reshape(in_sum.shape[0], kv_local, -1)

    def flat(x):
        return x.reshape(x.shape[0], -1)

    pieces = split(sums, cuts)
    paired = split(feed_sums, [end - at for at, end in spans for _ in range(2)])
    return (
        layer_out,
        ended[:, :own],
        ended[:, own:],
        table_sum,
        small_sum[0],
        flat(in_sum[:, :, :q_wide]),
        flat(in_sum[:, :, q_wide : q_wide + k_wide]),
        flat(in_sum[:, :, q_wide + k_wide :]),
        pieces[0].T,
        small_sum[1],
        pieces[1],
        pieces[2],
        pieces[3],
        pieces[4].T,
        small_sum[2],
        jnp.concatenate(paired[0::2], axis=1),
        jnp.concatenate(paired[1::2], axis=1),
        feed_sums[:, 2 * feed :].T,
    )


def on_either(*args):
    batches, kv_heads = args[0].shape[0], args[7].shape[1] * lax.axis_size(tensor_axis)
    head_size = args[6].shape[1] * lax.axis_size(tensor_axis) // args[4].shape[0]
    devices = lax.axis_size(fsdp_axis) * lax.axis_size(tensor_axis)
    if devices == batches * (kv_heads // head_size):
        return by_heads(*args)
    return on_device(*args)


def solution(mesh):
    placed = (
        P(None, (fsdp_axis, tensor_axis), None),
        P(None, (fsdp_axis, tensor_axis), None),
        P(None, (fsdp_axis, tensor_axis), None),
        P(),
        P(),
        P(),
        P(fsdp_axis, tensor_axis),
        P(fsdp_axis, tensor_axis),
        P(fsdp_axis, tensor_axis),
        P(tensor_axis, fsdp_axis),
        P(),
        P(fsdp_axis, tensor_axis),
        P(fsdp_axis, tensor_axis),
        P(fsdp_axis, tensor_axis),
        P(tensor_axis, fsdp_axis),
        P(),
        P(fsdp_axis, tensor_axis),
        P(fsdp_axis, tensor_axis),
        P(tensor_axis, fsdp_axis),
    )
    return jax.shard_map(
        on_either,
        mesh=mesh,
        in_specs=placed,
        out_specs=(
            P(None, (fsdp_axis, tensor_axis), None),
            P(None, (fsdp_axis, tensor_axis), None),
            P(None, (fsdp_axis, tensor_axis), None),
            P(),
            P(),
            P(fsdp_axis, tensor_axis),
            P(fsdp_axis, tensor_axis),
            P(fsdp_axis, tensor_axis),
            P(tensor_axis, fsdp_axis),
            P(),
            P(fsdp_axis, tensor_axis),
            P(fsdp_axis, tensor_axis),
            P(fsdp_axis, tensor_axis),
            P(tensor_axis, fsdp_axis),
            P(),
            P(fsdp_axis, tensor_axis),
            P(fsdp_axis, tensor_axis),
            P(tensor_axis, fsdp_axis),
        ),
        check_vma=False,
    )
```

```python
import functools
import math
import types

import jax
import jax.numpy as jnp
from jax import lax
from jax.experimental import pallas as pl
from jax.experimental.pallas import tpu as pltpu
from jax.sharding import PartitionSpec as P

norm_eps = 1e-06
masked_score = -1e30
highest = lax.Precision.HIGHEST
key_block_width = 256
tile = 256
fsdp_axis, tensor_axis = "fsdp", "tensor"


def matmul(left, right):
    return jnp.dot(left, right, preferred_element_type=jnp.float32)


def norm_rows(row_block, gain):
    return (
        row_block
        * lax.rsqrt(jnp.mean(row_block * row_block, axis=-1, keepdims=True) + norm_eps)
        * gain
    )


def gather_rows(row_block):
    return lax.all_gather(row_block, tensor_axis, axis=0, tiled=True)


def sum_rows(row_block):
    return lax.psum_scatter(
        row_block.astype(jnp.bfloat16), tensor_axis, scatter_dimension=0, tiled=True
    ).astype(jnp.float32)


def gather_weights(shards):
    (
        self_query,
        self_key,
        self_value,
        self_output,
        cross_query,
        cross_key,
        cross_value,
        cross_output,
        gate_weight,
        up_weight,
        down_weight,
    ) = shards
    inner = (
        lax.all_gather(self_query, fsdp_axis, axis=0, tiled=True),
        lax.all_gather(self_key, fsdp_axis, axis=0, tiled=True),
        lax.all_gather(self_value, fsdp_axis, axis=0, tiled=True),
        lax.all_gather(cross_query, fsdp_axis, axis=0, tiled=True),
        lax.all_gather(cross_key, fsdp_axis, axis=0, tiled=True),
        lax.all_gather(cross_value, fsdp_axis, axis=0, tiled=True),
        lax.all_gather(gate_weight, fsdp_axis, axis=0, tiled=True),
        lax.all_gather(up_weight, fsdp_axis, axis=0, tiled=True),
    )
    outer = (
        lax.all_gather(self_output, fsdp_axis, axis=1, tiled=True),
        lax.all_gather(cross_output, fsdp_axis, axis=1, tiled=True),
        lax.all_gather(down_weight, fsdp_axis, axis=1, tiled=True),
    )
    return (
        inner[0],
        inner[1],
        inner[2],
        outer[0],
        inner[3],
        inner[4],
        inner[5],
        outer[1],
        inner[6],
        inner[7],
        outer[2],
    )


def scatter_grads(grads_full):
    (
        self_query,
        self_key,
        self_value,
        self_output,
        cross_query,
        cross_key,
        cross_value,
        cross_output,
        gate_weight,
        up_weight,
        down_weight,
    ) = grads_full
    inner = (
        lax.psum_scatter(self_query, fsdp_axis, scatter_dimension=0, tiled=True),
        lax.psum_scatter(self_key, fsdp_axis, scatter_dimension=0, tiled=True),
        lax.psum_scatter(self_value, fsdp_axis, scatter_dimension=0, tiled=True),
        lax.psum_scatter(cross_query, fsdp_axis, scatter_dimension=0, tiled=True),
        lax.psum_scatter(cross_key, fsdp_axis, scatter_dimension=0, tiled=True),
        lax.psum_scatter(cross_value, fsdp_axis, scatter_dimension=0, tiled=True),
        lax.psum_scatter(gate_weight, fsdp_axis, scatter_dimension=0, tiled=True),
        lax.psum_scatter(up_weight, fsdp_axis, scatter_dimension=0, tiled=True),
    )
    outer = (
        lax.psum_scatter(self_output, fsdp_axis, scatter_dimension=1, tiled=True),
        lax.psum_scatter(cross_output, fsdp_axis, scatter_dimension=1, tiled=True),
        lax.psum_scatter(down_weight, fsdp_axis, scatter_dimension=1, tiled=True),
    )
    return (
        inner[0],
        inner[1],
        inner[2],
        outer[0],
        inner[3],
        inner[4],
        inner[5],
        outer[1],
        inner[6],
        inner[7],
        outer[2],
    )


def add_all(first, second):
    return tuple((left_item + right_item for left_item, right_item in zip(first, second)))


def fold_keys(key_rows, value_rows, step_fn, initial):
    return step_fn(
        initial,
        (
            lax.all_gather(key_rows, fsdp_axis, axis=0, tiled=True),
            lax.all_gather(value_rows, fsdp_axis, axis=0, tiled=True),
        ),
        jnp.int32(0),
    )


def on_device(
    inputs,
    encoder_out,
    out_cotangent,
    bucket_ids,
    position_table,
    self_gain,
    self_query,
    self_key,
    self_value,
    self_output,
    cross_gain,
    cross_query,
    cross_key,
    cross_value,
    cross_output,
    feed_gain,
    gate_weight,
    up_weight,
    down_weight,
):
    shards = (
        self_query,
        self_key,
        self_value,
        self_output,
        cross_query,
        cross_key,
        cross_value,
        cross_output,
        gate_weight,
        up_weight,
        down_weight,
    )
    batches = inputs.shape[0]
    tensor_size = lax.axis_size(tensor_axis)
    piece_rows = inputs.shape[1] * tensor_size
    length = bucket_ids.shape[0]
    heads_all = position_table.shape[0]
    buckets = position_table.shape[1]
    local_heads = heads_all // tensor_size
    head_size = self_query.shape[1] // local_heads
    kv_local = self_key.shape[1] // head_size
    group_size = local_heads // kv_local
    score_scale = head_size ** (-0.5)
    fsdp_rank = lax.axis_index(fsdp_axis)
    tensor_rank = lax.axis_index(tensor_axis)
    query_start = fsdp_rank * piece_rows
    encoder_rows = encoder_out.shape[1] * tensor_size
    table_local = lax.dynamic_slice_in_dim(
        position_table, tensor_rank * local_heads, local_heads, 0
    )
    bucket_range = jnp.arange(buckets, dtype=jnp.int32)
    lower_bounds = jnp.sum((bucket_ids[None, :] < bucket_range[:, None]).astype(jnp.int32), axis=1)
    upper_bounds = jnp.concatenate([lower_bounds[1:], jnp.full((1,), length, jnp.int32)])

    def position_bias(row_start, col_start, row_count, col_count):
        offsets = (
            row_start
            - col_start
            + jnp.arange(row_count, dtype=jnp.int32)[:, None]
            - jnp.arange(col_count, dtype=jnp.int32)[None, :]
        )
        indicator = (
            (offsets[None] >= lower_bounds[:, None, None])
            & (offsets[None] < upper_bounds[:, None, None])
        ).astype(jnp.float32)
        bias_values = jnp.einsum("hb,bij->hij", table_local, indicator, precision=highest).reshape(
            kv_local, group_size, row_count, col_count
        )
        return (bias_values, offsets >= 0, indicator)

    def split_heads(row_block):
        return row_block.reshape(row_block.shape[0], kv_local, group_size, head_size)

    def split_kv(row_block):
        return row_block.reshape(row_block.shape[0], kv_local, head_size)

    def backward(batch_index, saved_state, weights):
        (
            query_full,
            key_full,
            value_full,
            output_full,
            cross_query_full,
            cross_key_full,
            cross_value_full,
            cross_output_full,
            gate_full,
            up_full,
            down_full,
        ) = weights
        cotangent = out_cotangent[batch_index].astype(jnp.float32)
        grad_feed = gather_rows(out_cotangent[batch_index])
        hidden = saved_state.hidden
        normed_feed = saved_state.normed_feed
        down_grad = jnp.einsum("tf,td->fd", hidden, grad_feed, preferred_element_type=jnp.float32)
        grad_hidden = jnp.einsum(
            "td,fd->tf", grad_feed, down_full, preferred_element_type=jnp.float32
        )
        gelu_pull = jax.vjp(
            lambda gate_in, up_in: jax.nn.gelu(gate_in, approximate=True) * up_in,
            saved_state.gate_values,
            saved_state.up_values,
        )[1]
        grad_gate, grad_up = gelu_pull(grad_hidden)
        grad_gate = grad_gate.astype(jnp.bfloat16)
        grad_up = grad_up.astype(jnp.bfloat16)
        gate_grad = jnp.einsum(
            "td,tf->df", normed_feed, grad_gate, preferred_element_type=jnp.float32
        )
        up_grad = jnp.einsum("td,tf->df", normed_feed, grad_up, preferred_element_type=jnp.float32)
        feed_rows = sum_rows(
            jnp.einsum("tf,df->td", grad_gate, gate_full, preferred_element_type=jnp.float32)
            + jnp.einsum("tf,df->td", grad_up, up_full, preferred_element_type=jnp.float32)
        )
        grad_norm_feed, feed_gain_grad = jax.vjp(norm_rows, saved_state.after_cross, feed_gain)[
            1
        ](feed_rows)
        grad_after_cross = cotangent + grad_norm_feed
        cross_context = saved_state.cross_context
        cross_weights = saved_state.cross_weights
        encoded = saved_state.encoded
        grad_cross_branch = gather_rows(grad_after_cross.astype(jnp.bfloat16))
        cross_output_grad = jnp.einsum(
            "te,td->ed", cross_context, grad_cross_branch, preferred_element_type=jnp.float32
        )
        grad_cross_context = split_heads(
            jnp.einsum(
                "td,ed->te",
                grad_cross_branch,
                cross_output_full,
                preferred_element_type=jnp.float32,
            ).astype(jnp.bfloat16)
        )
        grad_cross_weights = jnp.einsum(
            "ikgd,jkd->kgij",
            grad_cross_context,
            split_kv(saved_state.cross_values),
            preferred_element_type=jnp.float32,
        )
        grad_cross_scores = (
            cross_weights
            * (
                grad_cross_weights
                - jnp.sum(cross_weights * grad_cross_weights, axis=-1, keepdims=True)
            )
        ).astype(jnp.bfloat16)
        grad_cross_queries = (
            (
                jnp.einsum(
                    "kgij,jkd->ikgd",
                    grad_cross_scores,
                    split_kv(saved_state.cross_keys),
                    preferred_element_type=jnp.float32,
                )
                * score_scale
            )
            .reshape(piece_rows, local_heads * head_size)
            .astype(jnp.bfloat16)
        )
        key_part = (
            jnp.einsum(
                "kgij,ikgd->jkd",
                grad_cross_scores,
                split_heads(saved_state.cross_queries),
                preferred_element_type=jnp.float32,
            )
            * score_scale
        ).reshape(encoded.shape[0], kv_local * head_size)
        value_part = jnp.einsum(
            "kgij,ikgd->jkd",
            saved_state.cross_low,
            grad_cross_context,
            preferred_element_type=jnp.float32,
        ).reshape(encoded.shape[0], kv_local * head_size)
        key_sum, value_sum = (
            lax.psum_scatter(key_part, fsdp_axis, scatter_dimension=0, tiled=True),
            lax.psum_scatter(value_part, fsdp_axis, scatter_dimension=0, tiled=True),
        )
        key_low = key_sum.astype(jnp.bfloat16)
        value_low = value_sum.astype(jnp.bfloat16)
        encoded_own = lax.dynamic_slice_in_dim(encoded, fsdp_rank * encoder_rows, encoder_rows, 0)
        cross_key_grad = jnp.einsum(
            "ed,ec->dc", encoded_own, key_low, preferred_element_type=jnp.float32
        )
        cross_value_grad = jnp.einsum(
            "ed,ec->dc", encoded_own, value_low, preferred_element_type=jnp.float32
        )
        encoder_grad = sum_rows(
            jnp.einsum("ec,dc->ed", key_low, cross_key_full, preferred_element_type=jnp.float32)
            + jnp.einsum(
                "ec,dc->ed", value_low, cross_value_full, preferred_element_type=jnp.float32
            )
        )
        cross_query_grad = jnp.einsum(
            "td,tc->dc",
            saved_state.normed_cross,
            grad_cross_queries,
            preferred_element_type=jnp.float32,
        )
        cross_rows = sum_rows(
            jnp.einsum(
                "tc,dc->td",
                grad_cross_queries,
                cross_query_full,
                preferred_element_type=jnp.float32,
            )
        )
        grad_norm_cross, cross_gain_grad = jax.vjp(
            norm_rows, saved_state.after_self, cross_gain
        )[1](cross_rows)
        grad_after_self = grad_after_cross + grad_norm_cross
        queries = saved_state.queries
        keys_own = saved_state.keys_own
        values_own = saved_state.values_own
        context = saved_state.context
        log_total = saved_state.log_total
        normed_self = saved_state.normed_self
        query_heads = split_heads(queries)
        grad_self_branch = gather_rows(grad_after_self.astype(jnp.bfloat16))
        self_output_grad = jnp.einsum(
            "te,td->ed",
            saved_state.context_low,
            grad_self_branch,
            preferred_element_type=jnp.float32,
        )
        grad_context = jnp.einsum(
            "td,ed->te", grad_self_branch, output_full, preferred_element_type=jnp.float32
        ).astype(jnp.bfloat16)
        grad_context_heads = split_heads(grad_context)
        row_delta = jnp.transpose(
            jnp.sum(grad_context_heads.astype(jnp.float32) * context, axis=-1), (1, 2, 0)
        )

        def query_step():

            def step(carried, pieces, piece_start):
                key_piece, value_piece = pieces
                piece_length = key_piece.shape[0]
                block_width = math.gcd(piece_length, key_block_width)
                block_count = piece_length // block_width
                key_blocks = key_piece.reshape(block_count, block_width, kv_local, head_size)
                value_blocks = value_piece.reshape(block_count, block_width, kv_local, head_size)
                block_starts = block_width * jnp.arange(block_count, dtype=jnp.int32)

                def step_one_block(current, block_data):
                    key_block, value_block, block_start = block_data
                    bias_values, allowed, indicator = position_bias(
                        query_start, block_start, piece_rows, block_width
                    )
                    scores = (
                        jnp.einsum(
                            "ikgd,jkd->kgij",
                            query_heads,
                            key_block,
                            preferred_element_type=jnp.float32,
                        )
                        * score_scale
                        + bias_values
                    )
                    shares = jnp.where(allowed, jnp.exp(scores - log_total[..., None]), 0.0)
                    grad_shares = jnp.einsum(
                        "ikgd,jkd->kgij",
                        grad_context_heads,
                        value_block,
                        preferred_element_type=jnp.float32,
                    )
                    grad_scores = shares * (grad_shares - row_delta[..., None])
                    bias_grad = current[1] + jnp.einsum(
                        "hij,bij->hb",
                        grad_scores.reshape(local_heads, piece_rows, block_width),
                        indicator,
                        precision=highest,
                    )
                    scores_low = grad_scores.astype(jnp.bfloat16)
                    query_grad = (
                        current[0]
                        + jnp.einsum(
                            "kgij,jkd->ikgd",
                            scores_low,
                            key_block,
                            preferred_element_type=jnp.float32,
                        )
                        * score_scale
                    )
                    key_block_grad = (
                        jnp.einsum(
                            "kgij,ikgd->jkd",
                            scores_low,
                            query_heads,
                            preferred_element_type=jnp.float32,
                        ).reshape(block_width, kv_local * head_size)
                        * score_scale
                    )
                    value_block_grad = jnp.einsum(
                        "kgij,ikgd->jkd",
                        shares.astype(jnp.bfloat16),
                        grad_context_heads,
                        preferred_element_type=jnp.float32,
                    ).reshape(block_width, kv_local * head_size)
                    keys_all = lax.dynamic_update_slice_in_dim(
                        current[2],
                        lax.dynamic_slice_in_dim(current[2], block_start, block_width, 0)
                        + key_block_grad,
                        block_start,
                        0,
                    )
                    values_all = lax.dynamic_update_slice_in_dim(
                        current[3],
                        lax.dynamic_slice_in_dim(current[3], block_start, block_width, 0)
                        + value_block_grad,
                        block_start,
                        0,
                    )
                    return ((query_grad, bias_grad, keys_all, values_all), None)

                carried, unused = lax.scan(
                    step_one_block, carried, (key_blocks, value_blocks, block_starts)
                )
                return carried

            return step

        query_zero = jnp.zeros((piece_rows, kv_local, group_size, head_size), jnp.float32)
        bias_zero = jnp.zeros((local_heads, buckets), jnp.float32)
        all_zero = jnp.zeros((length, kv_local * head_size), jnp.float32)
        query_grad, bias_grad, keys_all, values_all = fold_keys(
            keys_own, values_own, query_step(), (query_zero, bias_zero, all_zero, all_zero)
        )
        key_sum_self, value_sum_self = (
            lax.psum_scatter(keys_all, fsdp_axis, scatter_dimension=0, tiled=True),
            lax.psum_scatter(values_all, fsdp_axis, scatter_dimension=0, tiled=True),
        )
        key_grad_low = key_sum_self.astype(jnp.bfloat16)
        value_grad_low = value_sum_self.astype(jnp.bfloat16)
        query_grad_low = query_grad.reshape(piece_rows, local_heads * head_size).astype(
            jnp.bfloat16
        )
        self_query_grad = jnp.einsum(
            "td,tc->dc", normed_self, query_grad_low, preferred_element_type=jnp.float32
        )
        self_key_grad = jnp.einsum(
            "td,tc->dc", normed_self, key_grad_low, preferred_element_type=jnp.float32
        )
        self_value_grad = jnp.einsum(
            "td,tc->dc", normed_self, value_grad_low, preferred_element_type=jnp.float32
        )
        self_rows = sum_rows(
            jnp.einsum("tc,dc->td", query_grad_low, query_full, preferred_element_type=jnp.float32)
            + jnp.einsum("tc,dc->td", key_grad_low, key_full, preferred_element_type=jnp.float32)
            + jnp.einsum(
                "tc,dc->td", value_grad_low, value_full, preferred_element_type=jnp.float32
            )
        )
        grad_norm_self, self_gain_grad = jax.vjp(norm_rows, saved_state.own_rows, self_gain)[1](
            self_rows
        )
        input_grad = grad_after_self + grad_norm_self
        grads_full = (
            self_query_grad,
            self_key_grad,
            self_value_grad,
            self_output_grad,
            cross_query_grad,
            cross_key_grad,
            cross_value_grad,
            cross_output_grad,
            gate_grad,
            up_grad,
            down_grad,
        )
        extras = (bias_grad, self_gain_grad, cross_gain_grad, feed_gain_grad)
        return (grads_full, extras, input_grad, encoder_grad)

    layer_list = []
    input_list = []
    encoder_list = []
    small_sums = None
    shard_grads = None
    for batch_index in range(batches):
        weights_forward = gather_weights(shards)
        (
            forward_query_full,
            forward_key_full,
            forward_value_full,
            forward_output_full,
            forward_cross_query_full,
            forward_cross_key_full,
            forward_cross_value_full,
            forward_cross_output_full,
            forward_gate_full,
            forward_up_full,
            forward_down_full,
        ) = weights_forward
        own_rows = inputs[batch_index].astype(jnp.float32)
        forward_normed_self = gather_rows(norm_rows(own_rows, self_gain).astype(jnp.bfloat16))
        forward_queries = matmul(forward_normed_self, forward_query_full).astype(jnp.bfloat16)
        forward_keys_own = matmul(forward_normed_self, forward_key_full).astype(jnp.bfloat16)
        forward_values_own = matmul(forward_normed_self, forward_value_full).astype(jnp.bfloat16)
        forward_query_heads = split_heads(forward_queries)

        def forward_step(carried, pieces, piece_start):
            key_piece, value_piece = pieces
            piece_length = key_piece.shape[0]
            block_width = math.gcd(piece_length, key_block_width)
            block_count = piece_length // block_width
            key_blocks = key_piece.reshape(block_count, block_width, kv_local, head_size)
            value_blocks = value_piece.reshape(block_count, block_width, kv_local, head_size)
            block_starts = block_width * jnp.arange(block_count, dtype=jnp.int32)

            def forward_one_block(current, block_data):
                running_max, running_total, accumulated = current
                key_block, value_block, block_start = block_data
                bias_values, allowed, indicator = position_bias(
                    query_start, block_start, piece_rows, block_width
                )
                scores = (
                    jnp.einsum(
                        "ikgd,jkd->kgij",
                        forward_query_heads,
                        key_block,
                        preferred_element_type=jnp.float32,
                    )
                    * score_scale
                    + bias_values
                )
                scores = jnp.where(allowed, scores, masked_score)
                new_max = jnp.maximum(running_max, jnp.max(scores, axis=-1))
                factor = jnp.exp(running_max - new_max)
                shares = jnp.where(allowed, jnp.exp(scores - new_max[..., None]), 0.0)
                running_total = running_total * factor + jnp.sum(shares, axis=-1)
                update = jnp.einsum(
                    "kgij,jkd->ikgd",
                    shares.astype(jnp.bfloat16),
                    value_block,
                    preferred_element_type=jnp.float32,
                )
                accumulated = accumulated * jnp.transpose(factor, (2, 0, 1))[..., None] + update
                return ((new_max, running_total, accumulated), None)

            carried, unused = lax.scan(
                forward_one_block, carried, (key_blocks, value_blocks, block_starts)
            )
            return carried

        stat_shape = (kv_local, group_size, piece_rows)
        initial = (
            jnp.full(stat_shape, masked_score, jnp.float32),
            jnp.zeros(stat_shape, jnp.float32),
            jnp.zeros((piece_rows, kv_local, group_size, head_size), jnp.float32),
        )
        running_max, running_total, accumulated = fold_keys(
            forward_keys_own, forward_values_own, forward_step, initial
        )
        forward_context = accumulated / jnp.transpose(running_total, (2, 0, 1))[..., None]
        forward_log_total = running_max + jnp.log(running_total)
        context_low = forward_context.reshape(piece_rows, local_heads * head_size).astype(
            jnp.bfloat16
        )
        after_self = own_rows + sum_rows(matmul(context_low, forward_output_full))
        normed_cross = gather_rows(norm_rows(after_self, cross_gain).astype(jnp.bfloat16))
        cross_queries = matmul(normed_cross, forward_cross_query_full).astype(jnp.bfloat16)
        forward_encoded = lax.all_gather(
            encoder_out[batch_index], (fsdp_axis, tensor_axis), axis=0, tiled=True
        )
        cross_keys = matmul(forward_encoded, forward_cross_key_full).astype(jnp.bfloat16)
        cross_values = matmul(forward_encoded, forward_cross_value_full).astype(jnp.bfloat16)
        cross_scores = (
            jnp.einsum(
                "ikgd,jkd->kgij",
                split_heads(cross_queries),
                split_kv(cross_keys),
                preferred_element_type=jnp.float32,
            )
            * score_scale
        )
        forward_cross_weights = jax.nn.softmax(cross_scores, axis=-1)
        cross_low = forward_cross_weights.astype(jnp.bfloat16)
        forward_cross_context = (
            jnp.einsum(
                "kgij,jkd->ikgd",
                cross_low,
                split_kv(cross_values),
                preferred_element_type=jnp.float32,
            )
            .reshape(piece_rows, local_heads * head_size)
            .astype(jnp.bfloat16)
        )
        after_cross = after_self + sum_rows(
            matmul(forward_cross_context, forward_cross_output_full)
        )
        forward_normed_feed = gather_rows(norm_rows(after_cross, feed_gain).astype(jnp.bfloat16))
        gate_values = matmul(forward_normed_feed, forward_gate_full)
        up_values = matmul(forward_normed_feed, forward_up_full)
        forward_hidden = (jax.nn.gelu(gate_values, approximate=True) * up_values).astype(
            jnp.bfloat16
        )
        layer_rows = after_cross + sum_rows(matmul(forward_hidden, forward_down_full))
        forward_saved_state = types.SimpleNamespace(
            own_rows=own_rows,
            normed_self=forward_normed_self,
            queries=forward_queries,
            keys_own=forward_keys_own,
            values_own=forward_values_own,
            context=forward_context,
            log_total=forward_log_total,
            context_low=context_low,
            after_self=after_self,
            normed_cross=normed_cross,
            cross_queries=cross_queries,
            encoded=forward_encoded,
            cross_keys=cross_keys,
            cross_values=cross_values,
            cross_weights=forward_cross_weights,
            cross_low=cross_low,
            cross_context=forward_cross_context,
            after_cross=after_cross,
            normed_feed=forward_normed_feed,
            gate_values=gate_values,
            up_values=up_values,
            hidden=forward_hidden,
        )
        layer_rows, saved_state = (layer_rows.astype(jnp.bfloat16), forward_saved_state)
        weights_backward = gather_weights(shards)
        grads_full, extras, input_grad, encoder_grad = backward(
            batch_index, saved_state, weights_backward
        )
        reduced = scatter_grads(grads_full)
        shard_grads = reduced if shard_grads is None else add_all(shard_grads, reduced)
        small_sums = extras if small_sums is None else add_all(small_sums, extras)
        layer_list.append(layer_rows)
        input_list.append(input_grad)
        encoder_list.append(encoder_grad)
    table_full = lax.dynamic_update_slice_in_dim(
        jnp.zeros((heads_all, buckets), jnp.float32), small_sums[0], tensor_rank * local_heads, 0
    )
    table_sum, self_gain_sum, cross_gain_sum, feed_gain_sum = lax.psum(
        (table_full, small_sums[1], small_sums[2], small_sums[3]), (fsdp_axis, tensor_axis)
    )
    return (
        jnp.stack(layer_list),
        jnp.stack(input_list),
        jnp.stack(encoder_list),
        table_sum,
        self_gain_sum,
        shard_grads[0],
        shard_grads[1],
        shard_grads[2],
        shard_grads[3],
        cross_gain_sum,
        shard_grads[4],
        shard_grads[5],
        shard_grads[6],
        shard_grads[7],
        feed_gain_sum,
        shard_grads[8],
        shard_grads[9],
        shard_grads[10],
    )


def to_chip(fsdp):
    return dict(device_id={fsdp_axis: fsdp}, device_id_type=pl.DeviceIdType.MESH)


def to_core(core):
    return dict(device_id={tensor_axis: core}, device_id_type=pl.DeviceIdType.MESH)


def chip_place(layers):
    rank = lax.axis_index(fsdp_axis)
    return rank, rank // 4, rank // 2 % 2, rank % 2


def peers_of(rank, y, x):
    found = []
    for o in (1, 2, 3):
        other_y = 1 - y if o & 2 else y
        other_x = 1 - x if o & 1 else x
        spot = 2 * other_y + other_x
        found.append((rank - 2 * y - x + spot, spot))
    return found


def greet(layers):
    rank, z, y, x = chip_place(layers)
    barrier = pltpu.get_barrier_semaphore()
    for chip, spot in peers_of(rank, y, x):
        pl.semaphore_signal(barrier, inc=1, **to_chip(chip))
    for o in range(1, layers):
        pl.semaphore_signal(barrier, inc=1, **to_chip(rank - 4 * z + 4 * ((z + o) % layers)))
    pl.semaphore_signal(barrier, inc=1, **to_core(1 - lax.axis_index(tensor_axis)))
    pl.semaphore_wait(barrier, 3 + layers)


dma = pltpu.SemaphoreType.DMA


class Column:
    def __init__(self, layers, source, land, z_sem, core_sem=None):
        self.layers, self.source, self.land = layers, source, land
        self.z_sem, self.core_sem = z_sem, core_sem
        self.rank, self.z, self.y, self.x = chip_place(layers)
        self.core = lax.axis_index(tensor_axis)

    def place(self, layer):
        return (layer,) if self.core_sem is None else (layer, self.core)

    def hop(self, o):
        there = (self.z + o) % self.layers
        return pltpu.make_async_remote_copy(
            src_ref=self.source.at[there],
            dst_ref=self.land.at[self.place(self.z)],
            send_sem=self.z_sem.at[0, o],
            recv_sem=self.z_sem.at[1, self.z],
            **to_chip(self.rank + 4 * (there - self.z)),
        )

    def arrival(self, layer):
        return pltpu.make_async_remote_copy(
            src_ref=self.source.at[0],
            dst_ref=self.land.at[self.place(layer)],
            send_sem=self.z_sem.at[0, 0],
            recv_sem=self.z_sem.at[1, layer],
            **to_chip(self.rank + 4 - 8 * (self.z // 2)),
        )

    def over(self, layer):
        return pltpu.make_async_remote_copy(
            src_ref=self.land.at[layer, self.core],
            dst_ref=self.land.at[layer, self.core],
            send_sem=self.core_sem.at[0, layer],
            recv_sem=self.core_sem.at[1, layer],
            **to_core(1 - self.core),
        )

    def start(self):
        for o in range(1, self.layers):
            self.hop(o).start()
        self.land[self.place(self.z)] = self.source[self.z]

    def arrive(self):
        for o in range(1, self.layers):
            self.arrival((self.z + o) % self.layers).wait_recv()
        if self.core_sem is not None:
            for layer in range(self.layers):
                self.over(layer).start()

    def finish(self):
        for o in range(1, self.layers):
            self.hop(o).wait_send()
        if self.core_sem is not None:
            for layer in range(self.layers):
                self.over(layer).wait()


class PlaneSwap:
    def __init__(self, layers, source, land, sem):
        self.source, self.land, self.sem = source, land, sem
        self.rank, self.z, self.y, self.x = chip_place(layers)
        self.spot = 2 * self.y + self.x
        self.peers = peers_of(self.rank, self.y, self.x)

    def hop(self, o):
        chip, there = self.peers[o]
        return pltpu.make_async_remote_copy(
            src_ref=self.source.at[there],
            dst_ref=self.land.at[self.spot],
            send_sem=self.sem.at[0, o],
            recv_sem=self.sem.at[1, o],
            **to_chip(chip),
        )

    def start(self):
        for o in range(3):
            self.hop(o).start()
        self.land[self.spot] = self.source[self.spot]

    def arrival(self, o):
        chip, there = self.peers[o]
        return pltpu.make_async_remote_copy(
            src_ref=self.source.at[there],
            dst_ref=self.land.at[there],
            send_sem=self.sem.at[0, o],
            recv_sem=self.sem.at[1, o],
            **to_chip(chip),
        )

    def arrive(self):
        for o in range(3):
            self.arrival(o).wait_recv()

    def finish(self):
        for o in range(3):
            self.hop(o).wait_send()


class PlaneGather:
    def __init__(self, layers, source, land, sem, core_sem):
        self.source, self.land, self.sem, self.core_sem = source, land, sem, core_sem
        self.rank, self.z, self.y, self.x = chip_place(layers)
        self.core = lax.axis_index(tensor_axis)
        self.spot = 2 * self.y + self.x
        self.peers = peers_of(self.rank, self.y, self.x)

    def hop(self, o, spot):
        return pltpu.make_async_remote_copy(
            src_ref=self.source,
            dst_ref=self.land.at[spot, self.core],
            send_sem=self.sem.at[0, o],
            recv_sem=self.sem.at[1, o],
            **to_chip(self.peers[o][0]),
        )

    def over(self, spot):
        return pltpu.make_async_remote_copy(
            src_ref=self.land.at[spot, self.core],
            dst_ref=self.land.at[spot, self.core],
            send_sem=self.core_sem.at[0, spot],
            recv_sem=self.core_sem.at[1, spot],
            **to_core(1 - self.core),
        )

    def start(self):
        for o in range(3):
            self.hop(o, self.spot).start()
        self.land[self.spot, self.core] = self.source[...]

    def arrive(self):
        for o in range(3):
            self.hop(o, self.peers[o][1]).wait_recv()
        for spot in range(4):
            self.over(spot).start()

    def finish(self):
        for o in range(3):
            self.hop(o, self.spot).wait_send()
        for spot in range(4):
            self.over(spot).wait()


def open_kernel(
    layers,
    rows_ref,
    enc_ref,
    shard_ref,
    rows_out,
    enc_out,
    whole_ref,
    rows_land,
    enc_land,
    enc_all,
    rows_z,
    rows_core,
    enc_z,
    plane_sem,
    plane_core,
    *gather_refs,
):
    gather = RowGather(layers, False, shard_ref, whole_ref, *gather_refs)
    rows = Column(layers, rows_ref, rows_land, rows_z, rows_core)
    enc = Column(layers, enc_ref, enc_land, enc_z)
    plane = PlaneGather(layers, enc_land, enc_all, plane_sem, plane_core)
    gather.begin()
    greet(layers)
    rows.start()
    enc.start()
    gather.send_own()
    rows.arrive()
    enc.arrive()
    plane.start()

    def one(m, carry):
        gather.step(m)
        return carry

    lax.fori_loop(0, 2 * layers - 4, one, 0)
    plane.arrive()
    lax.fori_loop(2 * layers - 4, 2 * layers, one, 0)
    rows.finish()
    rows_out[...] = rows_land[...]
    enc.finish()
    plane.finish()
    enc_out[...] = enc_all[...]
    gather.finish()


def open_rows(layers, inputs, encoder, shard):
    bf16 = jnp.bfloat16
    own, width = inputs.shape[1:]
    enc_own = encoder.shape[1]
    cols = shard.shape[1]
    vmem, anywhere = pl.BlockSpec(memory_space=pltpu.VMEM), pl.BlockSpec(memory_space=pl.ANY)
    rows_shape, enc_shape = (layers, 2, own, width), (4, 2, layers, enc_own, width)
    rows, enc, whole = pl.pallas_call(
        functools.partial(open_kernel, layers),
        name="open_rows",
        out_shape=(
            jax.ShapeDtypeStruct(rows_shape, bf16),
            jax.ShapeDtypeStruct(enc_shape, bf16),
            jax.ShapeDtypeStruct((layers, 2, 2, 2, 2, 16, cols), bf16),
        ),
        in_specs=[vmem, vmem, anywhere],
        out_specs=(vmem, vmem, anywhere),
        scratch_shapes=[
            pltpu.VMEM(rows_shape, bf16),
            pltpu.VMEM((layers, enc_own, width), bf16),
            pltpu.VMEM(enc_shape, bf16),
            dma((2, layers)),
            dma((2, layers)),
            dma((2, layers)),
            dma((2, 3)),
            dma((2, 4)),
            *gather_scratch(layers, cols),
        ],
        compiler_params=pltpu.CompilerParams(collective_id=5, has_side_effects=True),
    )(inputs, encoder, shard.reshape(2, 2, 16, cols))
    return rows, enc, whole.reshape(layers * 256, cols)


def close_kernel(
    layers,
    heads,
    gq_ref,
    x_ref,
    win_ref,
    gas_ref,
    kvs_ref,
    gains_ref,
    mid_ref,
    sums_ref,
    hit_ref,
    wa_ref,
    query_out,
    key_out,
    value_out,
    input_out,
    enc_out,
    table_out,
    gain_out,
    nt_s,
    wkv_s,
    mine_s,
    halves_s,
    enc_s,
    ended_s,
    rows_land,
    small_s,
    small_l,
    small_z,
    sum_s,
    load_sem,
    core_sem,
    rows_z,
    small_sem,
    z_sem,
    *sum_refs,
):
    f32, bf16 = jnp.float32, jnp.bfloat16
    grads = GradSum(layers, None, (), sum_s, *sum_refs)
    rows = Column(layers, ended_s, rows_land, rows_z)
    rank, z, y, x = chip_place(layers)
    core = lax.axis_index(tensor_axis)
    own = gas_ref.shape[1]
    width = x_ref.shape[1]
    enc_own = kvs_ref.shape[0] // (2 * layers)
    wide = kvs_ref.shape[1]
    kv_local = query_out.shape[1] // 128
    blocks = sums_ref.shape[0] // 2
    buckets = hit_ref.shape[1]
    gain = gains_ref[...]
    loads = pltpu.make_async_copy(
        wa_ref.at[:, pl.ds(2 * wide, wide)], wkv_s, load_sem.at[0]
    )
    loads.start()
    greet(layers)

    def normed(n, carry):
        at = pl.ds(pl.multiple_of(n * 128, 128), 128)
        v = x_ref[at, :].astype(f32)
        nt_s[:, at] = jnp.transpose((v * norm_scale(v) * gain).astype(bf16))
        return carry

    lax.fori_loop(0, x_ref.shape[0] // 128, normed, 0)
    per_layer = width // layers

    def weigh(turn, carry):
        layer = grads.layer_of(2 * turn)
        at = pl.ds(pl.multiple_of(layer * per_layer, per_layer), per_layer)
        part = matmul(nt_s[at, :], gq_ref[...]).astype(bf16)
        grads.own[layer] = part.reshape(grads.own.shape[1:])
        grads.send_first(2 * turn)
        grads.send_first(2 * turn + 1)
        return carry

    lax.fori_loop(0, layers, weigh, 0)

    def gather(which):
        return jnp.concatenate(
            [
                gq_ref[pl.ds(pl.multiple_of((2 * layer + which) * own, own), own), :]
                for layer in range(layers)
            ],
            axis=0,
        )

    def across(n, shape_at):
        return pltpu.make_async_remote_copy(
            src_ref=halves_s.at[0, shape_at],
            dst_ref=halves_s.at[1, shape_at],
            send_sem=core_sem.at[0, n],
            recv_sem=core_sem.at[1, n],
            **to_core(1 - core),
        )

    body, tail = pl.ds(0, layers * own), pl.ds(layers * own, layers * enc_own)
    halves_s[0, body, :] = dot_t(gather(1 - core), win_ref[...]).astype(bf16)
    across(0, body).start()
    loads.wait()
    enc_s[...] = dot_t(kvs_ref[...], wkv_s[...])
    other = pl.ds(pl.multiple_of((1 - core) * layers * enc_own, enc_own), layers * enc_own)
    halves_s[0, tail, :] = enc_s[other, :].astype(bf16)
    across(1, tail).start()
    mine_s[...] = dot_t(gather(core), win_ref[...])
    grads.advance(1)
    grads.advance(2)

    found = [jnp.zeros((1, buckets), f32) for _ in range(2)]
    for d in range(blocks):
        by_bucket = lax.dot_general(
            sums_ref[...],
            hit_ref[d],
            (((1,), (1,)), ((), ())),
            precision=highest,
            preferred_element_type=f32,
        )
        for h in range(2):
            found[h] = found[h] + by_bucket[h * blocks + d : h * blocks + d + 1, :]
    lane = lax.broadcasted_iota(jnp.int32, (buckets, width), 1)
    spread = (lane % buckets == lax.broadcasted_iota(jnp.int32, (buckets, width), 0)).astype(f32)
    lane = lax.broadcasted_iota(jnp.int32, (1, width), 1)
    first_head = 2 * (core * kv_local + rank % 4)
    table = jnp.zeros((1, width), f32)
    for h in range(2):
        row = jnp.dot(found[h], spread, precision=highest, preferred_element_type=f32)
        table = table + jnp.where(lane // buckets == first_head + h, row, 0.0)
    small_s[0] = jnp.zeros_like(small_s[0])
    small_s[0, 1:3, :] = mid_ref[...]
    small_s[0, 3:4, :] = table

    across(0, body).wait()
    across(1, tail).wait()
    mine_enc = pl.ds(pl.multiple_of(core * layers * enc_own, enc_own), layers * enc_own)
    enc_sum = enc_s[mine_enc, :].astype(bf16).astype(f32) + halves_s[1, tail, :].astype(f32)

    total = jnp.zeros((1, width), f32)
    for layer in range(layers):
        at = slice(layer * own, (layer + 1) * own)
        both = mine_s[at, :].astype(bf16).astype(f32) + halves_s[1, at, :].astype(f32)
        v = x_ref[pl.ds(pl.multiple_of((2 * layer + core) * own, own), own), :].astype(f32)
        grad, gain_grad = norm_pull(v, gain, both)
        total = total + gain_grad
        ended_s[layer, :own, :] = (gas_ref[layer] + grad).astype(bf16)
        ended_s[layer, own:, :] = enc_sum[layer * enc_own : (layer + 1) * enc_own].astype(bf16)
    small_s[0, 0:1, :] = total

    def swap(n, where):
        return pltpu.make_async_remote_copy(
            src_ref=small_s.at[n],
            dst_ref=small_l.at[n],
            send_sem=small_sem.at[0, n],
            recv_sem=small_sem.at[1, n],
            **where,
        )

    across_x = swap(0, to_chip(rank + 1 - 2 * x))
    across_y = swap(1, to_chip(rank + 2 - 4 * y))
    across_core = swap(3, to_core(1 - core))

    def across_z(o, layer):
        there = (z + o) % layers
        return pltpu.make_async_remote_copy(
            src_ref=small_s.at[2],
            dst_ref=small_z.at[layer],
            send_sem=z_sem.at[0, o],
            recv_sem=z_sem.at[1, layer],
            **to_chip(rank + 4 * (there - z)),
        )

    across_x.start()
    grads.advance(3)
    rows.start()
    grads.advance(4)
    across_x.wait()
    small_s[1] = small_s[0] + small_l[0]
    across_y.start()
    grads.advance(5)
    across_y.wait()
    small_s[2] = small_s[1] + small_l[1]
    small_z[z] = small_s[2]
    for o in range(1, layers):
        across_z(o, z).start()
    grads.advance(6)
    grads.advance(7)
    for o in range(1, layers):
        across_z(o, (z + o) % layers).wait_recv()
        across_z(o, z).wait_send()
    summed = small_z[0]
    for layer in range(1, layers):
        summed = summed + small_z[layer]
    small_s[3] = summed
    across_core.start()

    def one(m, carry):
        grads.advance(m)
        return carry

    lax.fori_loop(8, sum_steps(layers), one, 0)
    across_core.wait()
    both = small_s[3] + small_l[3]
    low = jnp.where(core == 0, small_s[3], small_l[3])
    gain_out[0:1, :] = both[0:1, :]
    gain_out[1:3, :] = low[1:3, :]
    for h in range(heads):
        table_out[h : h + 1, :] = both[3:4, h * buckets : (h + 1) * buckets]
    whole = sum_s[...].reshape(64, sum_s.shape[-1])
    group = whole.shape[1] // kv_local
    half = group // 4
    pieces = [whole[:, n * group : (n + 1) * group] for n in range(kv_local)]
    query_out[...] = jnp.concatenate([p[:, : 2 * half] for p in pieces], axis=1)
    key_out[...] = jnp.concatenate([p[:, 2 * half : 3 * half] for p in pieces], axis=1)
    value_out[...] = jnp.concatenate([p[:, 3 * half :] for p in pieces], axis=1)
    rows.arrive()
    for layer in range(layers):
        input_out[layer] = rows_land[layer, :own, :].astype(f32)
        enc_out[layer] = rows_land[layer, own:, :].astype(f32)
    rows.finish()
    grads.finish()


def close_rows(
    layers, heads, grad_qkv, x_low, win, grad_rows, kv_sum, self_gain, mid, sums, hit, weights
):
    f32, bf16 = jnp.float32, jnp.bfloat16
    width, cols = win.shape
    own = grad_rows.shape[1]
    wide = kv_sum.shape[1]
    enc_own = kv_sum.shape[0] // (2 * layers)
    buckets = hit.shape[1]
    vmem, anywhere = pl.BlockSpec(memory_space=pltpu.VMEM), pl.BlockSpec(memory_space=pl.ANY)
    rows_shape = (layers, own + enc_own, width)
    return pl.pallas_call(
        functools.partial(close_kernel, layers, heads),
        name="close_rows",
        out_shape=(
            jax.ShapeDtypeStruct((64, cols // 2), f32),
            jax.ShapeDtypeStruct((64, cols // 4), f32),
            jax.ShapeDtypeStruct((64, cols // 4), f32),
            jax.ShapeDtypeStruct((layers, own, width), f32),
            jax.ShapeDtypeStruct((layers, enc_own, width), f32),
            jax.ShapeDtypeStruct((heads, buckets), f32),
            jax.ShapeDtypeStruct((3, width), f32),
        ),
        in_specs=[vmem] * 9 + [anywhere],
        out_specs=(vmem,) * 7,
        scratch_shapes=[
            pltpu.VMEM((width, x_low.shape[0]), bf16),
            pltpu.VMEM((width, wide), bf16),
            pltpu.VMEM((layers * own, width), f32),
            pltpu.VMEM((2, layers * (own + enc_own), width), bf16),
            pltpu.VMEM((2 * layers * enc_own, width), f32),
            pltpu.VMEM(rows_shape, bf16),
            pltpu.VMEM(rows_shape, bf16),
            pltpu.VMEM((4, 8, width), f32),
            pltpu.VMEM((4, 8, width), f32),
            pltpu.VMEM((layers, 8, width), f32),
            pltpu.VMEM((2, 2, 16, cols), f32),
            dma((1,)),
            dma((2, 2)),
            dma((2, layers)),
            dma((2, 4)),
            dma((2, layers)),
            *sum_scratch(layers, cols),
        ],
        compiler_params=pltpu.CompilerParams(
            collective_id=7, has_side_effects=True, vmem_limit_bytes=48 << 20
        ),
    )(grad_qkv, x_low, win, grad_rows, kv_sum, self_gain, mid, sums, hit, weights)

def sum_scratch(layers, cols):
    steps = 2 * layers
    bf16 = jnp.bfloat16
    return [
        pltpu.VMEM((layers, 2, 2, 2, 2, 16, cols), bf16),
        pltpu.VMEM((layers, 2, 2, 2, 16, cols), bf16),
        pltpu.VMEM((steps, 2, 16, cols), bf16),
        pltpu.VMEM((steps, 2, 16, cols), bf16),
        pltpu.VMEM((steps, 2, 16, cols), bf16),
        dma((3, layers)),
        dma((2, steps, 2, 2)),
        dma((2, steps, 2)),
        dma((2, steps)),
        dma((2, steps)),
    ]


def sum_steps(layers):
    return 2 * layers + layers + 3


class GradSum:
    def __init__(self, layers, whole, got, out, own, first, second, below, above, load, s1, s2, su, sd):
        self.got = got
        self.layers, self.whole, self.out, self.own = layers, whole, out, own
        self.first, self.second, self.below, self.above = first, second, below, above
        self.load, self.s1, self.s2, self.su, self.sd = load, s1, s2, su, sd
        self.rank, self.z, self.y, self.x = chip_place(layers)
        self.x_chip = self.rank + 1 - 2 * self.x
        self.y_chip = self.rank + 2 - 4 * self.y
        self.steps = 2 * layers

    def layer_of(self, n):
        turn = n // 2
        return jnp.where(turn % 2 == 1, turn // 2, self.layers - 1 - turn // 2)

    def loads(self, turn):
        layer = self.layer_of(2 * turn)
        copies = [
            pltpu.make_async_copy(self.whole.at[layer], self.own.at[layer], self.load.at[0, turn])
        ]
        for colour, came in enumerate(self.got):
            copies.append(
                pltpu.make_async_copy(
                    came.at[layer], self.first.at[layer, colour], self.load.at[1 + colour, turn]
                )
            )
        return copies

    def hop_one(self, n, colour, which):
        layer, chunk = self.layer_of(n), n % 2
        if colour == 0:
            source, chip = self.own.at[layer, which, 1 - self.x, 0, chunk], self.x_chip
        else:
            source, chip = self.own.at[layer, 1 - self.y, which, 1, chunk], self.y_chip
        return pltpu.make_async_remote_copy(
            src_ref=source,
            dst_ref=self.first.at[layer, colour, which, chunk],
            send_sem=self.s1.at[0, n, colour, which],
            recv_sem=self.s1.at[1, n, colour, which],
            **to_chip(chip),
        )

    def hop_two(self, n, colour):
        layer, chunk = self.layer_of(n), n % 2
        if colour == 0:
            source, chip = self.own.at[layer, 1 - self.y, self.x, 0, chunk], self.y_chip
        else:
            source, chip = self.own.at[layer, self.y, 1 - self.x, 1, chunk], self.x_chip
        return pltpu.make_async_remote_copy(
            src_ref=source,
            dst_ref=self.second.at[n, colour],
            send_sem=self.s2.at[0, n, colour],
            recv_sem=self.s2.at[1, n, colour],
            **to_chip(chip),
        )

    def hop_z(self, n, up):
        layer, chunk = self.layer_of(n), n % 2
        sems = self.su if up else self.sd
        return pltpu.make_async_remote_copy(
            src_ref=self.own.at[layer, self.y, self.x, :, chunk],
            dst_ref=(self.below if up else self.above).at[n],
            send_sem=sems.at[0, n],
            recv_sem=sems.at[1, n],
            **to_chip(self.rank + (4 if up else -4)),
        )

    def start(self):
        for turn in range(self.layers):
            for copy in self.loads(turn):
                copy.start()

    def send_first(self, n):
        @pl.when(n < self.steps)
        def _():
            if self.whole is not None:

                @pl.when(n % 2 == 0)
                def _():
                    for copy in self.loads(n // 2):
                        copy.wait()

            if not self.got:
                for which in range(2):
                    for colour in range(2):
                        self.hop_one(n, colour, which).start()

    def advance(self, m):
        steps, layers = self.steps, self.layers
        n = m - 1

        @pl.when((n >= 0) & (n < steps))
        def _():
            layer, chunk = self.layer_of(n), n % 2
            for colour in range(2):
                for other in range(2):
                    if colour == 0:
                        which = (1 - self.y) if other == 0 else self.y
                        place = (layer, which, self.x, 0, chunk)
                    else:
                        which = (1 - self.x) if other == 0 else self.x
                        place = (layer, self.y, which, 1, chunk)
                    if not self.got:
                        self.hop_one(n, colour, which).wait_recv()
                    self.own[place] = self.own[place] + self.first[layer, colour, which, chunk]
                    if other == 0:
                        self.hop_two(n, colour).start()

        n2 = m - 2

        @pl.when((n2 >= 0) & (n2 < steps))
        def _():
            layer, chunk = self.layer_of(n2), n2 % 2
            for colour in range(2):
                self.hop_two(n2, colour).wait_recv()
                place = (layer, self.y, self.x, colour, chunk)
                self.own[place] = self.own[place] + self.second[n2, colour]

        for up in (True, False):
            chain = self.z if up else layers - 1 - self.z
            nz = m - 2 - chain
            layer = self.layer_of(nz)
            beyond = (layer > self.z) if up else (layer < self.z)

            @pl.when((nz >= 0) & (nz < steps) & beyond)
            def _():
                @pl.when(chain > 0)
                def _():
                    self.hop_z(nz, up).wait_recv()
                    came = self.below if up else self.above
                    for colour in range(2):
                        place = (layer, self.y, self.x, colour, nz % 2)
                        self.own[place] = self.own[place] + came[nz, colour]

                self.hop_z(nz, up).start()

        nf = m - 2 - layers

        @pl.when((nf >= 0) & (nf < steps) & (self.layer_of(nf) == self.z))
        def _():
            layer, chunk = self.layer_of(nf), nf % 2
            for colour in range(2):
                self.out[colour, chunk] = self.own[layer, self.y, self.x, colour, chunk].astype(
                    jnp.float32
                )
            for up in (True, False):
                chain = self.z if up else layers - 1 - self.z

                @pl.when(chain > 0)
                def _():
                    self.hop_z(nf, up).wait_recv()
                    came = self.below if up else self.above
                    for colour in range(2):
                        self.out[colour, chunk] += came[nf, colour].astype(jnp.float32)

    def finish(self):
        def one(n, carry):
            for colour in range(2):
                if not self.got:
                    for which in range(2):
                        self.hop_one(n, colour, which).wait_send()
                self.hop_two(n, colour).wait_send()
            layer = self.layer_of(n)
            for up in (True, False):

                @pl.when((layer > self.z) if up else (layer < self.z))
                def _():
                    self.hop_z(n, up).wait_send()

            return carry

        lax.fori_loop(0, self.steps, one, 0)

def gather_scratch(layers, cols):
    return [
        pltpu.VMEM((2, 2, 16, cols), jnp.bfloat16),
        dma((2,)),
        dma((2, 2, layers, 2)),
        dma((2, layers, 2)),
        dma((2, layers, 2)),
        dma((2, layers, 2)),
        dma((2, layers, 2)),
    ]


class RowGather:
    def __init__(self, layers, short, shard, whole, here, local, sz, sx, sy, sfx, sfy):
        self.short = short
        self.layers, self.shard, self.whole, self.here = layers, shard, whole, here
        self.local, self.sz, self.sx, self.sy, self.sfx, self.sfy = local, sz, sx, sy, sfx, sfy
        self.rank, self.z, self.y, self.x = chip_place(layers)
        self.x_chip = self.rank + 1 - 2 * self.x
        self.y_chip = self.rank + 2 - 4 * self.y

    def take(self):
        return pltpu.make_async_copy(self.shard, self.here, self.local.at[0])

    def put(self):
        place = self.whole.at[self.z, self.y, self.x]
        return pltpu.make_async_copy(self.here, place, self.local.at[1])

    def source(self, layer, chunk, own, colours=slice(None)):
        if own:
            return self.shard.at[colours, chunk]
        return self.whole.at[layer, self.y, self.x, colours, chunk]

    def along_z(self, layer, chunk, up, own=False):
        return pltpu.make_async_remote_copy(
            src_ref=self.source(layer, chunk, own),
            dst_ref=self.whole.at[layer, self.y, self.x, :, chunk],
            send_sem=self.sz.at[0, int(up), layer, chunk],
            recv_sem=self.sz.at[1, int(up), layer, chunk],
            **to_chip(self.rank + (4 if up else -4)),
        )

    def in_plane(self, layer, chunk, along_x, own=False):
        sems = self.sx if along_x else self.sy
        colours = slice(None)
        if self.short:
            colours = 0 if along_x else 1
        return pltpu.make_async_remote_copy(
            src_ref=self.source(layer, chunk, own, colours),
            dst_ref=self.whole.at[layer, self.y, self.x, colours, chunk],
            send_sem=sems.at[0, layer, chunk],
            recv_sem=sems.at[1, layer, chunk],
            **to_chip(self.x_chip if along_x else self.y_chip),
        )

    def onward(self, layer, chunk, along_x):
        if along_x:
            place = (layer, 1 - self.y, self.x, 1, chunk)
            sems, chip = self.sfx, self.x_chip
        else:
            place = (layer, self.y, 1 - self.x, 0, chunk)
            sems, chip = self.sfy, self.y_chip
        return pltpu.make_async_remote_copy(
            src_ref=self.whole.at[place],
            dst_ref=self.whole.at[place],
            send_sem=sems.at[0, layer, chunk],
            recv_sem=sems.at[1, layer, chunk],
            **to_chip(chip),
        )

    def begin(self):
        self.take().start()

    def send_own(self):
        for chunk in range(2):

            @pl.when(self.z < self.layers - 1)
            def _():
                self.along_z(self.z, chunk, True, own=True).start()

            @pl.when(self.z > 0)
            def _():
                self.along_z(self.z, chunk, False, own=True).start()

            for along_x in (True, False):
                self.in_plane(self.z, chunk, along_x, own=True).start()
        self.take().wait()
        self.put().start()

    def pass_on(self, m):
        far, chunk = m // 2, m % 2
        for up in (True, False):
            layer = self.z - far if up else self.z + far
            near = (layer >= 0) if up else (layer < self.layers)

            @pl.when((far > 0) & near)
            def _():
                self.along_z(layer, chunk, up).wait_recv()

                @pl.when((self.z < self.layers - 1) if up else (self.z > 0))
                def _():
                    self.along_z(layer, chunk, up).start()

                for along_x in (True, False):
                    self.in_plane(layer, chunk, along_x).start()

    def turn(self, m):
        far, chunk = m // 2, m % 2
        for up in (True, False):
            layer = self.z - far if up else self.z + far
            near = (layer >= 0) if up else ((layer < self.layers) & (far > 0))

            @pl.when(near)
            def _():
                for along_x in (True, False):
                    self.in_plane(layer, chunk, along_x).wait_recv()
                    self.onward(layer, chunk, not along_x).start()

    def step(self, m):
        @pl.when(m + 2 < 2 * self.layers)
        def _():
            self.pass_on(m + 2)

        if not self.short:
            self.turn(m)

    def finish(self):
        self.put().wait()

        def one(n, carry):
            layer, chunk = n // 2, n % 2
            for along_x in (True, False):
                if self.short:
                    self.in_plane(layer, chunk, along_x).wait_recv()
                else:
                    self.onward(layer, chunk, along_x).wait()
                self.in_plane(layer, chunk, along_x).wait_send()

            @pl.when((self.z < self.layers - 1) & (layer <= self.z))
            def _():
                self.along_z(layer, chunk, True).wait_send()

            @pl.when((self.z > 0) & (layer >= self.z))
            def _():
                self.along_z(layer, chunk, False).wait_send()

            return carry

        lax.fori_loop(0, 2 * self.layers, one, 0)

def attend_forward_kernel(
    score_scale,
    layers,
    qkv_ref,
    bias_ref,
    cot_ref,
    shard_ref,
    feed_ref,
    kept_ref,
    low_ref,
    full_ref,
    total_ref,
    cot_out,
    whole_ref,
    feed_whole,
    came,
    landed,
    low_s,
    cot_land,
    q_s,
    k_s,
    v_s,
    bias_s,
    score_s,
    in_sem,
    out_send,
    out_recv,
    cot_z,
    cot_core,
    *gather_refs,
):
    blocks = bias_s.shape[1]
    sources = qkv_ref.shape[0]
    head = k_s.shape[1]
    half = len(gather_refs) // 2
    gathers = (
        RowGather(layers, True, feed_ref, feed_whole, *gather_refs[half:]),
        RowGather(layers, False, shard_ref, whole_ref, *gather_refs[:half]),
    )
    rank, z, y, x = chip_place(layers)
    spot = 2 * y + x
    peers = peers_of(rank, y, x)
    heads = PlaneSwap(layers, qkv_ref, came, in_sem)
    cot = Column(layers, cot_ref, cot_land, cot_z, cot_core)
    for gather in gathers:
        gather.begin()
    greet(layers)
    heads.start()
    for gather in gathers:
        gather.send_own()
    cot.start()

    def make_bias(n, carry):
        row = jnp.broadcast_to(bias_ref[pl.ds(n, 1), :], (tile, 2 * tile))
        turned = pltpu.roll(row, tile + 1, 1, stride=1, stride_axis=0)
        bias_s[n // blocks, n % blocks] = turned[:, :tile]
        return carry

    lax.fori_loop(0, 2 * blocks, make_bias, 0)
    heads.arrive()
    unpack_pair(came, q_s, k_s, v_s, score_scale)
    kept_ref[...] = came[...]

    def row_block(turn, carry):
        i = blocks - 1 - turn
        at = pl.ds(pl.multiple_of(i * tile, tile), tile)
        found = []
        for h in range(2):
            query = q_s[h, at, :]

            def score_step(j, top):
                key = k_s[pl.ds(pl.multiple_of(j * tile, tile), tile), :]
                score = dot_t(query, key) + bias_s[h, i - j]
                score_s[j] = score
                return jnp.maximum(top, jnp.maximum(score[:, :128], score[:, 128:]))

            top = lax.fori_loop(
                0, i + 1, score_step, jnp.full((tile, 128), masked_score, jnp.float32)
            )
            top = jnp.max(top, axis=1, keepdims=True)

            def share_step(j, state):
                total, summed = state
                share = jnp.exp(score_s[j] - top)
                value = v_s[pl.ds(pl.multiple_of(j * tile, tile), tile), :]
                summed = summed + jnp.dot(
                    share.astype(jnp.bfloat16), value, preferred_element_type=jnp.float32
                )
                return (total + share[:, :128] + share[:, 128:], summed)

            total, summed = lax.fori_loop(
                0,
                i + 1,
                share_step,
                (jnp.zeros((tile, 128), jnp.float32), jnp.zeros((tile, head), jnp.float32)),
            )
            total = jnp.sum(total, axis=1, keepdims=True)
            found.append(summed / total)
            log_total = jnp.broadcast_to(top + jnp.log(total), (tile, 128))
            total_ref[pl.ds(h * blocks + i, 1), :] = jnp.transpose(log_total)[0:1, :]
        both = jnp.concatenate(found, axis=1)
        full_ref[at, :] = both
        both = both.astype(jnp.bfloat16)
        for part in range(tile // 128):
            block = i * (tile // 128) + part
            low_s[block] = both[part * 128 : (part + 1) * 128]

        for gather in gathers:
            gather.step(turn)
        for part in range(tile // 128):
            block = i * (tile // 128) + part

            @pl.when(block % sources == spot)
            def _():
                landed[spot, block // sources] = low_s[block]

            @pl.when(block % sources != spot)
            def _():
                hand_back(block).start()

        return carry

    def hand_back(block):
        return pltpu.make_async_remote_copy(
            src_ref=low_s.at[block],
            dst_ref=landed.at[spot, block // sources],
            send_sem=out_send.at[block],
            recv_sem=out_recv.at[spot, block // sources],
            **to_chip(rank - spot + block % sources),
        )

    lax.fori_loop(0, blocks // 2, row_block, 0)
    cot.arrive()
    lax.fori_loop(blocks // 2, blocks, row_block, 0)
    for o in range(3):
        chip, there = peers[o]
        for turn in range(layers):
            pltpu.make_async_remote_copy(
                src_ref=low_s.at[0],
                dst_ref=landed.at[there, turn],
                send_sem=out_send.at[0],
                recv_sem=out_recv.at[there, turn],
                **to_chip(chip),
            ).wait_recv()
    for source in range(sources):
        for turn in range(layers):
            low_ref[turn * 128 : (turn + 1) * 128, source * 128 : (source + 1) * 128] = landed[
                source, turn
            ]
    heads.finish()
    cot.finish()
    cot_out[...] = cot_land[...]
    for block in range(sources * layers):

        @pl.when(block % sources != spot)
        def _():
            hand_back(block).wait_send()

    for gather in gathers:
        gather.finish()


def attend_forward(scale, layers, qkv, bias, cotangent, shard, feed_shard):
    f32, bf16 = jnp.float32, jnp.bfloat16
    sources, rows, wide = qkv.shape
    head = wide // 4
    length = sources * rows
    blocks = length // tile
    cols, feed_cols = shard.shape[1], feed_shard.shape[1]
    chips = (layers, 2, 2, 2, 2, 16)
    cot_shape = (layers, 2, *cotangent.shape[1:])
    vmem, anywhere = pl.BlockSpec(memory_space=pltpu.VMEM), pl.BlockSpec(memory_space=pl.ANY)
    kept, low, full, total, cot, whole, feed_whole = pl.pallas_call(
        functools.partial(attend_forward_kernel, scale, layers),
        name="attend_forward",
        out_shape=(
            jax.ShapeDtypeStruct(qkv.shape, bf16),
            jax.ShapeDtypeStruct((rows, sources * 2 * head), bf16),
            jax.ShapeDtypeStruct((length, 2 * head), f32),
            jax.ShapeDtypeStruct((2 * blocks, tile), f32),
            jax.ShapeDtypeStruct(cot_shape, bf16),
            jax.ShapeDtypeStruct((*chips, cols), bf16),
            jax.ShapeDtypeStruct((*chips, feed_cols), bf16),
        ),
        in_specs=[vmem, vmem, vmem, anywhere, anywhere],
        out_specs=(vmem, vmem, vmem, vmem, vmem, anywhere, anywhere),
        scratch_shapes=[
            pltpu.VMEM(qkv.shape, bf16),
            pltpu.VMEM((sources, layers, 128, 2 * head), bf16),
            pltpu.VMEM((length // 128, 128, 2 * head), bf16),
            pltpu.VMEM(cot_shape, bf16),
            pltpu.VMEM((2, length, head), bf16),
            pltpu.VMEM((length, head), bf16),
            pltpu.VMEM((length, head), bf16),
            pltpu.VMEM((2, blocks, tile, tile), f32),
            pltpu.VMEM((blocks, tile, tile), f32),
            dma((2, 3)),
            dma((length // 128,)),
            dma((sources, layers)),
            dma((2, layers)),
            dma((2, layers)),
            *gather_scratch(layers, cols),
            *gather_scratch(layers, feed_cols),
        ],
        compiler_params=pltpu.CompilerParams(
            collective_id=6, has_side_effects=True, vmem_limit_bytes=56 << 20
        ),
    )(
        qkv,
        bias,
        cotangent,
        shard.reshape(2, 2, 16, cols),
        feed_shard.reshape(2, 2, 16, feed_cols),
    )
    return kept, low, full, total, cot, whole.reshape(layers * 256, cols), feed_whole

def attend_backward_kernel(
    score_scale,
    layers,
    kept_ref,
    ctx_ref,
    full_ref,
    total_ref,
    bias_ref,
    kv_ref,
    rows_ref,
    grads_ref,
    feed_ref,
    got_x,
    got_y,
    out_ref,
    sums_ref,
    kv_out,
    rows_out,
    out_grad,
    cq_grad,
    ck_grad,
    cv_grad,
    co_grad,
    gate_grad,
    up_grad,
    down_grad,
    ctx_land,
    kv_land,
    rows_land,
    out_s,
    out_land,
    q_s,
    k_s,
    v_s,
    g_s,
    bias_s,
    sum_s,
    delta_s,
    dq_s,
    dk_s,
    dv_s,
    ctx_sem,
    kv_sem,
    rows_z,
    out_sem,
    sum_a,
    sum_b,
    *sum_refs,
):
    blocks = bias_s.shape[1]
    sources, rows, _ = kept_ref.shape
    head = k_s.shape[1]
    half = len(sum_refs) // 2
    sums = (
        GradSum(layers, feed_ref, (got_x, got_y), sum_b, *sum_refs[half:]),
        GradSum(layers, grads_ref, (), sum_a, *sum_refs[:half]),
    )
    context = PlaneSwap(layers, ctx_ref, ctx_land, ctx_sem)
    cross = PlaneSwap(layers, kv_ref, kv_land, kv_sem)
    ended = Column(layers, rows_ref, rows_land, rows_z)
    back = PlaneSwap(layers, out_s, out_land, out_sem)
    for grads in sums:
        grads.start()
    greet(layers)
    context.start()
    for grads in sums:
        grads.send_first(0)
    cross.start()
    ended.start()
    unpack_pair(kept_ref, q_s, k_s, v_s, score_scale)

    def make_bias(n, carry):
        row = jnp.broadcast_to(bias_ref[pl.ds(n, 1), :], (tile, 2 * tile))
        turned = pltpu.roll(row, 0, 1, stride=1, stride_axis=0)
        bias_s[n // blocks, n % blocks] = turned[:, tile:]
        return carry

    lax.fori_loop(0, 2 * blocks, make_bias, 0)
    sum_s[...] = jnp.zeros_like(sum_s)
    dq_s[...] = jnp.zeros_like(dq_s)
    dk_s[...] = jnp.zeros_like(dk_s)
    dv_s[...] = jnp.zeros_like(dv_s)
    context.arrive()
    for block in range(rows // 128 * sources):
        source, turn = block % sources, block // sources
        part = ctx_land[source, turn * 128 : (turn + 1) * 128, :]
        at = slice(block * 128, (block + 1) * 128)
        g_s[0, at, :] = part[:, :head]
        g_s[1, at, :] = part[:, head:]

    def make_delta(i, carry):
        at = pl.ds(pl.multiple_of(i * tile, tile), tile)
        for h in range(2):
            product = g_s[h, at, :].astype(jnp.float32) * full_ref[at, h * head : (h + 1) * head]
            column = jnp.broadcast_to(jnp.sum(product, axis=1, keepdims=True), (tile, 128))
            delta_s[pl.ds(h * blocks + i, 1), :] = jnp.transpose(column)[0:1, :]
        return carry

    lax.fori_loop(0, blocks, make_delta, 0)

    def one_tile(n, carry):
        line, at = n // blocks, n % blocks
        first = at < blocks - line
        d = jnp.where(first, line, blocks - line)
        i = jnp.where(first, at + line, at)
        at_q = pl.ds(pl.multiple_of(i * tile, tile), tile)
        at_k = pl.ds(pl.multiple_of((i - d) * tile, tile), tile)
        key, value = k_s[at_k, :], v_s[at_k, :]
        for h in range(2):
            query, grad = q_s[h, at_q, :], g_s[h, at_q, :]
            score = dot_t(key, query) + bias_s[h, d]
            share = jnp.exp(score - total_ref[pl.ds(h * blocks + i, 1), :])
            pull = dot_t(value, grad)
            grad_score = share * (pull - delta_s[pl.ds(h * blocks + i, 1), :])
            sum_s[h, d] += grad_score
            share_low = share.astype(jnp.bfloat16)
            grad_low = grad_score.astype(jnp.bfloat16)
            dv_s[at_k, :] += jnp.dot(share_low, grad, preferred_element_type=jnp.float32)
            dk_s[at_k, :] += jnp.dot(grad_low, query, preferred_element_type=jnp.float32)
            dq_s[h, at_q, :] += dot_first(grad_low, key)
        return carry

    tiles = blocks * (blocks + 1) // 2
    busy = 6

    def work(m, carry):
        for grads in sums:
            grads.send_first(m)
        low = (m - 1) * tiles // busy
        lax.fori_loop(low, m * tiles // busy, one_tile, 0)
        for grads in sums:
            grads.advance(m)
        return carry

    lax.fori_loop(1, 1 + busy, work, 0)

    for block in range(rows // 128 * sources):
        source, turn = block % sources, block // sources
        at = slice(block * 128, (block + 1) * 128)
        out_s[source, turn * 128 : (turn + 1) * 128, :] = jnp.concatenate(
            [dq_s[0, at, :] * score_scale, dq_s[1, at, :] * score_scale, dk_s[at, :], dv_s[at, :]],
            axis=1,
        ).astype(jnp.bfloat16)
    back.start()

    row_at = lax.broadcasted_iota(jnp.int32, (tile, tile), 0)
    col_at = lax.broadcasted_iota(jnp.int32, (tile, tile), 1)
    turn_rows = (row_at + col_at == tile - 1).astype(jnp.float32)

    def make_sums(n, carry):
        turned = jnp.dot(
            turn_rows,
            sum_s[n // blocks, n % blocks],
            precision=highest,
            preferred_element_type=jnp.float32,
        )
        wide = jnp.concatenate([turned, jnp.zeros_like(turned)], axis=1)
        wide = pltpu.roll(wide, 0, 1, stride=1, stride_axis=0)
        sums_ref[pl.ds(n, 1), :] = jnp.sum(wide, axis=0, keepdims=True)
        return carry

    lax.fori_loop(0, 2 * blocks, make_sums, 0)
    cross.arrive()
    both = kv_land[0].astype(jnp.float32)
    for source in range(1, sources):
        both = both + kv_land[source].astype(jnp.float32)
    kv_out[...] = both.astype(jnp.bfloat16)
    ended.arrive()
    rows_out[...] = rows_land[...]

    def rest(m, carry):
        for grads in sums:
            grads.send_first(m)
        for grads in sums:
            grads.advance(m)
        return carry

    lax.fori_loop(1 + busy, sum_steps(layers), rest, 0)
    back.arrive()
    wide = 4 * head
    for source in range(sources):
        out_ref[:, source * wide : (source + 1) * wide] = out_land[source]
    whole = sum_a[...].reshape(64, sum_a.shape[-1])
    at = 0
    for ref, turned in (
        (out_grad, True),
        (cq_grad, False),
        (ck_grad, False),
        (cv_grad, False),
        (co_grad, True),
    ):
        count = ref.shape[0] if turned else ref.shape[1]
        part = whole[:, at : at + count]
        ref[...] = jnp.transpose(part) if turned else part
        at += count
    whole = sum_b[...].reshape(64, sum_b.shape[-1])
    feed = gate_grad.shape[1]
    for at in range(0, feed, tile):
        units = min(tile, feed - at)
        gate_grad[:, at : at + units] = whole[:, 2 * at : 2 * at + units]
        up_grad[:, at : at + units] = whole[:, 2 * at + units : 2 * at + 2 * units]
    down_grad[...] = jnp.transpose(whole[:, 2 * feed :])
    context.finish()
    cross.finish()
    ended.finish()
    back.finish()
    for grads in sums:
        grads.finish()


def attend_backward(
    scale, layers, feed, kept, ctx_grad, full, total, bias, kv, layer_rows, grads, feed_grads, got
):
    f32, bf16 = jnp.float32, jnp.bfloat16
    sources, rows, wide = kept.shape
    head = wide // 4
    length = sources * rows
    blocks = length // tile
    cols, feed_cols = grads.shape[1], feed_grads.shape[1]
    chips = (layers, 2, 2, 2, 2, 16)
    vmem, anywhere = pl.BlockSpec(memory_space=pltpu.VMEM), pl.BlockSpec(memory_space=pl.ANY)
    half = cols // 4
    return pl.pallas_call(
        functools.partial(attend_backward_kernel, scale, layers),
        name="attend_backward",
        out_shape=(
            jax.ShapeDtypeStruct((rows, sources * wide), bf16),
            jax.ShapeDtypeStruct((2 * blocks, 2 * tile), f32),
            jax.ShapeDtypeStruct(kv.shape[1:], bf16),
            jax.ShapeDtypeStruct(layer_rows.shape, bf16),
            jax.ShapeDtypeStruct((half, 64), f32),
            jax.ShapeDtypeStruct((64, half), f32),
            jax.ShapeDtypeStruct((64, half // 2), f32),
            jax.ShapeDtypeStruct((64, half // 2), f32),
            jax.ShapeDtypeStruct((half, 64), f32),
            jax.ShapeDtypeStruct((64, feed), f32),
            jax.ShapeDtypeStruct((64, feed), f32),
            jax.ShapeDtypeStruct((feed, 64), f32),
        ),
        in_specs=[vmem] * 7 + [anywhere] * 4,
        out_specs=(vmem,) * 12,
        scratch_shapes=[
            pltpu.VMEM(ctx_grad.shape, bf16),
            pltpu.VMEM(kv.shape, bf16),
            pltpu.VMEM(layer_rows.shape, bf16),
            pltpu.VMEM(kept.shape, bf16),
            pltpu.VMEM(kept.shape, bf16),
            pltpu.VMEM((2, length, head), bf16),
            pltpu.VMEM((length, head), bf16),
            pltpu.VMEM((length, head), bf16),
            pltpu.VMEM((2, length, head), bf16),
            pltpu.VMEM((2, blocks, tile, tile), f32),
            pltpu.VMEM((2, blocks, tile, tile), f32),
            pltpu.VMEM((2 * blocks, tile), f32),
            pltpu.VMEM((2, length, head), f32),
            pltpu.VMEM((length, head), f32),
            pltpu.VMEM((length, head), f32),
            dma((2, 3)),
            dma((2, 3)),
            dma((2, layers)),
            dma((2, 3)),
            pltpu.VMEM((2, 2, 16, cols), f32),
            pltpu.VMEM((2, 2, 16, feed_cols), f32),
            *sum_scratch(layers, cols),
            *sum_scratch(layers, feed_cols),
        ],
        compiler_params=pltpu.CompilerParams(
            collective_id=8, has_side_effects=True, vmem_limit_bytes=62 << 20
        ),
    )(
        kept,
        ctx_grad,
        full,
        total,
        bias,
        kv,
        layer_rows,
        grads.reshape(*chips, cols),
        feed_grads.reshape(*chips, feed_cols),
        *got,
    )

def norm_scale(v):
    return lax.rsqrt(jnp.mean(v * v, axis=-1, keepdims=True) + norm_eps)


def norm_pull(v, gain, grad):
    scale = norm_scale(v)
    turned = v * scale
    pulled = grad * gain
    mean = jnp.mean(pulled * turned, axis=-1, keepdims=True)
    return scale * (pulled - turned * mean), jnp.sum(grad * turned, axis=0, keepdims=True)


def middle_kernel(
    score_scale,
    layers,
    feed,
    ctx_ref,
    x_ref,
    cot_ref,
    enc_ref,
    wa_ref,
    gains_ref,
    wf_ref,
    layer_out,
    grad_out,
    gctx_out,
    kv_out,
    ga_out,
    gain_out,
    gb_out,
    got_x,
    got_y,
    w_s,
    gb_s,
    after_self,
    after_cross,
    nc_s,
    nf_s,
    nft_s,
    cott_s,
    down_s,
    dx_s,
    send_s,
    land_s,
    half_s,
    q_s,
    k_s,
    v_s,
    g_s,
    pair_s,
    cc_s,
    dq_s,
    dk_s,
    low_s,
    w_load,
    w_send,
    w_recv,
    g_send,
    g_recv,
    g_store,
    swap_sem,
):
    f32, bf16 = jnp.float32, jnp.bfloat16
    rank, z, y, x = chip_place(layers)
    core = lax.axis_index(tensor_axis)
    x_chip, y_chip = rank + 1 - 2 * x, rank + 2 - 4 * y
    rows, width = x_ref.shape
    heads, _, head = q_s.shape
    kv_heads = heads // 2
    wide = heads * head
    enc_rows = enc_ref.shape[0]
    block = send_s.shape[2]
    chunks = rows // block
    at_out, at_cq, at_ck = 0, wide, 2 * wide
    at_cv, at_co = at_ck + wide // 2, at_ck + wide
    row_chip = 64

    def row_of(layer, at_y, at_x, colour=0):
        return pl.multiple_of(((layer * 2 + at_y) * 2 + at_x) * row_chip + 32 * colour, 32)

    def loads():
        copies = []
        for layer in range(layers):
            for n, (start, count) in enumerate(
                (
                    (row_of(layer, y, x), 64),
                    (row_of(layer, y, 1 - x, 0), 32),
                    (row_of(layer, 1 - y, x, 1), 32),
                )
            ):
                at = pl.ds(start, count)
                copies.append(
                    pltpu.make_async_copy(wf_ref.at[at], w_s.at[at], w_load.at[layer, n])
                )
        return copies

    def weights_hop(layer, along_y, which):
        spot = row_of(layer, y, which, 0) if along_y else row_of(layer, which, x, 1)
        at = pl.ds(spot, 32)
        return pltpu.make_async_remote_copy(
            src_ref=wf_ref.at[at],
            dst_ref=w_s.at[at],
            send_sem=w_send.at[int(along_y), layer, which],
            recv_sem=w_recv.at[int(along_y), layer, which],
            **to_chip(y_chip if along_y else x_chip),
        )

    def grads_hop(layer, along_y, which):
        spot = row_of(layer, 1 - y, which, 1) if along_y else row_of(layer, which, 1 - x, 0)
        return pltpu.make_async_remote_copy(
            src_ref=gb_s.at[pl.ds(spot, 32)],
            dst_ref=(got_y if along_y else got_x).at[layer, which],
            send_sem=g_send.at[int(along_y), layer, which],
            recv_sem=g_recv.at[int(along_y), layer, which],
            **to_chip(y_chip if along_y else x_chip),
        )

    hops = [(layer, a, w) for layer in range(layers) for w in range(2) for a in (True, False)]
    greet(layers)
    for hop in hops:
        weights_hop(*hop).start()
    for copy in loads():
        copy.start()

    def swap(n, chunk):
        half = n == 3
        return pltpu.make_async_remote_copy(
            src_ref=half_s.at[0] if half else send_s.at[slots[n], chunk],
            dst_ref=half_s.at[1] if half else land_s.at[slots[n], chunk],
            send_sem=swap_sem.at[0, n, chunk],
            recv_sem=swap_sem.at[1, n, chunk],
            **to_core(1 - core),
        )

    slots = (0, 1, 0, None, 1)

    def span(chunk):
        return pl.ds(pl.multiple_of(chunk * block, block), block)

    def send_parts(n, part_of):
        def one(chunk, carry):
            send_s[slots[n], chunk] = part_of(span(chunk)).astype(bf16)
            swap(n, chunk).start()
            return carry

        lax.fori_loop(0, chunks, one, 0)

    def take_parts(n, use):
        def one(chunk, carry):
            swap(n, chunk).wait()
            both = send_s[slots[n], chunk].astype(f32) + land_s[slots[n], chunk].astype(f32)
            use(span(chunk), both)
            return carry

        lax.fori_loop(0, chunks, one, 0)

    cross_gain, feed_gain = gains_ref[0:1, :], gains_ref[1:2, :]

    send_parts(0, lambda at: dot_t(ctx_ref[at, :], wa_ref[:, at_out : at_out + wide]))
    key_value = matmul(enc_ref[...], wa_ref[:, at_ck : at_ck + wide]).astype(bf16)
    for kv in range(kv_heads):
        k_s[kv] = key_value[:, kv * head : (kv + 1) * head]
        v_s[kv] = key_value[:, wide // 2 + kv * head : wide // 2 + (kv + 1) * head]
    cott_s[...] = jnp.transpose(cot_ref[...])

    def enter_cross(at, both):
        v = x_ref[at, :].astype(f32) + both
        after_self[at, :] = v
        nc_s[at, :] = (v * norm_scale(v) * cross_gain).astype(bf16)
        query = matmul(nc_s[at, :], wa_ref[:, at_cq : at_cq + wide]).astype(bf16)
        for h in range(heads):
            q_s[h, at, :] = (query[:, h * head : (h + 1) * head] * score_scale).astype(bf16)

    take_parts(0, enter_cross)

    def attend(kv, carry):
        key, value = k_s[kv], v_s[kv]
        for chunk in range(chunks):
            at = slice(chunk * block, (chunk + 1) * block)
            found = []
            for h in range(2):
                score = dot_t(q_s[2 * kv + h, at, :], key)
                share = jnp.exp(score - jnp.max(score, axis=1, keepdims=True))
                total = jnp.sum(share, axis=1, keepdims=True)
                found.append(matmul(share.astype(bf16), value) / total)
            pair_s[kv, at, :] = jnp.concatenate(found, axis=1).astype(bf16)
        return carry

    lax.fori_loop(0, kv_heads, attend, 0)
    for kv in range(kv_heads):
        cc_s[:, 2 * kv * head : 2 * (kv + 1) * head] = pair_s[kv]
    send_parts(1, lambda at: dot_t(cc_s[at, :], wa_ref[:, at_co : at_co + wide]))

    def enter_feed(at, both):
        v = after_self[at, :] + both
        after_cross[at, :] = v
        nf_s[at, :] = (v * norm_scale(v) * feed_gain).astype(bf16)

    take_parts(1, enter_feed)
    nft_s[...] = jnp.transpose(nf_s[...])
    for copy in loads():
        copy.wait()
    for hop in hops:
        weights_hop(*hop).wait_recv()

    down_s[...] = jnp.zeros_like(down_s)
    dx_s[...] = jnp.zeros_like(dx_s)
    slope = math.sqrt(2.0 / math.pi)

    def feed_block(at_gu, at_down, units):
        pair = w_s[:, pl.ds(at_gu, 2 * units)]
        down = w_s[:, pl.ds(at_down, units)]
        both = matmul(nf_s[...], pair)
        gate, up = both[:, :units], both[:, units:]
        square = gate * gate
        bend = jnp.tanh(slope * (gate + 0.044715 * square * gate))
        bent = 0.5 * gate * (1.0 + bend)
        pull = 0.5 * (1.0 + bend) + 0.5 * gate * (1.0 - bend * bend) * slope * (
            1.0 + 3.0 * 0.044715 * square
        )
        hidden = (bent * up).astype(bf16)
        down_s[...] += dot_t(hidden, down)
        grad = matmul(cot_ref[...], down)
        grads = jnp.concatenate([grad * up * pull, grad * bent], axis=1).astype(bf16)
        dx_s[...] += dot_t(grads, pair)
        gb_s[:, pl.ds(at_gu, 2 * units)] = matmul(nft_s[...], grads).astype(bf16)
        gb_s[:, pl.ds(at_down, units)] = matmul(cott_s[...], hidden).astype(bf16)

    full_blocks = feed // tile

    def one_block(n, carry):
        feed_block(
            pl.multiple_of(n * 2 * tile, 2 * tile),
            pl.multiple_of(2 * feed + n * tile, 128),
            tile,
        )
        return carry

    lax.fori_loop(0, full_blocks, one_block, 0)
    if feed % tile:
        feed_block(full_blocks * 2 * tile, 2 * feed + full_blocks * tile, feed % tile)

    send_parts(2, lambda at: dx_s[at, :])
    store = pltpu.make_async_copy(gb_s, gb_out, g_store.at[0])
    store.start()
    for hop in hops:
        grads_hop(*hop).start()
    own = rows // (2 * layers)

    def halves(ref, which):
        return [ref[pl.ds((2 * layer + which) * own, own), :] for layer in range(layers)]

    low = jnp.concatenate(halves(down_s, 1 - core), axis=0).astype(bf16)
    half_s[0] = low
    swap(3, 0).start()

    def leave_feed(at, both):
        grad, gain = norm_pull(after_cross[at, :], feed_gain, both)
        dx_s[at, :] = cot_ref[at, :].astype(f32) + grad
        low = dx_s[at, :].astype(bf16)
        low_s[at, :] = low
        gain_out[1:2, :] += gain
        context = matmul(low, wa_ref[:, at_co : at_co + wide]).astype(bf16)
        for h in range(heads):
            g_s[h, at, :] = context[:, h * head : (h + 1) * head]

    gain_out[...] = jnp.zeros_like(gain_out)
    take_parts(2, leave_feed)
    swap(3, 0).wait()
    mine = halves(after_cross, core)
    down = halves(down_s, core)
    for layer in range(layers):
        came = half_s[1, layer * own : (layer + 1) * own, :].astype(f32)
        layer_out[layer] = (mine[layer] + (down[layer].astype(bf16).astype(f32) + came)).astype(bf16)

    ga_out[:, at_co : at_co + wide] = dot_first(low_s[...], cc_s[...]).astype(bf16)

    def attend_back(kv, carry):
        key, value = k_s[kv], v_s[kv]
        key_grad = jnp.zeros((enc_rows, head), f32)
        value_grad = jnp.zeros((enc_rows, head), f32)
        for chunk in range(chunks):
            at = slice(chunk * block, (chunk + 1) * block)
            found = []
            for h in range(2):
                query, grad = q_s[2 * kv + h, at, :], g_s[2 * kv + h, at, :]
                score = dot_t(key, query)
                share = jnp.exp(score - jnp.max(score, axis=0, keepdims=True))
                share = share * (1.0 / jnp.sum(share, axis=0, keepdims=True))
                pull = dot_t(value, grad)
                delta = jnp.sum(share * pull, axis=0, keepdims=True)
                grad_low = (share * (pull - delta)).astype(bf16)
                found.append(dot_first(grad_low, key) * score_scale)
                key_grad = key_grad + matmul(grad_low, query)
                value_grad = value_grad + matmul(share.astype(bf16), grad)
            pair_s[kv, at, :] = jnp.concatenate(found, axis=1).astype(bf16)
        dk_s[0, kv] = key_grad.astype(bf16)
        dk_s[1, kv] = value_grad.astype(bf16)
        return carry

    lax.fori_loop(0, kv_heads, attend_back, 0)
    for kv in range(kv_heads):
        dq_s[:, 2 * kv * head : 2 * (kv + 1) * head] = pair_s[kv]
    send_parts(4, lambda at: dot_t(dq_s[at, :], wa_ref[:, at_cq : at_cq + wide]))
    for n in range(2):
        kv_out[:, n * wide // 2 : (n + 1) * wide // 2] = jnp.concatenate(
            [dk_s[n, kv] for kv in range(kv_heads)], axis=1
        )
    ga_out[:, at_cq : at_cq + wide] = dot_first(nc_s[...], dq_s[...]).astype(bf16)
    ga_out[:, at_ck : at_ck + wide] = dot_first(enc_ref[...], kv_out[...]).astype(bf16)

    def leave_cross(at, both):
        grad, gain = norm_pull(after_self[at, :], cross_gain, both)
        dx_s[at, :] += grad
        low = dx_s[at, :].astype(bf16)
        low_s[at, :] = low
        gain_out[0:1, :] += gain
        context = matmul(low, wa_ref[:, at_out : at_out + wide]).astype(bf16)
        for q in range(4):
            gctx_out[q, at, :] = context[:, q * wide // 4 : (q + 1) * wide // 4]

    take_parts(4, leave_cross)
    ga_out[:, at_out : at_out + wide] = dot_first(low_s[...], ctx_ref[...]).astype(bf16)
    mine = halves(dx_s, core)
    for layer in range(layers):
        grad_out[layer] = mine[layer]

    store.wait()
    for hop in hops:
        weights_hop(*hop).wait_send()
        grads_hop(*hop).wait()


def middle(scale, layers, feed, context, x_low, cot, enc, weights, gains, feed_whole):
    f32, bf16 = jnp.float32, jnp.bfloat16
    rows, width = x_low.shape
    wide = context.shape[1]
    head = round(scale**-2)
    heads = wide // head
    own = rows // (2 * layers)
    cols = feed_whole.shape[1]
    block = rows // 2
    vmem, anywhere = pl.BlockSpec(memory_space=pltpu.VMEM), pl.BlockSpec(memory_space=pl.ANY)
    got = jax.ShapeDtypeStruct((layers, 2, 32, cols), bf16)
    return pl.pallas_call(
        functools.partial(middle_kernel, scale, layers, feed),
        name="middle",
        out_shape=(
            jax.ShapeDtypeStruct((layers, own, width), bf16),
            jax.ShapeDtypeStruct((layers, own, width), f32),
            jax.ShapeDtypeStruct((4, rows, wide // 4), bf16),
            jax.ShapeDtypeStruct((enc.shape[0], wide), bf16),
            jax.ShapeDtypeStruct((width, weights.shape[1]), bf16),
            jax.ShapeDtypeStruct((2, width), f32),
            jax.ShapeDtypeStruct((width, cols), bf16),
            got,
            got,
        ),
        in_specs=[vmem] * 6 + [anywhere],
        out_specs=(vmem,) * 6 + (anywhere,) * 3,
        scratch_shapes=[
            pltpu.VMEM((width, cols), bf16),
            pltpu.VMEM((width, cols), bf16),
            pltpu.VMEM((rows, width), f32),
            pltpu.VMEM((rows, width), f32),
            pltpu.VMEM((rows, width), bf16),
            pltpu.VMEM((rows, width), bf16),
            pltpu.VMEM((width, rows), bf16),
            pltpu.VMEM((width, rows), bf16),
            pltpu.VMEM((rows, width), f32),
            pltpu.VMEM((rows, width), f32),
            pltpu.VMEM((2, 2, block, width), bf16),
            pltpu.VMEM((2, 2, block, width), bf16),
            pltpu.VMEM((2, rows // 2, width), bf16),
            pltpu.VMEM((heads, rows, head), bf16),
            pltpu.VMEM((heads // 2, enc.shape[0], head), bf16),
            pltpu.VMEM((heads // 2, enc.shape[0], head), bf16),
            pltpu.VMEM((heads, rows, head), bf16),
            pltpu.VMEM((heads // 2, rows, 2 * head), bf16),
            pltpu.VMEM((rows, wide), bf16),
            pltpu.VMEM((rows, wide), bf16),
            pltpu.VMEM((2, heads // 2, enc.shape[0], head), bf16),
            pltpu.VMEM((rows, width), bf16),
            dma((layers, 3)),
            dma((2, layers, 2)),
            dma((2, layers, 2)),
            dma((2, layers, 2)),
            dma((2, layers, 2)),
            dma((1,)),
            dma((2, 5, 2)),
        ],
        compiler_params=pltpu.CompilerParams(
            collective_id=9, has_side_effects=True, vmem_limit_bytes=67043328
        ),
    )(context, x_low, cot, enc, weights, gains, feed_whole)

def dot_t(left, right):
    return lax.dot_general(
        left, right, (((1,), (1,)), ((), ())), preferred_element_type=jnp.float32
    )


def dot_first(left, right):
    return lax.dot_general(
        left, right, (((0,), (0,)), ((), ())), preferred_element_type=jnp.float32
    )


def unpack_pair(qkv_ref, q_s, k_s, v_s, score_scale):
    sources, rows, _ = qkv_ref.shape
    blocks = rows // 128 * sources
    head = k_s.shape[1]
    for block in range(blocks):
        source, turn = block % sources, block // sources
        tile = qkv_ref[source, turn * 128 : (turn + 1) * 128, :]
        at = slice(block * 128, (block + 1) * 128)
        q_s[0, at, :] = (tile[:, :head] * score_scale).astype(jnp.bfloat16)
        q_s[1, at, :] = (tile[:, head : 2 * head] * score_scale).astype(jnp.bfloat16)
        k_s[at, :] = tile[:, 2 * head : 3 * head]
        v_s[at, :] = tile[:, 3 * head :]


def by_heads(
    inputs,
    encoder_out,
    out_cotangent,
    bucket_ids,
    position_table,
    self_gain,
    self_query,
    self_key,
    self_value,
    self_output,
    cross_gain,
    cross_query,
    cross_key,
    cross_value,
    cross_output,
    feed_gain,
    gate_weight,
    up_weight,
    down_weight,
):
    f32, bf16 = jnp.float32, jnp.bfloat16
    batches, own, width = inputs.shape
    enc_own = encoder_out.shape[1]
    length = bucket_ids.shape[0]
    heads_all, buckets = position_table.shape
    fsdp = lax.axis_size(fsdp_axis)
    plane = fsdp // batches
    rank, core = lax.axis_index(fsdp_axis), lax.axis_index(tensor_axis)
    head = self_query.shape[1] // (heads_all // 2)
    kv_local = self_key.shape[1] // head
    scale = head ** (-0.5)
    blocks = length // tile
    rows = batches * 2 * own
    enc_rows = batches * 2 * enc_own
    feed = gate_weight.shape[1]
    def by_kv(weight):
        return weight.reshape(weight.shape[0], kv_local, -1)

    self_in = jnp.concatenate([by_kv(self_query), by_kv(self_key), by_kv(self_value)], axis=2)
    self_in = self_in.reshape(self_in.shape[0], -1)
    rest_shard = jnp.concatenate(
        [self_output.T, cross_query, cross_key, cross_value, cross_output.T], axis=1
    )
    spans = [(at, min(at + tile, feed)) for at in range(0, feed, tile)]
    paired = [side[:, at:end] for at, end in spans for side in (gate_weight, up_weight)]
    feed_shard = jnp.concatenate([*paired, down_weight.T], axis=1)
    started, enc_all, in_full = open_rows(batches, inputs, encoder_out, self_in)
    x_low = started.reshape(rows, width)
    x_rows = x_low.astype(f32)
    enc_all = enc_all.reshape(-1, width)

    kv_index = core * kv_local + rank % plane
    table_here = lax.dynamic_slice_in_dim(position_table, 2 * kv_index, 2, 0)
    bucket_range = jnp.arange(buckets, dtype=jnp.int32)
    lower = jnp.sum((bucket_ids[None, :] < bucket_range[:, None]).astype(jnp.int32), axis=1)
    upper = jnp.concatenate([lower[1:], jnp.full((1,), length, jnp.int32)])
    offsets = (
        tile * jnp.arange(blocks, dtype=jnp.int32)[:, None]
        + jnp.arange(2 * tile, dtype=jnp.int32)[None, :]
    ).reshape(-1)

    def bias_of(offset):
        hit = (offset[None] >= lower[:, None]) & (offset[None] < upper[:, None])
        value = jnp.dot(table_here, hit.astype(f32), precision=highest)
        return jnp.where(offset[None] >= 0, value, masked_score).reshape(2 * blocks, 2 * tile)

    down_steps = (
        tile * jnp.arange(blocks, dtype=jnp.int32)[:, None]
        + (tile - 1)
        - jnp.arange(2 * tile, dtype=jnp.int32)[None, :]
    ).reshape(-1)
    bias_down = bias_of(down_steps)
    bias_up = bias_of(offsets - tile)

    def swap_add(partial):
        low = partial.astype(bf16)
        return low.astype(f32) + swap_cores(low).astype(f32)

    normed_self = norm_rows(x_rows, self_gain).astype(bf16)
    qkv = jnp.einsum(
        "rd,dkc->krc",
        normed_self,
        in_full.reshape(width, kv_local, -1),
        preferred_element_type=f32,
    ).astype(bf16)
    qkv_here, context_low, context_full, log_total, cot_low, rest_full, feed_full = attend_forward(
        scale, batches, qkv, bias_down, out_cotangent, rest_shard, feed_shard
    )
    layer_rows, grad_after_self, grad_context, cross_kv, grads, mid_gains, feed_grads, *feed_got = (
        middle(
            scale,
            batches,
            feed,
            context_low,
            x_low,
            cot_low.reshape(rows, width),
            enc_all,
            rest_full,
            jnp.stack([cross_gain, feed_gain]),
            feed_full.reshape(width, -1),
        )
    )
    feed_got = [came.reshape(batches, 2, 2, 16, -1) for came in feed_got]

    grad_qkv, diagonal_sums, kv_sum, layer_out, *most_grads = attend_backward(
        scale,
        batches,
        feed,
        qkv_here,
        grad_context,
        context_full,
        log_total,
        bias_up,
        cross_kv.reshape(plane, enc_rows, -1),
        layer_rows,
        grads,
        feed_grads,
        feed_got,
    )
    spread = offsets - (tile - 1)
    hit = ((spread[None] >= lower[:, None]) & (spread[None] < upper[:, None])).astype(f32)
    hit = jnp.transpose(hit.reshape(buckets, blocks, 2 * tile), (1, 0, 2))
    query_grad, key_grad, value_grad, input_grad, encoder_grad, table_sum, gain_sums = close_rows(
        batches,
        heads_all,
        grad_qkv,
        x_low,
        in_full,
        grad_after_self,
        kv_sum,
        self_gain[None],
        mid_gains,
        diagonal_sums,
        hit,
        rest_full,
    )
    out_grad, cq_grad, ck_grad, cv_grad, co_grad, gate_grad, up_grad, down_grad = most_grads
    return (
        layer_out,
        input_grad,
        encoder_grad,
        table_sum,
        gain_sums[0],
        query_grad,
        key_grad,
        value_grad,
        out_grad,
        gain_sums[1],
        cq_grad,
        ck_grad,
        cv_grad,
        co_grad,
        gain_sums[2],
        gate_grad,
        up_grad,
        down_grad,
    )


def on_either(*args):
    batches, kv_heads = args[0].shape[0], args[7].shape[1] * lax.axis_size(tensor_axis)
    head_size = args[6].shape[1] * lax.axis_size(tensor_axis) // args[4].shape[0]
    devices = lax.axis_size(fsdp_axis) * lax.axis_size(tensor_axis)
    if devices == batches * (kv_heads // head_size):
        return by_heads(*args)
    return on_device(*args)


def solution(mesh):
    placed = (
        P(None, (fsdp_axis, tensor_axis), None),
        P(None, (fsdp_axis, tensor_axis), None),
        P(None, (fsdp_axis, tensor_axis), None),
        P(),
        P(),
        P(),
        P(fsdp_axis, tensor_axis),
        P(fsdp_axis, tensor_axis),
        P(fsdp_axis, tensor_axis),
        P(tensor_axis, fsdp_axis),
        P(),
        P(fsdp_axis, tensor_axis),
        P(fsdp_axis, tensor_axis),
        P(fsdp_axis, tensor_axis),
        P(tensor_axis, fsdp_axis),
        P(),
        P(fsdp_axis, tensor_axis),
        P(fsdp_axis, tensor_axis),
        P(tensor_axis, fsdp_axis),
    )
    return jax.shard_map(
        on_either,
        mesh=mesh,
        in_specs=placed,
        out_specs=(
            P(None, (fsdp_axis, tensor_axis), None),
            P(None, (fsdp_axis, tensor_axis), None),
            P(None, (fsdp_axis, tensor_axis), None),
            P(),
            P(),
            P(fsdp_axis, tensor_axis),
            P(fsdp_axis, tensor_axis),
            P(fsdp_axis, tensor_axis),
            P(tensor_axis, fsdp_axis),
            P(),
            P(fsdp_axis, tensor_axis),
            P(fsdp_axis, tensor_axis),
            P(fsdp_axis, tensor_axis),
            P(tensor_axis, fsdp_axis),
            P(),
            P(fsdp_axis, tensor_axis),
            P(fsdp_axis, tensor_axis),
            P(tensor_axis, fsdp_axis),
        ),
        check_vma=False,
    )
```

```python
import functools
import math
import types

import jax
import jax.numpy as jnp
from jax import lax
from jax.experimental import pallas as pl
from jax.experimental.pallas import tpu as pltpu
from jax.sharding import PartitionSpec as P

norm_eps = 1e-06
masked_score = -1e30
highest = lax.Precision.HIGHEST
key_block_width = 256
tile = 256
fsdp_axis, tensor_axis = "fsdp", "tensor"


def matmul(left, right):
    return jnp.dot(left, right, preferred_element_type=jnp.float32)


def norm_rows(row_block, gain):
    return (
        row_block
        * lax.rsqrt(jnp.mean(row_block * row_block, axis=-1, keepdims=True) + norm_eps)
        * gain
    )


def gather_rows(row_block):
    return lax.all_gather(row_block, tensor_axis, axis=0, tiled=True)


def sum_rows(row_block):
    return lax.psum_scatter(
        row_block.astype(jnp.bfloat16), tensor_axis, scatter_dimension=0, tiled=True
    ).astype(jnp.float32)


def gather_weights(shards):
    (
        self_query,
        self_key,
        self_value,
        self_output,
        cross_query,
        cross_key,
        cross_value,
        cross_output,
        gate_weight,
        up_weight,
        down_weight,
    ) = shards
    inner = (
        lax.all_gather(self_query, fsdp_axis, axis=0, tiled=True),
        lax.all_gather(self_key, fsdp_axis, axis=0, tiled=True),
        lax.all_gather(self_value, fsdp_axis, axis=0, tiled=True),
        lax.all_gather(cross_query, fsdp_axis, axis=0, tiled=True),
        lax.all_gather(cross_key, fsdp_axis, axis=0, tiled=True),
        lax.all_gather(cross_value, fsdp_axis, axis=0, tiled=True),
        lax.all_gather(gate_weight, fsdp_axis, axis=0, tiled=True),
        lax.all_gather(up_weight, fsdp_axis, axis=0, tiled=True),
    )
    outer = (
        lax.all_gather(self_output, fsdp_axis, axis=1, tiled=True),
        lax.all_gather(cross_output, fsdp_axis, axis=1, tiled=True),
        lax.all_gather(down_weight, fsdp_axis, axis=1, tiled=True),
    )
    return (
        inner[0],
        inner[1],
        inner[2],
        outer[0],
        inner[3],
        inner[4],
        inner[5],
        outer[1],
        inner[6],
        inner[7],
        outer[2],
    )


def scatter_grads(grads_full):
    (
        self_query,
        self_key,
        self_value,
        self_output,
        cross_query,
        cross_key,
        cross_value,
        cross_output,
        gate_weight,
        up_weight,
        down_weight,
    ) = grads_full
    inner = (
        lax.psum_scatter(self_query, fsdp_axis, scatter_dimension=0, tiled=True),
        lax.psum_scatter(self_key, fsdp_axis, scatter_dimension=0, tiled=True),
        lax.psum_scatter(self_value, fsdp_axis, scatter_dimension=0, tiled=True),
        lax.psum_scatter(cross_query, fsdp_axis, scatter_dimension=0, tiled=True),
        lax.psum_scatter(cross_key, fsdp_axis, scatter_dimension=0, tiled=True),
        lax.psum_scatter(cross_value, fsdp_axis, scatter_dimension=0, tiled=True),
        lax.psum_scatter(gate_weight, fsdp_axis, scatter_dimension=0, tiled=True),
        lax.psum_scatter(up_weight, fsdp_axis, scatter_dimension=0, tiled=True),
    )
    outer = (
        lax.psum_scatter(self_output, fsdp_axis, scatter_dimension=1, tiled=True),
        lax.psum_scatter(cross_output, fsdp_axis, scatter_dimension=1, tiled=True),
        lax.psum_scatter(down_weight, fsdp_axis, scatter_dimension=1, tiled=True),
    )
    return (
        inner[0],
        inner[1],
        inner[2],
        outer[0],
        inner[3],
        inner[4],
        inner[5],
        outer[1],
        inner[6],
        inner[7],
        outer[2],
    )


def add_all(first, second):
    return tuple((left_item + right_item for left_item, right_item in zip(first, second)))


def fold_keys(key_rows, value_rows, step_fn, initial):
    return step_fn(
        initial,
        (
            lax.all_gather(key_rows, fsdp_axis, axis=0, tiled=True),
            lax.all_gather(value_rows, fsdp_axis, axis=0, tiled=True),
        ),
        jnp.int32(0),
    )


def on_device(
    inputs,
    encoder_out,
    out_cotangent,
    bucket_ids,
    position_table,
    self_gain,
    self_query,
    self_key,
    self_value,
    self_output,
    cross_gain,
    cross_query,
    cross_key,
    cross_value,
    cross_output,
    feed_gain,
    gate_weight,
    up_weight,
    down_weight,
):
    shards = (
        self_query,
        self_key,
        self_value,
        self_output,
        cross_query,
        cross_key,
        cross_value,
        cross_output,
        gate_weight,
        up_weight,
        down_weight,
    )
    batches = inputs.shape[0]
    tensor_size = lax.axis_size(tensor_axis)
    piece_rows = inputs.shape[1] * tensor_size
    length = bucket_ids.shape[0]
    heads_all = position_table.shape[0]
    buckets = position_table.shape[1]
    local_heads = heads_all // tensor_size
    head_size = self_query.shape[1] // local_heads
    kv_local = self_key.shape[1] // head_size
    group_size = local_heads // kv_local
    score_scale = head_size ** (-0.5)
    fsdp_rank = lax.axis_index(fsdp_axis)
    tensor_rank = lax.axis_index(tensor_axis)
    query_start = fsdp_rank * piece_rows
    encoder_rows = encoder_out.shape[1] * tensor_size
    table_local = lax.dynamic_slice_in_dim(
        position_table, tensor_rank * local_heads, local_heads, 0
    )
    bucket_range = jnp.arange(buckets, dtype=jnp.int32)
    lower_bounds = jnp.sum((bucket_ids[None, :] < bucket_range[:, None]).astype(jnp.int32), axis=1)
    upper_bounds = jnp.concatenate([lower_bounds[1:], jnp.full((1,), length, jnp.int32)])

    def position_bias(row_start, col_start, row_count, col_count):
        offsets = (
            row_start
            - col_start
            + jnp.arange(row_count, dtype=jnp.int32)[:, None]
            - jnp.arange(col_count, dtype=jnp.int32)[None, :]
        )
        indicator = (
            (offsets[None] >= lower_bounds[:, None, None])
            & (offsets[None] < upper_bounds[:, None, None])
        ).astype(jnp.float32)
        bias_values = jnp.einsum("hb,bij->hij", table_local, indicator, precision=highest).reshape(
            kv_local, group_size, row_count, col_count
        )
        return (bias_values, offsets >= 0, indicator)

    def split_heads(row_block):
        return row_block.reshape(row_block.shape[0], kv_local, group_size, head_size)

    def split_kv(row_block):
        return row_block.reshape(row_block.shape[0], kv_local, head_size)

    def backward(batch_index, saved_state, weights):
        (
            query_full,
            key_full,
            value_full,
            output_full,
            cross_query_full,
            cross_key_full,
            cross_value_full,
            cross_output_full,
            gate_full,
            up_full,
            down_full,
        ) = weights
        cotangent = out_cotangent[batch_index].astype(jnp.float32)
        grad_feed = gather_rows(out_cotangent[batch_index])
        hidden = saved_state.hidden
        normed_feed = saved_state.normed_feed
        down_grad = jnp.einsum("tf,td->fd", hidden, grad_feed, preferred_element_type=jnp.float32)
        grad_hidden = jnp.einsum(
            "td,fd->tf", grad_feed, down_full, preferred_element_type=jnp.float32
        )
        gelu_pull = jax.vjp(
            lambda gate_in, up_in: jax.nn.gelu(gate_in, approximate=True) * up_in,
            saved_state.gate_values,
            saved_state.up_values,
        )[1]
        grad_gate, grad_up = gelu_pull(grad_hidden)
        grad_gate = grad_gate.astype(jnp.bfloat16)
        grad_up = grad_up.astype(jnp.bfloat16)
        gate_grad = jnp.einsum(
            "td,tf->df", normed_feed, grad_gate, preferred_element_type=jnp.float32
        )
        up_grad = jnp.einsum("td,tf->df", normed_feed, grad_up, preferred_element_type=jnp.float32)
        feed_rows = sum_rows(
            jnp.einsum("tf,df->td", grad_gate, gate_full, preferred_element_type=jnp.float32)
            + jnp.einsum("tf,df->td", grad_up, up_full, preferred_element_type=jnp.float32)
        )
        grad_norm_feed, feed_gain_grad = jax.vjp(norm_rows, saved_state.after_cross, feed_gain)[
            1
        ](feed_rows)
        grad_after_cross = cotangent + grad_norm_feed
        cross_context = saved_state.cross_context
        cross_weights = saved_state.cross_weights
        encoded = saved_state.encoded
        grad_cross_branch = gather_rows(grad_after_cross.astype(jnp.bfloat16))
        cross_output_grad = jnp.einsum(
            "te,td->ed", cross_context, grad_cross_branch, preferred_element_type=jnp.float32
        )
        grad_cross_context = split_heads(
            jnp.einsum(
                "td,ed->te",
                grad_cross_branch,
                cross_output_full,
                preferred_element_type=jnp.float32,
            ).astype(jnp.bfloat16)
        )
        grad_cross_weights = jnp.einsum(
            "ikgd,jkd->kgij",
            grad_cross_context,
            split_kv(saved_state.cross_values),
            preferred_element_type=jnp.float32,
        )
        grad_cross_scores = (
            cross_weights
            * (
                grad_cross_weights
                - jnp.sum(cross_weights * grad_cross_weights, axis=-1, keepdims=True)
            )
        ).astype(jnp.bfloat16)
        grad_cross_queries = (
            (
                jnp.einsum(
                    "kgij,jkd->ikgd",
                    grad_cross_scores,
                    split_kv(saved_state.cross_keys),
                    preferred_element_type=jnp.float32,
                )
                * score_scale
            )
            .reshape(piece_rows, local_heads * head_size)
            .astype(jnp.bfloat16)
        )
        key_part = (
            jnp.einsum(
                "kgij,ikgd->jkd",
                grad_cross_scores,
                split_heads(saved_state.cross_queries),
                preferred_element_type=jnp.float32,
            )
            * score_scale
        ).reshape(encoded.shape[0], kv_local * head_size)
        value_part = jnp.einsum(
            "kgij,ikgd->jkd",
            saved_state.cross_low,
            grad_cross_context,
            preferred_element_type=jnp.float32,
        ).reshape(encoded.shape[0], kv_local * head_size)
        key_sum, value_sum = (
            lax.psum_scatter(key_part, fsdp_axis, scatter_dimension=0, tiled=True),
            lax.psum_scatter(value_part, fsdp_axis, scatter_dimension=0, tiled=True),
        )
        key_low = key_sum.astype(jnp.bfloat16)
        value_low = value_sum.astype(jnp.bfloat16)
        encoded_own = lax.dynamic_slice_in_dim(encoded, fsdp_rank * encoder_rows, encoder_rows, 0)
        cross_key_grad = jnp.einsum(
            "ed,ec->dc", encoded_own, key_low, preferred_element_type=jnp.float32
        )
        cross_value_grad = jnp.einsum(
            "ed,ec->dc", encoded_own, value_low, preferred_element_type=jnp.float32
        )
        encoder_grad = sum_rows(
            jnp.einsum("ec,dc->ed", key_low, cross_key_full, preferred_element_type=jnp.float32)
            + jnp.einsum(
                "ec,dc->ed", value_low, cross_value_full, preferred_element_type=jnp.float32
            )
        )
        cross_query_grad = jnp.einsum(
            "td,tc->dc",
            saved_state.normed_cross,
            grad_cross_queries,
            preferred_element_type=jnp.float32,
        )
        cross_rows = sum_rows(
            jnp.einsum(
                "tc,dc->td",
                grad_cross_queries,
                cross_query_full,
                preferred_element_type=jnp.float32,
            )
        )
        grad_norm_cross, cross_gain_grad = jax.vjp(
            norm_rows, saved_state.after_self, cross_gain
        )[1](cross_rows)
        grad_after_self = grad_after_cross + grad_norm_cross
        queries = saved_state.queries
        keys_own = saved_state.keys_own
        values_own = saved_state.values_own
        context = saved_state.context
        log_total = saved_state.log_total
        normed_self = saved_state.normed_self
        query_heads = split_heads(queries)
        grad_self_branch = gather_rows(grad_after_self.astype(jnp.bfloat16))
        self_output_grad = jnp.einsum(
            "te,td->ed",
            saved_state.context_low,
            grad_self_branch,
            preferred_element_type=jnp.float32,
        )
        grad_context = jnp.einsum(
            "td,ed->te", grad_self_branch, output_full, preferred_element_type=jnp.float32
        ).astype(jnp.bfloat16)
        grad_context_heads = split_heads(grad_context)
        row_delta = jnp.transpose(
            jnp.sum(grad_context_heads.astype(jnp.float32) * context, axis=-1), (1, 2, 0)
        )

        def query_step():

            def step(carried, pieces, piece_start):
                key_piece, value_piece = pieces
                piece_length = key_piece.shape[0]
                block_width = math.gcd(piece_length, key_block_width)
                block_count = piece_length // block_width
                key_blocks = key_piece.reshape(block_count, block_width, kv_local, head_size)
                value_blocks = value_piece.reshape(block_count, block_width, kv_local, head_size)
                block_starts = block_width * jnp.arange(block_count, dtype=jnp.int32)

                def step_one_block(current, block_data):
                    key_block, value_block, block_start = block_data
                    bias_values, allowed, indicator = position_bias(
                        query_start, block_start, piece_rows, block_width
                    )
                    scores = (
                        jnp.einsum(
                            "ikgd,jkd->kgij",
                            query_heads,
                            key_block,
                            preferred_element_type=jnp.float32,
                        )
                        * score_scale
                        + bias_values
                    )
                    shares = jnp.where(allowed, jnp.exp(scores - log_total[..., None]), 0.0)
                    grad_shares = jnp.einsum(
                        "ikgd,jkd->kgij",
                        grad_context_heads,
                        value_block,
                        preferred_element_type=jnp.float32,
                    )
                    grad_scores = shares * (grad_shares - row_delta[..., None])
                    bias_grad = current[1] + jnp.einsum(
                        "hij,bij->hb",
                        grad_scores.reshape(local_heads, piece_rows, block_width),
                        indicator,
                        precision=highest,
                    )
                    scores_low = grad_scores.astype(jnp.bfloat16)
                    query_grad = (
                        current[0]
                        + jnp.einsum(
                            "kgij,jkd->ikgd",
                            scores_low,
                            key_block,
                            preferred_element_type=jnp.float32,
                        )
                        * score_scale
                    )
                    key_block_grad = (
                        jnp.einsum(
                            "kgij,ikgd->jkd",
                            scores_low,
                            query_heads,
                            preferred_element_type=jnp.float32,
                        ).reshape(block_width, kv_local * head_size)
                        * score_scale
                    )
                    value_block_grad = jnp.einsum(
                        "kgij,ikgd->jkd",
                        shares.astype(jnp.bfloat16),
                        grad_context_heads,
                        preferred_element_type=jnp.float32,
                    ).reshape(block_width, kv_local * head_size)
                    keys_all = lax.dynamic_update_slice_in_dim(
                        current[2],
                        lax.dynamic_slice_in_dim(current[2], block_start, block_width, 0)
                        + key_block_grad,
                        block_start,
                        0,
                    )
                    values_all = lax.dynamic_update_slice_in_dim(
                        current[3],
                        lax.dynamic_slice_in_dim(current[3], block_start, block_width, 0)
                        + value_block_grad,
                        block_start,
                        0,
                    )
                    return ((query_grad, bias_grad, keys_all, values_all), None)

                carried, unused = lax.scan(
                    step_one_block, carried, (key_blocks, value_blocks, block_starts)
                )
                return carried

            return step

        query_zero = jnp.zeros((piece_rows, kv_local, group_size, head_size), jnp.float32)
        bias_zero = jnp.zeros((local_heads, buckets), jnp.float32)
        all_zero = jnp.zeros((length, kv_local * head_size), jnp.float32)
        query_grad, bias_grad, keys_all, values_all = fold_keys(
            keys_own, values_own, query_step(), (query_zero, bias_zero, all_zero, all_zero)
        )
        key_sum_self, value_sum_self = (
            lax.psum_scatter(keys_all, fsdp_axis, scatter_dimension=0, tiled=True),
            lax.psum_scatter(values_all, fsdp_axis, scatter_dimension=0, tiled=True),
        )
        key_grad_low = key_sum_self.astype(jnp.bfloat16)
        value_grad_low = value_sum_self.astype(jnp.bfloat16)
        query_grad_low = query_grad.reshape(piece_rows, local_heads * head_size).astype(
            jnp.bfloat16
        )
        self_query_grad = jnp.einsum(
            "td,tc->dc", normed_self, query_grad_low, preferred_element_type=jnp.float32
        )
        self_key_grad = jnp.einsum(
            "td,tc->dc", normed_self, key_grad_low, preferred_element_type=jnp.float32
        )
        self_value_grad = jnp.einsum(
            "td,tc->dc", normed_self, value_grad_low, preferred_element_type=jnp.float32
        )
        self_rows = sum_rows(
            jnp.einsum("tc,dc->td", query_grad_low, query_full, preferred_element_type=jnp.float32)
            + jnp.einsum("tc,dc->td", key_grad_low, key_full, preferred_element_type=jnp.float32)
            + jnp.einsum(
                "tc,dc->td", value_grad_low, value_full, preferred_element_type=jnp.float32
            )
        )
        grad_norm_self, self_gain_grad = jax.vjp(norm_rows, saved_state.own_rows, self_gain)[1](
            self_rows
        )
        input_grad = grad_after_self + grad_norm_self
        grads_full = (
            self_query_grad,
            self_key_grad,
            self_value_grad,
            self_output_grad,
            cross_query_grad,
            cross_key_grad,
            cross_value_grad,
            cross_output_grad,
            gate_grad,
            up_grad,
            down_grad,
        )
        extras = (bias_grad, self_gain_grad, cross_gain_grad, feed_gain_grad)
        return (grads_full, extras, input_grad, encoder_grad)

    layer_list = []
    input_list = []
    encoder_list = []
    small_sums = None
    shard_grads = None
    for batch_index in range(batches):
        weights_forward = gather_weights(shards)
        (
            forward_query_full,
            forward_key_full,
            forward_value_full,
            forward_output_full,
            forward_cross_query_full,
            forward_cross_key_full,
            forward_cross_value_full,
            forward_cross_output_full,
            forward_gate_full,
            forward_up_full,
            forward_down_full,
        ) = weights_forward
        own_rows = inputs[batch_index].astype(jnp.float32)
        forward_normed_self = gather_rows(norm_rows(own_rows, self_gain).astype(jnp.bfloat16))
        forward_queries = matmul(forward_normed_self, forward_query_full).astype(jnp.bfloat16)
        forward_keys_own = matmul(forward_normed_self, forward_key_full).astype(jnp.bfloat16)
        forward_values_own = matmul(forward_normed_self, forward_value_full).astype(jnp.bfloat16)
        forward_query_heads = split_heads(forward_queries)

        def forward_step(carried, pieces, piece_start):
            key_piece, value_piece = pieces
            piece_length = key_piece.shape[0]
            block_width = math.gcd(piece_length, key_block_width)
            block_count = piece_length // block_width
            key_blocks = key_piece.reshape(block_count, block_width, kv_local, head_size)
            value_blocks = value_piece.reshape(block_count, block_width, kv_local, head_size)
            block_starts = block_width * jnp.arange(block_count, dtype=jnp.int32)

            def forward_one_block(current, block_data):
                running_max, running_total, accumulated = current
                key_block, value_block, block_start = block_data
                bias_values, allowed, indicator = position_bias(
                    query_start, block_start, piece_rows, block_width
                )
                scores = (
                    jnp.einsum(
                        "ikgd,jkd->kgij",
                        forward_query_heads,
                        key_block,
                        preferred_element_type=jnp.float32,
                    )
                    * score_scale
                    + bias_values
                )
                scores = jnp.where(allowed, scores, masked_score)
                new_max = jnp.maximum(running_max, jnp.max(scores, axis=-1))
                factor = jnp.exp(running_max - new_max)
                shares = jnp.where(allowed, jnp.exp(scores - new_max[..., None]), 0.0)
                running_total = running_total * factor + jnp.sum(shares, axis=-1)
                update = jnp.einsum(
                    "kgij,jkd->ikgd",
                    shares.astype(jnp.bfloat16),
                    value_block,
                    preferred_element_type=jnp.float32,
                )
                accumulated = accumulated * jnp.transpose(factor, (2, 0, 1))[..., None] + update
                return ((new_max, running_total, accumulated), None)

            carried, unused = lax.scan(
                forward_one_block, carried, (key_blocks, value_blocks, block_starts)
            )
            return carried

        stat_shape = (kv_local, group_size, piece_rows)
        initial = (
            jnp.full(stat_shape, masked_score, jnp.float32),
            jnp.zeros(stat_shape, jnp.float32),
            jnp.zeros((piece_rows, kv_local, group_size, head_size), jnp.float32),
        )
        running_max, running_total, accumulated = fold_keys(
            forward_keys_own, forward_values_own, forward_step, initial
        )
        forward_context = accumulated / jnp.transpose(running_total, (2, 0, 1))[..., None]
        forward_log_total = running_max + jnp.log(running_total)
        context_low = forward_context.reshape(piece_rows, local_heads * head_size).astype(
            jnp.bfloat16
        )
        after_self = own_rows + sum_rows(matmul(context_low, forward_output_full))
        normed_cross = gather_rows(norm_rows(after_self, cross_gain).astype(jnp.bfloat16))
        cross_queries = matmul(normed_cross, forward_cross_query_full).astype(jnp.bfloat16)
        forward_encoded = lax.all_gather(
            encoder_out[batch_index], (fsdp_axis, tensor_axis), axis=0, tiled=True
        )
        cross_keys = matmul(forward_encoded, forward_cross_key_full).astype(jnp.bfloat16)
        cross_values = matmul(forward_encoded, forward_cross_value_full).astype(jnp.bfloat16)
        cross_scores = (
            jnp.einsum(
                "ikgd,jkd->kgij",
                split_heads(cross_queries),
                split_kv(cross_keys),
                preferred_element_type=jnp.float32,
            )
            * score_scale
        )
        forward_cross_weights = jax.nn.softmax(cross_scores, axis=-1)
        cross_low = forward_cross_weights.astype(jnp.bfloat16)
        forward_cross_context = (
            jnp.einsum(
                "kgij,jkd->ikgd",
                cross_low,
                split_kv(cross_values),
                preferred_element_type=jnp.float32,
            )
            .reshape(piece_rows, local_heads * head_size)
            .astype(jnp.bfloat16)
        )
        after_cross = after_self + sum_rows(
            matmul(forward_cross_context, forward_cross_output_full)
        )
        forward_normed_feed = gather_rows(norm_rows(after_cross, feed_gain).astype(jnp.bfloat16))
        gate_values = matmul(forward_normed_feed, forward_gate_full)
        up_values = matmul(forward_normed_feed, forward_up_full)
        forward_hidden = (jax.nn.gelu(gate_values, approximate=True) * up_values).astype(
            jnp.bfloat16
        )
        layer_rows = after_cross + sum_rows(matmul(forward_hidden, forward_down_full))
        forward_saved_state = types.SimpleNamespace(
            own_rows=own_rows,
            normed_self=forward_normed_self,
            queries=forward_queries,
            keys_own=forward_keys_own,
            values_own=forward_values_own,
            context=forward_context,
            log_total=forward_log_total,
            context_low=context_low,
            after_self=after_self,
            normed_cross=normed_cross,
            cross_queries=cross_queries,
            encoded=forward_encoded,
            cross_keys=cross_keys,
            cross_values=cross_values,
            cross_weights=forward_cross_weights,
            cross_low=cross_low,
            cross_context=forward_cross_context,
            after_cross=after_cross,
            normed_feed=forward_normed_feed,
            gate_values=gate_values,
            up_values=up_values,
            hidden=forward_hidden,
        )
        layer_rows, saved_state = (layer_rows.astype(jnp.bfloat16), forward_saved_state)
        weights_backward = gather_weights(shards)
        grads_full, extras, input_grad, encoder_grad = backward(
            batch_index, saved_state, weights_backward
        )
        reduced = scatter_grads(grads_full)
        shard_grads = reduced if shard_grads is None else add_all(shard_grads, reduced)
        small_sums = extras if small_sums is None else add_all(small_sums, extras)
        layer_list.append(layer_rows)
        input_list.append(input_grad)
        encoder_list.append(encoder_grad)
    table_full = lax.dynamic_update_slice_in_dim(
        jnp.zeros((heads_all, buckets), jnp.float32), small_sums[0], tensor_rank * local_heads, 0
    )
    table_sum, self_gain_sum, cross_gain_sum, feed_gain_sum = lax.psum(
        (table_full, small_sums[1], small_sums[2], small_sums[3]), (fsdp_axis, tensor_axis)
    )
    return (
        jnp.stack(layer_list),
        jnp.stack(input_list),
        jnp.stack(encoder_list),
        table_sum,
        self_gain_sum,
        shard_grads[0],
        shard_grads[1],
        shard_grads[2],
        shard_grads[3],
        cross_gain_sum,
        shard_grads[4],
        shard_grads[5],
        shard_grads[6],
        shard_grads[7],
        feed_gain_sum,
        shard_grads[8],
        shard_grads[9],
        shard_grads[10],
    )


def to_chip(fsdp):
    return dict(device_id={fsdp_axis: fsdp}, device_id_type=pl.DeviceIdType.MESH)


def to_core(core):
    return dict(device_id={tensor_axis: core}, device_id_type=pl.DeviceIdType.MESH)


def chip_place(layers):
    rank = lax.axis_index(fsdp_axis)
    return rank, rank // 4, rank // 2 % 2, rank % 2


def peers_of(rank, y, x):
    found = []
    for o in (1, 2, 3):
        other_y = 1 - y if o & 2 else y
        other_x = 1 - x if o & 1 else x
        spot = 2 * other_y + other_x
        found.append((rank - 2 * y - x + spot, spot))
    return found


def greet(layers):
    rank, z, y, x = chip_place(layers)
    barrier = pltpu.get_barrier_semaphore()
    for chip, spot in peers_of(rank, y, x):
        pl.semaphore_signal(barrier, inc=1, **to_chip(chip))
    for o in range(1, layers):
        pl.semaphore_signal(barrier, inc=1, **to_chip(rank - 4 * z + 4 * ((z + o) % layers)))
    pl.semaphore_signal(barrier, inc=1, **to_core(1 - lax.axis_index(tensor_axis)))
    pl.semaphore_wait(barrier, 3 + layers)


dma = pltpu.SemaphoreType.DMA


class Column:
    def __init__(self, layers, source, land, z_sem, core_sem=None):
        self.layers, self.source, self.land = layers, source, land
        self.z_sem, self.core_sem = z_sem, core_sem
        self.rank, self.z, self.y, self.x = chip_place(layers)
        self.core = lax.axis_index(tensor_axis)

    def place(self, layer):
        return (layer,) if self.core_sem is None else (layer, self.core)

    def hop(self, o):
        there = (self.z + o) % self.layers
        return pltpu.make_async_remote_copy(
            src_ref=self.source.at[there],
            dst_ref=self.land.at[self.place(self.z)],
            send_sem=self.z_sem.at[0, o],
            recv_sem=self.z_sem.at[1, self.z],
            **to_chip(self.rank + 4 * (there - self.z)),
        )

    def arrival(self, layer):
        return pltpu.make_async_remote_copy(
            src_ref=self.source.at[0],
            dst_ref=self.land.at[self.place(layer)],
            send_sem=self.z_sem.at[0, 0],
            recv_sem=self.z_sem.at[1, layer],
            **to_chip(self.rank + 4 - 8 * (self.z // 2)),
        )

    def over(self, layer):
        return pltpu.make_async_remote_copy(
            src_ref=self.land.at[layer, self.core],
            dst_ref=self.land.at[layer, self.core],
            send_sem=self.core_sem.at[0, layer],
            recv_sem=self.core_sem.at[1, layer],
            **to_core(1 - self.core),
        )

    def start(self):
        for o in range(1, self.layers):
            self.hop(o).start()
        self.land[self.place(self.z)] = self.source[self.z]

    def arrive(self):
        for o in range(1, self.layers):
            self.arrival((self.z + o) % self.layers).wait_recv()
        if self.core_sem is not None:
            for layer in range(self.layers):
                self.over(layer).start()

    def finish(self):
        for o in range(1, self.layers):
            self.hop(o).wait_send()
        if self.core_sem is not None:
            for layer in range(self.layers):
                self.over(layer).wait()


class PlaneSwap:
    def __init__(self, layers, source, land, sem):
        self.source, self.land, self.sem = source, land, sem
        self.rank, self.z, self.y, self.x = chip_place(layers)
        self.spot = 2 * self.y + self.x
        self.peers = peers_of(self.rank, self.y, self.x)

    def hop(self, o):
        chip, there = self.peers[o]
        return pltpu.make_async_remote_copy(
            src_ref=self.source.at[there],
            dst_ref=self.land.at[self.spot],
            send_sem=self.sem.at[0, o],
            recv_sem=self.sem.at[1, o],
            **to_chip(chip),
        )

    def start(self):
        for o in range(3):
            self.hop(o).start()
        self.land[self.spot] = self.source[self.spot]

    def arrival(self, o):
        chip, there = self.peers[o]
        return pltpu.make_async_remote_copy(
            src_ref=self.source.at[there],
            dst_ref=self.land.at[there],
            send_sem=self.sem.at[0, o],
            recv_sem=self.sem.at[1, o],
            **to_chip(chip),
        )

    def arrive(self):
        for o in range(3):
            self.arrival(o).wait_recv()

    def finish(self):
        for o in range(3):
            self.hop(o).wait_send()


class PlaneGather:
    def __init__(self, layers, source, land, sem, core_sem):
        self.source, self.land, self.sem, self.core_sem = source, land, sem, core_sem
        self.rank, self.z, self.y, self.x = chip_place(layers)
        self.core = lax.axis_index(tensor_axis)
        self.spot = 2 * self.y + self.x
        self.peers = peers_of(self.rank, self.y, self.x)

    def hop(self, o, spot):
        return pltpu.make_async_remote_copy(
            src_ref=self.source,
            dst_ref=self.land.at[spot, self.core],
            send_sem=self.sem.at[0, o],
            recv_sem=self.sem.at[1, o],
            **to_chip(self.peers[o][0]),
        )

    def over(self, spot):
        return pltpu.make_async_remote_copy(
            src_ref=self.land.at[spot, self.core],
            dst_ref=self.land.at[spot, self.core],
            send_sem=self.core_sem.at[0, spot],
            recv_sem=self.core_sem.at[1, spot],
            **to_core(1 - self.core),
        )

    def start(self):
        for o in range(3):
            self.hop(o, self.spot).start()
        self.land[self.spot, self.core] = self.source[...]

    def arrive(self):
        for o in range(3):
            self.hop(o, self.peers[o][1]).wait_recv()
        for spot in range(4):
            self.over(spot).start()

    def finish(self):
        for o in range(3):
            self.hop(o, self.spot).wait_send()
        for spot in range(4):
            self.over(spot).wait()


def close_kernel(
    layers,
    heads,
    gq_ref,
    x_ref,
    win_ref,
    gas_ref,
    kvs_ref,
    gains_ref,
    mid_ref,
    sums_ref,
    hit_ref,
    wa_ref,
    query_out,
    key_out,
    value_out,
    input_out,
    enc_out,
    table_out,
    gain_out,
    nt_s,
    wkv_s,
    mine_s,
    halves_s,
    enc_s,
    ended_s,
    rows_land,
    small_s,
    small_l,
    small_z,
    sum_s,
    load_sem,
    core_sem,
    rows_z,
    small_sem,
    z_sem,
    *sum_refs,
):
    f32, bf16 = jnp.float32, jnp.bfloat16
    grads = GradSum(layers, None, (), sum_s, *sum_refs)
    rows = Column(layers, ended_s, rows_land, rows_z)
    rank, z, y, x = chip_place(layers)
    core = lax.axis_index(tensor_axis)
    own = gas_ref.shape[1]
    width = x_ref.shape[1]
    enc_own = kvs_ref.shape[0] // (2 * layers)
    wide = kvs_ref.shape[1]
    kv_local = query_out.shape[1] // 128
    blocks = sums_ref.shape[0] // 2
    buckets = hit_ref.shape[1]
    gain = gains_ref[...]
    loads = pltpu.make_async_copy(
        wa_ref.at[:, pl.ds(2 * wide, wide)], wkv_s, load_sem.at[0]
    )
    loads.start()
    greet(layers)

    def normed(n, carry):
        at = pl.ds(pl.multiple_of(n * 128, 128), 128)
        v = x_ref[at, :].astype(f32)
        nt_s[:, at] = jnp.transpose((v * norm_scale(v) * gain).astype(bf16))
        return carry

    lax.fori_loop(0, x_ref.shape[0] // 128, normed, 0)
    per_layer = width // layers

    def weigh(turn, carry):
        layer = grads.layer_of(2 * turn)
        at = pl.ds(pl.multiple_of(layer * per_layer, per_layer), per_layer)
        part = matmul(nt_s[at, :], gq_ref[...]).astype(bf16)
        grads.own[layer] = part.reshape(grads.own.shape[1:])
        grads.send_first(2 * turn)
        grads.send_first(2 * turn + 1)
        return carry

    lax.fori_loop(0, layers, weigh, 0)

    def gather(which):
        return jnp.concatenate(
            [
                gq_ref[pl.ds(pl.multiple_of((2 * layer + which) * own, own), own), :]
                for layer in range(layers)
            ],
            axis=0,
        )

    def across(n, shape_at):
        return pltpu.make_async_remote_copy(
            src_ref=halves_s.at[0, shape_at],
            dst_ref=halves_s.at[1, shape_at],
            send_sem=core_sem.at[0, n],
            recv_sem=core_sem.at[1, n],
            **to_core(1 - core),
        )

    body, tail = pl.ds(0, layers * own), pl.ds(layers * own, layers * enc_own)
    halves_s[0, body, :] = dot_t(gather(1 - core), win_ref[...]).astype(bf16)
    across(0, body).start()
    loads.wait()
    enc_s[...] = dot_t(kvs_ref[...], wkv_s[...])
    other = pl.ds(pl.multiple_of((1 - core) * layers * enc_own, enc_own), layers * enc_own)
    halves_s[0, tail, :] = enc_s[other, :].astype(bf16)
    across(1, tail).start()
    mine_s[...] = dot_t(gather(core), win_ref[...])
    grads.advance(1)
    grads.advance(2)

    found = [jnp.zeros((1, buckets), f32) for _ in range(2)]
    for d in range(blocks):
        by_bucket = lax.dot_general(
            sums_ref[...],
            hit_ref[d],
            (((1,), (1,)), ((), ())),
            precision=highest,
            preferred_element_type=f32,
        )
        for h in range(2):
            found[h] = found[h] + by_bucket[h * blocks + d : h * blocks + d + 1, :]
    lane = lax.broadcasted_iota(jnp.int32, (buckets, width), 1)
    spread = (lane % buckets == lax.broadcasted_iota(jnp.int32, (buckets, width), 0)).astype(f32)
    lane = lax.broadcasted_iota(jnp.int32, (1, width), 1)
    first_head = 2 * (core * kv_local + rank % 4)
    table = jnp.zeros((1, width), f32)
    for h in range(2):
        row = jnp.dot(found[h], spread, precision=highest, preferred_element_type=f32)
        table = table + jnp.where(lane // buckets == first_head + h, row, 0.0)
    small_s[0] = jnp.zeros_like(small_s[0])
    small_s[0, 1:3, :] = mid_ref[...]
    small_s[0, 3:4, :] = table

    across(0, body).wait()
    across(1, tail).wait()
    mine_enc = pl.ds(pl.multiple_of(core * layers * enc_own, enc_own), layers * enc_own)
    enc_sum = enc_s[mine_enc, :].astype(bf16).astype(f32) + halves_s[1, tail, :].astype(f32)

    total = jnp.zeros((1, width), f32)
    for layer in range(layers):
        at = slice(layer * own, (layer + 1) * own)
        both = mine_s[at, :].astype(bf16).astype(f32) + halves_s[1, at, :].astype(f32)
        v = x_ref[pl.ds(pl.multiple_of((2 * layer + core) * own, own), own), :].astype(f32)
        grad, gain_grad = norm_pull(v, gain, both)
        total = total + gain_grad
        ended_s[layer, :own, :] = (gas_ref[layer] + grad).astype(bf16)
        ended_s[layer, own:, :] = enc_sum[layer * enc_own : (layer + 1) * enc_own].astype(bf16)
    small_s[0, 0:1, :] = total

    def swap(n, where):
        return pltpu.make_async_remote_copy(
            src_ref=small_s.at[n],
            dst_ref=small_l.at[n],
            send_sem=small_sem.at[0, n],
            recv_sem=small_sem.at[1, n],
            **where,
        )

    across_x = swap(0, to_chip(rank + 1 - 2 * x))
    across_y = swap(1, to_chip(rank + 2 - 4 * y))
    across_core = swap(3, to_core(1 - core))

    def across_z(o, layer):
        there = (z + o) % layers
        return pltpu.make_async_remote_copy(
            src_ref=small_s.at[2],
            dst_ref=small_z.at[layer],
            send_sem=z_sem.at[0, o],
            recv_sem=z_sem.at[1, layer],
            **to_chip(rank + 4 * (there - z)),
        )

    across_x.start()
    grads.advance(3)
    rows.start()
    grads.advance(4)
    across_x.wait()
    small_s[1] = small_s[0] + small_l[0]
    across_y.start()
    grads.advance(5)
    across_y.wait()
    small_s[2] = small_s[1] + small_l[1]
    small_z[z] = small_s[2]
    for o in range(1, layers):
        across_z(o, z).start()
    grads.advance(6)
    grads.advance(7)
    for o in range(1, layers):
        across_z(o, (z + o) % layers).wait_recv()
        across_z(o, z).wait_send()
    summed = small_z[0]
    for layer in range(1, layers):
        summed = summed + small_z[layer]
    small_s[3] = summed
    across_core.start()

    def one(m, carry):
        grads.advance(m)
        return carry

    lax.fori_loop(8, sum_steps(layers), one, 0)
    across_core.wait()
    both = small_s[3] + small_l[3]
    low = jnp.where(core == 0, small_s[3], small_l[3])
    gain_out[0:1, :] = both[0:1, :]
    gain_out[1:3, :] = low[1:3, :]
    for h in range(heads):
        table_out[h : h + 1, :] = both[3:4, h * buckets : (h + 1) * buckets]
    whole = sum_s[...].reshape(64, sum_s.shape[-1])
    group = whole.shape[1] // kv_local
    half = group // 4
    pieces = [whole[:, n * group : (n + 1) * group] for n in range(kv_local)]
    query_out[...] = jnp.concatenate([p[:, : 2 * half] for p in pieces], axis=1)
    key_out[...] = jnp.concatenate([p[:, 2 * half : 3 * half] for p in pieces], axis=1)
    value_out[...] = jnp.concatenate([p[:, 3 * half :] for p in pieces], axis=1)
    rows.arrive()
    for layer in range(layers):
        input_out[layer] = rows_land[layer, :own, :].astype(f32)
        enc_out[layer] = rows_land[layer, own:, :].astype(f32)
    rows.finish()
    grads.finish()


def close_rows(
    layers, heads, grad_qkv, x_low, win, grad_rows, kv_sum, self_gain, mid, sums, hit, weights
):
    f32, bf16 = jnp.float32, jnp.bfloat16
    width, cols = win.shape
    own = grad_rows.shape[1]
    wide = kv_sum.shape[1]
    enc_own = kv_sum.shape[0] // (2 * layers)
    buckets = hit.shape[1]
    vmem, anywhere = pl.BlockSpec(memory_space=pltpu.VMEM), pl.BlockSpec(memory_space=pl.ANY)
    rows_shape = (layers, own + enc_own, width)
    return pl.pallas_call(
        functools.partial(close_kernel, layers, heads),
        name="close_rows",
        out_shape=(
            jax.ShapeDtypeStruct((64, cols // 2), f32),
            jax.ShapeDtypeStruct((64, cols // 4), f32),
            jax.ShapeDtypeStruct((64, cols // 4), f32),
            jax.ShapeDtypeStruct((layers, own, width), f32),
            jax.ShapeDtypeStruct((layers, enc_own, width), f32),
            jax.ShapeDtypeStruct((heads, buckets), f32),
            jax.ShapeDtypeStruct((3, width), f32),
        ),
        in_specs=[vmem] * 9 + [anywhere],
        out_specs=(vmem,) * 7,
        scratch_shapes=[
            pltpu.VMEM((width, x_low.shape[0]), bf16),
            pltpu.VMEM((width, wide), bf16),
            pltpu.VMEM((layers * own, width), f32),
            pltpu.VMEM((2, layers * (own + enc_own), width), bf16),
            pltpu.VMEM((2 * layers * enc_own, width), f32),
            pltpu.VMEM(rows_shape, bf16),
            pltpu.VMEM(rows_shape, bf16),
            pltpu.VMEM((4, 8, width), f32),
            pltpu.VMEM((4, 8, width), f32),
            pltpu.VMEM((layers, 8, width), f32),
            pltpu.VMEM((2, 2, 16, cols), f32),
            dma((1,)),
            dma((2, 2)),
            dma((2, layers)),
            dma((2, 4)),
            dma((2, layers)),
            *sum_scratch(layers, cols),
        ],
        compiler_params=pltpu.CompilerParams(
            collective_id=7, has_side_effects=True, vmem_limit_bytes=48 << 20
        ),
    )(grad_qkv, x_low, win, grad_rows, kv_sum, self_gain, mid, sums, hit, weights)

def sum_scratch(layers, cols):
    steps = 2 * layers
    bf16 = jnp.bfloat16
    return [
        pltpu.VMEM((layers, 2, 2, 2, 2, 16, cols), bf16),
        pltpu.VMEM((layers, 2, 2, 2, 16, cols), bf16),
        pltpu.VMEM((steps, 2, 16, cols), bf16),
        pltpu.VMEM((steps, 2, 16, cols), bf16),
        pltpu.VMEM((steps, 2, 16, cols), bf16),
        dma((3, layers)),
        dma((2, steps, 2, 2)),
        dma((2, steps, 2)),
        dma((2, steps)),
        dma((2, steps)),
    ]


def sum_steps(layers):
    return 2 * layers + layers + 3


class GradSum:
    def __init__(self, layers, whole, got, out, own, first, second, below, above, load, s1, s2, su, sd):
        self.got = got
        self.layers, self.whole, self.out, self.own = layers, whole, out, own
        self.first, self.second, self.below, self.above = first, second, below, above
        self.load, self.s1, self.s2, self.su, self.sd = load, s1, s2, su, sd
        self.rank, self.z, self.y, self.x = chip_place(layers)
        self.x_chip = self.rank + 1 - 2 * self.x
        self.y_chip = self.rank + 2 - 4 * self.y
        self.steps = 2 * layers

    def layer_of(self, n):
        turn = n // 2
        return jnp.where(turn % 2 == 1, turn // 2, self.layers - 1 - turn // 2)

    def loads(self, turn):
        layer = self.layer_of(2 * turn)
        copies = [
            pltpu.make_async_copy(self.whole.at[layer], self.own.at[layer], self.load.at[0, turn])
        ]
        for colour, came in enumerate(self.got):
            copies.append(
                pltpu.make_async_copy(
                    came.at[layer], self.first.at[layer, colour], self.load.at[1 + colour, turn]
                )
            )
        return copies

    def hop_one(self, n, colour, which):
        layer, chunk = self.layer_of(n), n % 2
        if colour == 0:
            source, chip = self.own.at[layer, which, 1 - self.x, 0, chunk], self.x_chip
        else:
            source, chip = self.own.at[layer, 1 - self.y, which, 1, chunk], self.y_chip
        return pltpu.make_async_remote_copy(
            src_ref=source,
            dst_ref=self.first.at[layer, colour, which, chunk],
            send_sem=self.s1.at[0, n, colour, which],
            recv_sem=self.s1.at[1, n, colour, which],
            **to_chip(chip),
        )

    def hop_two(self, n, colour):
        layer, chunk = self.layer_of(n), n % 2
        if colour == 0:
            source, chip = self.own.at[layer, 1 - self.y, self.x, 0, chunk], self.y_chip
        else:
            source, chip = self.own.at[layer, self.y, 1 - self.x, 1, chunk], self.x_chip
        return pltpu.make_async_remote_copy(
            src_ref=source,
            dst_ref=self.second.at[n, colour],
            send_sem=self.s2.at[0, n, colour],
            recv_sem=self.s2.at[1, n, colour],
            **to_chip(chip),
        )

    def hop_z(self, n, up):
        layer, chunk = self.layer_of(n), n % 2
        sems = self.su if up else self.sd
        return pltpu.make_async_remote_copy(
            src_ref=self.own.at[layer, self.y, self.x, :, chunk],
            dst_ref=(self.below if up else self.above).at[n],
            send_sem=sems.at[0, n],
            recv_sem=sems.at[1, n],
            **to_chip(self.rank + (4 if up else -4)),
        )

    def start(self):
        for turn in range(self.layers):
            for copy in self.loads(turn):
                copy.start()

    def send_first(self, n):
        @pl.when(n < self.steps)
        def _():
            if self.whole is not None:

                @pl.when(n % 2 == 0)
                def _():
                    for copy in self.loads(n // 2):
                        copy.wait()

            if not self.got:
                for which in range(2):
                    for colour in range(2):
                        self.hop_one(n, colour, which).start()

    def advance(self, m):
        steps, layers = self.steps, self.layers
        n = m - 1

        @pl.when((n >= 0) & (n < steps))
        def _():
            layer, chunk = self.layer_of(n), n % 2
            for colour in range(2):
                for other in range(2):
                    if colour == 0:
                        which = (1 - self.y) if other == 0 else self.y
                        place = (layer, which, self.x, 0, chunk)
                    else:
                        which = (1 - self.x) if other == 0 else self.x
                        place = (layer, self.y, which, 1, chunk)
                    if not self.got:
                        self.hop_one(n, colour, which).wait_recv()
                    self.own[place] = self.own[place] + self.first[layer, colour, which, chunk]
                    if other == 0:
                        self.hop_two(n, colour).start()

        n2 = m - 2

        @pl.when((n2 >= 0) & (n2 < steps))
        def _():
            layer, chunk = self.layer_of(n2), n2 % 2
            for colour in range(2):
                self.hop_two(n2, colour).wait_recv()
                place = (layer, self.y, self.x, colour, chunk)
                self.own[place] = self.own[place] + self.second[n2, colour]

        for up in (True, False):
            chain = self.z if up else layers - 1 - self.z
            nz = m - 2 - chain
            layer = self.layer_of(nz)
            beyond = (layer > self.z) if up else (layer < self.z)

            @pl.when((nz >= 0) & (nz < steps) & beyond)
            def _():
                @pl.when(chain > 0)
                def _():
                    self.hop_z(nz, up).wait_recv()
                    came = self.below if up else self.above
                    for colour in range(2):
                        place = (layer, self.y, self.x, colour, nz % 2)
                        self.own[place] = self.own[place] + came[nz, colour]

                self.hop_z(nz, up).start()

        nf = m - 2 - layers

        @pl.when((nf >= 0) & (nf < steps) & (self.layer_of(nf) == self.z))
        def _():
            layer, chunk = self.layer_of(nf), nf % 2
            for colour in range(2):
                self.out[colour, chunk] = self.own[layer, self.y, self.x, colour, chunk].astype(
                    jnp.float32
                )
            for up in (True, False):
                chain = self.z if up else layers - 1 - self.z

                @pl.when(chain > 0)
                def _():
                    self.hop_z(nf, up).wait_recv()
                    came = self.below if up else self.above
                    for colour in range(2):
                        self.out[colour, chunk] += came[nf, colour].astype(jnp.float32)

    def finish(self):
        def one(n, carry):
            for colour in range(2):
                if not self.got:
                    for which in range(2):
                        self.hop_one(n, colour, which).wait_send()
                self.hop_two(n, colour).wait_send()
            layer = self.layer_of(n)
            for up in (True, False):

                @pl.when((layer > self.z) if up else (layer < self.z))
                def _():
                    self.hop_z(n, up).wait_send()

            return carry

        lax.fori_loop(0, self.steps, one, 0)

def gather_scratch(layers, cols):
    return [
        pltpu.VMEM((2, 2, 16, cols), jnp.bfloat16),
        dma((1,)),
        dma((2, 2, layers, 2)),
        dma((2, layers, 2)),
        dma((2, layers, 2)),
        dma((2, layers, 2)),
        dma((2, layers, 2)),
    ]


class RowGather:
    def __init__(self, layers, short, whole, here, local, sz, sx, sy, sfx, sfy):
        self.short = short
        self.layers, self.whole, self.here = layers, whole, here
        self.local, self.sz, self.sx, self.sy, self.sfx, self.sfy = local, sz, sx, sy, sfx, sfy
        self.rank, self.z, self.y, self.x = chip_place(layers)
        self.x_chip = self.rank + 1 - 2 * self.x
        self.y_chip = self.rank + 2 - 4 * self.y

    def put(self):
        place = self.whole.at[self.z, self.y, self.x]
        return pltpu.make_async_copy(self.here, place, self.local.at[0])

    def source(self, layer, chunk, own, colours=slice(None)):
        if own:
            return self.here.at[colours, chunk]
        return self.whole.at[layer, self.y, self.x, colours, chunk]

    def along_z(self, layer, chunk, up, own=False):
        return pltpu.make_async_remote_copy(
            src_ref=self.source(layer, chunk, own),
            dst_ref=self.whole.at[layer, self.y, self.x, :, chunk],
            send_sem=self.sz.at[0, int(up), layer, chunk],
            recv_sem=self.sz.at[1, int(up), layer, chunk],
            **to_chip(self.rank + (4 if up else -4)),
        )

    def in_plane(self, layer, chunk, along_x, own=False):
        sems = self.sx if along_x else self.sy
        colours = slice(None)
        if self.short:
            colours = 0 if along_x else 1
        return pltpu.make_async_remote_copy(
            src_ref=self.source(layer, chunk, own, colours),
            dst_ref=self.whole.at[layer, self.y, self.x, colours, chunk],
            send_sem=sems.at[0, layer, chunk],
            recv_sem=sems.at[1, layer, chunk],
            **to_chip(self.x_chip if along_x else self.y_chip),
        )

    def onward(self, layer, chunk, along_x):
        if along_x:
            place = (layer, 1 - self.y, self.x, 1, chunk)
            sems, chip = self.sfx, self.x_chip
        else:
            place = (layer, self.y, 1 - self.x, 0, chunk)
            sems, chip = self.sfy, self.y_chip
        return pltpu.make_async_remote_copy(
            src_ref=self.whole.at[place],
            dst_ref=self.whole.at[place],
            send_sem=sems.at[0, layer, chunk],
            recv_sem=sems.at[1, layer, chunk],
            **to_chip(chip),
        )

    def send_z(self):
        for chunk in range(2):

            @pl.when(self.z < self.layers - 1)
            def _():
                self.along_z(self.z, chunk, True, own=True).start()

            @pl.when(self.z > 0)
            def _():
                self.along_z(self.z, chunk, False, own=True).start()

    def send_plane(self):
        for chunk in range(2):
            for along_x in (True, False):
                self.in_plane(self.z, chunk, along_x, own=True).start()
        self.put().start()

    def pass_on(self, m):
        far, chunk = m // 2, m % 2
        for up in (True, False):
            layer = self.z - far if up else self.z + far
            near = (layer >= 0) if up else (layer < self.layers)

            @pl.when((far > 0) & near)
            def _():
                self.along_z(layer, chunk, up).wait_recv()

                @pl.when((self.z < self.layers - 1) if up else (self.z > 0))
                def _():
                    self.along_z(layer, chunk, up).start()

                for along_x in (True, False):
                    self.in_plane(layer, chunk, along_x).start()

    def turn(self, m):
        far, chunk = m // 2, m % 2
        for up in (True, False):
            layer = self.z - far if up else self.z + far
            near = (layer >= 0) if up else ((layer < self.layers) & (far > 0))

            @pl.when(near)
            def _():
                for along_x in (True, False):
                    self.in_plane(layer, chunk, along_x).wait_recv()
                    self.onward(layer, chunk, not along_x).start()

    def step(self, m):
        @pl.when(m + 2 < 2 * self.layers)
        def _():
            self.pass_on(m + 2)

        if not self.short:
            self.turn(m)

    def finish(self):
        self.put().wait()

        def one(n, carry):
            layer, chunk = n // 2, n % 2
            for along_x in (True, False):
                if self.short:
                    self.in_plane(layer, chunk, along_x).wait_recv()
                else:
                    self.onward(layer, chunk, along_x).wait()
                self.in_plane(layer, chunk, along_x).wait_send()

            @pl.when((self.z < self.layers - 1) & (layer <= self.z))
            def _():
                self.along_z(layer, chunk, True).wait_send()

            @pl.when((self.z > 0) & (layer >= self.z))
            def _():
                self.along_z(layer, chunk, False).wait_send()

            return carry

        lax.fori_loop(0, 2 * self.layers, one, 0)

def begin_kernel(
    score_scale,
    layers,
    rows_ref,
    enc_ref,
    cot_ref,
    gain_ref,
    bias_ref,
    query_ref,
    key_ref,
    value_ref,
    out_ref,
    cq_ref,
    ck_ref,
    cv_ref,
    co_ref,
    gate_ref,
    up_ref,
    down_ref,
    rows_out,
    enc_out,
    cot_out,
    kept_ref,
    low_ref,
    full_ref,
    total_ref,
    win_out,
    whole_ref,
    feed_whole,
    rows_land,
    enc_land,
    enc_all,
    cot_land,
    win_s,
    norm_s,
    qkv_s,
    came,
    landed,
    low_s,
    q_s,
    k_s,
    v_s,
    bias_s,
    score_s,
    rows_z,
    rows_core,
    enc_z,
    plane_sem,
    plane_core,
    cot_z,
    cot_core,
    in_sem,
    out_send,
    out_recv,
    win_sem,
    *gather_refs,
):
    f32, bf16 = jnp.float32, jnp.bfloat16
    blocks = bias_s.shape[1]
    sources = qkv_s.shape[0]
    head = k_s.shape[1]
    third = len(gather_refs) // 3
    first = RowGather(layers, False, win_s, *gather_refs[:third])
    gathers = (
        RowGather(layers, True, feed_whole, *gather_refs[2 * third :]),
        RowGather(layers, False, whole_ref, *gather_refs[third : 2 * third]),
    )
    rank, z, y, x = chip_place(layers)
    spot = 2 * y + x
    peers = peers_of(rank, y, x)
    rows = Column(layers, rows_ref, rows_land, rows_z, rows_core)
    enc = Column(layers, enc_ref, enc_land, enc_z)
    plane = PlaneGather(layers, enc_land, enc_all, plane_sem, plane_core)
    cot = Column(layers, cot_ref, cot_land, cot_z, cot_core)
    heads = PlaneSwap(layers, qkv_s, came, in_sem)

    def shard(gather, parts):
        gather.here[...] = jnp.concatenate(parts, axis=1).reshape(gather.here.shape)

    parts = []
    for kv in range(sources):
        parts.append(query_ref[:, 2 * kv * head : 2 * (kv + 1) * head])
        parts.append(key_ref[:, kv * head : (kv + 1) * head])
        parts.append(value_ref[:, kv * head : (kv + 1) * head])
    shard(first, parts)
    greet(layers)
    first.send_z()
    first.send_plane()
    shard(
        gathers[1],
        [jnp.transpose(out_ref[...]), cq_ref[...], ck_ref[...], cv_ref[...], jnp.transpose(co_ref[...])],
    )
    feed = gate_ref.shape[1]
    parts = []
    for at in range(0, feed, tile):
        end = min(at + tile, feed)
        parts += [gate_ref[:, at:end], up_ref[:, at:end], jnp.transpose(down_ref[at:end, :])]
    shard(gathers[0], parts)

    def one(m, carry):
        first.step(m)
        return carry

    lax.fori_loop(0, layers, one, 0)
    rows.start()
    enc.start()
    lax.fori_loop(layers, 2 * layers, one, 0)
    for gather in gathers:
        gather.send_z()

    def make_bias(n, carry):
        row = jnp.broadcast_to(bias_ref[pl.ds(n, 1), :], (tile, 2 * tile))
        turned = pltpu.roll(row, tile + 1, 1, stride=1, stride_axis=0)
        bias_s[n // blocks, n % blocks] = turned[:, :tile]
        return carry

    lax.fori_loop(0, 2 * blocks, make_bias, 0)
    rows.arrive()
    first.finish()
    keep = pltpu.make_async_copy(win_s, win_out, win_sem.at[0])
    keep.start()
    rows.finish()
    rows_out[...] = rows_land[...]
    width = rows_ref.shape[2]
    for layer in range(layers):
        v = rows_land[layer].reshape(-1, width).astype(f32)
        at = slice(layer * v.shape[0], (layer + 1) * v.shape[0])
        norm_s[at, :] = (v * norm_scale(v) * gain_ref[...]).astype(bf16)
    for kv in range(sources):
        columns = win_s[..., 4 * head * kv : 4 * head * (kv + 1)].reshape(-1, 4 * head)
        qkv_s[kv] = matmul(norm_s[...], columns).astype(bf16)
    heads.start()
    for gather in gathers:
        gather.send_plane()
    enc.arrive()
    plane.start()
    cot.start()
    heads.arrive()
    unpack_pair(came, q_s, k_s, v_s, score_scale)
    kept_ref[...] = came[...]

    def row_block(turn, carry):
        i = blocks - 1 - turn
        at = pl.ds(pl.multiple_of(i * tile, tile), tile)
        found = []
        for h in range(2):
            query = q_s[h, at, :]

            def score_step(j, top):
                key = k_s[pl.ds(pl.multiple_of(j * tile, tile), tile), :]
                score = dot_t(query, key) + bias_s[h, i - j]
                score_s[j] = score
                return jnp.maximum(top, jnp.maximum(score[:, :128], score[:, 128:]))

            top = lax.fori_loop(
                0, i + 1, score_step, jnp.full((tile, 128), masked_score, jnp.float32)
            )
            top = jnp.max(top, axis=1, keepdims=True)

            def share_step(j, state):
                total, summed = state
                share = jnp.exp(score_s[j] - top)
                value = v_s[pl.ds(pl.multiple_of(j * tile, tile), tile), :]
                summed = summed + jnp.dot(
                    share.astype(jnp.bfloat16), value, preferred_element_type=jnp.float32
                )
                return (total + share[:, :128] + share[:, 128:], summed)

            total, summed = lax.fori_loop(
                0,
                i + 1,
                share_step,
                (jnp.zeros((tile, 128), jnp.float32), jnp.zeros((tile, head), jnp.float32)),
            )
            total = jnp.sum(total, axis=1, keepdims=True)
            found.append(summed / total)
            log_total = jnp.broadcast_to(top + jnp.log(total), (tile, 128))
            total_ref[pl.ds(h * blocks + i, 1), :] = jnp.transpose(log_total)[0:1, :]
        both = jnp.concatenate(found, axis=1)
        full_ref[at, :] = both
        both = both.astype(jnp.bfloat16)
        for part in range(tile // 128):
            block = i * (tile // 128) + part
            low_s[block] = both[part * 128 : (part + 1) * 128]

        for gather in gathers:
            gather.step(turn)
        for part in range(tile // 128):
            block = i * (tile // 128) + part

            @pl.when(block % sources == spot)
            def _():
                landed[spot, block // sources] = low_s[block]

            @pl.when(block % sources != spot)
            def _():
                hand_back(block).start()

        return carry

    def hand_back(block):
        return pltpu.make_async_remote_copy(
            src_ref=low_s.at[block],
            dst_ref=landed.at[spot, block // sources],
            send_sem=out_send.at[block],
            recv_sem=out_recv.at[spot, block // sources],
            **to_chip(rank - spot + block % sources),
        )

    lax.fori_loop(0, blocks // 2, row_block, 0)
    plane.arrive()
    cot.arrive()
    lax.fori_loop(blocks // 2, blocks, row_block, 0)
    for o in range(3):
        chip, there = peers[o]
        for turn in range(layers):
            pltpu.make_async_remote_copy(
                src_ref=low_s.at[0],
                dst_ref=landed.at[there, turn],
                send_sem=out_send.at[0],
                recv_sem=out_recv.at[there, turn],
                **to_chip(chip),
            ).wait_recv()
    for source in range(sources):
        for turn in range(layers):
            low_ref[turn * 128 : (turn + 1) * 128, source * 128 : (source + 1) * 128] = landed[
                source, turn
            ]
    heads.finish()
    cot.finish()
    cot_out[...] = cot_land[...]
    enc.finish()
    plane.finish()
    enc_out[...] = enc_all[...]
    keep.wait()
    for block in range(sources * layers):

        @pl.when(block % sources != spot)
        def _():
            hand_back(block).wait_send()

    for gather in gathers:
        gather.finish()


def begin(scale, layers, inputs, encoder, cotangent, gain, bias, *shards):
    f32, bf16 = jnp.float32, jnp.bfloat16
    own, width = inputs.shape[1:]
    enc_own = encoder.shape[1]
    rows = 2 * layers * own
    head = round(scale**-2)
    sources = 4
    length = sources * rows
    blocks = length // tile
    cols = sum(shard.shape[1] for shard in shards[:3])
    rest_cols = 4 * shards[3].shape[0]
    feed_cols = 3 * shards[8].shape[1]
    rows_shape, enc_shape = (layers, 2, own, width), (4, 2, layers, enc_own, width)
    qkv_shape = (sources, rows, 4 * head)
    chips = (layers, 2, 2, 2, 2, 16)
    vmem, anywhere = pl.BlockSpec(memory_space=pltpu.VMEM), pl.BlockSpec(memory_space=pl.ANY)
    return pl.pallas_call(
        functools.partial(begin_kernel, scale, layers),
        name="begin",
        out_shape=(
            jax.ShapeDtypeStruct(rows_shape, bf16),
            jax.ShapeDtypeStruct(enc_shape, bf16),
            jax.ShapeDtypeStruct(rows_shape, bf16),
            jax.ShapeDtypeStruct(qkv_shape, bf16),
            jax.ShapeDtypeStruct((rows, sources * 2 * head), bf16),
            jax.ShapeDtypeStruct((length, 2 * head), f32),
            jax.ShapeDtypeStruct((2 * blocks, tile), f32),
            jax.ShapeDtypeStruct((*chips, cols), bf16),
            jax.ShapeDtypeStruct((*chips, rest_cols), bf16),
            jax.ShapeDtypeStruct((*chips, feed_cols), bf16),
        ),
        in_specs=[vmem] * 16,
        out_specs=(vmem,) * 7 + (anywhere,) * 3,
        scratch_shapes=[
            pltpu.VMEM(rows_shape, bf16),
            pltpu.VMEM((layers, enc_own, width), bf16),
            pltpu.VMEM(enc_shape, bf16),
            pltpu.VMEM(rows_shape, bf16),
            pltpu.VMEM((*chips, cols), bf16),
            pltpu.VMEM((rows, width), bf16),
            pltpu.VMEM(qkv_shape, bf16),
            pltpu.VMEM(qkv_shape, bf16),
            pltpu.VMEM((sources, layers, 128, 2 * head), bf16),
            pltpu.VMEM((length // 128, 128, 2 * head), bf16),
            pltpu.VMEM((2, length, head), bf16),
            pltpu.VMEM((length, head), bf16),
            pltpu.VMEM((length, head), bf16),
            pltpu.VMEM((2, blocks, tile, tile), f32),
            pltpu.VMEM((blocks, tile, tile), f32),
            dma((2, layers)),
            dma((2, layers)),
            dma((2, layers)),
            dma((2, 3)),
            dma((2, 4)),
            dma((2, layers)),
            dma((2, layers)),
            dma((2, 3)),
            dma((length // 128,)),
            dma((sources, layers)),
            dma((1,)),
            *gather_scratch(layers, cols),
            *gather_scratch(layers, rest_cols),
            *gather_scratch(layers, feed_cols),
        ],
        compiler_params=pltpu.CompilerParams(
            collective_id=6, has_side_effects=True, vmem_limit_bytes=56 << 20
        ),
    )(inputs, encoder, cotangent, gain, bias, *shards)

def attend_backward_kernel(
    score_scale,
    layers,
    kept_ref,
    ctx_ref,
    full_ref,
    total_ref,
    bias_ref,
    kv_ref,
    rows_ref,
    grads_ref,
    feed_ref,
    got_x,
    got_y,
    out_ref,
    sums_ref,
    kv_out,
    rows_out,
    out_grad,
    cq_grad,
    ck_grad,
    cv_grad,
    co_grad,
    gate_grad,
    up_grad,
    down_grad,
    ctx_land,
    kv_land,
    rows_land,
    out_s,
    out_land,
    q_s,
    k_s,
    v_s,
    g_s,
    bias_s,
    sum_s,
    delta_s,
    dq_s,
    dk_s,
    dv_s,
    ctx_sem,
    kv_sem,
    rows_z,
    out_sem,
    sum_a,
    sum_b,
    *sum_refs,
):
    blocks = bias_s.shape[1]
    sources, rows, _ = kept_ref.shape
    head = k_s.shape[1]
    half = len(sum_refs) // 2
    sums = (
        GradSum(layers, feed_ref, (got_x, got_y), sum_b, *sum_refs[half:]),
        GradSum(layers, grads_ref, (), sum_a, *sum_refs[:half]),
    )
    context = PlaneSwap(layers, ctx_ref, ctx_land, ctx_sem)
    cross = PlaneSwap(layers, kv_ref, kv_land, kv_sem)
    ended = Column(layers, rows_ref, rows_land, rows_z)
    back = PlaneSwap(layers, out_s, out_land, out_sem)
    for grads in sums:
        grads.start()
    greet(layers)
    context.start()
    for grads in sums:
        grads.send_first(0)
    cross.start()
    ended.start()
    unpack_pair(kept_ref, q_s, k_s, v_s, score_scale)

    def make_bias(n, carry):
        row = jnp.broadcast_to(bias_ref[pl.ds(n, 1), :], (tile, 2 * tile))
        turned = pltpu.roll(row, 0, 1, stride=1, stride_axis=0)
        bias_s[n // blocks, n % blocks] = turned[:, tile:]
        return carry

    lax.fori_loop(0, 2 * blocks, make_bias, 0)
    sum_s[...] = jnp.zeros_like(sum_s)
    dq_s[...] = jnp.zeros_like(dq_s)
    dk_s[...] = jnp.zeros_like(dk_s)
    dv_s[...] = jnp.zeros_like(dv_s)
    context.arrive()
    for block in range(rows // 128 * sources):
        source, turn = block % sources, block // sources
        part = ctx_land[source, turn * 128 : (turn + 1) * 128, :]
        at = slice(block * 128, (block + 1) * 128)
        g_s[0, at, :] = part[:, :head]
        g_s[1, at, :] = part[:, head:]

    def make_delta(i, carry):
        at = pl.ds(pl.multiple_of(i * tile, tile), tile)
        for h in range(2):
            product = g_s[h, at, :].astype(jnp.float32) * full_ref[at, h * head : (h + 1) * head]
            column = jnp.broadcast_to(jnp.sum(product, axis=1, keepdims=True), (tile, 128))
            delta_s[pl.ds(h * blocks + i, 1), :] = jnp.transpose(column)[0:1, :]
        return carry

    lax.fori_loop(0, blocks, make_delta, 0)

    def one_tile(n, carry):
        line, at = n // blocks, n % blocks
        first = at < blocks - line
        d = jnp.where(first, line, blocks - line)
        i = jnp.where(first, at + line, at)
        at_q = pl.ds(pl.multiple_of(i * tile, tile), tile)
        at_k = pl.ds(pl.multiple_of((i - d) * tile, tile), tile)
        key, value = k_s[at_k, :], v_s[at_k, :]
        for h in range(2):
            query, grad = q_s[h, at_q, :], g_s[h, at_q, :]
            score = dot_t(key, query) + bias_s[h, d]
            share = jnp.exp(score - total_ref[pl.ds(h * blocks + i, 1), :])
            pull = dot_t(value, grad)
            grad_score = share * (pull - delta_s[pl.ds(h * blocks + i, 1), :])
            sum_s[h, d] += grad_score
            share_low = share.astype(jnp.bfloat16)
            grad_low = grad_score.astype(jnp.bfloat16)
            dv_s[at_k, :] += jnp.dot(share_low, grad, preferred_element_type=jnp.float32)
            dk_s[at_k, :] += jnp.dot(grad_low, query, preferred_element_type=jnp.float32)
            dq_s[h, at_q, :] += dot_first(grad_low, key)
        return carry

    tiles = blocks * (blocks + 1) // 2
    busy = 6

    def work(m, carry):
        for grads in sums:
            grads.send_first(m)
        low = (m - 1) * tiles // busy
        lax.fori_loop(low, m * tiles // busy, one_tile, 0)
        for grads in sums:
            grads.advance(m)
        return carry

    lax.fori_loop(1, 1 + busy, work, 0)

    for block in range(rows // 128 * sources):
        source, turn = block % sources, block // sources
        at = slice(block * 128, (block + 1) * 128)
        out_s[source, turn * 128 : (turn + 1) * 128, :] = jnp.concatenate(
            [dq_s[0, at, :] * score_scale, dq_s[1, at, :] * score_scale, dk_s[at, :], dv_s[at, :]],
            axis=1,
        ).astype(jnp.bfloat16)
    back.start()

    row_at = lax.broadcasted_iota(jnp.int32, (tile, tile), 0)
    col_at = lax.broadcasted_iota(jnp.int32, (tile, tile), 1)
    turn_rows = (row_at + col_at == tile - 1).astype(jnp.float32)

    def make_sums(n, carry):
        turned = jnp.dot(
            turn_rows,
            sum_s[n // blocks, n % blocks],
            precision=highest,
            preferred_element_type=jnp.float32,
        )
        wide = jnp.concatenate([turned, jnp.zeros_like(turned)], axis=1)
        wide = pltpu.roll(wide, 0, 1, stride=1, stride_axis=0)
        sums_ref[pl.ds(n, 1), :] = jnp.sum(wide, axis=0, keepdims=True)
        return carry

    lax.fori_loop(0, 2 * blocks, make_sums, 0)
    cross.arrive()
    both = kv_land[0].astype(jnp.float32)
    for source in range(1, sources):
        both = both + kv_land[source].astype(jnp.float32)
    kv_out[...] = both.astype(jnp.bfloat16)
    ended.arrive()
    rows_out[...] = rows_land[...]

    def rest(m, carry):
        for grads in sums:
            grads.send_first(m)
        for grads in sums:
            grads.advance(m)
        return carry

    lax.fori_loop(1 + busy, sum_steps(layers), rest, 0)
    back.arrive()
    wide = 4 * head
    for source in range(sources):
        out_ref[:, source * wide : (source + 1) * wide] = out_land[source]
    whole = sum_a[...].reshape(64, sum_a.shape[-1])
    at = 0
    for ref, turned in (
        (out_grad, True),
        (cq_grad, False),
        (ck_grad, False),
        (cv_grad, False),
        (co_grad, True),
    ):
        count = ref.shape[0] if turned else ref.shape[1]
        part = whole[:, at : at + count]
        ref[...] = jnp.transpose(part) if turned else part
        at += count
    whole = sum_b[...].reshape(64, sum_b.shape[-1])
    feed = gate_grad.shape[1]
    for at in range(0, feed, tile):
        units = min(tile, feed - at)
        gate_grad[:, at : at + units] = whole[:, 3 * at : 3 * at + units]
        up_grad[:, at : at + units] = whole[:, 3 * at + units : 3 * at + 2 * units]
        down_grad[at : at + units, :] = jnp.transpose(
            whole[:, 3 * at + 2 * units : 3 * at + 3 * units]
        )
    context.finish()
    cross.finish()
    ended.finish()
    back.finish()
    for grads in sums:
        grads.finish()


def attend_backward(
    scale, layers, feed, kept, ctx_grad, full, total, bias, kv, layer_rows, grads, feed_grads, got
):
    f32, bf16 = jnp.float32, jnp.bfloat16
    sources, rows, wide = kept.shape
    head = wide // 4
    length = sources * rows
    blocks = length // tile
    cols, feed_cols = grads.shape[1], feed_grads.shape[1]
    chips = (layers, 2, 2, 2, 2, 16)
    vmem, anywhere = pl.BlockSpec(memory_space=pltpu.VMEM), pl.BlockSpec(memory_space=pl.ANY)
    half = cols // 4
    return pl.pallas_call(
        functools.partial(attend_backward_kernel, scale, layers),
        name="attend_backward",
        out_shape=(
            jax.ShapeDtypeStruct((rows, sources * wide), bf16),
            jax.ShapeDtypeStruct((2 * blocks, 2 * tile), f32),
            jax.ShapeDtypeStruct(kv.shape[1:], bf16),
            jax.ShapeDtypeStruct(layer_rows.shape, bf16),
            jax.ShapeDtypeStruct((half, 64), f32),
            jax.ShapeDtypeStruct((64, half), f32),
            jax.ShapeDtypeStruct((64, half // 2), f32),
            jax.ShapeDtypeStruct((64, half // 2), f32),
            jax.ShapeDtypeStruct((half, 64), f32),
            jax.ShapeDtypeStruct((64, feed), f32),
            jax.ShapeDtypeStruct((64, feed), f32),
            jax.ShapeDtypeStruct((feed, 64), f32),
        ),
        in_specs=[vmem] * 7 + [anywhere] * 4,
        out_specs=(vmem,) * 12,
        scratch_shapes=[
            pltpu.VMEM(ctx_grad.shape, bf16),
            pltpu.VMEM(kv.shape, bf16),
            pltpu.VMEM(layer_rows.shape, bf16),
            pltpu.VMEM(kept.shape, bf16),
            pltpu.VMEM(kept.shape, bf16),
            pltpu.VMEM((2, length, head), bf16),
            pltpu.VMEM((length, head), bf16),
            pltpu.VMEM((length, head), bf16),
            pltpu.VMEM((2, length, head), bf16),
            pltpu.VMEM((2, blocks, tile, tile), f32),
            pltpu.VMEM((2, blocks, tile, tile), f32),
            pltpu.VMEM((2 * blocks, tile), f32),
            pltpu.VMEM((2, length, head), f32),
            pltpu.VMEM((length, head), f32),
            pltpu.VMEM((length, head), f32),
            dma((2, 3)),
            dma((2, 3)),
            dma((2, layers)),
            dma((2, 3)),
            pltpu.VMEM((2, 2, 16, cols), f32),
            pltpu.VMEM((2, 2, 16, feed_cols), f32),
            *sum_scratch(layers, cols),
            *sum_scratch(layers, feed_cols),
        ],
        compiler_params=pltpu.CompilerParams(
            collective_id=8, has_side_effects=True, vmem_limit_bytes=62 << 20
        ),
    )(
        kept,
        ctx_grad,
        full,
        total,
        bias,
        kv,
        layer_rows,
        grads.reshape(*chips, cols),
        feed_grads.reshape(*chips, feed_cols),
        *got,
    )

def norm_scale(v):
    return lax.rsqrt(jnp.mean(v * v, axis=-1, keepdims=True) + norm_eps)


def norm_pull(v, gain, grad):
    scale = norm_scale(v)
    turned = v * scale
    pulled = grad * gain
    mean = jnp.mean(pulled * turned, axis=-1, keepdims=True)
    return scale * (pulled - turned * mean), jnp.sum(grad * turned, axis=0, keepdims=True)


def middle_kernel(
    score_scale,
    layers,
    feed,
    ctx_ref,
    x_ref,
    cot_ref,
    enc_ref,
    wa_ref,
    gains_ref,
    wf_ref,
    layer_out,
    grad_out,
    gctx_out,
    kv_out,
    ga_out,
    gain_out,
    gb_out,
    got_x,
    got_y,
    w_s,
    gb_s,
    after_self,
    after_cross,
    nc_s,
    nf_s,
    nft_s,
    cott_s,
    down_s,
    dx_s,
    send_s,
    land_s,
    half_s,
    q_s,
    k_s,
    v_s,
    g_s,
    pair_s,
    cc_s,
    dq_s,
    dk_s,
    low_s,
    w_load,
    w_send,
    w_recv,
    g_send,
    g_recv,
    g_store,
    swap_sem,
):
    f32, bf16 = jnp.float32, jnp.bfloat16
    rank, z, y, x = chip_place(layers)
    core = lax.axis_index(tensor_axis)
    x_chip, y_chip = rank + 1 - 2 * x, rank + 2 - 4 * y
    rows, width = x_ref.shape
    heads, _, head = q_s.shape
    kv_heads = heads // 2
    wide = heads * head
    enc_rows = enc_ref.shape[0]
    block = send_s.shape[2]
    chunks = rows // block
    at_out, at_cq, at_ck = 0, wide, 2 * wide
    at_cv, at_co = at_ck + wide // 2, at_ck + wide
    row_chip = 64

    def row_of(layer, at_y, at_x, colour=0):
        return pl.multiple_of(((layer * 2 + at_y) * 2 + at_x) * row_chip + 32 * colour, 32)

    def loads(n, cols):
        copies = []
        for layer in range(layers):
            for start, count in (
                (row_of(layer, y, x), 64),
                (row_of(layer, y, 1 - x, 0), 32),
                (row_of(layer, 1 - y, x, 1), 32),
            ):
                at = (pl.ds(start, count), cols)
                copies.append(pltpu.make_async_copy(wf_ref.at[at], w_s.at[at], w_load.at[n]))
        return copies

    def weights_hop(n, cols, layer, along_y, which):
        spot = row_of(layer, y, which, 0) if along_y else row_of(layer, which, x, 1)
        at = (pl.ds(spot, 32), cols)
        return pltpu.make_async_remote_copy(
            src_ref=wf_ref.at[at],
            dst_ref=w_s.at[at],
            send_sem=w_send.at[int(along_y), n],
            recv_sem=w_recv.at[int(along_y), n],
            **to_chip(y_chip if along_y else x_chip),
        )

    def weights_all(n, cols, along_y):
        at = (pl.ds(0, 64 * layers), cols)
        return pltpu.make_async_remote_copy(
            src_ref=wf_ref.at[at],
            dst_ref=w_s.at[at],
            send_sem=w_send.at[int(along_y), n],
            recv_sem=w_recv.at[int(along_y), n],
            **to_chip(y_chip if along_y else x_chip),
        )

    def grads_hop(n, cols, layer, along_y, which):
        spot = row_of(layer, 1 - y, which, 1) if along_y else row_of(layer, which, 1 - x, 0)
        return pltpu.make_async_remote_copy(
            src_ref=gb_s.at[pl.ds(spot, 32), cols],
            dst_ref=(got_y if along_y else got_x).at[layer, which, :, cols],
            send_sem=g_send.at[int(along_y), n],
            recv_sem=g_recv.at[int(along_y), n],
            **to_chip(y_chip if along_y else x_chip),
        )

    def grads_all(n, cols, along_y):
        return pltpu.make_async_remote_copy(
            src_ref=gb_s.at[pl.ds(0, 64 * layers), cols],
            dst_ref=(got_y if along_y else got_x).at[:, :, :, cols],
            send_sem=g_send.at[int(along_y), n],
            recv_sem=g_recv.at[int(along_y), n],
            **to_chip(y_chip if along_y else x_chip),
        )

    hops = [(layer, a, w) for layer in range(layers) for w in range(2) for a in (True, False)]
    full_blocks, last = feed // tile, feed % tile

    def each_block(work):
        def one(n, carry):
            work(n, pl.ds(pl.multiple_of(n * 3 * tile, 3 * tile), 3 * tile), tile)
            return carry

        lax.fori_loop(0, full_blocks, one, 0)
        if last:
            work(full_blocks, pl.ds(full_blocks * 3 * tile, 3 * last), last)

    def bring(n, cols, units):
        for hop in hops:
            weights_hop(n, cols, *hop).start()
        for copy in loads(n, cols):
            copy.start()

    greet(layers)
    each_block(bring)

    def swap(n, chunk):
        half = n == 3
        return pltpu.make_async_remote_copy(
            src_ref=half_s.at[0] if half else send_s.at[slots[n], chunk],
            dst_ref=half_s.at[1] if half else land_s.at[slots[n], chunk],
            send_sem=swap_sem.at[0, n, chunk],
            recv_sem=swap_sem.at[1, n, chunk],
            **to_core(1 - core),
        )

    slots = (0, 1, 0, None, 1)

    def span(chunk):
        return pl.ds(pl.multiple_of(chunk * block, block), block)

    def send_parts(n, part_of):
        def one(chunk, carry):
            send_s[slots[n], chunk] = part_of(span(chunk)).astype(bf16)
            swap(n, chunk).start()
            return carry

        lax.fori_loop(0, chunks, one, 0)

    def take_parts(n, use):
        def one(chunk, carry):
            swap(n, chunk).wait()
            both = send_s[slots[n], chunk].astype(f32) + land_s[slots[n], chunk].astype(f32)
            use(span(chunk), both)
            return carry

        lax.fori_loop(0, chunks, one, 0)

    cross_gain, feed_gain = gains_ref[0:1, :], gains_ref[1:2, :]

    send_parts(0, lambda at: dot_t(ctx_ref[at, :], wa_ref[:, at_out : at_out + wide]))
    key_value = matmul(enc_ref[...], wa_ref[:, at_ck : at_ck + wide]).astype(bf16)
    for kv in range(kv_heads):
        k_s[kv] = key_value[:, kv * head : (kv + 1) * head]
        v_s[kv] = key_value[:, wide // 2 + kv * head : wide // 2 + (kv + 1) * head]
    cott_s[...] = jnp.transpose(cot_ref[...])

    def enter_cross(at, both):
        v = x_ref[at, :].astype(f32) + both
        after_self[at, :] = v
        nc_s[at, :] = (v * norm_scale(v) * cross_gain).astype(bf16)
        query = matmul(nc_s[at, :], wa_ref[:, at_cq : at_cq + wide]).astype(bf16)
        for h in range(heads):
            q_s[h, at, :] = (query[:, h * head : (h + 1) * head] * score_scale).astype(bf16)

    take_parts(0, enter_cross)

    def attend(kv, carry):
        key, value = k_s[kv], v_s[kv]
        for chunk in range(chunks):
            at = slice(chunk * block, (chunk + 1) * block)
            found = []
            for h in range(2):
                score = dot_t(q_s[2 * kv + h, at, :], key)
                share = jnp.exp(score - jnp.max(score, axis=1, keepdims=True))
                total = jnp.sum(share, axis=1, keepdims=True)
                found.append(matmul(share.astype(bf16), value) / total)
            pair_s[kv, at, :] = jnp.concatenate(found, axis=1).astype(bf16)
        return carry

    lax.fori_loop(0, kv_heads, attend, 0)
    for kv in range(kv_heads):
        cc_s[:, 2 * kv * head : 2 * (kv + 1) * head] = pair_s[kv]
    send_parts(1, lambda at: dot_t(cc_s[at, :], wa_ref[:, at_co : at_co + wide]))

    def enter_feed(at, both):
        v = after_self[at, :] + both
        after_cross[at, :] = v
        nf_s[at, :] = (v * norm_scale(v) * feed_gain).astype(bf16)

    take_parts(1, enter_feed)
    nft_s[...] = jnp.transpose(nf_s[...])

    down_s[...] = jnp.zeros_like(down_s)
    dx_s[...] = jnp.zeros_like(dx_s)
    slope = math.sqrt(2.0 / math.pi)

    def feed_block(n, cols, units):
        have = (pl.ds(0, 128 * layers), cols)
        pltpu.make_async_copy(wf_ref.at[have], w_s.at[have], w_load.at[n]).wait()
        for along_y in (True, False):
            weights_all(n, cols, along_y).wait_recv()
        pair = w_s[:, pl.ds(cols.start, 2 * units)]
        down = w_s[:, pl.ds(cols.start + 2 * units, units)]
        both = matmul(nf_s[...], pair)
        gate, up = both[:, :units], both[:, units:]
        square = gate * gate
        bend = jnp.tanh(slope * (gate + 0.044715 * square * gate))
        bent = 0.5 * gate * (1.0 + bend)
        pull = 0.5 * (1.0 + bend) + 0.5 * gate * (1.0 - bend * bend) * slope * (
            1.0 + 3.0 * 0.044715 * square
        )
        hidden = (bent * up).astype(bf16)
        down_s[...] += dot_t(hidden, down)
        grad = matmul(cot_ref[...], down)
        grads = jnp.concatenate([grad * up * pull, grad * bent], axis=1).astype(bf16)
        dx_s[...] += dot_t(grads, pair)
        gb_s[:, pl.ds(cols.start, 2 * units)] = matmul(nft_s[...], grads).astype(bf16)
        gb_s[:, pl.ds(cols.start + 2 * units, units)] = matmul(cott_s[...], hidden).astype(bf16)
        for hop in hops:
            grads_hop(n, cols, *hop).start()

    each_block(feed_block)

    send_parts(2, lambda at: dx_s[at, :])
    store = pltpu.make_async_copy(gb_s, gb_out, g_store.at[0])
    store.start()
    own = rows // (2 * layers)

    def halves(ref, which):
        return [ref[pl.ds((2 * layer + which) * own, own), :] for layer in range(layers)]

    low = jnp.concatenate(halves(down_s, 1 - core), axis=0).astype(bf16)
    half_s[0] = low
    swap(3, 0).start()

    def leave_feed(at, both):
        grad, gain = norm_pull(after_cross[at, :], feed_gain, both)
        dx_s[at, :] = cot_ref[at, :].astype(f32) + grad
        low = dx_s[at, :].astype(bf16)
        low_s[at, :] = low
        gain_out[1:2, :] += gain
        context = matmul(low, wa_ref[:, at_co : at_co + wide]).astype(bf16)
        for h in range(heads):
            g_s[h, at, :] = context[:, h * head : (h + 1) * head]

    gain_out[...] = jnp.zeros_like(gain_out)
    take_parts(2, leave_feed)
    swap(3, 0).wait()
    mine = halves(after_cross, core)
    down = halves(down_s, core)
    for layer in range(layers):
        came = half_s[1, layer * own : (layer + 1) * own, :].astype(f32)
        layer_out[layer] = (mine[layer] + (down[layer].astype(bf16).astype(f32) + came)).astype(bf16)

    ga_out[:, at_co : at_co + wide] = dot_first(low_s[...], cc_s[...]).astype(bf16)

    def attend_back(kv, carry):
        key, value = k_s[kv], v_s[kv]
        key_grad = jnp.zeros((enc_rows, head), f32)
        value_grad = jnp.zeros((enc_rows, head), f32)
        for chunk in range(chunks):
            at = slice(chunk * block, (chunk + 1) * block)
            found = []
            for h in range(2):
                query, grad = q_s[2 * kv + h, at, :], g_s[2 * kv + h, at, :]
                score = dot_t(key, query)
                share = jnp.exp(score - jnp.max(score, axis=0, keepdims=True))
                share = share * (1.0 / jnp.sum(share, axis=0, keepdims=True))
                pull = dot_t(value, grad)
                delta = jnp.sum(share * pull, axis=0, keepdims=True)
                grad_low = (share * (pull - delta)).astype(bf16)
                found.append(dot_first(grad_low, key) * score_scale)
                key_grad = key_grad + matmul(grad_low, query)
                value_grad = value_grad + matmul(share.astype(bf16), grad)
            pair_s[kv, at, :] = jnp.concatenate(found, axis=1).astype(bf16)
        dk_s[0, kv] = key_grad.astype(bf16)
        dk_s[1, kv] = value_grad.astype(bf16)
        return carry

    lax.fori_loop(0, kv_heads, attend_back, 0)
    for kv in range(kv_heads):
        dq_s[:, 2 * kv * head : 2 * (kv + 1) * head] = pair_s[kv]
    send_parts(4, lambda at: dot_t(dq_s[at, :], wa_ref[:, at_cq : at_cq + wide]))
    for n in range(2):
        kv_out[:, n * wide // 2 : (n + 1) * wide // 2] = jnp.concatenate(
            [dk_s[n, kv] for kv in range(kv_heads)], axis=1
        )
    ga_out[:, at_cq : at_cq + wide] = dot_first(nc_s[...], dq_s[...]).astype(bf16)
    ga_out[:, at_ck : at_ck + wide] = dot_first(enc_ref[...], kv_out[...]).astype(bf16)

    def leave_cross(at, both):
        grad, gain = norm_pull(after_self[at, :], cross_gain, both)
        dx_s[at, :] += grad
        low = dx_s[at, :].astype(bf16)
        low_s[at, :] = low
        gain_out[0:1, :] += gain
        context = matmul(low, wa_ref[:, at_out : at_out + wide]).astype(bf16)
        for q in range(4):
            gctx_out[q, at, :] = context[:, q * wide // 4 : (q + 1) * wide // 4]

    take_parts(4, leave_cross)
    ga_out[:, at_out : at_out + wide] = dot_first(low_s[...], ctx_ref[...]).astype(bf16)
    mine = halves(dx_s, core)
    for layer in range(layers):
        grad_out[layer] = mine[layer]

    store.wait()

    def settle(n, cols, units):
        for along_y in (True, False):
            weights_all(n, cols, along_y).wait_send()
            grads_all(n, cols, along_y).wait()

    each_block(settle)


def middle(scale, layers, feed, context, x_low, cot, enc, weights, gains, feed_whole):
    f32, bf16 = jnp.float32, jnp.bfloat16
    rows, width = x_low.shape
    wide = context.shape[1]
    head = round(scale**-2)
    heads = wide // head
    own = rows // (2 * layers)
    cols = feed_whole.shape[1]
    block = rows // 2
    vmem, anywhere = pl.BlockSpec(memory_space=pltpu.VMEM), pl.BlockSpec(memory_space=pl.ANY)
    got = jax.ShapeDtypeStruct((layers, 2, 32, cols), bf16)
    return pl.pallas_call(
        functools.partial(middle_kernel, scale, layers, feed),
        name="middle",
        out_shape=(
            jax.ShapeDtypeStruct((layers, own, width), bf16),
            jax.ShapeDtypeStruct((layers, own, width), f32),
            jax.ShapeDtypeStruct((4, rows, wide // 4), bf16),
            jax.ShapeDtypeStruct((enc.shape[0], wide), bf16),
            jax.ShapeDtypeStruct((width, weights.shape[1]), bf16),
            jax.ShapeDtypeStruct((2, width), f32),
            jax.ShapeDtypeStruct((width, cols), bf16),
            got,
            got,
        ),
        in_specs=[vmem] * 6 + [anywhere],
        out_specs=(vmem,) * 6 + (anywhere,) * 3,
        scratch_shapes=[
            pltpu.VMEM((width, cols), bf16),
            pltpu.VMEM((width, cols), bf16),
            pltpu.VMEM((rows, width), f32),
            pltpu.VMEM((rows, width), f32),
            pltpu.VMEM((rows, width), bf16),
            pltpu.VMEM((rows, width), bf16),
            pltpu.VMEM((width, rows), bf16),
            pltpu.VMEM((width, rows), bf16),
            pltpu.VMEM((rows, width), f32),
            pltpu.VMEM((rows, width), f32),
            pltpu.VMEM((2, 2, block, width), bf16),
            pltpu.VMEM((2, 2, block, width), bf16),
            pltpu.VMEM((2, rows // 2, width), bf16),
            pltpu.VMEM((heads, rows, head), bf16),
            pltpu.VMEM((heads // 2, enc.shape[0], head), bf16),
            pltpu.VMEM((heads // 2, enc.shape[0], head), bf16),
            pltpu.VMEM((heads, rows, head), bf16),
            pltpu.VMEM((heads // 2, rows, 2 * head), bf16),
            pltpu.VMEM((rows, wide), bf16),
            pltpu.VMEM((rows, wide), bf16),
            pltpu.VMEM((2, heads // 2, enc.shape[0], head), bf16),
            pltpu.VMEM((rows, width), bf16),
            dma((pl.cdiv(feed, tile),)),
            dma((2, pl.cdiv(feed, tile))),
            dma((2, pl.cdiv(feed, tile))),
            dma((2, pl.cdiv(feed, tile))),
            dma((2, pl.cdiv(feed, tile))),
            dma((1,)),
            dma((2, 5, 2)),
        ],
        compiler_params=pltpu.CompilerParams(
            collective_id=9, has_side_effects=True, vmem_limit_bytes=67043328
        ),
    )(context, x_low, cot, enc, weights, gains, feed_whole)

def dot_t(left, right):
    return lax.dot_general(
        left, right, (((1,), (1,)), ((), ())), preferred_element_type=jnp.float32
    )


def dot_first(left, right):
    return lax.dot_general(
        left, right, (((0,), (0,)), ((), ())), preferred_element_type=jnp.float32
    )


def unpack_pair(qkv_ref, q_s, k_s, v_s, score_scale):
    sources, rows, _ = qkv_ref.shape
    blocks = rows // 128 * sources
    head = k_s.shape[1]
    for block in range(blocks):
        source, turn = block % sources, block // sources
        tile = qkv_ref[source, turn * 128 : (turn + 1) * 128, :]
        at = slice(block * 128, (block + 1) * 128)
        q_s[0, at, :] = (tile[:, :head] * score_scale).astype(jnp.bfloat16)
        q_s[1, at, :] = (tile[:, head : 2 * head] * score_scale).astype(jnp.bfloat16)
        k_s[at, :] = tile[:, 2 * head : 3 * head]
        v_s[at, :] = tile[:, 3 * head :]


def by_heads(
    inputs,
    encoder_out,
    out_cotangent,
    bucket_ids,
    position_table,
    self_gain,
    self_query,
    self_key,
    self_value,
    self_output,
    cross_gain,
    cross_query,
    cross_key,
    cross_value,
    cross_output,
    feed_gain,
    gate_weight,
    up_weight,
    down_weight,
):
    f32, bf16 = jnp.float32, jnp.bfloat16
    batches, own, width = inputs.shape
    enc_own = encoder_out.shape[1]
    length = bucket_ids.shape[0]
    heads_all, buckets = position_table.shape
    fsdp = lax.axis_size(fsdp_axis)
    plane = fsdp // batches
    rank, core = lax.axis_index(fsdp_axis), lax.axis_index(tensor_axis)
    head = self_query.shape[1] // (heads_all // 2)
    kv_local = self_key.shape[1] // head
    scale = head ** (-0.5)
    blocks = length // tile
    rows = batches * 2 * own
    enc_rows = batches * 2 * enc_own
    feed = gate_weight.shape[1]
    kv_index = core * kv_local + rank % plane
    table_here = lax.dynamic_slice_in_dim(position_table, 2 * kv_index, 2, 0)
    bucket_range = jnp.arange(buckets, dtype=jnp.int32)
    lower = jnp.sum((bucket_ids[None, :] < bucket_range[:, None]).astype(jnp.int32), axis=1)
    upper = jnp.concatenate([lower[1:], jnp.full((1,), length, jnp.int32)])
    offsets = (
        tile * jnp.arange(blocks, dtype=jnp.int32)[:, None]
        + jnp.arange(2 * tile, dtype=jnp.int32)[None, :]
    ).reshape(-1)

    def bias_of(offset):
        hit = (offset[None] >= lower[:, None]) & (offset[None] < upper[:, None])
        value = jnp.dot(table_here, hit.astype(f32), precision=highest)
        return jnp.where(offset[None] >= 0, value, masked_score).reshape(2 * blocks, 2 * tile)

    down_steps = (
        tile * jnp.arange(blocks, dtype=jnp.int32)[:, None]
        + (tile - 1)
        - jnp.arange(2 * tile, dtype=jnp.int32)[None, :]
    ).reshape(-1)
    bias_down = bias_of(down_steps)
    bias_up = bias_of(offsets - tile)

    def swap_add(partial):
        low = partial.astype(bf16)
        return low.astype(f32) + swap_cores(low).astype(f32)

    x_low, enc_all, cot_low, qkv_here, context_low, context_full, log_total, *wholes = begin(
        scale,
        batches,
        inputs,
        encoder_out,
        out_cotangent,
        self_gain[None],
        bias_down,
        self_query,
        self_key,
        self_value,
        self_output,
        cross_query,
        cross_key,
        cross_value,
        cross_output,
        gate_weight,
        up_weight,
        down_weight,
    )
    x_low, enc_all = x_low.reshape(rows, width), enc_all.reshape(-1, width)
    in_full, rest_full, feed_full = [whole.reshape(width, -1) for whole in wholes]
    layer_rows, grad_after_self, grad_context, cross_kv, grads, mid_gains, feed_grads, *feed_got = (
        middle(
            scale,
            batches,
            feed,
            context_low,
            x_low,
            cot_low.reshape(rows, width),
            enc_all,
            rest_full,
            jnp.stack([cross_gain, feed_gain]),
            feed_full,
        )
    )
    feed_got = [came.reshape(batches, 2, 2, 16, -1) for came in feed_got]

    grad_qkv, diagonal_sums, kv_sum, layer_out, *most_grads = attend_backward(
        scale,
        batches,
        feed,
        qkv_here,
        grad_context,
        context_full,
        log_total,
        bias_up,
        cross_kv.reshape(plane, enc_rows, -1),
        layer_rows,
        grads,
        feed_grads,
        feed_got,
    )
    spread = offsets - (tile - 1)
    hit = ((spread[None] >= lower[:, None]) & (spread[None] < upper[:, None])).astype(f32)
    hit = jnp.transpose(hit.reshape(buckets, blocks, 2 * tile), (1, 0, 2))
    query_grad, key_grad, value_grad, input_grad, encoder_grad, table_sum, gain_sums = close_rows(
        batches,
        heads_all,
        grad_qkv,
        x_low,
        in_full,
        grad_after_self,
        kv_sum,
        self_gain[None],
        mid_gains,
        diagonal_sums,
        hit,
        rest_full,
    )
    out_grad, cq_grad, ck_grad, cv_grad, co_grad, gate_grad, up_grad, down_grad = most_grads
    return (
        layer_out,
        input_grad,
        encoder_grad,
        table_sum,
        gain_sums[0],
        query_grad,
        key_grad,
        value_grad,
        out_grad,
        gain_sums[1],
        cq_grad,
        ck_grad,
        cv_grad,
        co_grad,
        gain_sums[2],
        gate_grad,
        up_grad,
        down_grad,
    )


def on_either(*args):
    batches, kv_heads = args[0].shape[0], args[7].shape[1] * lax.axis_size(tensor_axis)
    head_size = args[6].shape[1] * lax.axis_size(tensor_axis) // args[4].shape[0]
    devices = lax.axis_size(fsdp_axis) * lax.axis_size(tensor_axis)
    if devices == batches * (kv_heads // head_size):
        return by_heads(*args)
    return on_device(*args)


def solution(mesh):
    placed = (
        P(None, (fsdp_axis, tensor_axis), None),
        P(None, (fsdp_axis, tensor_axis), None),
        P(None, (fsdp_axis, tensor_axis), None),
        P(),
        P(),
        P(),
        P(fsdp_axis, tensor_axis),
        P(fsdp_axis, tensor_axis),
        P(fsdp_axis, tensor_axis),
        P(tensor_axis, fsdp_axis),
        P(),
        P(fsdp_axis, tensor_axis),
        P(fsdp_axis, tensor_axis),
        P(fsdp_axis, tensor_axis),
        P(tensor_axis, fsdp_axis),
        P(),
        P(fsdp_axis, tensor_axis),
        P(fsdp_axis, tensor_axis),
        P(tensor_axis, fsdp_axis),
    )
    return jax.shard_map(
        on_either,
        mesh=mesh,
        in_specs=placed,
        out_specs=(
            P(None, (fsdp_axis, tensor_axis), None),
            P(None, (fsdp_axis, tensor_axis), None),
            P(None, (fsdp_axis, tensor_axis), None),
            P(),
            P(),
            P(fsdp_axis, tensor_axis),
            P(fsdp_axis, tensor_axis),
            P(fsdp_axis, tensor_axis),
            P(tensor_axis, fsdp_axis),
            P(),
            P(fsdp_axis, tensor_axis),
            P(fsdp_axis, tensor_axis),
            P(fsdp_axis, tensor_axis),
            P(tensor_axis, fsdp_axis),
            P(),
            P(fsdp_axis, tensor_axis),
            P(fsdp_axis, tensor_axis),
            P(tensor_axis, fsdp_axis),
        ),
        check_vma=False,
    )
```

```python
import functools
import math
import types

import jax
import jax.numpy as jnp
from jax import lax
from jax.experimental import pallas as pl
from jax.experimental.pallas import tpu as pltpu
from jax.sharding import PartitionSpec as P

norm_eps = 1e-06
masked_score = -1e30
highest = lax.Precision.HIGHEST
key_block_width = 256
tile = 256
fsdp_axis, tensor_axis = "fsdp", "tensor"


def matmul(left, right):
    return jnp.dot(left, right, preferred_element_type=jnp.float32)


def norm_rows(row_block, gain):
    return (
        row_block
        * lax.rsqrt(jnp.mean(row_block * row_block, axis=-1, keepdims=True) + norm_eps)
        * gain
    )


def gather_rows(row_block):
    return lax.all_gather(row_block, tensor_axis, axis=0, tiled=True)


def sum_rows(row_block):
    return lax.psum_scatter(
        row_block.astype(jnp.bfloat16), tensor_axis, scatter_dimension=0, tiled=True
    ).astype(jnp.float32)


def gather_weights(shards):
    (
        self_query,
        self_key,
        self_value,
        self_output,
        cross_query,
        cross_key,
        cross_value,
        cross_output,
        gate_weight,
        up_weight,
        down_weight,
    ) = shards
    inner = (
        lax.all_gather(self_query, fsdp_axis, axis=0, tiled=True),
        lax.all_gather(self_key, fsdp_axis, axis=0, tiled=True),
        lax.all_gather(self_value, fsdp_axis, axis=0, tiled=True),
        lax.all_gather(cross_query, fsdp_axis, axis=0, tiled=True),
        lax.all_gather(cross_key, fsdp_axis, axis=0, tiled=True),
        lax.all_gather(cross_value, fsdp_axis, axis=0, tiled=True),
        lax.all_gather(gate_weight, fsdp_axis, axis=0, tiled=True),
        lax.all_gather(up_weight, fsdp_axis, axis=0, tiled=True),
    )
    outer = (
        lax.all_gather(self_output, fsdp_axis, axis=1, tiled=True),
        lax.all_gather(cross_output, fsdp_axis, axis=1, tiled=True),
        lax.all_gather(down_weight, fsdp_axis, axis=1, tiled=True),
    )
    return (
        inner[0],
        inner[1],
        inner[2],
        outer[0],
        inner[3],
        inner[4],
        inner[5],
        outer[1],
        inner[6],
        inner[7],
        outer[2],
    )


def scatter_grads(grads_full):
    (
        self_query,
        self_key,
        self_value,
        self_output,
        cross_query,
        cross_key,
        cross_value,
        cross_output,
        gate_weight,
        up_weight,
        down_weight,
    ) = grads_full
    inner = (
        lax.psum_scatter(self_query, fsdp_axis, scatter_dimension=0, tiled=True),
        lax.psum_scatter(self_key, fsdp_axis, scatter_dimension=0, tiled=True),
        lax.psum_scatter(self_value, fsdp_axis, scatter_dimension=0, tiled=True),
        lax.psum_scatter(cross_query, fsdp_axis, scatter_dimension=0, tiled=True),
        lax.psum_scatter(cross_key, fsdp_axis, scatter_dimension=0, tiled=True),
        lax.psum_scatter(cross_value, fsdp_axis, scatter_dimension=0, tiled=True),
        lax.psum_scatter(gate_weight, fsdp_axis, scatter_dimension=0, tiled=True),
        lax.psum_scatter(up_weight, fsdp_axis, scatter_dimension=0, tiled=True),
    )
    outer = (
        lax.psum_scatter(self_output, fsdp_axis, scatter_dimension=1, tiled=True),
        lax.psum_scatter(cross_output, fsdp_axis, scatter_dimension=1, tiled=True),
        lax.psum_scatter(down_weight, fsdp_axis, scatter_dimension=1, tiled=True),
    )
    return (
        inner[0],
        inner[1],
        inner[2],
        outer[0],
        inner[3],
        inner[4],
        inner[5],
        outer[1],
        inner[6],
        inner[7],
        outer[2],
    )


def add_all(first, second):
    return tuple((left_item + right_item for left_item, right_item in zip(first, second)))


def fold_keys(key_rows, value_rows, step_fn, initial):
    return step_fn(
        initial,
        (
            lax.all_gather(key_rows, fsdp_axis, axis=0, tiled=True),
            lax.all_gather(value_rows, fsdp_axis, axis=0, tiled=True),
        ),
        jnp.int32(0),
    )


def on_device(
    inputs,
    encoder_out,
    out_cotangent,
    bucket_ids,
    position_table,
    self_gain,
    self_query,
    self_key,
    self_value,
    self_output,
    cross_gain,
    cross_query,
    cross_key,
    cross_value,
    cross_output,
    feed_gain,
    gate_weight,
    up_weight,
    down_weight,
):
    shards = (
        self_query,
        self_key,
        self_value,
        self_output,
        cross_query,
        cross_key,
        cross_value,
        cross_output,
        gate_weight,
        up_weight,
        down_weight,
    )
    batches = inputs.shape[0]
    tensor_size = lax.axis_size(tensor_axis)
    piece_rows = inputs.shape[1] * tensor_size
    length = bucket_ids.shape[0]
    heads_all = position_table.shape[0]
    buckets = position_table.shape[1]
    local_heads = heads_all // tensor_size
    head_size = self_query.shape[1] // local_heads
    kv_local = self_key.shape[1] // head_size
    group_size = local_heads // kv_local
    score_scale = head_size ** (-0.5)
    fsdp_rank = lax.axis_index(fsdp_axis)
    tensor_rank = lax.axis_index(tensor_axis)
    query_start = fsdp_rank * piece_rows
    encoder_rows = encoder_out.shape[1] * tensor_size
    table_local = lax.dynamic_slice_in_dim(
        position_table, tensor_rank * local_heads, local_heads, 0
    )
    bucket_range = jnp.arange(buckets, dtype=jnp.int32)
    lower_bounds = jnp.sum((bucket_ids[None, :] < bucket_range[:, None]).astype(jnp.int32), axis=1)
    upper_bounds = jnp.concatenate([lower_bounds[1:], jnp.full((1,), length, jnp.int32)])

    def position_bias(row_start, col_start, row_count, col_count):
        offsets = (
            row_start
            - col_start
            + jnp.arange(row_count, dtype=jnp.int32)[:, None]
            - jnp.arange(col_count, dtype=jnp.int32)[None, :]
        )
        indicator = (
            (offsets[None] >= lower_bounds[:, None, None])
            & (offsets[None] < upper_bounds[:, None, None])
        ).astype(jnp.float32)
        bias_values = jnp.einsum("hb,bij->hij", table_local, indicator, precision=highest).reshape(
            kv_local, group_size, row_count, col_count
        )
        return (bias_values, offsets >= 0, indicator)

    def split_heads(row_block):
        return row_block.reshape(row_block.shape[0], kv_local, group_size, head_size)

    def split_kv(row_block):
        return row_block.reshape(row_block.shape[0], kv_local, head_size)

    def backward(batch_index, saved_state, weights):
        (
            query_full,
            key_full,
            value_full,
            output_full,
            cross_query_full,
            cross_key_full,
            cross_value_full,
            cross_output_full,
            gate_full,
            up_full,
            down_full,
        ) = weights
        cotangent = out_cotangent[batch_index].astype(jnp.float32)
        grad_feed = gather_rows(out_cotangent[batch_index])
        hidden = saved_state.hidden
        normed_feed = saved_state.normed_feed
        down_grad = jnp.einsum("tf,td->fd", hidden, grad_feed, preferred_element_type=jnp.float32)
        grad_hidden = jnp.einsum(
            "td,fd->tf", grad_feed, down_full, preferred_element_type=jnp.float32
        )
        gelu_pull = jax.vjp(
            lambda gate_in, up_in: jax.nn.gelu(gate_in, approximate=True) * up_in,
            saved_state.gate_values,
            saved_state.up_values,
        )[1]
        grad_gate, grad_up = gelu_pull(grad_hidden)
        grad_gate = grad_gate.astype(jnp.bfloat16)
        grad_up = grad_up.astype(jnp.bfloat16)
        gate_grad = jnp.einsum(
            "td,tf->df", normed_feed, grad_gate, preferred_element_type=jnp.float32
        )
        up_grad = jnp.einsum("td,tf->df", normed_feed, grad_up, preferred_element_type=jnp.float32)
        feed_rows = sum_rows(
            jnp.einsum("tf,df->td", grad_gate, gate_full, preferred_element_type=jnp.float32)
            + jnp.einsum("tf,df->td", grad_up, up_full, preferred_element_type=jnp.float32)
        )
        grad_norm_feed, feed_gain_grad = jax.vjp(norm_rows, saved_state.after_cross, feed_gain)[
            1
        ](feed_rows)
        grad_after_cross = cotangent + grad_norm_feed
        cross_context = saved_state.cross_context
        cross_weights = saved_state.cross_weights
        encoded = saved_state.encoded
        grad_cross_branch = gather_rows(grad_after_cross.astype(jnp.bfloat16))
        cross_output_grad = jnp.einsum(
            "te,td->ed", cross_context, grad_cross_branch, preferred_element_type=jnp.float32
        )
        grad_cross_context = split_heads(
            jnp.einsum(
                "td,ed->te",
                grad_cross_branch,
                cross_output_full,
                preferred_element_type=jnp.float32,
            ).astype(jnp.bfloat16)
        )
        grad_cross_weights = jnp.einsum(
            "ikgd,jkd->kgij",
            grad_cross_context,
            split_kv(saved_state.cross_values),
            preferred_element_type=jnp.float32,
        )
        grad_cross_scores = (
            cross_weights
            * (
                grad_cross_weights
                - jnp.sum(cross_weights * grad_cross_weights, axis=-1, keepdims=True)
            )
        ).astype(jnp.bfloat16)
        grad_cross_queries = (
            (
                jnp.einsum(
                    "kgij,jkd->ikgd",
                    grad_cross_scores,
                    split_kv(saved_state.cross_keys),
                    preferred_element_type=jnp.float32,
                )
                * score_scale
            )
            .reshape(piece_rows, local_heads * head_size)
            .astype(jnp.bfloat16)
        )
        key_part = (
            jnp.einsum(
                "kgij,ikgd->jkd",
                grad_cross_scores,
                split_heads(saved_state.cross_queries),
                preferred_element_type=jnp.float32,
            )
            * score_scale
        ).reshape(encoded.shape[0], kv_local * head_size)
        value_part = jnp.einsum(
            "kgij,ikgd->jkd",
            saved_state.cross_low,
            grad_cross_context,
            preferred_element_type=jnp.float32,
        ).reshape(encoded.shape[0], kv_local * head_size)
        key_sum, value_sum = (
            lax.psum_scatter(key_part, fsdp_axis, scatter_dimension=0, tiled=True),
            lax.psum_scatter(value_part, fsdp_axis, scatter_dimension=0, tiled=True),
        )
        key_low = key_sum.astype(jnp.bfloat16)
        value_low = value_sum.astype(jnp.bfloat16)
        encoded_own = lax.dynamic_slice_in_dim(encoded, fsdp_rank * encoder_rows, encoder_rows, 0)
        cross_key_grad = jnp.einsum(
            "ed,ec->dc", encoded_own, key_low, preferred_element_type=jnp.float32
        )
        cross_value_grad = jnp.einsum(
            "ed,ec->dc", encoded_own, value_low, preferred_element_type=jnp.float32
        )
        encoder_grad = sum_rows(
            jnp.einsum("ec,dc->ed", key_low, cross_key_full, preferred_element_type=jnp.float32)
            + jnp.einsum(
                "ec,dc->ed", value_low, cross_value_full, preferred_element_type=jnp.float32
            )
        )
        cross_query_grad = jnp.einsum(
            "td,tc->dc",
            saved_state.normed_cross,
            grad_cross_queries,
            preferred_element_type=jnp.float32,
        )
        cross_rows = sum_rows(
            jnp.einsum(
                "tc,dc->td",
                grad_cross_queries,
                cross_query_full,
                preferred_element_type=jnp.float32,
            )
        )
        grad_norm_cross, cross_gain_grad = jax.vjp(
            norm_rows, saved_state.after_self, cross_gain
        )[1](cross_rows)
        grad_after_self = grad_after_cross + grad_norm_cross
        queries = saved_state.queries
        keys_own = saved_state.keys_own
        values_own = saved_state.values_own
        context = saved_state.context
        log_total = saved_state.log_total
        normed_self = saved_state.normed_self
        query_heads = split_heads(queries)
        grad_self_branch = gather_rows(grad_after_self.astype(jnp.bfloat16))
        self_output_grad = jnp.einsum(
            "te,td->ed",
            saved_state.context_low,
            grad_self_branch,
            preferred_element_type=jnp.float32,
        )
        grad_context = jnp.einsum(
            "td,ed->te", grad_self_branch, output_full, preferred_element_type=jnp.float32
        ).astype(jnp.bfloat16)
        grad_context_heads = split_heads(grad_context)
        row_delta = jnp.transpose(
            jnp.sum(grad_context_heads.astype(jnp.float32) * context, axis=-1), (1, 2, 0)
        )

        def query_step():

            def step(carried, pieces, piece_start):
                key_piece, value_piece = pieces
                piece_length = key_piece.shape[0]
                block_width = math.gcd(piece_length, key_block_width)
                block_count = piece_length // block_width
                key_blocks = key_piece.reshape(block_count, block_width, kv_local, head_size)
                value_blocks = value_piece.reshape(block_count, block_width, kv_local, head_size)
                block_starts = block_width * jnp.arange(block_count, dtype=jnp.int32)

                def step_one_block(current, block_data):
                    key_block, value_block, block_start = block_data
                    bias_values, allowed, indicator = position_bias(
                        query_start, block_start, piece_rows, block_width
                    )
                    scores = (
                        jnp.einsum(
                            "ikgd,jkd->kgij",
                            query_heads,
                            key_block,
                            preferred_element_type=jnp.float32,
                        )
                        * score_scale
                        + bias_values
                    )
                    shares = jnp.where(allowed, jnp.exp(scores - log_total[..., None]), 0.0)
                    grad_shares = jnp.einsum(
                        "ikgd,jkd->kgij",
                        grad_context_heads,
                        value_block,
                        preferred_element_type=jnp.float32,
                    )
                    grad_scores = shares * (grad_shares - row_delta[..., None])
                    bias_grad = current[1] + jnp.einsum(
                        "hij,bij->hb",
                        grad_scores.reshape(local_heads, piece_rows, block_width),
                        indicator,
                        precision=highest,
                    )
                    scores_low = grad_scores.astype(jnp.bfloat16)
                    query_grad = (
                        current[0]
                        + jnp.einsum(
                            "kgij,jkd->ikgd",
                            scores_low,
                            key_block,
                            preferred_element_type=jnp.float32,
                        )
                        * score_scale
                    )
                    key_block_grad = (
                        jnp.einsum(
                            "kgij,ikgd->jkd",
                            scores_low,
                            query_heads,
                            preferred_element_type=jnp.float32,
                        ).reshape(block_width, kv_local * head_size)
                        * score_scale
                    )
                    value_block_grad = jnp.einsum(
                        "kgij,ikgd->jkd",
                        shares.astype(jnp.bfloat16),
                        grad_context_heads,
                        preferred_element_type=jnp.float32,
                    ).reshape(block_width, kv_local * head_size)
                    keys_all = lax.dynamic_update_slice_in_dim(
                        current[2],
                        lax.dynamic_slice_in_dim(current[2], block_start, block_width, 0)
                        + key_block_grad,
                        block_start,
                        0,
                    )
                    values_all = lax.dynamic_update_slice_in_dim(
                        current[3],
                        lax.dynamic_slice_in_dim(current[3], block_start, block_width, 0)
                        + value_block_grad,
                        block_start,
                        0,
                    )
                    return ((query_grad, bias_grad, keys_all, values_all), None)

                carried, unused = lax.scan(
                    step_one_block, carried, (key_blocks, value_blocks, block_starts)
                )
                return carried

            return step

        query_zero = jnp.zeros((piece_rows, kv_local, group_size, head_size), jnp.float32)
        bias_zero = jnp.zeros((local_heads, buckets), jnp.float32)
        all_zero = jnp.zeros((length, kv_local * head_size), jnp.float32)
        query_grad, bias_grad, keys_all, values_all = fold_keys(
            keys_own, values_own, query_step(), (query_zero, bias_zero, all_zero, all_zero)
        )
        key_sum_self, value_sum_self = (
            lax.psum_scatter(keys_all, fsdp_axis, scatter_dimension=0, tiled=True),
            lax.psum_scatter(values_all, fsdp_axis, scatter_dimension=0, tiled=True),
        )
        key_grad_low = key_sum_self.astype(jnp.bfloat16)
        value_grad_low = value_sum_self.astype(jnp.bfloat16)
        query_grad_low = query_grad.reshape(piece_rows, local_heads * head_size).astype(
            jnp.bfloat16
        )
        self_query_grad = jnp.einsum(
            "td,tc->dc", normed_self, query_grad_low, preferred_element_type=jnp.float32
        )
        self_key_grad = jnp.einsum(
            "td,tc->dc", normed_self, key_grad_low, preferred_element_type=jnp.float32
        )
        self_value_grad = jnp.einsum(
            "td,tc->dc", normed_self, value_grad_low, preferred_element_type=jnp.float32
        )
        self_rows = sum_rows(
            jnp.einsum("tc,dc->td", query_grad_low, query_full, preferred_element_type=jnp.float32)
            + jnp.einsum("tc,dc->td", key_grad_low, key_full, preferred_element_type=jnp.float32)
            + jnp.einsum(
                "tc,dc->td", value_grad_low, value_full, preferred_element_type=jnp.float32
            )
        )
        grad_norm_self, self_gain_grad = jax.vjp(norm_rows, saved_state.own_rows, self_gain)[1](
            self_rows
        )
        input_grad = grad_after_self + grad_norm_self
        grads_full = (
            self_query_grad,
            self_key_grad,
            self_value_grad,
            self_output_grad,
            cross_query_grad,
            cross_key_grad,
            cross_value_grad,
            cross_output_grad,
            gate_grad,
            up_grad,
            down_grad,
        )
        extras = (bias_grad, self_gain_grad, cross_gain_grad, feed_gain_grad)
        return (grads_full, extras, input_grad, encoder_grad)

    layer_list = []
    input_list = []
    encoder_list = []
    small_sums = None
    shard_grads = None
    for batch_index in range(batches):
        weights_forward = gather_weights(shards)
        (
            forward_query_full,
            forward_key_full,
            forward_value_full,
            forward_output_full,
            forward_cross_query_full,
            forward_cross_key_full,
            forward_cross_value_full,
            forward_cross_output_full,
            forward_gate_full,
            forward_up_full,
            forward_down_full,
        ) = weights_forward
        own_rows = inputs[batch_index].astype(jnp.float32)
        forward_normed_self = gather_rows(norm_rows(own_rows, self_gain).astype(jnp.bfloat16))
        forward_queries = matmul(forward_normed_self, forward_query_full).astype(jnp.bfloat16)
        forward_keys_own = matmul(forward_normed_self, forward_key_full).astype(jnp.bfloat16)
        forward_values_own = matmul(forward_normed_self, forward_value_full).astype(jnp.bfloat16)
        forward_query_heads = split_heads(forward_queries)

        def forward_step(carried, pieces, piece_start):
            key_piece, value_piece = pieces
            piece_length = key_piece.shape[0]
            block_width = math.gcd(piece_length, key_block_width)
            block_count = piece_length // block_width
            key_blocks = key_piece.reshape(block_count, block_width, kv_local, head_size)
            value_blocks = value_piece.reshape(block_count, block_width, kv_local, head_size)
            block_starts = block_width * jnp.arange(block_count, dtype=jnp.int32)

            def forward_one_block(current, block_data):
                running_max, running_total, accumulated = current
                key_block, value_block, block_start = block_data
                bias_values, allowed, indicator = position_bias(
                    query_start, block_start, piece_rows, block_width
                )
                scores = (
                    jnp.einsum(
                        "ikgd,jkd->kgij",
                        forward_query_heads,
                        key_block,
                        preferred_element_type=jnp.float32,
                    )
                    * score_scale
                    + bias_values
                )
                scores = jnp.where(allowed, scores, masked_score)
                new_max = jnp.maximum(running_max, jnp.max(scores, axis=-1))
                factor = jnp.exp(running_max - new_max)
                shares = jnp.where(allowed, jnp.exp(scores - new_max[..., None]), 0.0)
                running_total = running_total * factor + jnp.sum(shares, axis=-1)
                update = jnp.einsum(
                    "kgij,jkd->ikgd",
                    shares.astype(jnp.bfloat16),
                    value_block,
                    preferred_element_type=jnp.float32,
                )
                accumulated = accumulated * jnp.transpose(factor, (2, 0, 1))[..., None] + update
                return ((new_max, running_total, accumulated), None)

            carried, unused = lax.scan(
                forward_one_block, carried, (key_blocks, value_blocks, block_starts)
            )
            return carried

        stat_shape = (kv_local, group_size, piece_rows)
        initial = (
            jnp.full(stat_shape, masked_score, jnp.float32),
            jnp.zeros(stat_shape, jnp.float32),
            jnp.zeros((piece_rows, kv_local, group_size, head_size), jnp.float32),
        )
        running_max, running_total, accumulated = fold_keys(
            forward_keys_own, forward_values_own, forward_step, initial
        )
        forward_context = accumulated / jnp.transpose(running_total, (2, 0, 1))[..., None]
        forward_log_total = running_max + jnp.log(running_total)
        context_low = forward_context.reshape(piece_rows, local_heads * head_size).astype(
            jnp.bfloat16
        )
        after_self = own_rows + sum_rows(matmul(context_low, forward_output_full))
        normed_cross = gather_rows(norm_rows(after_self, cross_gain).astype(jnp.bfloat16))
        cross_queries = matmul(normed_cross, forward_cross_query_full).astype(jnp.bfloat16)
        forward_encoded = lax.all_gather(
            encoder_out[batch_index], (fsdp_axis, tensor_axis), axis=0, tiled=True
        )
        cross_keys = matmul(forward_encoded, forward_cross_key_full).astype(jnp.bfloat16)
        cross_values = matmul(forward_encoded, forward_cross_value_full).astype(jnp.bfloat16)
        cross_scores = (
            jnp.einsum(
                "ikgd,jkd->kgij",
                split_heads(cross_queries),
                split_kv(cross_keys),
                preferred_element_type=jnp.float32,
            )
            * score_scale
        )
        forward_cross_weights = jax.nn.softmax(cross_scores, axis=-1)
        cross_low = forward_cross_weights.astype(jnp.bfloat16)
        forward_cross_context = (
            jnp.einsum(
                "kgij,jkd->ikgd",
                cross_low,
                split_kv(cross_values),
                preferred_element_type=jnp.float32,
            )
            .reshape(piece_rows, local_heads * head_size)
            .astype(jnp.bfloat16)
        )
        after_cross = after_self + sum_rows(
            matmul(forward_cross_context, forward_cross_output_full)
        )
        forward_normed_feed = gather_rows(norm_rows(after_cross, feed_gain).astype(jnp.bfloat16))
        gate_values = matmul(forward_normed_feed, forward_gate_full)
        up_values = matmul(forward_normed_feed, forward_up_full)
        forward_hidden = (jax.nn.gelu(gate_values, approximate=True) * up_values).astype(
            jnp.bfloat16
        )
        layer_rows = after_cross + sum_rows(matmul(forward_hidden, forward_down_full))
        forward_saved_state = types.SimpleNamespace(
            own_rows=own_rows,
            normed_self=forward_normed_self,
            queries=forward_queries,
            keys_own=forward_keys_own,
            values_own=forward_values_own,
            context=forward_context,
            log_total=forward_log_total,
            context_low=context_low,
            after_self=after_self,
            normed_cross=normed_cross,
            cross_queries=cross_queries,
            encoded=forward_encoded,
            cross_keys=cross_keys,
            cross_values=cross_values,
            cross_weights=forward_cross_weights,
            cross_low=cross_low,
            cross_context=forward_cross_context,
            after_cross=after_cross,
            normed_feed=forward_normed_feed,
            gate_values=gate_values,
            up_values=up_values,
            hidden=forward_hidden,
        )
        layer_rows, saved_state = (layer_rows.astype(jnp.bfloat16), forward_saved_state)
        weights_backward = gather_weights(shards)
        grads_full, extras, input_grad, encoder_grad = backward(
            batch_index, saved_state, weights_backward
        )
        reduced = scatter_grads(grads_full)
        shard_grads = reduced if shard_grads is None else add_all(shard_grads, reduced)
        small_sums = extras if small_sums is None else add_all(small_sums, extras)
        layer_list.append(layer_rows)
        input_list.append(input_grad)
        encoder_list.append(encoder_grad)
    table_full = lax.dynamic_update_slice_in_dim(
        jnp.zeros((heads_all, buckets), jnp.float32), small_sums[0], tensor_rank * local_heads, 0
    )
    table_sum, self_gain_sum, cross_gain_sum, feed_gain_sum = lax.psum(
        (table_full, small_sums[1], small_sums[2], small_sums[3]), (fsdp_axis, tensor_axis)
    )
    return (
        jnp.stack(layer_list),
        jnp.stack(input_list),
        jnp.stack(encoder_list),
        table_sum,
        self_gain_sum,
        shard_grads[0],
        shard_grads[1],
        shard_grads[2],
        shard_grads[3],
        cross_gain_sum,
        shard_grads[4],
        shard_grads[5],
        shard_grads[6],
        shard_grads[7],
        feed_gain_sum,
        shard_grads[8],
        shard_grads[9],
        shard_grads[10],
    )


def to_chip(fsdp):
    return dict(device_id={fsdp_axis: fsdp}, device_id_type=pl.DeviceIdType.MESH)


def to_core(core):
    return dict(device_id={tensor_axis: core}, device_id_type=pl.DeviceIdType.MESH)


def chip_place(layers):
    rank = lax.axis_index(fsdp_axis)
    return rank, rank // 4, rank // 2 % 2, rank % 2


def peers_of(rank, y, x):
    found = []
    for o in (1, 2, 3):
        other_y = 1 - y if o & 2 else y
        other_x = 1 - x if o & 1 else x
        spot = 2 * other_y + other_x
        found.append((rank - 2 * y - x + spot, spot))
    return found


def greet_all(layers):
    chips = 4 * layers
    rank = lax.axis_index(fsdp_axis)
    barrier = pltpu.get_barrier_semaphore()
    for o in range(1, chips):
        pl.semaphore_signal(barrier, inc=1, **to_chip((rank + o) % chips))
    pl.semaphore_signal(barrier, inc=1, **to_core(1 - lax.axis_index(tensor_axis)))
    pl.semaphore_wait(barrier, chips)


def greet(layers):
    rank, z, y, x = chip_place(layers)
    barrier = pltpu.get_barrier_semaphore()
    for chip, spot in peers_of(rank, y, x):
        pl.semaphore_signal(barrier, inc=1, **to_chip(chip))
    for o in range(1, layers):
        pl.semaphore_signal(barrier, inc=1, **to_chip(rank - 4 * z + 4 * ((z + o) % layers)))
    pl.semaphore_signal(barrier, inc=1, **to_core(1 - lax.axis_index(tensor_axis)))
    pl.semaphore_wait(barrier, 3 + layers)


dma = pltpu.SemaphoreType.DMA


class Column:
    def __init__(self, layers, source, land, z_sem, core_sem=None):
        self.layers, self.source, self.land = layers, source, land
        self.z_sem, self.core_sem = z_sem, core_sem
        self.rank, self.z, self.y, self.x = chip_place(layers)
        self.core = lax.axis_index(tensor_axis)

    def place(self, layer):
        return (layer,) if self.core_sem is None else (layer, self.core)

    def hop(self, o):
        there = (self.z + o) % self.layers
        return pltpu.make_async_remote_copy(
            src_ref=self.source.at[there],
            dst_ref=self.land.at[self.place(self.z)],
            send_sem=self.z_sem.at[0, o],
            recv_sem=self.z_sem.at[1, self.z],
            **to_chip(self.rank + 4 * (there - self.z)),
        )

    def arrival(self, layer):
        return pltpu.make_async_remote_copy(
            src_ref=self.source.at[0],
            dst_ref=self.land.at[self.place(layer)],
            send_sem=self.z_sem.at[0, 0],
            recv_sem=self.z_sem.at[1, layer],
            **to_chip(self.rank + 4 - 8 * (self.z // 2)),
        )

    def over(self, layer):
        return pltpu.make_async_remote_copy(
            src_ref=self.land.at[layer, self.core],
            dst_ref=self.land.at[layer, self.core],
            send_sem=self.core_sem.at[0, layer],
            recv_sem=self.core_sem.at[1, layer],
            **to_core(1 - self.core),
        )

    def piece(self, o, n):
        there = (self.z + o) % self.layers
        at = pl.ds(pl.multiple_of(16 * n, 16), 16)
        return pltpu.make_async_remote_copy(
            src_ref=self.source.at[there, at],
            dst_ref=self.land.at[self.z, at],
            send_sem=self.z_sem.at[0, o],
            recv_sem=self.z_sem.at[1, self.z],
            **to_chip(self.rank + 4 * (there - self.z)),
        )

    def start(self):
        for o in range(1, self.layers):
            self.hop(o).start()
        self.land[self.place(self.z)] = self.source[self.z]

    def arrive(self):
        for o in range(1, self.layers):
            self.arrival((self.z + o) % self.layers).wait_recv()
        if self.core_sem is not None:
            for layer in range(self.layers):
                self.over(layer).start()

    def finish(self):
        for o in range(1, self.layers):
            self.hop(o).wait_send()
        if self.core_sem is not None:
            for layer in range(self.layers):
                self.over(layer).wait()


class PlaneSwap:
    def __init__(self, layers, source, land, sem):
        self.source, self.land, self.sem = source, land, sem
        self.rank, self.z, self.y, self.x = chip_place(layers)
        self.spot = 2 * self.y + self.x
        self.peers = peers_of(self.rank, self.y, self.x)

    def hop(self, o):
        chip, there = self.peers[o]
        return pltpu.make_async_remote_copy(
            src_ref=self.source.at[there],
            dst_ref=self.land.at[self.spot],
            send_sem=self.sem.at[0, o],
            recv_sem=self.sem.at[1, o],
            **to_chip(chip),
        )

    def start(self):
        for o in range(3):
            self.hop(o).start()
        self.land[self.spot] = self.source[self.spot]

    def arrival(self, o):
        chip, there = self.peers[o]
        return pltpu.make_async_remote_copy(
            src_ref=self.source.at[there],
            dst_ref=self.land.at[there],
            send_sem=self.sem.at[0, o],
            recv_sem=self.sem.at[1, o],
            **to_chip(chip),
        )

    def arrive(self):
        for o in range(3):
            self.arrival(o).wait_recv()

    def finish(self):
        for o in range(3):
            self.hop(o).wait_send()


class PlaneGather:
    def __init__(self, layers, source, land, sem, core_sem):
        self.source, self.land, self.sem, self.core_sem = source, land, sem, core_sem
        self.rank, self.z, self.y, self.x = chip_place(layers)
        self.core = lax.axis_index(tensor_axis)
        self.spot = 2 * self.y + self.x
        self.peers = peers_of(self.rank, self.y, self.x)

    def hop(self, o, spot):
        return pltpu.make_async_remote_copy(
            src_ref=self.source,
            dst_ref=self.land.at[spot, self.core],
            send_sem=self.sem.at[0, o],
            recv_sem=self.sem.at[1, o],
            **to_chip(self.peers[o][0]),
        )

    def over(self, spot):
        return pltpu.make_async_remote_copy(
            src_ref=self.land.at[spot, self.core],
            dst_ref=self.land.at[spot, self.core],
            send_sem=self.core_sem.at[0, spot],
            recv_sem=self.core_sem.at[1, spot],
            **to_core(1 - self.core),
        )

    def start(self):
        for o in range(3):
            self.hop(o, self.spot).start()
        self.land[self.spot, self.core] = self.source[...]

    def arrive(self):
        for o in range(3):
            self.hop(o, self.peers[o][1]).wait_recv()
        for spot in range(4):
            self.over(spot).start()

    def finish(self):
        for o in range(3):
            self.hop(o, self.spot).wait_send()
        for spot in range(4):
            self.over(spot).wait()


def close_kernel(
    layers,
    heads,
    gq_ref,
    x_ref,
    win_ref,
    gas_ref,
    kvs_ref,
    gains_ref,
    mid_ref,
    sums_ref,
    hit_ref,
    nt_s,
    wa_ref,
    sum_s,
    rows_land,
    table_out,
    gain_out,
    wkv_s,
    mine_s,
    halves_s,
    enc_s,
    ended_s,
    small_s,
    small_z,
    load_sem,
    core_sem,
    rows_z,
    small_sem,
    z_sem,
    *sum_refs,
):
    f32, bf16 = jnp.float32, jnp.bfloat16
    grads = GradSum(layers, slice(None), None, (), sum_s, *sum_refs)
    rows = Column(layers, ended_s, rows_land, rows_z)
    rank, z, y, x = chip_place(layers)
    core = lax.axis_index(tensor_axis)
    own = gas_ref.shape[1]
    width = x_ref.shape[1]
    enc_own = kvs_ref.shape[0] // (2 * layers)
    wide = kvs_ref.shape[1]
    kv_local = 4
    blocks = sums_ref.shape[0] // 2
    buckets = hit_ref.shape[1]
    gain = gains_ref[...]
    loads = pltpu.make_async_copy(
        wa_ref.at[:, pl.ds(2 * wide, wide)], wkv_s, load_sem.at[0]
    )
    loads.start()
    greet_all(layers)

    per_layer = width // layers

    def weigh(turn, carry):
        layer = grads.layer_of(2 * turn)
        at = pl.ds(pl.multiple_of(layer * per_layer, per_layer), per_layer)
        part = matmul(nt_s[at, :], gq_ref[...]).astype(bf16)
        grads.own[layer] = part.reshape(grads.own.shape[1:])
        grads.send_first(2 * turn)
        grads.send_first(2 * turn + 1)
        return carry

    lax.fori_loop(0, layers, weigh, 0)

    def gather(which):
        return jnp.concatenate(
            [
                gq_ref[pl.ds(pl.multiple_of((2 * layer + which) * own, own), own), :]
                for layer in range(layers)
            ],
            axis=0,
        )

    def across(n, shape_at):
        return pltpu.make_async_remote_copy(
            src_ref=halves_s.at[0, shape_at],
            dst_ref=halves_s.at[1, shape_at],
            send_sem=core_sem.at[0, n],
            recv_sem=core_sem.at[1, n],
            **to_core(1 - core),
        )

    body, tail = pl.ds(0, layers * own), pl.ds(layers * own, layers * enc_own)
    halves_s[0, body, :] = dot_t(gather(1 - core), win_ref[...]).astype(bf16)
    across(0, body).start()
    loads.wait()
    enc_s[...] = dot_t(kvs_ref[...], wkv_s[...])
    other = pl.ds(pl.multiple_of((1 - core) * layers * enc_own, enc_own), layers * enc_own)
    halves_s[0, tail, :] = enc_s[other, :].astype(bf16)
    across(1, tail).start()
    mine_s[...] = dot_t(gather(core), win_ref[...])
    grads.advance(1)
    grads.advance(2)

    found = [jnp.zeros((1, buckets), f32) for _ in range(2)]
    for d in range(blocks):
        by_bucket = lax.dot_general(
            sums_ref[...],
            hit_ref[d],
            (((1,), (1,)), ((), ())),
            precision=highest,
            preferred_element_type=f32,
        )
        for h in range(2):
            found[h] = found[h] + by_bucket[h * blocks + d : h * blocks + d + 1, :]
    half = width // 2
    lane = lax.broadcasted_iota(jnp.int32, (buckets, half), 1)
    spread = (lane % buckets == lax.broadcasted_iota(jnp.int32, (buckets, half), 0)).astype(f32)
    lane = lax.broadcasted_iota(jnp.int32, (1, half), 1)
    first_head = 2 * (core * kv_local + rank % 4)
    table = jnp.zeros((1, half), f32)
    for h in range(2):
        row = jnp.dot(found[h], spread, precision=highest, preferred_element_type=f32)
        table = table + jnp.where(lane // buckets == first_head + h, row, 0.0)
    small = [table, jnp.zeros((1, half), f32)]
    for n in (1, 0):
        small = [mid_ref[n : n + 1, :half], mid_ref[n : n + 1, half:]] + small

    across(0, body).wait()
    across(1, tail).wait()
    mine_enc = pl.ds(pl.multiple_of(core * layers * enc_own, enc_own), layers * enc_own)
    enc_sum = enc_s[mine_enc, :].astype(bf16).astype(f32) + halves_s[1, tail, :].astype(f32)

    total = jnp.zeros((1, width), f32)
    for layer in range(layers):
        at = slice(layer * own, (layer + 1) * own)
        both = mine_s[at, :].astype(bf16).astype(f32) + halves_s[1, at, :].astype(f32)
        v = x_ref[pl.ds(pl.multiple_of((2 * layer + core) * own, own), own), :].astype(f32)
        grad, gain_grad = norm_pull(v, gain, both)
        total = total + gain_grad
        ended_s[layer, :own, :] = (gas_ref[layer] + grad).astype(bf16)
        ended_s[layer, own:, :] = enc_sum[layer * enc_own : (layer + 1) * enc_own].astype(bf16)
    small_s[0] = jnp.concatenate([total[:, :half], total[:, half:]] + small, axis=0)
    chips = 4 * layers

    def spread_to(o):
        there = (rank + o) % chips
        return pltpu.make_async_remote_copy(
            src_ref=small_s.at[0],
            dst_ref=small_z.at[rank],
            send_sem=small_sem.at[0, o],
            recv_sem=small_sem.at[1, rank],
            **to_chip(there),
        )

    def came_from(o):
        there = (rank + o) % chips
        return pltpu.make_async_remote_copy(
            src_ref=small_s.at[0],
            dst_ref=small_z.at[there],
            send_sem=small_sem.at[0, o],
            recv_sem=small_sem.at[1, there],
            **to_chip(there),
        )

    across_core = pltpu.make_async_remote_copy(
        src_ref=small_s.at[1],
        dst_ref=small_s.at[2],
        send_sem=z_sem.at[0],
        recv_sem=z_sem.at[1],
        **to_core(1 - core),
    )
    for o in range(1, chips):
        spread_to(o).start()
    small_z[rank] = small_s[0]
    rows_land[z] = ended_s[z]

    def one(m, carry):
        grads.advance(m)
        return carry

    def feed_links(m, carry):
        for o in range(1, layers):
            rows.piece(o, m - 3).start()
        grads.advance(m)
        return carry

    pieces = (own + enc_own) // 16
    lax.fori_loop(3, 3 + pieces, feed_links, 0)
    lax.fori_loop(3 + pieces, 9, one, 0)
    for o in range(1, chips):
        came_from(o).wait_recv()
    summed = small_z[0]
    for chip in range(1, chips):
        summed = summed + small_z[chip]
    small_s[1] = summed
    across_core.start()
    lax.fori_loop(9, sum_steps(layers), one, 0)
    across_core.wait()
    for o in range(1, chips):
        spread_to(o).wait_send()
    both = small_s[1] + small_s[2]
    low = jnp.where(core == 0, small_s[1], small_s[2])
    for n, part in enumerate((both, low, low)):
        gain_out[n : n + 1, :half] = part[2 * n : 2 * n + 1, :]
        gain_out[n : n + 1, half:] = part[2 * n + 1 : 2 * n + 2, :]
    for h in range(heads):
        table_out[h : h + 1, :] = both[6:7, h * buckets : (h + 1) * buckets]
    rows.arrive()
    rows.finish()
    grads.finish()


def close_rows(
    layers, heads, grad_qkv, x_low, win, grad_rows, kv_sum, self_gain, mid, sums, hit, nt, weights
):
    f32, bf16 = jnp.float32, jnp.bfloat16
    width, cols = win.shape
    own = grad_rows.shape[1]
    wide = kv_sum.shape[1]
    enc_own = kv_sum.shape[0] // (2 * layers)
    buckets = hit.shape[1]
    vmem, anywhere = pl.BlockSpec(memory_space=pltpu.VMEM), pl.BlockSpec(memory_space=pl.ANY)
    rows_shape = (layers, own + enc_own, width)
    return pl.pallas_call(
        functools.partial(close_kernel, layers, heads),
        name="close_rows",
        out_shape=(
            jax.ShapeDtypeStruct((2, 2, 16, cols), f32),
            jax.ShapeDtypeStruct(rows_shape, bf16),
            jax.ShapeDtypeStruct((heads, buckets), f32),
            jax.ShapeDtypeStruct((3, width), f32),
        ),
        in_specs=[vmem] * 10 + [anywhere],
        out_specs=(vmem,) * 4,
        scratch_shapes=[
            pltpu.VMEM((width, wide), bf16),
            pltpu.VMEM((layers * own, width), f32),
            pltpu.VMEM((2, layers * (own + enc_own), width), bf16),
            pltpu.VMEM((2 * layers * enc_own, width), f32),
            pltpu.VMEM(rows_shape, bf16),
            pltpu.VMEM((3, 8, width // 2), f32),
            pltpu.VMEM((4 * layers, 8, width // 2), f32),
            dma((1,)),
            dma((2, 2)),
            dma((2, layers)),
            dma((2, 4 * layers)),
            dma((2,)),
            *sum_scratch(layers, cols),
        ],
        compiler_params=pltpu.CompilerParams(
            collective_id=7, has_side_effects=True, vmem_limit_bytes=48 << 20
        ),
    )(grad_qkv, x_low, win, grad_rows, kv_sum, self_gain, mid, sums, hit, nt, weights)


def finish_kernel(
    in_ref,
    rest_ref,
    feed_ref,
    rows_ref,
    layer_ref,
    table_ref,
    gain_ref,
    layer_out,
    input_out,
    enc_out,
    table_out,
    self_gain,
    query_out,
    key_out,
    value_out,
    out_out,
    cross_gain,
    cq_out,
    ck_out,
    cv_out,
    co_out,
    feed_gain,
    gate_out,
    up_out,
    down_out,
):
    layer_out[...] = layer_ref[...]
    own = input_out.shape[1]
    input_out[...] = rows_ref[:, :own, :].astype(jnp.float32)
    enc_out[...] = rows_ref[:, own:, :].astype(jnp.float32)
    table_out[...] = table_ref[...]
    for n, ref in enumerate((self_gain, cross_gain, feed_gain)):
        ref[...] = gain_ref[n : n + 1, :]
    group = in_ref.shape[1] // 4
    half = group // 4
    pieces = [in_ref[:, n * group : (n + 1) * group] for n in range(4)]
    query_out[...] = jnp.concatenate([p[:, : 2 * half] for p in pieces], axis=1)
    key_out[...] = jnp.concatenate([p[:, 2 * half : 3 * half] for p in pieces], axis=1)
    value_out[...] = jnp.concatenate([p[:, 3 * half :] for p in pieces], axis=1)
    at = 0
    for ref in (out_out, cq_out, ck_out, cv_out, co_out):
        ref[...] = rest_ref[:, at : at + ref.shape[1]]
        at += ref.shape[1]
    feed = gate_out.shape[1]
    for at in range(0, feed, tile):
        units = min(tile, feed - at)
        for n, ref in enumerate((gate_out, up_out, down_out)):
            start = 3 * at + n * units
            ref[:, at : at + units] = feed_ref[:, start : start + units]


def finish(in_sum, rest_sum, feed_sum, rows, layer_rows, table, gains):
    f32 = jnp.float32
    own = layer_rows.shape[1]
    layers, both, width = rows.shape

    def flat(x):
        return x.reshape(64, x.shape[-1])

    def out(*shape, dtype=f32):
        return jax.ShapeDtypeStruct(shape, dtype)

    wide, feed = in_sum.shape[-1] // 2, feed_sum.shape[-1] // 3
    gain = out(1, width)
    vmem = pl.BlockSpec(memory_space=pltpu.VMEM)
    return pl.pallas_call(
        finish_kernel,
        name="finish",
        out_shape=(
            out(*layer_rows.shape, dtype=layer_rows.dtype),
            out(layers, own, width),
            out(layers, both - own, width),
            out(*table.shape),
            gain,
            out(64, wide),
            out(64, wide // 2),
            out(64, wide // 2),
            out(64, wide),
            gain,
            out(64, wide),
            out(64, wide // 2),
            out(64, wide // 2),
            out(64, wide),
            gain,
            out(64, feed),
            out(64, feed),
            out(64, feed),
        ),
        in_specs=[vmem] * 7,
        out_specs=(vmem,) * 18,
        compiler_params=pltpu.CompilerParams(vmem_limit_bytes=32 << 20),
    )(flat(in_sum), flat(rest_sum), flat(feed_sum), rows, layer_rows, table, gains)

def sum_scratch(layers, cols):
    steps = 2 * layers
    bf16 = jnp.bfloat16
    return [
        pltpu.VMEM((layers, 2, 2, 2, 2, 16, cols), bf16),
        pltpu.VMEM((layers, 2, 2, 2, 16, cols), bf16),
        pltpu.VMEM((steps, 2, 16, cols), bf16),
        pltpu.VMEM((steps, 2, 16, cols), bf16),
        pltpu.VMEM((steps, 2, 16, cols), bf16),
        dma((3, layers)),
        dma((2, steps, 2, 2)),
        dma((2, steps, 2)),
        dma((2, steps)),
        dma((2, steps)),
    ]


def sum_steps(layers):
    return 2 * layers + layers + 3


class GradSum:
    def __init__(self, layers, cols, whole, got, out, own, first, second, below, above, load, s1, s2, su, sd):
        self.cols = cols
        self.got = got
        self.layers, self.whole, self.out, self.own = layers, whole, out, own
        self.first, self.second, self.below, self.above = first, second, below, above
        self.load, self.s1, self.s2, self.su, self.sd = load, s1, s2, su, sd
        self.rank, self.z, self.y, self.x = chip_place(layers)
        self.x_chip = self.rank + 1 - 2 * self.x
        self.y_chip = self.rank + 2 - 4 * self.y
        self.steps = 2 * layers

    def layer_of(self, n):
        turn = n // 2
        return jnp.where(turn % 2 == 1, turn // 2, self.layers - 1 - turn // 2)

    def loads(self, turn):
        layer = self.layer_of(2 * turn)
        copies = [
            pltpu.make_async_copy(
                self.whole.at[(layer, *[slice(None)] * 5, self.cols)],
                self.own.at[layer],
                self.load.at[0, turn],
            )
        ]
        for colour, came in enumerate(self.got):
            copies.append(
                pltpu.make_async_copy(
                    came.at[layer, :, :, :, self.cols],
                    self.first.at[layer, colour],
                    self.load.at[1 + colour, turn],
                )
            )
        return copies

    def hop_one(self, n, colour, which):
        layer, chunk = self.layer_of(n), n % 2
        if colour == 0:
            source, chip = self.own.at[layer, which, 1 - self.x, 0, chunk], self.x_chip
        else:
            source, chip = self.own.at[layer, 1 - self.y, which, 1, chunk], self.y_chip
        return pltpu.make_async_remote_copy(
            src_ref=source,
            dst_ref=self.first.at[layer, colour, which, chunk],
            send_sem=self.s1.at[0, n, colour, which],
            recv_sem=self.s1.at[1, n, colour, which],
            **to_chip(chip),
        )

    def hop_two(self, n, colour):
        layer, chunk = self.layer_of(n), n % 2
        if colour == 0:
            source, chip = self.own.at[layer, 1 - self.y, self.x, 0, chunk], self.y_chip
        else:
            source, chip = self.own.at[layer, self.y, 1 - self.x, 1, chunk], self.x_chip
        return pltpu.make_async_remote_copy(
            src_ref=source,
            dst_ref=self.second.at[n, colour],
            send_sem=self.s2.at[0, n, colour],
            recv_sem=self.s2.at[1, n, colour],
            **to_chip(chip),
        )

    def hop_z(self, n, up):
        layer, chunk = self.layer_of(n), n % 2
        sems = self.su if up else self.sd
        return pltpu.make_async_remote_copy(
            src_ref=self.own.at[layer, self.y, self.x, :, chunk],
            dst_ref=(self.below if up else self.above).at[n],
            send_sem=sems.at[0, n],
            recv_sem=sems.at[1, n],
            **to_chip(self.rank + (4 if up else -4)),
        )

    def start(self):
        for turn in range(self.layers):
            for copy in self.loads(turn):
                copy.start()

    def send_first(self, n):
        @pl.when(n < self.steps)
        def _():
            if self.whole is not None:

                @pl.when(n % 2 == 0)
                def _():
                    for copy in self.loads(n // 2):
                        copy.wait()

            if not self.got:
                for which in range(2):
                    for colour in range(2):
                        self.hop_one(n, colour, which).start()

    def advance(self, m):
        steps, layers = self.steps, self.layers
        n = m - 1

        @pl.when((n >= 0) & (n < steps))
        def _():
            layer, chunk = self.layer_of(n), n % 2
            for colour in range(2):
                for other in range(2):
                    if colour == 0:
                        which = (1 - self.y) if other == 0 else self.y
                        place = (layer, which, self.x, 0, chunk)
                    else:
                        which = (1 - self.x) if other == 0 else self.x
                        place = (layer, self.y, which, 1, chunk)
                    if not self.got:
                        self.hop_one(n, colour, which).wait_recv()
                    self.own[place] = self.own[place] + self.first[layer, colour, which, chunk]
                    if other == 0:
                        self.hop_two(n, colour).start()

        n2 = m - 2

        @pl.when((n2 >= 0) & (n2 < steps))
        def _():
            layer, chunk = self.layer_of(n2), n2 % 2
            for colour in range(2):
                self.hop_two(n2, colour).wait_recv()
                place = (layer, self.y, self.x, colour, chunk)
                self.own[place] = self.own[place] + self.second[n2, colour]

        for up in (True, False):
            chain = self.z if up else layers - 1 - self.z
            nz = m - 2 - chain
            layer = self.layer_of(nz)
            beyond = (layer > self.z) if up else (layer < self.z)

            @pl.when((nz >= 0) & (nz < steps) & beyond)
            def _():
                @pl.when(chain > 0)
                def _():
                    self.hop_z(nz, up).wait_recv()
                    came = self.below if up else self.above
                    for colour in range(2):
                        place = (layer, self.y, self.x, colour, nz % 2)
                        self.own[place] = self.own[place] + came[nz, colour]

                self.hop_z(nz, up).start()

        nf = m - 2 - layers

        @pl.when((nf >= 0) & (nf < steps) & (self.layer_of(nf) == self.z))
        def _():
            layer, chunk = self.layer_of(nf), nf % 2
            for colour in range(2):
                self.out[colour, chunk, :, self.cols] = self.own[layer, self.y, self.x, colour, chunk].astype(
                    jnp.float32
                )
            for up in (True, False):
                chain = self.z if up else layers - 1 - self.z

                @pl.when(chain > 0)
                def _():
                    self.hop_z(nf, up).wait_recv()
                    came = self.below if up else self.above
                    for colour in range(2):
                        self.out[colour, chunk, :, self.cols] += came[nf, colour].astype(jnp.float32)

    def finish(self):
        def one(n, carry):
            for colour in range(2):
                if not self.got:
                    for which in range(2):
                        self.hop_one(n, colour, which).wait_send()
                self.hop_two(n, colour).wait_send()
            layer = self.layer_of(n)
            for up in (True, False):

                @pl.when((layer > self.z) if up else (layer < self.z))
                def _():
                    self.hop_z(n, up).wait_send()

            return carry

        lax.fori_loop(0, self.steps, one, 0)

def gather_scratch(layers, cols):
    return [
        pltpu.VMEM((2, 2, 16, cols), jnp.bfloat16),
        dma((1,)),
        dma((2, 2, layers, 2)),
        dma((2, layers, 2)),
        dma((2, layers, 2)),
        dma((2, layers, 2)),
        dma((2, layers, 2)),
    ]


class RowGather:
    def __init__(self, layers, short, whole, here, local, sz, sx, sy, sfx, sfy):
        self.short = short
        self.layers, self.whole, self.here = layers, whole, here
        self.local, self.sz, self.sx, self.sy, self.sfx, self.sfy = local, sz, sx, sy, sfx, sfy
        self.rank, self.z, self.y, self.x = chip_place(layers)
        self.x_chip = self.rank + 1 - 2 * self.x
        self.y_chip = self.rank + 2 - 4 * self.y

    def put(self):
        place = self.whole.at[self.z, self.y, self.x]
        return pltpu.make_async_copy(self.here, place, self.local.at[0])

    def source(self, layer, chunk, own, colours=slice(None)):
        if own:
            return self.here.at[colours, chunk]
        return self.whole.at[layer, self.y, self.x, colours, chunk]

    def along_z(self, layer, chunk, up, own=False):
        return pltpu.make_async_remote_copy(
            src_ref=self.source(layer, chunk, own),
            dst_ref=self.whole.at[layer, self.y, self.x, :, chunk],
            send_sem=self.sz.at[0, int(up), layer, chunk],
            recv_sem=self.sz.at[1, int(up), layer, chunk],
            **to_chip(self.rank + (4 if up else -4)),
        )

    def in_plane(self, layer, chunk, along_x, own=False):
        sems = self.sx if along_x else self.sy
        colours = slice(None)
        if self.short:
            colours = 0 if along_x else 1
        return pltpu.make_async_remote_copy(
            src_ref=self.source(layer, chunk, own, colours),
            dst_ref=self.whole.at[layer, self.y, self.x, colours, chunk],
            send_sem=sems.at[0, layer, chunk],
            recv_sem=sems.at[1, layer, chunk],
            **to_chip(self.x_chip if along_x else self.y_chip),
        )

    def onward(self, layer, chunk, along_x):
        if along_x:
            place = (layer, 1 - self.y, self.x, 1, chunk)
            sems, chip = self.sfx, self.x_chip
        else:
            place = (layer, self.y, 1 - self.x, 0, chunk)
            sems, chip = self.sfy, self.y_chip
        return pltpu.make_async_remote_copy(
            src_ref=self.whole.at[place],
            dst_ref=self.whole.at[place],
            send_sem=sems.at[0, layer, chunk],
            recv_sem=sems.at[1, layer, chunk],
            **to_chip(chip),
        )

    def send_z(self):
        for chunk in range(2):

            @pl.when(self.z < self.layers - 1)
            def _():
                self.along_z(self.z, chunk, True, own=True).start()

            @pl.when(self.z > 0)
            def _():
                self.along_z(self.z, chunk, False, own=True).start()

    def send_plane(self):
        for chunk in range(2):
            for along_x in (True, False):
                self.in_plane(self.z, chunk, along_x, own=True).start()
        self.put().start()

    def pass_on(self, m):
        far, chunk = m // 2, m % 2
        for up in (True, False):
            layer = self.z - far if up else self.z + far
            near = (layer >= 0) if up else (layer < self.layers)

            @pl.when((far > 0) & near)
            def _():
                self.along_z(layer, chunk, up).wait_recv()

                @pl.when((self.z < self.layers - 1) if up else (self.z > 0))
                def _():
                    self.along_z(layer, chunk, up).start()

                for along_x in (True, False):
                    self.in_plane(layer, chunk, along_x).start()

    def turn(self, m):
        far, chunk = m // 2, m % 2
        for up in (True, False):
            layer = self.z - far if up else self.z + far
            near = (layer >= 0) if up else ((layer < self.layers) & (far > 0))

            @pl.when(near)
            def _():
                for along_x in (True, False):
                    self.in_plane(layer, chunk, along_x).wait_recv()
                    self.onward(layer, chunk, not along_x).start()

    def step(self, m):
        @pl.when(m + 2 < 2 * self.layers)
        def _():
            self.pass_on(m + 2)

        if not self.short:
            self.turn(m)

    def finish(self):
        self.put().wait()

        def one(n, carry):
            layer, chunk = n // 2, n % 2
            for along_x in (True, False):
                if self.short:
                    self.in_plane(layer, chunk, along_x).wait_recv()
                else:
                    self.onward(layer, chunk, along_x).wait()
                self.in_plane(layer, chunk, along_x).wait_send()

            @pl.when((self.z < self.layers - 1) & (layer <= self.z))
            def _():
                self.along_z(layer, chunk, True).wait_send()

            @pl.when((self.z > 0) & (layer >= self.z))
            def _():
                self.along_z(layer, chunk, False).wait_send()

            return carry

        lax.fori_loop(0, 2 * self.layers, one, 0)

def begin_kernel(
    score_scale,
    layers,
    rows_ref,
    enc_ref,
    cot_ref,
    gain_ref,
    bias_ref,
    query_ref,
    key_ref,
    value_ref,
    out_ref,
    cq_ref,
    ck_ref,
    cv_ref,
    co_ref,
    gate_ref,
    up_ref,
    down_ref,
    rows_out,
    enc_out,
    cot_out,
    kept_ref,
    low_ref,
    full_ref,
    total_ref,
    nt_out,
    win_out,
    whole_ref,
    feed_whole,
    rows_land,
    enc_land,
    enc_all,
    cot_land,
    win_s,
    norm_s,
    qkv_s,
    came,
    landed,
    low_s,
    q_s,
    k_s,
    v_s,
    bias_s,
    score_s,
    rows_z,
    rows_core,
    enc_z,
    plane_sem,
    plane_core,
    cot_z,
    cot_core,
    in_sem,
    out_send,
    out_recv,
    win_sem,
    *gather_refs,
):
    f32, bf16 = jnp.float32, jnp.bfloat16
    blocks = bias_s.shape[1]
    sources = qkv_s.shape[0]
    head = k_s.shape[1]
    third = len(gather_refs) // 3
    first = RowGather(layers, False, win_s, *gather_refs[:third])
    gathers = (
        RowGather(layers, True, feed_whole, *gather_refs[2 * third :]),
        RowGather(layers, False, whole_ref, *gather_refs[third : 2 * third]),
    )
    rank, z, y, x = chip_place(layers)
    spot = 2 * y + x
    peers = peers_of(rank, y, x)
    rows = Column(layers, rows_ref, rows_land, rows_z, rows_core)
    enc = Column(layers, enc_ref, enc_land, enc_z)
    plane = PlaneGather(layers, enc_land, enc_all, plane_sem, plane_core)
    cot = Column(layers, cot_ref, cot_land, cot_z, cot_core)
    heads = PlaneSwap(layers, qkv_s, came, in_sem)

    def shard(gather, parts):
        gather.here[...] = jnp.concatenate(parts, axis=1).reshape(gather.here.shape)

    parts = []
    for kv in range(sources):
        parts.append(query_ref[:, 2 * kv * head : 2 * (kv + 1) * head])
        parts.append(key_ref[:, kv * head : (kv + 1) * head])
        parts.append(value_ref[:, kv * head : (kv + 1) * head])
    shard(first, parts)
    greet(layers)
    first.send_z()
    first.send_plane()
    shard(
        gathers[1],
        [out_ref[...], cq_ref[...], ck_ref[...], cv_ref[...], co_ref[...]],
    )
    feed = gate_ref.shape[1]
    parts = []
    for at in range(0, feed, tile):
        end = min(at + tile, feed)
        parts += [gate_ref[:, at:end], up_ref[:, at:end], down_ref[:, at:end]]
    shard(gathers[0], parts)

    def one(m, carry):
        first.step(m)
        return carry

    lax.fori_loop(0, layers, one, 0)
    rows.start()
    enc.start()
    lax.fori_loop(layers, 2 * layers, one, 0)
    for gather in gathers:
        gather.send_z()
    for gather in gathers:
        gather.send_plane()

    def make_bias(n, carry):
        row = jnp.broadcast_to(bias_ref[pl.ds(n, 1), :], (tile, 2 * tile))
        turned = pltpu.roll(row, tile + 1, 1, stride=1, stride_axis=0)
        bias_s[n // blocks, n % blocks] = turned[:, :tile]
        return carry

    lax.fori_loop(0, 2 * blocks, make_bias, 0)
    rows.arrive()
    first.finish()
    keep = pltpu.make_async_copy(win_s, win_out, win_sem.at[0])
    keep.start()
    rows.finish()
    rows_out[...] = rows_land[...]
    width = rows_ref.shape[2]
    for layer in range(layers):
        v = rows_land[layer].reshape(-1, width).astype(f32)
        at = slice(layer * v.shape[0], (layer + 1) * v.shape[0])
        norm_s[at, :] = (v * norm_scale(v) * gain_ref[...]).astype(bf16)
    for kv in range(sources):
        columns = win_s[..., 4 * head * kv : 4 * head * (kv + 1)].reshape(-1, 4 * head)
        qkv_s[kv] = matmul(norm_s[...], columns).astype(bf16)
    heads.start()
    enc.arrive()
    plane.start()
    cot.start()
    nt_out[...] = jnp.transpose(norm_s[...])
    heads.arrive()
    unpack_pair(came, q_s, k_s, v_s, score_scale)
    kept_ref[...] = came[...]

    def row_block(turn, carry):
        i = blocks - 1 - turn
        at = pl.ds(pl.multiple_of(i * tile, tile), tile)
        query = [q_s[h, at, :] for h in range(2)]

        def score_step(j, tops):
            key = k_s[pl.ds(pl.multiple_of(j * tile, tile), tile), :]
            found = []
            for h in range(2):
                score = dot_t(query[h], key) + bias_s[h, i - j]
                score_s[h, j] = score
                found.append(jnp.maximum(tops[h], jnp.maximum(score[:, :128], score[:, 128:])))
            return tuple(found)

        start = jnp.full((tile, 128), masked_score, jnp.float32)
        tops = lax.fori_loop(0, i + 1, score_step, (start, start))
        tops = [jnp.max(top, axis=1, keepdims=True) for top in tops]

        def share_step(j, state):
            value = v_s[pl.ds(pl.multiple_of(j * tile, tile), tile), :]
            found = []
            for h in range(2):
                total, summed = state[h]
                share = jnp.exp(score_s[h, j] - tops[h])
                summed = summed + jnp.dot(
                    share.astype(jnp.bfloat16), value, preferred_element_type=jnp.float32
                )
                found.append((total + share[:, :128] + share[:, 128:], summed))
            return tuple(found)

        nothing = (jnp.zeros((tile, 128), jnp.float32), jnp.zeros((tile, head), jnp.float32))
        state = lax.fori_loop(0, i + 1, share_step, (nothing, nothing))
        found = []
        for h in range(2):
            total = jnp.sum(state[h][0], axis=1, keepdims=True)
            found.append(state[h][1] / total)
            log_total = jnp.broadcast_to(tops[h] + jnp.log(total), (tile, 128))
            total_ref[pl.ds(h * blocks + i, 1), :] = jnp.transpose(log_total)[0:1, :]
        both = jnp.concatenate(found, axis=1)
        full_ref[at, :] = both
        both = both.astype(jnp.bfloat16)
        for part in range(tile // 128):
            block = i * (tile // 128) + part
            low_s[block] = both[part * 128 : (part + 1) * 128]

        for gather in gathers:
            gather.step(turn)
        for part in range(tile // 128):
            block = i * (tile // 128) + part

            @pl.when(block % sources == spot)
            def _():
                landed[spot, block // sources] = low_s[block]

            @pl.when(block % sources != spot)
            def _():
                hand_back(block).start()

        return carry

    def hand_back(block):
        return pltpu.make_async_remote_copy(
            src_ref=low_s.at[block],
            dst_ref=landed.at[spot, block // sources],
            send_sem=out_send.at[block],
            recv_sem=out_recv.at[spot, block // sources],
            **to_chip(rank - spot + block % sources),
        )

    lax.fori_loop(0, blocks // 2, row_block, 0)
    plane.arrive()
    cot.arrive()
    lax.fori_loop(blocks // 2, blocks, row_block, 0)
    for o in range(3):
        chip, there = peers[o]
        for turn in range(layers):
            pltpu.make_async_remote_copy(
                src_ref=low_s.at[0],
                dst_ref=landed.at[there, turn],
                send_sem=out_send.at[0],
                recv_sem=out_recv.at[there, turn],
                **to_chip(chip),
            ).wait_recv()
    for source in range(sources):
        for turn in range(layers):
            low_ref[turn * 128 : (turn + 1) * 128, source * 128 : (source + 1) * 128] = landed[
                source, turn
            ]
    heads.finish()
    cot.finish()
    cot_out[...] = cot_land[...]
    enc.finish()
    plane.finish()
    enc_out[...] = enc_all[...]
    keep.wait()
    for block in range(sources * layers):

        @pl.when(block % sources != spot)
        def _():
            hand_back(block).wait_send()

    for gather in gathers:
        gather.finish()


def begin(scale, layers, inputs, encoder, cotangent, gain, bias, *shards):
    f32, bf16 = jnp.float32, jnp.bfloat16
    own, width = inputs.shape[1:]
    enc_own = encoder.shape[1]
    rows = 2 * layers * own
    head = round(scale**-2)
    sources = 4
    length = sources * rows
    blocks = length // tile
    cols = sum(shard.shape[1] for shard in shards[:3])
    rest_cols = 4 * shards[3].shape[1]
    feed_cols = 3 * shards[8].shape[1]
    rows_shape, enc_shape = (layers, 2, own, width), (4, 2, layers, enc_own, width)
    qkv_shape = (sources, rows, 4 * head)
    chips = (layers, 2, 2, 2, 2, 16)
    vmem, anywhere = pl.BlockSpec(memory_space=pltpu.VMEM), pl.BlockSpec(memory_space=pl.ANY)
    return pl.pallas_call(
        functools.partial(begin_kernel, scale, layers),
        name="begin",
        out_shape=(
            jax.ShapeDtypeStruct(rows_shape, bf16),
            jax.ShapeDtypeStruct(enc_shape, bf16),
            jax.ShapeDtypeStruct(rows_shape, bf16),
            jax.ShapeDtypeStruct(qkv_shape, bf16),
            jax.ShapeDtypeStruct((rows, sources * 2 * head), bf16),
            jax.ShapeDtypeStruct((length, 2 * head), f32),
            jax.ShapeDtypeStruct((2 * blocks, tile), f32),
            jax.ShapeDtypeStruct((width, rows), bf16),
            jax.ShapeDtypeStruct((*chips, cols), bf16),
            jax.ShapeDtypeStruct((*chips, rest_cols), bf16),
            jax.ShapeDtypeStruct((*chips, feed_cols), bf16),
        ),
        in_specs=[vmem] * 16,
        out_specs=(vmem,) * 8 + (anywhere,) * 3,
        scratch_shapes=[
            pltpu.VMEM(rows_shape, bf16),
            pltpu.VMEM((layers, enc_own, width), bf16),
            pltpu.VMEM(enc_shape, bf16),
            pltpu.VMEM(rows_shape, bf16),
            pltpu.VMEM((*chips, cols), bf16),
            pltpu.VMEM((rows, width), bf16),
            pltpu.VMEM(qkv_shape, bf16),
            pltpu.VMEM(qkv_shape, bf16),
            pltpu.VMEM((sources, layers, 128, 2 * head), bf16),
            pltpu.VMEM((length // 128, 128, 2 * head), bf16),
            pltpu.VMEM((2, length, head), bf16),
            pltpu.VMEM((length, head), bf16),
            pltpu.VMEM((length, head), bf16),
            pltpu.VMEM((2, blocks, tile, tile), f32),
            pltpu.VMEM((2, blocks, tile, tile), f32),
            dma((2, layers)),
            dma((2, layers)),
            dma((2, layers)),
            dma((2, 3)),
            dma((2, 4)),
            dma((2, layers)),
            dma((2, layers)),
            dma((2, 3)),
            dma((length // 128,)),
            dma((sources, layers)),
            dma((1,)),
            *gather_scratch(layers, cols),
            *gather_scratch(layers, rest_cols),
            *gather_scratch(layers, feed_cols),
        ],
        compiler_params=pltpu.CompilerParams(
            collective_id=6, has_side_effects=True, vmem_limit_bytes=56 << 20
        ),
    )(inputs, encoder, cotangent, gain, bias, *shards)

def feed_cut(cols):
    return (cols // 128 + 1) // 2 * 128


def attend_backward_kernel(
    score_scale,
    layers,
    kept_ref,
    ctx_ref,
    full_ref,
    total_ref,
    bias_ref,
    kv_ref,
    rows_ref,
    grads_ref,
    feed_ref,
    got_x,
    got_y,
    out_ref,
    sums_ref,
    kv_out,
    rows_out,
    sum_a,
    sum_b,
    ctx_land,
    kv_land,
    rows_land,
    out_s,
    out_land,
    q_s,
    k_s,
    v_s,
    g_s,
    bias_s,
    sum_s,
    delta_s,
    dq_s,
    dk_s,
    dv_s,
    ctx_sem,
    kv_sem,
    rows_z,
    out_sem,
    *sum_refs,
):
    blocks = bias_s.shape[1]
    sources, rows, _ = kept_ref.shape
    head = k_s.shape[1]
    each = len(sum_refs) // 3
    cut = feed_cut(feed_ref.shape[-1])
    sums = (
        GradSum(layers, pl.ds(0, cut), feed_ref, (got_x, got_y), sum_b, *sum_refs[:each]),
        GradSum(
            layers,
            pl.ds(cut, feed_ref.shape[-1] - cut),
            feed_ref,
            (got_x, got_y),
            sum_b,
            *sum_refs[each : 2 * each],
        ),
        GradSum(layers, slice(None), grads_ref, (), sum_a, *sum_refs[2 * each :]),
    )
    context = PlaneSwap(layers, ctx_ref, ctx_land, ctx_sem)
    cross = PlaneSwap(layers, kv_ref, kv_land, kv_sem)
    ended = Column(layers, rows_ref, rows_land, rows_z)
    back = PlaneSwap(layers, out_s, out_land, out_sem)
    for grads in sums:
        grads.start()
    greet(layers)
    context.start()
    for grads in sums:
        grads.send_first(0)
    cross.start()
    ended.start()
    unpack_pair(kept_ref, q_s, k_s, v_s, score_scale)

    def make_bias(n, carry):
        row = jnp.broadcast_to(bias_ref[pl.ds(n, 1), :], (tile, 2 * tile))
        turned = pltpu.roll(row, 0, 1, stride=1, stride_axis=0)
        bias_s[n // blocks, n % blocks] = turned[:, tile:]
        return carry

    lax.fori_loop(0, 2 * blocks, make_bias, 0)
    sum_s[...] = jnp.zeros_like(sum_s)
    dq_s[...] = jnp.zeros_like(dq_s)
    dk_s[...] = jnp.zeros_like(dk_s)
    dv_s[...] = jnp.zeros_like(dv_s)
    context.arrive()
    for block in range(rows // 128 * sources):
        source, turn = block % sources, block // sources
        part = ctx_land[source, turn * 128 : (turn + 1) * 128, :]
        at = slice(block * 128, (block + 1) * 128)
        g_s[0, at, :] = part[:, :head]
        g_s[1, at, :] = part[:, head:]

    def make_delta(i, carry):
        at = pl.ds(pl.multiple_of(i * tile, tile), tile)
        for h in range(2):
            product = g_s[h, at, :].astype(jnp.float32) * full_ref[at, h * head : (h + 1) * head]
            column = jnp.broadcast_to(jnp.sum(product, axis=1, keepdims=True), (tile, 128))
            delta_s[pl.ds(h * blocks + i, 1), :] = jnp.transpose(column)[0:1, :]
        return carry

    lax.fori_loop(0, blocks, make_delta, 0)

    def one_tile(n, carry):
        line, at = n // blocks, n % blocks
        first = at < blocks - line
        d = jnp.where(first, line, blocks - line)
        i = jnp.where(first, at + line, at)
        at_q = pl.ds(pl.multiple_of(i * tile, tile), tile)
        at_k = pl.ds(pl.multiple_of((i - d) * tile, tile), tile)
        key, value = k_s[at_k, :], v_s[at_k, :]
        for h in range(2):
            query, grad = q_s[h, at_q, :], g_s[h, at_q, :]
            score = dot_t(key, query) + bias_s[h, d]
            share = jnp.exp(score - total_ref[pl.ds(h * blocks + i, 1), :])
            pull = dot_t(value, grad)
            grad_score = share * (pull - delta_s[pl.ds(h * blocks + i, 1), :])
            sum_s[h, d] += grad_score
            share_low = share.astype(jnp.bfloat16)
            grad_low = grad_score.astype(jnp.bfloat16)
            dv_s[at_k, :] += jnp.dot(share_low, grad, preferred_element_type=jnp.float32)
            dk_s[at_k, :] += jnp.dot(grad_low, query, preferred_element_type=jnp.float32)
            dq_s[h, at_q, :] += dot_first(grad_low, key)
        return carry

    tiles = blocks * (blocks + 1) // 2
    busy = 2 * layers

    def work(m, carry):
        for grads in sums:
            grads.send_first(m)
        low = (m - 1) * tiles // busy
        lax.fori_loop(low, m * tiles // busy, one_tile, 0)
        for grads in sums:
            grads.advance(m)
        return carry

    lax.fori_loop(1, 1 + busy, work, 0)

    for block in range(rows // 128 * sources):
        source, turn = block % sources, block // sources
        at = slice(block * 128, (block + 1) * 128)
        out_s[source, turn * 128 : (turn + 1) * 128, :] = jnp.concatenate(
            [dq_s[0, at, :] * score_scale, dq_s[1, at, :] * score_scale, dk_s[at, :], dv_s[at, :]],
            axis=1,
        ).astype(jnp.bfloat16)
    back.start()

    row_at = lax.broadcasted_iota(jnp.int32, (tile, tile), 0)
    col_at = lax.broadcasted_iota(jnp.int32, (tile, tile), 1)
    turn_rows = (row_at + col_at == tile - 1).astype(jnp.float32)

    def make_sums(n, carry):
        turned = jnp.dot(
            turn_rows,
            sum_s[n // blocks, n % blocks],
            precision=highest,
            preferred_element_type=jnp.float32,
        )
        wide = jnp.concatenate([turned, jnp.zeros_like(turned)], axis=1)
        wide = pltpu.roll(wide, 0, 1, stride=1, stride_axis=0)
        sums_ref[pl.ds(n, 1), :] = jnp.sum(wide, axis=0, keepdims=True)
        return carry

    cross.arrive()
    both = kv_land[0].astype(jnp.float32)
    for source in range(1, sources):
        both = both + kv_land[source].astype(jnp.float32)
    kv_out[...] = both.astype(jnp.bfloat16)
    ended.arrive()
    rows_out[...] = rows_land[...]

    left = sum_steps(layers) - 1 - busy

    def rest(m, carry):
        for grads in sums:
            grads.send_first(m)
        for grads in sums:
            grads.advance(m)
        n = m - 1 - busy
        lax.fori_loop(n * 2 * blocks // left, (n + 1) * 2 * blocks // left, make_sums, 0)
        return carry

    lax.fori_loop(1 + busy, sum_steps(layers), rest, 0)
    back.arrive()
    wide = 4 * head
    for source in range(sources):
        out_ref[:, source * wide : (source + 1) * wide] = out_land[source]
    context.finish()
    cross.finish()
    ended.finish()
    back.finish()
    for grads in sums:
        grads.finish()


def attend_backward(
    scale, layers, kept, ctx_grad, full, total, bias, kv, layer_rows, grads, feed_grads, got
):
    f32, bf16 = jnp.float32, jnp.bfloat16
    sources, rows, wide = kept.shape
    head = wide // 4
    length = sources * rows
    blocks = length // tile
    cols, feed_cols = grads.shape[1], feed_grads.shape[1]
    chips = (layers, 2, 2, 2, 2, 16)
    vmem, anywhere = pl.BlockSpec(memory_space=pltpu.VMEM), pl.BlockSpec(memory_space=pl.ANY)
    return pl.pallas_call(
        functools.partial(attend_backward_kernel, scale, layers),
        name="attend_backward",
        out_shape=(
            jax.ShapeDtypeStruct((rows, sources * wide), bf16),
            jax.ShapeDtypeStruct((2 * blocks, 2 * tile), f32),
            jax.ShapeDtypeStruct(kv.shape[1:], bf16),
            jax.ShapeDtypeStruct(layer_rows.shape, bf16),
            jax.ShapeDtypeStruct((2, 2, 16, cols), f32),
            jax.ShapeDtypeStruct((2, 2, 16, feed_cols), f32),
        ),
        in_specs=[vmem] * 7 + [anywhere] * 4,
        out_specs=(vmem,) * 6,
        scratch_shapes=[
            pltpu.VMEM(ctx_grad.shape, bf16),
            pltpu.VMEM(kv.shape, bf16),
            pltpu.VMEM(layer_rows.shape, bf16),
            pltpu.VMEM(kept.shape, bf16),
            pltpu.VMEM(kept.shape, bf16),
            pltpu.VMEM((2, length, head), bf16),
            pltpu.VMEM((length, head), bf16),
            pltpu.VMEM((length, head), bf16),
            pltpu.VMEM((2, length, head), bf16),
            pltpu.VMEM((2, blocks, tile, tile), f32),
            pltpu.VMEM((2, blocks, tile, tile), f32),
            pltpu.VMEM((2 * blocks, tile), f32),
            pltpu.VMEM((2, length, head), f32),
            pltpu.VMEM((length, head), f32),
            pltpu.VMEM((length, head), f32),
            dma((2, 3)),
            dma((2, 3)),
            dma((2, layers)),
            dma((2, 3)),
            *sum_scratch(layers, feed_cut(feed_cols)),
            *sum_scratch(layers, feed_cols - feed_cut(feed_cols)),
            *sum_scratch(layers, cols),
        ],
        compiler_params=pltpu.CompilerParams(
            collective_id=8, has_side_effects=True, vmem_limit_bytes=62 << 20
        ),
    )(
        kept,
        ctx_grad,
        full,
        total,
        bias,
        kv,
        layer_rows,
        grads.reshape(*chips, cols),
        feed_grads.reshape(*chips, feed_cols),
        *got,
    )

def norm_scale(v):
    return lax.rsqrt(jnp.mean(v * v, axis=-1, keepdims=True) + norm_eps)


def norm_pull(v, gain, grad):
    scale = norm_scale(v)
    turned = v * scale
    pulled = grad * gain
    mean = jnp.mean(pulled * turned, axis=-1, keepdims=True)
    return scale * (pulled - turned * mean), jnp.sum(grad * turned, axis=0, keepdims=True)


def middle_kernel(
    score_scale,
    layers,
    feed,
    ctx_ref,
    x_ref,
    cot_ref,
    enc_ref,
    wa_ref,
    gains_ref,
    wf_ref,
    layer_out,
    grad_out,
    gctx_out,
    kv_out,
    ga_out,
    gain_out,
    gb_out,
    got_x,
    got_y,
    w_s,
    gb_s,
    after_self,
    after_cross,
    nc_s,
    nf_s,
    nft_s,
    cott_s,
    down_s,
    dx_s,
    send_s,
    land_s,
    half_s,
    q_s,
    k_s,
    v_s,
    g_s,
    pair_s,
    cc_s,
    dq_s,
    dk_s,
    low_s,
    w_load,
    w_send,
    w_recv,
    g_send,
    g_recv,
    g_store,
    swap_sem,
):
    f32, bf16 = jnp.float32, jnp.bfloat16
    rank, z, y, x = chip_place(layers)
    core = lax.axis_index(tensor_axis)
    x_chip, y_chip = rank + 1 - 2 * x, rank + 2 - 4 * y
    rows, width = x_ref.shape
    heads, _, head = q_s.shape
    kv_heads = heads // 2
    wide = heads * head
    enc_rows = enc_ref.shape[0]
    block = send_s.shape[2]
    chunks = rows // block
    at_out, at_cq, at_ck = 0, wide, 2 * wide
    at_cv, at_co = at_ck + wide // 2, at_ck + wide
    row_chip = 64

    def row_of(layer, at_y, at_x, colour=0):
        return pl.multiple_of(((layer * 2 + at_y) * 2 + at_x) * row_chip + 32 * colour, 32)

    def loads(n, cols):
        copies = []
        for layer in range(layers):
            for start, count in (
                (row_of(layer, y, x), 64),
                (row_of(layer, y, 1 - x, 0), 32),
                (row_of(layer, 1 - y, x, 1), 32),
            ):
                at = (pl.ds(start, count), cols)
                copies.append(pltpu.make_async_copy(wf_ref.at[at], w_s.at[at], w_load.at[n]))
        return copies

    def weights_hop(n, cols, layer, along_y, which):
        spot = row_of(layer, y, which, 0) if along_y else row_of(layer, which, x, 1)
        at = (pl.ds(spot, 32), cols)
        return pltpu.make_async_remote_copy(
            src_ref=wf_ref.at[at],
            dst_ref=w_s.at[at],
            send_sem=w_send.at[int(along_y), n],
            recv_sem=w_recv.at[int(along_y), n],
            **to_chip(y_chip if along_y else x_chip),
        )

    def weights_all(n, cols, along_y):
        at = (pl.ds(0, 64 * layers), cols)
        return pltpu.make_async_remote_copy(
            src_ref=wf_ref.at[at],
            dst_ref=w_s.at[at],
            send_sem=w_send.at[int(along_y), n],
            recv_sem=w_recv.at[int(along_y), n],
            **to_chip(y_chip if along_y else x_chip),
        )

    def grads_hop(n, cols, layer, along_y, which):
        spot = row_of(layer, 1 - y, which, 1) if along_y else row_of(layer, which, 1 - x, 0)
        return pltpu.make_async_remote_copy(
            src_ref=gb_s.at[pl.ds(spot, 32), cols],
            dst_ref=(got_y if along_y else got_x).at[layer, which, :, cols],
            send_sem=g_send.at[int(along_y), n],
            recv_sem=g_recv.at[int(along_y), n],
            **to_chip(y_chip if along_y else x_chip),
        )

    def grads_all(n, cols, along_y):
        return pltpu.make_async_remote_copy(
            src_ref=gb_s.at[pl.ds(0, 64 * layers), cols],
            dst_ref=(got_y if along_y else got_x).at[:, :, :, cols],
            send_sem=g_send.at[int(along_y), n],
            recv_sem=g_recv.at[int(along_y), n],
            **to_chip(y_chip if along_y else x_chip),
        )

    hops = [(layer, a, w) for layer in range(layers) for w in range(2) for a in (True, False)]
    full_blocks, last = feed // tile, feed % tile

    def each_block(work):
        def one(n, carry):
            work(n, pl.ds(pl.multiple_of(n * 3 * tile, 3 * tile), 3 * tile), tile)
            return carry

        lax.fori_loop(0, full_blocks, one, 0)
        if last:
            work(full_blocks, pl.ds(full_blocks * 3 * tile, 3 * last), last)

    def bring(n, cols, units):
        for hop in hops:
            weights_hop(n, cols, *hop).start()
        for copy in loads(n, cols):
            copy.start()

    greet(layers)
    each_block(bring)

    def swap(n, chunk):
        half = n == 3
        return pltpu.make_async_remote_copy(
            src_ref=half_s.at[0] if half else send_s.at[slots[n], chunk],
            dst_ref=half_s.at[1] if half else land_s.at[slots[n], chunk],
            send_sem=swap_sem.at[0, n, chunk],
            recv_sem=swap_sem.at[1, n, chunk],
            **to_core(1 - core),
        )

    slots = (0, 1, 0, None, 1)

    def span(chunk):
        return pl.ds(pl.multiple_of(chunk * block, block), block)

    def send_parts(n, part_of):
        def one(chunk, carry):
            send_s[slots[n], chunk] = part_of(span(chunk)).astype(bf16)
            swap(n, chunk).start()
            return carry

        lax.fori_loop(0, chunks, one, 0)

    def take_parts(n, use):
        def one(chunk, carry):
            swap(n, chunk).wait()
            both = send_s[slots[n], chunk].astype(f32) + land_s[slots[n], chunk].astype(f32)
            use(span(chunk), both)
            return carry

        lax.fori_loop(0, chunks, one, 0)

    cross_gain, feed_gain = gains_ref[0:1, :], gains_ref[1:2, :]

    send_parts(0, lambda at: dot_t(ctx_ref[at, :], wa_ref[:, at_out : at_out + wide]))
    key_value = matmul(enc_ref[...], wa_ref[:, at_ck : at_ck + wide]).astype(bf16)
    for kv in range(kv_heads):
        k_s[kv] = key_value[:, kv * head : (kv + 1) * head]
        v_s[kv] = key_value[:, wide // 2 + kv * head : wide // 2 + (kv + 1) * head]
    cott_s[...] = jnp.transpose(cot_ref[...])

    def enter_cross(at, both):
        v = x_ref[at, :].astype(f32) + both
        after_self[at, :] = v
        nc_s[at, :] = (v * norm_scale(v) * cross_gain).astype(bf16)
        query = matmul(nc_s[at, :], wa_ref[:, at_cq : at_cq + wide]).astype(bf16)
        for h in range(heads):
            q_s[h, at, :] = (query[:, h * head : (h + 1) * head] * score_scale).astype(bf16)

    take_parts(0, enter_cross)

    def attend(kv, carry):
        key, value = k_s[kv], v_s[kv]
        for chunk in range(chunks):
            at = slice(chunk * block, (chunk + 1) * block)
            found = []
            for h in range(2):
                score = dot_t(q_s[2 * kv + h, at, :], key)
                share = jnp.exp(score - jnp.max(score, axis=1, keepdims=True))
                total = jnp.sum(share, axis=1, keepdims=True)
                found.append(matmul(share.astype(bf16), value) / total)
            pair_s[kv, at, :] = jnp.concatenate(found, axis=1).astype(bf16)
        return carry

    lax.fori_loop(0, kv_heads, attend, 0)
    for kv in range(kv_heads):
        cc_s[:, 2 * kv * head : 2 * (kv + 1) * head] = pair_s[kv]
    send_parts(1, lambda at: dot_t(cc_s[at, :], wa_ref[:, at_co : at_co + wide]))

    def enter_feed(at, both):
        v = after_self[at, :] + both
        after_cross[at, :] = v
        nf_s[at, :] = (v * norm_scale(v) * feed_gain).astype(bf16)

    take_parts(1, enter_feed)
    nft_s[...] = jnp.transpose(nf_s[...])

    down_s[...] = jnp.zeros_like(down_s)
    dx_s[...] = jnp.zeros_like(dx_s)
    slope = math.sqrt(2.0 / math.pi)

    def feed_block(n, cols, units):
        have = (pl.ds(0, 128 * layers), cols)
        pltpu.make_async_copy(wf_ref.at[have], w_s.at[have], w_load.at[n]).wait()
        for along_y in (True, False):
            weights_all(n, cols, along_y).wait_recv()
        pair = w_s[:, pl.ds(cols.start, 2 * units)]
        down = w_s[:, pl.ds(cols.start + 2 * units, units)]
        both = matmul(nf_s[...], pair)
        gate, up = both[:, :units], both[:, units:]
        square = gate * gate
        bend = jnp.tanh(slope * (gate + 0.044715 * square * gate))
        bent = 0.5 * gate * (1.0 + bend)
        pull = 0.5 * (1.0 + bend) + 0.5 * gate * (1.0 - bend * bend) * slope * (
            1.0 + 3.0 * 0.044715 * square
        )
        hidden = (bent * up).astype(bf16)
        down_s[...] += dot_t(hidden, down)
        grad = matmul(cot_ref[...], down)
        grads = jnp.concatenate([grad * up * pull, grad * bent], axis=1).astype(bf16)
        dx_s[...] += dot_t(grads, pair)
        gb_s[:, pl.ds(cols.start, 2 * units)] = matmul(nft_s[...], grads).astype(bf16)
        gb_s[:, pl.ds(cols.start + 2 * units, units)] = matmul(cott_s[...], hidden).astype(bf16)
        for hop in hops:
            grads_hop(n, cols, *hop).start()

    each_block(feed_block)

    send_parts(2, lambda at: dx_s[at, :])
    store = pltpu.make_async_copy(gb_s, gb_out, g_store.at[0])
    store.start()
    own = rows // (2 * layers)

    def halves(ref, which):
        return [ref[pl.ds((2 * layer + which) * own, own), :] for layer in range(layers)]

    low = jnp.concatenate(halves(down_s, 1 - core), axis=0).astype(bf16)
    half_s[0] = low
    swap(3, 0).start()

    def leave_feed(at, both):
        grad, gain = norm_pull(after_cross[at, :], feed_gain, both)
        dx_s[at, :] = cot_ref[at, :].astype(f32) + grad
        low = dx_s[at, :].astype(bf16)
        low_s[at, :] = low
        gain_out[1:2, :] += gain
        context = matmul(low, wa_ref[:, at_co : at_co + wide]).astype(bf16)
        for h in range(heads):
            g_s[h, at, :] = context[:, h * head : (h + 1) * head]

    gain_out[...] = jnp.zeros_like(gain_out)
    take_parts(2, leave_feed)
    swap(3, 0).wait()
    mine = halves(after_cross, core)
    down = halves(down_s, core)
    for layer in range(layers):
        came = half_s[1, layer * own : (layer + 1) * own, :].astype(f32)
        layer_out[layer] = (mine[layer] + (down[layer].astype(bf16).astype(f32) + came)).astype(bf16)

    ga_out[:, at_co : at_co + wide] = dot_first(low_s[...], cc_s[...]).astype(bf16)

    def attend_back(kv, carry):
        key, value = k_s[kv], v_s[kv]
        key_grad = jnp.zeros((enc_rows, head), f32)
        value_grad = jnp.zeros((enc_rows, head), f32)
        for chunk in range(chunks):
            at = slice(chunk * block, (chunk + 1) * block)
            found = []
            for h in range(2):
                query, grad = q_s[2 * kv + h, at, :], g_s[2 * kv + h, at, :]
                score = dot_t(key, query)
                share = jnp.exp(score - jnp.max(score, axis=0, keepdims=True))
                share = share * (1.0 / jnp.sum(share, axis=0, keepdims=True))
                pull = dot_t(value, grad)
                delta = jnp.sum(share * pull, axis=0, keepdims=True)
                grad_low = (share * (pull - delta)).astype(bf16)
                found.append(dot_first(grad_low, key) * score_scale)
                key_grad = key_grad + matmul(grad_low, query)
                value_grad = value_grad + matmul(share.astype(bf16), grad)
            pair_s[kv, at, :] = jnp.concatenate(found, axis=1).astype(bf16)
        dk_s[0, kv] = key_grad.astype(bf16)
        dk_s[1, kv] = value_grad.astype(bf16)
        return carry

    lax.fori_loop(0, kv_heads, attend_back, 0)
    for kv in range(kv_heads):
        dq_s[:, 2 * kv * head : 2 * (kv + 1) * head] = pair_s[kv]
    send_parts(4, lambda at: dot_t(dq_s[at, :], wa_ref[:, at_cq : at_cq + wide]))
    for n in range(2):
        kv_out[:, n * wide // 2 : (n + 1) * wide // 2] = jnp.concatenate(
            [dk_s[n, kv] for kv in range(kv_heads)], axis=1
        )
    ga_out[:, at_cq : at_cq + wide] = dot_first(nc_s[...], dq_s[...]).astype(bf16)
    ga_out[:, at_ck : at_ck + wide] = dot_first(enc_ref[...], kv_out[...]).astype(bf16)

    def leave_cross(at, both):
        grad, gain = norm_pull(after_self[at, :], cross_gain, both)
        dx_s[at, :] += grad
        low = dx_s[at, :].astype(bf16)
        low_s[at, :] = low
        gain_out[0:1, :] += gain
        context = matmul(low, wa_ref[:, at_out : at_out + wide]).astype(bf16)
        for q in range(4):
            gctx_out[q, at, :] = context[:, q * wide // 4 : (q + 1) * wide // 4]

    take_parts(4, leave_cross)
    ga_out[:, at_out : at_out + wide] = dot_first(low_s[...], ctx_ref[...]).astype(bf16)
    mine = halves(dx_s, core)
    for layer in range(layers):
        grad_out[layer] = mine[layer]

    store.wait()

    def settle(n, cols, units):
        for along_y in (True, False):
            weights_all(n, cols, along_y).wait_send()
            grads_all(n, cols, along_y).wait()

    each_block(settle)


def middle(scale, layers, feed, context, x_low, cot, enc, weights, gains, feed_whole):
    f32, bf16 = jnp.float32, jnp.bfloat16
    rows, width = x_low.shape
    wide = context.shape[1]
    head = round(scale**-2)
    heads = wide // head
    own = rows // (2 * layers)
    cols = feed_whole.shape[1]
    block = rows // 2
    vmem, anywhere = pl.BlockSpec(memory_space=pltpu.VMEM), pl.BlockSpec(memory_space=pl.ANY)
    got = jax.ShapeDtypeStruct((layers, 2, 32, cols), bf16)
    return pl.pallas_call(
        functools.partial(middle_kernel, scale, layers, feed),
        name="middle",
        out_shape=(
            jax.ShapeDtypeStruct((layers, own, width), bf16),
            jax.ShapeDtypeStruct((layers, own, width), f32),
            jax.ShapeDtypeStruct((4, rows, wide // 4), bf16),
            jax.ShapeDtypeStruct((enc.shape[0], wide), bf16),
            jax.ShapeDtypeStruct((width, weights.shape[1]), bf16),
            jax.ShapeDtypeStruct((2, width), f32),
            jax.ShapeDtypeStruct((width, cols), bf16),
            got,
            got,
        ),
        in_specs=[vmem] * 6 + [anywhere],
        out_specs=(vmem,) * 6 + (anywhere,) * 3,
        scratch_shapes=[
            pltpu.VMEM((width, cols), bf16),
            pltpu.VMEM((width, cols), bf16),
            pltpu.VMEM((rows, width), f32),
            pltpu.VMEM((rows, width), f32),
            pltpu.VMEM((rows, width), bf16),
            pltpu.VMEM((rows, width), bf16),
            pltpu.VMEM((width, rows), bf16),
            pltpu.VMEM((width, rows), bf16),
            pltpu.VMEM((rows, width), f32),
            pltpu.VMEM((rows, width), f32),
            pltpu.VMEM((2, 2, block, width), bf16),
            pltpu.VMEM((2, 2, block, width), bf16),
            pltpu.VMEM((2, rows // 2, width), bf16),
            pltpu.VMEM((heads, rows, head), bf16),
            pltpu.VMEM((heads // 2, enc.shape[0], head), bf16),
            pltpu.VMEM((heads // 2, enc.shape[0], head), bf16),
            pltpu.VMEM((heads, rows, head), bf16),
            pltpu.VMEM((heads // 2, rows, 2 * head), bf16),
            pltpu.VMEM((rows, wide), bf16),
            pltpu.VMEM((rows, wide), bf16),
            pltpu.VMEM((2, heads // 2, enc.shape[0], head), bf16),
            pltpu.VMEM((rows, width), bf16),
            dma((pl.cdiv(feed, tile),)),
            dma((2, pl.cdiv(feed, tile))),
            dma((2, pl.cdiv(feed, tile))),
            dma((2, pl.cdiv(feed, tile))),
            dma((2, pl.cdiv(feed, tile))),
            dma((1,)),
            dma((2, 5, 2)),
        ],
        compiler_params=pltpu.CompilerParams(
            collective_id=9, has_side_effects=True, vmem_limit_bytes=67043328
        ),
    )(context, x_low, cot, enc, weights, gains, feed_whole)

def dot_t(left, right):
    return lax.dot_general(
        left, right, (((1,), (1,)), ((), ())), preferred_element_type=jnp.float32
    )


def dot_first(left, right):
    return lax.dot_general(
        left, right, (((0,), (0,)), ((), ())), preferred_element_type=jnp.float32
    )


def unpack_pair(qkv_ref, q_s, k_s, v_s, score_scale):
    sources, rows, _ = qkv_ref.shape
    blocks = rows // 128 * sources
    head = k_s.shape[1]
    for block in range(blocks):
        source, turn = block % sources, block // sources
        tile = qkv_ref[source, turn * 128 : (turn + 1) * 128, :]
        at = slice(block * 128, (block + 1) * 128)
        q_s[0, at, :] = (tile[:, :head] * score_scale).astype(jnp.bfloat16)
        q_s[1, at, :] = (tile[:, head : 2 * head] * score_scale).astype(jnp.bfloat16)
        k_s[at, :] = tile[:, 2 * head : 3 * head]
        v_s[at, :] = tile[:, 3 * head :]


def by_heads(
    inputs,
    encoder_out,
    out_cotangent,
    bucket_ids,
    position_table,
    self_gain,
    self_query,
    self_key,
    self_value,
    self_output,
    cross_gain,
    cross_query,
    cross_key,
    cross_value,
    cross_output,
    feed_gain,
    gate_weight,
    up_weight,
    down_weight,
):
    f32, bf16 = jnp.float32, jnp.bfloat16
    batches, own, width = inputs.shape
    enc_own = encoder_out.shape[1]
    length = bucket_ids.shape[0]
    heads_all, buckets = position_table.shape
    fsdp = lax.axis_size(fsdp_axis)
    plane = fsdp // batches
    rank, core = lax.axis_index(fsdp_axis), lax.axis_index(tensor_axis)
    head = self_query.shape[1] // (heads_all // 2)
    kv_local = self_key.shape[1] // head
    scale = head ** (-0.5)
    blocks = length // tile
    rows = batches * 2 * own
    enc_rows = batches * 2 * enc_own
    feed = gate_weight.shape[1]
    kv_index = core * kv_local + rank % plane
    table_here = lax.dynamic_slice_in_dim(position_table, 2 * kv_index, 2, 0)
    bucket_range = jnp.arange(buckets, dtype=jnp.int32)
    lower = jnp.sum((bucket_ids[None, :] < bucket_range[:, None]).astype(jnp.int32), axis=1)
    upper = jnp.concatenate([lower[1:], jnp.full((1,), length, jnp.int32)])
    offsets = (
        tile * jnp.arange(blocks, dtype=jnp.int32)[:, None]
        + jnp.arange(2 * tile, dtype=jnp.int32)[None, :]
    ).reshape(-1)

    def bias_of(offset):
        hit = (offset[None] >= lower[:, None]) & (offset[None] < upper[:, None])
        value = jnp.dot(table_here, hit.astype(f32), precision=highest)
        return jnp.where(offset[None] >= 0, value, masked_score).reshape(2 * blocks, 2 * tile)

    down_steps = (
        tile * jnp.arange(blocks, dtype=jnp.int32)[:, None]
        + (tile - 1)
        - jnp.arange(2 * tile, dtype=jnp.int32)[None, :]
    ).reshape(-1)
    bias_down = bias_of(down_steps)
    bias_up = bias_of(offsets - tile)

    def swap_add(partial):
        low = partial.astype(bf16)
        return low.astype(f32) + swap_cores(low).astype(f32)

    x_low, enc_all, cot_low, qkv_here, context_low, context_full, log_total, norm_t, *wholes = begin(
        scale,
        batches,
        inputs,
        encoder_out,
        out_cotangent,
        self_gain[None],
        bias_down,
        self_query,
        self_key,
        self_value,
        self_output.T,
        cross_query,
        cross_key,
        cross_value,
        cross_output.T,
        gate_weight,
        up_weight,
        down_weight.T,
    )
    x_low, enc_all = x_low.reshape(rows, width), enc_all.reshape(-1, width)
    in_full, rest_full, feed_full = [whole.reshape(width, -1) for whole in wholes]
    layer_rows, grad_after_self, grad_context, cross_kv, grads, mid_gains, feed_grads, *feed_got = (
        middle(
            scale,
            batches,
            feed,
            context_low,
            x_low,
            cot_low.reshape(rows, width),
            enc_all,
            rest_full,
            jnp.stack([cross_gain, feed_gain]),
            feed_full,
        )
    )
    feed_got = [came.reshape(batches, 2, 2, 16, -1) for came in feed_got]

    grad_qkv, diagonal_sums, kv_sum, layer_out, *most_sums = attend_backward(
        scale,
        batches,
        qkv_here,
        grad_context,
        context_full,
        log_total,
        bias_up,
        cross_kv.reshape(plane, enc_rows, -1),
        layer_rows,
        grads,
        feed_grads,
        feed_got,
    )
    spread = offsets - (tile - 1)
    hit = ((spread[None] >= lower[:, None]) & (spread[None] < upper[:, None])).astype(f32)
    hit = jnp.transpose(hit.reshape(buckets, blocks, 2 * tile), (1, 0, 2))
    in_sum, ended, table_sum, gain_sums = close_rows(
        batches,
        heads_all,
        grad_qkv,
        x_low,
        in_full,
        grad_after_self,
        kv_sum,
        self_gain[None],
        mid_gains,
        diagonal_sums,
        hit,
        norm_t,
        rest_full,
    )
    results = finish(in_sum, *most_sums, ended, layer_out, table_sum, gain_sums)
    turned, gains = (8, 13, 17), (4, 9, 14)
    return tuple(
        result.T if n in turned else result.reshape(-1) if n in gains else result
        for n, result in enumerate(results)
    )


def on_either(*args):
    batches, kv_heads = args[0].shape[0], args[7].shape[1] * lax.axis_size(tensor_axis)
    head_size = args[6].shape[1] * lax.axis_size(tensor_axis) // args[4].shape[0]
    devices = lax.axis_size(fsdp_axis) * lax.axis_size(tensor_axis)
    if devices == batches * (kv_heads // head_size):
        return by_heads(*args)
    return on_device(*args)


def solution(mesh):
    placed = (
        P(None, (fsdp_axis, tensor_axis), None),
        P(None, (fsdp_axis, tensor_axis), None),
        P(None, (fsdp_axis, tensor_axis), None),
        P(),
        P(),
        P(),
        P(fsdp_axis, tensor_axis),
        P(fsdp_axis, tensor_axis),
        P(fsdp_axis, tensor_axis),
        P(tensor_axis, fsdp_axis),
        P(),
        P(fsdp_axis, tensor_axis),
        P(fsdp_axis, tensor_axis),
        P(fsdp_axis, tensor_axis),
        P(tensor_axis, fsdp_axis),
        P(),
        P(fsdp_axis, tensor_axis),
        P(fsdp_axis, tensor_axis),
        P(tensor_axis, fsdp_axis),
    )
    return jax.shard_map(
        on_either,
        mesh=mesh,
        in_specs=placed,
        out_specs=(
            P(None, (fsdp_axis, tensor_axis), None),
            P(None, (fsdp_axis, tensor_axis), None),
            P(None, (fsdp_axis, tensor_axis), None),
            P(),
            P(),
            P(fsdp_axis, tensor_axis),
            P(fsdp_axis, tensor_axis),
            P(fsdp_axis, tensor_axis),
            P(tensor_axis, fsdp_axis),
            P(),
            P(fsdp_axis, tensor_axis),
            P(fsdp_axis, tensor_axis),
            P(fsdp_axis, tensor_axis),
            P(tensor_axis, fsdp_axis),
            P(),
            P(fsdp_axis, tensor_axis),
            P(fsdp_axis, tensor_axis),
            P(tensor_axis, fsdp_axis),
        ),
        check_vma=False,
    )
```

```python
import functools
import math
import types

import jax
import jax.numpy as jnp
from jax import lax
from jax.experimental import pallas as pl
from jax.experimental.pallas import tpu as pltpu
from jax.sharding import PartitionSpec as P

norm_eps = 1e-06
masked_score = -1e30
highest = lax.Precision.HIGHEST
key_block_width = 256
tile = 256
fsdp_axis, tensor_axis = "fsdp", "tensor"


def matmul(left, right):
    return jnp.dot(left, right, preferred_element_type=jnp.float32)


def norm_rows(row_block, gain):
    return (
        row_block
        * lax.rsqrt(jnp.mean(row_block * row_block, axis=-1, keepdims=True) + norm_eps)
        * gain
    )


def gather_rows(row_block):
    return lax.all_gather(row_block, tensor_axis, axis=0, tiled=True)


def sum_rows(row_block):
    return lax.psum_scatter(
        row_block.astype(jnp.bfloat16), tensor_axis, scatter_dimension=0, tiled=True
    ).astype(jnp.float32)


def gather_weights(shards):
    (
        self_query,
        self_key,
        self_value,
        self_output,
        cross_query,
        cross_key,
        cross_value,
        cross_output,
        gate_weight,
        up_weight,
        down_weight,
    ) = shards
    inner = (
        lax.all_gather(self_query, fsdp_axis, axis=0, tiled=True),
        lax.all_gather(self_key, fsdp_axis, axis=0, tiled=True),
        lax.all_gather(self_value, fsdp_axis, axis=0, tiled=True),
        lax.all_gather(cross_query, fsdp_axis, axis=0, tiled=True),
        lax.all_gather(cross_key, fsdp_axis, axis=0, tiled=True),
        lax.all_gather(cross_value, fsdp_axis, axis=0, tiled=True),
        lax.all_gather(gate_weight, fsdp_axis, axis=0, tiled=True),
        lax.all_gather(up_weight, fsdp_axis, axis=0, tiled=True),
    )
    outer = (
        lax.all_gather(self_output, fsdp_axis, axis=1, tiled=True),
        lax.all_gather(cross_output, fsdp_axis, axis=1, tiled=True),
        lax.all_gather(down_weight, fsdp_axis, axis=1, tiled=True),
    )
    return (
        inner[0],
        inner[1],
        inner[2],
        outer[0],
        inner[3],
        inner[4],
        inner[5],
        outer[1],
        inner[6],
        inner[7],
        outer[2],
    )


def scatter_grads(grads_full):
    (
        self_query,
        self_key,
        self_value,
        self_output,
        cross_query,
        cross_key,
        cross_value,
        cross_output,
        gate_weight,
        up_weight,
        down_weight,
    ) = grads_full
    inner = (
        lax.psum_scatter(self_query, fsdp_axis, scatter_dimension=0, tiled=True),
        lax.psum_scatter(self_key, fsdp_axis, scatter_dimension=0, tiled=True),
        lax.psum_scatter(self_value, fsdp_axis, scatter_dimension=0, tiled=True),
        lax.psum_scatter(cross_query, fsdp_axis, scatter_dimension=0, tiled=True),
        lax.psum_scatter(cross_key, fsdp_axis, scatter_dimension=0, tiled=True),
        lax.psum_scatter(cross_value, fsdp_axis, scatter_dimension=0, tiled=True),
        lax.psum_scatter(gate_weight, fsdp_axis, scatter_dimension=0, tiled=True),
        lax.psum_scatter(up_weight, fsdp_axis, scatter_dimension=0, tiled=True),
    )
    outer = (
        lax.psum_scatter(self_output, fsdp_axis, scatter_dimension=1, tiled=True),
        lax.psum_scatter(cross_output, fsdp_axis, scatter_dimension=1, tiled=True),
        lax.psum_scatter(down_weight, fsdp_axis, scatter_dimension=1, tiled=True),
    )
    return (
        inner[0],
        inner[1],
        inner[2],
        outer[0],
        inner[3],
        inner[4],
        inner[5],
        outer[1],
        inner[6],
        inner[7],
        outer[2],
    )


def add_all(first, second):
    return tuple((left_item + right_item for left_item, right_item in zip(first, second)))


def fold_keys(key_rows, value_rows, step_fn, initial):
    return step_fn(
        initial,
        (
            lax.all_gather(key_rows, fsdp_axis, axis=0, tiled=True),
            lax.all_gather(value_rows, fsdp_axis, axis=0, tiled=True),
        ),
        jnp.int32(0),
    )


def on_device(
    inputs,
    encoder_out,
    out_cotangent,
    bucket_ids,
    position_table,
    self_gain,
    self_query,
    self_key,
    self_value,
    self_output,
    cross_gain,
    cross_query,
    cross_key,
    cross_value,
    cross_output,
    feed_gain,
    gate_weight,
    up_weight,
    down_weight,
):
    shards = (
        self_query,
        self_key,
        self_value,
        self_output,
        cross_query,
        cross_key,
        cross_value,
        cross_output,
        gate_weight,
        up_weight,
        down_weight,
    )
    batches = inputs.shape[0]
    tensor_size = lax.axis_size(tensor_axis)
    piece_rows = inputs.shape[1] * tensor_size
    length = bucket_ids.shape[0]
    heads_all = position_table.shape[0]
    buckets = position_table.shape[1]
    local_heads = heads_all // tensor_size
    head_size = self_query.shape[1] // local_heads
    kv_local = self_key.shape[1] // head_size
    group_size = local_heads // kv_local
    score_scale = head_size ** (-0.5)
    fsdp_rank = lax.axis_index(fsdp_axis)
    tensor_rank = lax.axis_index(tensor_axis)
    query_start = fsdp_rank * piece_rows
    encoder_rows = encoder_out.shape[1] * tensor_size
    table_local = lax.dynamic_slice_in_dim(
        position_table, tensor_rank * local_heads, local_heads, 0
    )
    bucket_range = jnp.arange(buckets, dtype=jnp.int32)
    lower_bounds = jnp.sum((bucket_ids[None, :] < bucket_range[:, None]).astype(jnp.int32), axis=1)
    upper_bounds = jnp.concatenate([lower_bounds[1:], jnp.full((1,), length, jnp.int32)])

    def position_bias(row_start, col_start, row_count, col_count):
        offsets = (
            row_start
            - col_start
            + jnp.arange(row_count, dtype=jnp.int32)[:, None]
            - jnp.arange(col_count, dtype=jnp.int32)[None, :]
        )
        indicator = (
            (offsets[None] >= lower_bounds[:, None, None])
            & (offsets[None] < upper_bounds[:, None, None])
        ).astype(jnp.float32)
        bias_values = jnp.einsum("hb,bij->hij", table_local, indicator, precision=highest).reshape(
            kv_local, group_size, row_count, col_count
        )
        return (bias_values, offsets >= 0, indicator)

    def split_heads(row_block):
        return row_block.reshape(row_block.shape[0], kv_local, group_size, head_size)

    def split_kv(row_block):
        return row_block.reshape(row_block.shape[0], kv_local, head_size)

    def backward(batch_index, saved_state, weights):
        (
            query_full,
            key_full,
            value_full,
            output_full,
            cross_query_full,
            cross_key_full,
            cross_value_full,
            cross_output_full,
            gate_full,
            up_full,
            down_full,
        ) = weights
        cotangent = out_cotangent[batch_index].astype(jnp.float32)
        grad_feed = gather_rows(out_cotangent[batch_index])
        hidden = saved_state.hidden
        normed_feed = saved_state.normed_feed
        down_grad = jnp.einsum("tf,td->fd", hidden, grad_feed, preferred_element_type=jnp.float32)
        grad_hidden = jnp.einsum(
            "td,fd->tf", grad_feed, down_full, preferred_element_type=jnp.float32
        )
        gelu_pull = jax.vjp(
            lambda gate_in, up_in: jax.nn.gelu(gate_in, approximate=True) * up_in,
            saved_state.gate_values,
            saved_state.up_values,
        )[1]
        grad_gate, grad_up = gelu_pull(grad_hidden)
        grad_gate = grad_gate.astype(jnp.bfloat16)
        grad_up = grad_up.astype(jnp.bfloat16)
        gate_grad = jnp.einsum(
            "td,tf->df", normed_feed, grad_gate, preferred_element_type=jnp.float32
        )
        up_grad = jnp.einsum("td,tf->df", normed_feed, grad_up, preferred_element_type=jnp.float32)
        feed_rows = sum_rows(
            jnp.einsum("tf,df->td", grad_gate, gate_full, preferred_element_type=jnp.float32)
            + jnp.einsum("tf,df->td", grad_up, up_full, preferred_element_type=jnp.float32)
        )
        grad_norm_feed, feed_gain_grad = jax.vjp(norm_rows, saved_state.after_cross, feed_gain)[
            1
        ](feed_rows)
        grad_after_cross = cotangent + grad_norm_feed
        cross_context = saved_state.cross_context
        cross_weights = saved_state.cross_weights
        encoded = saved_state.encoded
        grad_cross_branch = gather_rows(grad_after_cross.astype(jnp.bfloat16))
        cross_output_grad = jnp.einsum(
            "te,td->ed", cross_context, grad_cross_branch, preferred_element_type=jnp.float32
        )
        grad_cross_context = split_heads(
            jnp.einsum(
                "td,ed->te",
                grad_cross_branch,
                cross_output_full,
                preferred_element_type=jnp.float32,
            ).astype(jnp.bfloat16)
        )
        grad_cross_weights = jnp.einsum(
            "ikgd,jkd->kgij",
            grad_cross_context,
            split_kv(saved_state.cross_values),
            preferred_element_type=jnp.float32,
        )
        grad_cross_scores = (
            cross_weights
            * (
                grad_cross_weights
                - jnp.sum(cross_weights * grad_cross_weights, axis=-1, keepdims=True)
            )
        ).astype(jnp.bfloat16)
        grad_cross_queries = (
            (
                jnp.einsum(
                    "kgij,jkd->ikgd",
                    grad_cross_scores,
                    split_kv(saved_state.cross_keys),
                    preferred_element_type=jnp.float32,
                )
                * score_scale
            )
            .reshape(piece_rows, local_heads * head_size)
            .astype(jnp.bfloat16)
        )
        key_part = (
            jnp.einsum(
                "kgij,ikgd->jkd",
                grad_cross_scores,
                split_heads(saved_state.cross_queries),
                preferred_element_type=jnp.float32,
            )
            * score_scale
        ).reshape(encoded.shape[0], kv_local * head_size)
        value_part = jnp.einsum(
            "kgij,ikgd->jkd",
            saved_state.cross_low,
            grad_cross_context,
            preferred_element_type=jnp.float32,
        ).reshape(encoded.shape[0], kv_local * head_size)
        key_sum, value_sum = (
            lax.psum_scatter(key_part, fsdp_axis, scatter_dimension=0, tiled=True),
            lax.psum_scatter(value_part, fsdp_axis, scatter_dimension=0, tiled=True),
        )
        key_low = key_sum.astype(jnp.bfloat16)
        value_low = value_sum.astype(jnp.bfloat16)
        encoded_own = lax.dynamic_slice_in_dim(encoded, fsdp_rank * encoder_rows, encoder_rows, 0)
        cross_key_grad = jnp.einsum(
            "ed,ec->dc", encoded_own, key_low, preferred_element_type=jnp.float32
        )
        cross_value_grad = jnp.einsum(
            "ed,ec->dc", encoded_own, value_low, preferred_element_type=jnp.float32
        )
        encoder_grad = sum_rows(
            jnp.einsum("ec,dc->ed", key_low, cross_key_full, preferred_element_type=jnp.float32)
            + jnp.einsum(
                "ec,dc->ed", value_low, cross_value_full, preferred_element_type=jnp.float32
            )
        )
        cross_query_grad = jnp.einsum(
            "td,tc->dc",
            saved_state.normed_cross,
            grad_cross_queries,
            preferred_element_type=jnp.float32,
        )
        cross_rows = sum_rows(
            jnp.einsum(
                "tc,dc->td",
                grad_cross_queries,
                cross_query_full,
                preferred_element_type=jnp.float32,
            )
        )
        grad_norm_cross, cross_gain_grad = jax.vjp(
            norm_rows, saved_state.after_self, cross_gain
        )[1](cross_rows)
        grad_after_self = grad_after_cross + grad_norm_cross
        queries = saved_state.queries
        keys_own = saved_state.keys_own
        values_own = saved_state.values_own
        context = saved_state.context
        log_total = saved_state.log_total
        normed_self = saved_state.normed_self
        query_heads = split_heads(queries)
        grad_self_branch = gather_rows(grad_after_self.astype(jnp.bfloat16))
        self_output_grad = jnp.einsum(
            "te,td->ed",
            saved_state.context_low,
            grad_self_branch,
            preferred_element_type=jnp.float32,
        )
        grad_context = jnp.einsum(
            "td,ed->te", grad_self_branch, output_full, preferred_element_type=jnp.float32
        ).astype(jnp.bfloat16)
        grad_context_heads = split_heads(grad_context)
        row_delta = jnp.transpose(
            jnp.sum(grad_context_heads.astype(jnp.float32) * context, axis=-1), (1, 2, 0)
        )

        def query_step():

            def step(carried, pieces, piece_start):
                key_piece, value_piece = pieces
                piece_length = key_piece.shape[0]
                block_width = math.gcd(piece_length, key_block_width)
                block_count = piece_length // block_width
                key_blocks = key_piece.reshape(block_count, block_width, kv_local, head_size)
                value_blocks = value_piece.reshape(block_count, block_width, kv_local, head_size)
                block_starts = block_width * jnp.arange(block_count, dtype=jnp.int32)

                def step_one_block(current, block_data):
                    key_block, value_block, block_start = block_data
                    bias_values, allowed, indicator = position_bias(
                        query_start, block_start, piece_rows, block_width
                    )
                    scores = (
                        jnp.einsum(
                            "ikgd,jkd->kgij",
                            query_heads,
                            key_block,
                            preferred_element_type=jnp.float32,
                        )
                        * score_scale
                        + bias_values
                    )
                    shares = jnp.where(allowed, jnp.exp(scores - log_total[..., None]), 0.0)
                    grad_shares = jnp.einsum(
                        "ikgd,jkd->kgij",
                        grad_context_heads,
                        value_block,
                        preferred_element_type=jnp.float32,
                    )
                    grad_scores = shares * (grad_shares - row_delta[..., None])
                    bias_grad = current[1] + jnp.einsum(
                        "hij,bij->hb",
                        grad_scores.reshape(local_heads, piece_rows, block_width),
                        indicator,
                        precision=highest,
                    )
                    scores_low = grad_scores.astype(jnp.bfloat16)
                    query_grad = (
                        current[0]
                        + jnp.einsum(
                            "kgij,jkd->ikgd",
                            scores_low,
                            key_block,
                            preferred_element_type=jnp.float32,
                        )
                        * score_scale
                    )
                    key_block_grad = (
                        jnp.einsum(
                            "kgij,ikgd->jkd",
                            scores_low,
                            query_heads,
                            preferred_element_type=jnp.float32,
                        ).reshape(block_width, kv_local * head_size)
                        * score_scale
                    )
                    value_block_grad = jnp.einsum(
                        "kgij,ikgd->jkd",
                        shares.astype(jnp.bfloat16),
                        grad_context_heads,
                        preferred_element_type=jnp.float32,
                    ).reshape(block_width, kv_local * head_size)
                    keys_all = lax.dynamic_update_slice_in_dim(
                        current[2],
                        lax.dynamic_slice_in_dim(current[2], block_start, block_width, 0)
                        + key_block_grad,
                        block_start,
                        0,
                    )
                    values_all = lax.dynamic_update_slice_in_dim(
                        current[3],
                        lax.dynamic_slice_in_dim(current[3], block_start, block_width, 0)
                        + value_block_grad,
                        block_start,
                        0,
                    )
                    return ((query_grad, bias_grad, keys_all, values_all), None)

                carried, unused = lax.scan(
                    step_one_block, carried, (key_blocks, value_blocks, block_starts)
                )
                return carried

            return step

        query_zero = jnp.zeros((piece_rows, kv_local, group_size, head_size), jnp.float32)
        bias_zero = jnp.zeros((local_heads, buckets), jnp.float32)
        all_zero = jnp.zeros((length, kv_local * head_size), jnp.float32)
        query_grad, bias_grad, keys_all, values_all = fold_keys(
            keys_own, values_own, query_step(), (query_zero, bias_zero, all_zero, all_zero)
        )
        key_sum_self, value_sum_self = (
            lax.psum_scatter(keys_all, fsdp_axis, scatter_dimension=0, tiled=True),
            lax.psum_scatter(values_all, fsdp_axis, scatter_dimension=0, tiled=True),
        )
        key_grad_low = key_sum_self.astype(jnp.bfloat16)
        value_grad_low = value_sum_self.astype(jnp.bfloat16)
        query_grad_low = query_grad.reshape(piece_rows, local_heads * head_size).astype(
            jnp.bfloat16
        )
        self_query_grad = jnp.einsum(
            "td,tc->dc", normed_self, query_grad_low, preferred_element_type=jnp.float32
        )
        self_key_grad = jnp.einsum(
            "td,tc->dc", normed_self, key_grad_low, preferred_element_type=jnp.float32
        )
        self_value_grad = jnp.einsum(
            "td,tc->dc", normed_self, value_grad_low, preferred_element_type=jnp.float32
        )
        self_rows = sum_rows(
            jnp.einsum("tc,dc->td", query_grad_low, query_full, preferred_element_type=jnp.float32)
            + jnp.einsum("tc,dc->td", key_grad_low, key_full, preferred_element_type=jnp.float32)
            + jnp.einsum(
                "tc,dc->td", value_grad_low, value_full, preferred_element_type=jnp.float32
            )
        )
        grad_norm_self, self_gain_grad = jax.vjp(norm_rows, saved_state.own_rows, self_gain)[1](
            self_rows
        )
        input_grad = grad_after_self + grad_norm_self
        grads_full = (
            self_query_grad,
            self_key_grad,
            self_value_grad,
            self_output_grad,
            cross_query_grad,
            cross_key_grad,
            cross_value_grad,
            cross_output_grad,
            gate_grad,
            up_grad,
            down_grad,
        )
        extras = (bias_grad, self_gain_grad, cross_gain_grad, feed_gain_grad)
        return (grads_full, extras, input_grad, encoder_grad)

    layer_list = []
    input_list = []
    encoder_list = []
    small_sums = None
    shard_grads = None
    for batch_index in range(batches):
        weights_forward = gather_weights(shards)
        (
            forward_query_full,
            forward_key_full,
            forward_value_full,
            forward_output_full,
            forward_cross_query_full,
            forward_cross_key_full,
            forward_cross_value_full,
            forward_cross_output_full,
            forward_gate_full,
            forward_up_full,
            forward_down_full,
        ) = weights_forward
        own_rows = inputs[batch_index].astype(jnp.float32)
        forward_normed_self = gather_rows(norm_rows(own_rows, self_gain).astype(jnp.bfloat16))
        forward_queries = matmul(forward_normed_self, forward_query_full).astype(jnp.bfloat16)
        forward_keys_own = matmul(forward_normed_self, forward_key_full).astype(jnp.bfloat16)
        forward_values_own = matmul(forward_normed_self, forward_value_full).astype(jnp.bfloat16)
        forward_query_heads = split_heads(forward_queries)

        def forward_step(carried, pieces, piece_start):
            key_piece, value_piece = pieces
            piece_length = key_piece.shape[0]
            block_width = math.gcd(piece_length, key_block_width)
            block_count = piece_length // block_width
            key_blocks = key_piece.reshape(block_count, block_width, kv_local, head_size)
            value_blocks = value_piece.reshape(block_count, block_width, kv_local, head_size)
            block_starts = block_width * jnp.arange(block_count, dtype=jnp.int32)

            def forward_one_block(current, block_data):
                running_max, running_total, accumulated = current
                key_block, value_block, block_start = block_data
                bias_values, allowed, indicator = position_bias(
                    query_start, block_start, piece_rows, block_width
                )
                scores = (
                    jnp.einsum(
                        "ikgd,jkd->kgij",
                        forward_query_heads,
                        key_block,
                        preferred_element_type=jnp.float32,
                    )
                    * score_scale
                    + bias_values
                )
                scores = jnp.where(allowed, scores, masked_score)
                new_max = jnp.maximum(running_max, jnp.max(scores, axis=-1))
                factor = jnp.exp(running_max - new_max)
                shares = jnp.where(allowed, jnp.exp(scores - new_max[..., None]), 0.0)
                running_total = running_total * factor + jnp.sum(shares, axis=-1)
                update = jnp.einsum(
                    "kgij,jkd->ikgd",
                    shares.astype(jnp.bfloat16),
                    value_block,
                    preferred_element_type=jnp.float32,
                )
                accumulated = accumulated * jnp.transpose(factor, (2, 0, 1))[..., None] + update
                return ((new_max, running_total, accumulated), None)

            carried, unused = lax.scan(
                forward_one_block, carried, (key_blocks, value_blocks, block_starts)
            )
            return carried

        stat_shape = (kv_local, group_size, piece_rows)
        initial = (
            jnp.full(stat_shape, masked_score, jnp.float32),
            jnp.zeros(stat_shape, jnp.float32),
            jnp.zeros((piece_rows, kv_local, group_size, head_size), jnp.float32),
        )
        running_max, running_total, accumulated = fold_keys(
            forward_keys_own, forward_values_own, forward_step, initial
        )
        forward_context = accumulated / jnp.transpose(running_total, (2, 0, 1))[..., None]
        forward_log_total = running_max + jnp.log(running_total)
        context_low = forward_context.reshape(piece_rows, local_heads * head_size).astype(
            jnp.bfloat16
        )
        after_self = own_rows + sum_rows(matmul(context_low, forward_output_full))
        normed_cross = gather_rows(norm_rows(after_self, cross_gain).astype(jnp.bfloat16))
        cross_queries = matmul(normed_cross, forward_cross_query_full).astype(jnp.bfloat16)
        forward_encoded = lax.all_gather(
            encoder_out[batch_index], (fsdp_axis, tensor_axis), axis=0, tiled=True
        )
        cross_keys = matmul(forward_encoded, forward_cross_key_full).astype(jnp.bfloat16)
        cross_values = matmul(forward_encoded, forward_cross_value_full).astype(jnp.bfloat16)
        cross_scores = (
            jnp.einsum(
                "ikgd,jkd->kgij",
                split_heads(cross_queries),
                split_kv(cross_keys),
                preferred_element_type=jnp.float32,
            )
            * score_scale
        )
        forward_cross_weights = jax.nn.softmax(cross_scores, axis=-1)
        cross_low = forward_cross_weights.astype(jnp.bfloat16)
        forward_cross_context = (
            jnp.einsum(
                "kgij,jkd->ikgd",
                cross_low,
                split_kv(cross_values),
                preferred_element_type=jnp.float32,
            )
            .reshape(piece_rows, local_heads * head_size)
            .astype(jnp.bfloat16)
        )
        after_cross = after_self + sum_rows(
            matmul(forward_cross_context, forward_cross_output_full)
        )
        forward_normed_feed = gather_rows(norm_rows(after_cross, feed_gain).astype(jnp.bfloat16))
        gate_values = matmul(forward_normed_feed, forward_gate_full)
        up_values = matmul(forward_normed_feed, forward_up_full)
        forward_hidden = (jax.nn.gelu(gate_values, approximate=True) * up_values).astype(
            jnp.bfloat16
        )
        layer_rows = after_cross + sum_rows(matmul(forward_hidden, forward_down_full))
        forward_saved_state = types.SimpleNamespace(
            own_rows=own_rows,
            normed_self=forward_normed_self,
            queries=forward_queries,
            keys_own=forward_keys_own,
            values_own=forward_values_own,
            context=forward_context,
            log_total=forward_log_total,
            context_low=context_low,
            after_self=after_self,
            normed_cross=normed_cross,
            cross_queries=cross_queries,
            encoded=forward_encoded,
            cross_keys=cross_keys,
            cross_values=cross_values,
            cross_weights=forward_cross_weights,
            cross_low=cross_low,
            cross_context=forward_cross_context,
            after_cross=after_cross,
            normed_feed=forward_normed_feed,
            gate_values=gate_values,
            up_values=up_values,
            hidden=forward_hidden,
        )
        layer_rows, saved_state = (layer_rows.astype(jnp.bfloat16), forward_saved_state)
        weights_backward = gather_weights(shards)
        grads_full, extras, input_grad, encoder_grad = backward(
            batch_index, saved_state, weights_backward
        )
        reduced = scatter_grads(grads_full)
        shard_grads = reduced if shard_grads is None else add_all(shard_grads, reduced)
        small_sums = extras if small_sums is None else add_all(small_sums, extras)
        layer_list.append(layer_rows)
        input_list.append(input_grad)
        encoder_list.append(encoder_grad)
    table_full = lax.dynamic_update_slice_in_dim(
        jnp.zeros((heads_all, buckets), jnp.float32), small_sums[0], tensor_rank * local_heads, 0
    )
    table_sum, self_gain_sum, cross_gain_sum, feed_gain_sum = lax.psum(
        (table_full, small_sums[1], small_sums[2], small_sums[3]), (fsdp_axis, tensor_axis)
    )
    return (
        jnp.stack(layer_list),
        jnp.stack(input_list),
        jnp.stack(encoder_list),
        table_sum,
        self_gain_sum,
        shard_grads[0],
        shard_grads[1],
        shard_grads[2],
        shard_grads[3],
        cross_gain_sum,
        shard_grads[4],
        shard_grads[5],
        shard_grads[6],
        shard_grads[7],
        feed_gain_sum,
        shard_grads[8],
        shard_grads[9],
        shard_grads[10],
    )


def to_chip(fsdp):
    return dict(device_id={fsdp_axis: fsdp}, device_id_type=pl.DeviceIdType.MESH)


def to_core(core):
    return dict(device_id={tensor_axis: core}, device_id_type=pl.DeviceIdType.MESH)


def chip_place(layers):
    rank = lax.axis_index(fsdp_axis)
    return rank, rank // 4, rank // 2 % 2, rank % 2


def peers_of(rank, y, x):
    found = []
    for o in (1, 2, 3):
        other_y = 1 - y if o & 2 else y
        other_x = 1 - x if o & 1 else x
        spot = 2 * other_y + other_x
        found.append((rank - 2 * y - x + spot, spot))
    return found


def greet_all(layers):
    chips = 4 * layers
    rank = lax.axis_index(fsdp_axis)
    barrier = pltpu.get_barrier_semaphore()
    for o in range(1, chips):
        pl.semaphore_signal(barrier, inc=1, **to_chip((rank + o) % chips))
    pl.semaphore_signal(barrier, inc=1, **to_core(1 - lax.axis_index(tensor_axis)))
    pl.semaphore_wait(barrier, chips)


def greet(layers):
    rank, z, y, x = chip_place(layers)
    barrier = pltpu.get_barrier_semaphore()
    for chip, spot in peers_of(rank, y, x):
        pl.semaphore_signal(barrier, inc=1, **to_chip(chip))
    for o in range(1, layers):
        pl.semaphore_signal(barrier, inc=1, **to_chip(rank - 4 * z + 4 * ((z + o) % layers)))
    pl.semaphore_signal(barrier, inc=1, **to_core(1 - lax.axis_index(tensor_axis)))
    pl.semaphore_wait(barrier, 3 + layers)


dma = pltpu.SemaphoreType.DMA


class Column:
    def __init__(self, layers, source, land, z_sem, core_sem=None):
        self.layers, self.source, self.land = layers, source, land
        self.z_sem, self.core_sem = z_sem, core_sem
        self.rank, self.z, self.y, self.x = chip_place(layers)
        self.core = lax.axis_index(tensor_axis)

    def place(self, layer):
        return (layer,) if self.core_sem is None else (layer, self.core)

    def hop(self, o):
        there = (self.z + o) % self.layers
        return pltpu.make_async_remote_copy(
            src_ref=self.source.at[there],
            dst_ref=self.land.at[self.place(self.z)],
            send_sem=self.z_sem.at[0, o],
            recv_sem=self.z_sem.at[1, self.z],
            **to_chip(self.rank + 4 * (there - self.z)),
        )

    def arrival(self, layer):
        return pltpu.make_async_remote_copy(
            src_ref=self.source.at[0],
            dst_ref=self.land.at[self.place(layer)],
            send_sem=self.z_sem.at[0, 0],
            recv_sem=self.z_sem.at[1, layer],
            **to_chip(self.rank + 4 - 8 * (self.z // 2)),
        )

    def over(self, layer):
        return pltpu.make_async_remote_copy(
            src_ref=self.land.at[layer, self.core],
            dst_ref=self.land.at[layer, self.core],
            send_sem=self.core_sem.at[0, layer],
            recv_sem=self.core_sem.at[1, layer],
            **to_core(1 - self.core),
        )

    def piece(self, o, n):
        there = (self.z + o) % self.layers
        at = pl.ds(pl.multiple_of(16 * n, 16), 16)
        return pltpu.make_async_remote_copy(
            src_ref=self.source.at[there, at],
            dst_ref=self.land.at[self.z, at],
            send_sem=self.z_sem.at[0, o],
            recv_sem=self.z_sem.at[1, self.z],
            **to_chip(self.rank + 4 * (there - self.z)),
        )

    def start(self):
        for o in range(1, self.layers):
            self.hop(o).start()
        self.land[self.place(self.z)] = self.source[self.z]

    def arrive(self):
        for o in range(1, self.layers):
            self.arrival((self.z + o) % self.layers).wait_recv()
        if self.core_sem is not None:
            for layer in range(self.layers):
                self.over(layer).start()

    def finish(self):
        for o in range(1, self.layers):
            self.hop(o).wait_send()
        if self.core_sem is not None:
            for layer in range(self.layers):
                self.over(layer).wait()


class PlaneSwap:
    def __init__(self, layers, source, land, sem):
        self.source, self.land, self.sem = source, land, sem
        self.rank, self.z, self.y, self.x = chip_place(layers)
        self.spot = 2 * self.y + self.x
        self.peers = peers_of(self.rank, self.y, self.x)

    def hop(self, o):
        chip, there = self.peers[o]
        return pltpu.make_async_remote_copy(
            src_ref=self.source.at[there],
            dst_ref=self.land.at[self.spot],
            send_sem=self.sem.at[0, o],
            recv_sem=self.sem.at[1, o],
            **to_chip(chip),
        )

    def start(self):
        for o in range(3):
            self.hop(o).start()
        self.land[self.spot] = self.source[self.spot]

    def arrival(self, o):
        chip, there = self.peers[o]
        return pltpu.make_async_remote_copy(
            src_ref=self.source.at[there],
            dst_ref=self.land.at[there],
            send_sem=self.sem.at[0, o],
            recv_sem=self.sem.at[1, o],
            **to_chip(chip),
        )

    def arrive(self):
        for o in range(3):
            self.arrival(o).wait_recv()

    def finish(self):
        for o in range(3):
            self.hop(o).wait_send()


class PlaneGather:
    def __init__(self, layers, source, land, sem, core_sem):
        self.source, self.land, self.sem, self.core_sem = source, land, sem, core_sem
        self.rank, self.z, self.y, self.x = chip_place(layers)
        self.core = lax.axis_index(tensor_axis)
        self.spot = 2 * self.y + self.x
        self.peers = peers_of(self.rank, self.y, self.x)

    def hop(self, o, spot):
        return pltpu.make_async_remote_copy(
            src_ref=self.source,
            dst_ref=self.land.at[spot, self.core],
            send_sem=self.sem.at[0, o],
            recv_sem=self.sem.at[1, o],
            **to_chip(self.peers[o][0]),
        )

    def over(self, spot):
        return pltpu.make_async_remote_copy(
            src_ref=self.land.at[spot, self.core],
            dst_ref=self.land.at[spot, self.core],
            send_sem=self.core_sem.at[0, spot],
            recv_sem=self.core_sem.at[1, spot],
            **to_core(1 - self.core),
        )

    def start(self):
        for o in range(3):
            self.hop(o, self.spot).start()
        self.land[self.spot, self.core] = self.source[...]

    def arrive(self):
        for o in range(3):
            self.hop(o, self.peers[o][1]).wait_recv()
        for spot in range(4):
            self.over(spot).start()

    def finish(self):
        for o in range(3):
            self.hop(o, self.spot).wait_send()
        for spot in range(4):
            self.over(spot).wait()


def close_kernel(
    layers,
    heads,
    gq_ref,
    x_ref,
    win_ref,
    gas_ref,
    kvs_ref,
    gains_ref,
    mid_ref,
    sums_ref,
    hit_ref,
    nt_s,
    wa_ref,
    sum_s,
    rows_land,
    table_out,
    gain_out,
    wkv_s,
    mine_s,
    halves_s,
    enc_s,
    ended_s,
    small_s,
    small_z,
    load_sem,
    core_sem,
    rows_z,
    small_sem,
    z_sem,
    *sum_refs,
):
    f32, bf16 = jnp.float32, jnp.bfloat16
    grads = GradSum(layers, slice(None), None, (), sum_s, *sum_refs)
    rows = Column(layers, ended_s, rows_land, rows_z)
    rank, z, y, x = chip_place(layers)
    core = lax.axis_index(tensor_axis)
    own = gas_ref.shape[1]
    width = x_ref.shape[1]
    enc_own = kvs_ref.shape[0] // (2 * layers)
    wide = kvs_ref.shape[1]
    kv_local = 4
    blocks = sums_ref.shape[0] // 2
    buckets = hit_ref.shape[1]
    gain = gains_ref[...]
    loads = pltpu.make_async_copy(
        wa_ref.at[:, pl.ds(2 * wide, wide)], wkv_s, load_sem.at[0]
    )
    loads.start()
    greet_all(layers)

    per_layer = width // layers

    def weigh(turn, carry):
        layer = grads.layer_of(2 * turn)
        at = pl.ds(pl.multiple_of(layer * per_layer, per_layer), per_layer)
        part = matmul(nt_s[at, :], gq_ref[...]).astype(bf16)
        grads.own[layer] = part.reshape(grads.own.shape[1:])
        grads.send_first(2 * turn)
        grads.send_first(2 * turn + 1)
        return carry

    lax.fori_loop(0, layers, weigh, 0)

    def gather(which):
        return jnp.concatenate(
            [
                gq_ref[pl.ds(pl.multiple_of((2 * layer + which) * own, own), own), :]
                for layer in range(layers)
            ],
            axis=0,
        )

    def across(n, shape_at):
        return pltpu.make_async_remote_copy(
            src_ref=halves_s.at[0, shape_at],
            dst_ref=halves_s.at[1, shape_at],
            send_sem=core_sem.at[0, n],
            recv_sem=core_sem.at[1, n],
            **to_core(1 - core),
        )

    body, tail = pl.ds(0, layers * own), pl.ds(layers * own, layers * enc_own)
    halves_s[0, body, :] = dot_t(gather(1 - core), win_ref[...]).astype(bf16)
    across(0, body).start()
    loads.wait()
    enc_s[...] = dot_t(kvs_ref[...], wkv_s[...])
    other = pl.ds(pl.multiple_of((1 - core) * layers * enc_own, enc_own), layers * enc_own)
    halves_s[0, tail, :] = enc_s[other, :].astype(bf16)
    across(1, tail).start()
    mine_s[...] = dot_t(gather(core), win_ref[...])
    grads.advance(1)
    grads.advance(2)

    found = [jnp.zeros((1, buckets), f32) for _ in range(2)]
    for d in range(blocks):
        by_bucket = lax.dot_general(
            sums_ref[...],
            hit_ref[d],
            (((1,), (1,)), ((), ())),
            precision=highest,
            preferred_element_type=f32,
        )
        for h in range(2):
            found[h] = found[h] + by_bucket[h * blocks + d : h * blocks + d + 1, :]
    half = width // 2
    lane = lax.broadcasted_iota(jnp.int32, (buckets, half), 1)
    spread = (lane % buckets == lax.broadcasted_iota(jnp.int32, (buckets, half), 0)).astype(f32)
    lane = lax.broadcasted_iota(jnp.int32, (1, half), 1)
    first_head = 2 * (core * kv_local + rank % 4)
    table = jnp.zeros((1, half), f32)
    for h in range(2):
        row = jnp.dot(found[h], spread, precision=highest, preferred_element_type=f32)
        table = table + jnp.where(lane // buckets == first_head + h, row, 0.0)
    small = [table, jnp.zeros((1, half), f32)]
    for n in (1, 0):
        small = [mid_ref[n : n + 1, :half], mid_ref[n : n + 1, half:]] + small

    across(0, body).wait()
    across(1, tail).wait()
    mine_enc = pl.ds(pl.multiple_of(core * layers * enc_own, enc_own), layers * enc_own)
    enc_sum = enc_s[mine_enc, :].astype(bf16).astype(f32) + halves_s[1, tail, :].astype(f32)

    total = jnp.zeros((1, width), f32)
    for layer in range(layers):
        at = slice(layer * own, (layer + 1) * own)
        both = mine_s[at, :].astype(bf16).astype(f32) + halves_s[1, at, :].astype(f32)
        v = x_ref[pl.ds(pl.multiple_of((2 * layer + core) * own, own), own), :].astype(f32)
        grad, gain_grad = norm_pull(v, gain, both)
        total = total + gain_grad
        ended_s[layer, :own, :] = (gas_ref[layer] + grad).astype(bf16)
        ended_s[layer, own:, :] = enc_sum[layer * enc_own : (layer + 1) * enc_own].astype(bf16)
    small_s[0] = jnp.concatenate([total[:, :half], total[:, half:]] + small, axis=0)
    chips = 4 * layers

    def spread_to(o):
        there = (rank + o) % chips
        return pltpu.make_async_remote_copy(
            src_ref=small_s.at[0],
            dst_ref=small_z.at[rank],
            send_sem=small_sem.at[0, o],
            recv_sem=small_sem.at[1, rank],
            **to_chip(there),
        )

    def came_from(o):
        there = (rank + o) % chips
        return pltpu.make_async_remote_copy(
            src_ref=small_s.at[0],
            dst_ref=small_z.at[there],
            send_sem=small_sem.at[0, o],
            recv_sem=small_sem.at[1, there],
            **to_chip(there),
        )

    across_core = pltpu.make_async_remote_copy(
        src_ref=small_s.at[1],
        dst_ref=small_s.at[2],
        send_sem=z_sem.at[0],
        recv_sem=z_sem.at[1],
        **to_core(1 - core),
    )
    for o in range(1, chips):
        spread_to(o).start()
    small_z[rank] = small_s[0]
    rows_land[z] = ended_s[z]

    def one(m, carry):
        grads.advance(m)
        return carry

    def feed_links(m, carry):
        for o in range(1, layers):
            rows.piece(o, m - 3).start()
        grads.advance(m)
        return carry

    pieces = (own + enc_own) // 16
    lax.fori_loop(3, 3 + pieces, feed_links, 0)
    lax.fori_loop(3 + pieces, 9, one, 0)
    for o in range(1, chips):
        came_from(o).wait_recv()
    summed = small_z[0]
    for chip in range(1, chips):
        summed = summed + small_z[chip]
    small_s[1] = summed
    across_core.start()
    lax.fori_loop(9, sum_steps(layers), one, 0)
    across_core.wait()
    for o in range(1, chips):
        spread_to(o).wait_send()
    both = small_s[1] + small_s[2]
    low = jnp.where(core == 0, small_s[1], small_s[2])
    for n, part in enumerate((both, low, low)):
        gain_out[n : n + 1, :half] = part[2 * n : 2 * n + 1, :]
        gain_out[n : n + 1, half:] = part[2 * n + 1 : 2 * n + 2, :]
    for h in range(heads):
        table_out[h : h + 1, :] = both[6:7, h * buckets : (h + 1) * buckets]
    rows.arrive()
    rows.finish()
    grads.finish()


def close_rows(
    layers, heads, grad_qkv, x_low, win, grad_rows, kv_sum, self_gain, mid, sums, hit, nt, weights
):
    f32, bf16 = jnp.float32, jnp.bfloat16
    width, cols = win.shape
    own = grad_rows.shape[1]
    wide = kv_sum.shape[1]
    enc_own = kv_sum.shape[0] // (2 * layers)
    buckets = hit.shape[1]
    vmem, anywhere = pl.BlockSpec(memory_space=pltpu.VMEM), pl.BlockSpec(memory_space=pl.ANY)
    rows_shape = (layers, own + enc_own, width)
    return pl.pallas_call(
        functools.partial(close_kernel, layers, heads),
        name="close_rows",
        out_shape=(
            jax.ShapeDtypeStruct((2, 2, 16, cols), f32),
            jax.ShapeDtypeStruct(rows_shape, bf16),
            jax.ShapeDtypeStruct((heads, buckets), f32),
            jax.ShapeDtypeStruct((3, width), f32),
        ),
        in_specs=[vmem] * 10 + [anywhere],
        out_specs=(vmem,) * 4,
        scratch_shapes=[
            pltpu.VMEM((width, wide), bf16),
            pltpu.VMEM((layers * own, width), f32),
            pltpu.VMEM((2, layers * (own + enc_own), width), bf16),
            pltpu.VMEM((2 * layers * enc_own, width), f32),
            pltpu.VMEM(rows_shape, bf16),
            pltpu.VMEM((3, 8, width // 2), f32),
            pltpu.VMEM((4 * layers, 8, width // 2), f32),
            dma((1,)),
            dma((2, 2)),
            dma((2, layers)),
            dma((2, 4 * layers)),
            dma((2,)),
            *sum_scratch(layers, cols),
        ],
        compiler_params=pltpu.CompilerParams(
            collective_id=7, has_side_effects=True, vmem_limit_bytes=67043328
        ),
    )(grad_qkv, x_low, win, grad_rows, kv_sum, self_gain, mid, sums, hit, nt, weights)


def finish_kernel(
    in_ref,
    rest_ref,
    feed_ref,
    rows_ref,
    layer_ref,
    table_ref,
    gain_ref,
    layer_out,
    input_out,
    enc_out,
    table_out,
    self_gain,
    query_out,
    key_out,
    value_out,
    out_out,
    cross_gain,
    cq_out,
    ck_out,
    cv_out,
    co_out,
    feed_gain,
    gate_out,
    up_out,
    down_out,
):
    layer_out[...] = layer_ref[...]
    own = input_out.shape[1]
    input_out[...] = rows_ref[:, :own, :].astype(jnp.float32)
    enc_out[...] = rows_ref[:, own:, :].astype(jnp.float32)
    table_out[...] = table_ref[...]
    for n, ref in enumerate((self_gain, cross_gain, feed_gain)):
        ref[...] = gain_ref[n : n + 1, :]
    group = in_ref.shape[1] // 4
    half = group // 4
    pieces = [in_ref[:, n * group : (n + 1) * group] for n in range(4)]
    query_out[...] = jnp.concatenate([p[:, : 2 * half] for p in pieces], axis=1)
    key_out[...] = jnp.concatenate([p[:, 2 * half : 3 * half] for p in pieces], axis=1)
    value_out[...] = jnp.concatenate([p[:, 3 * half :] for p in pieces], axis=1)
    at = 0
    for ref in (out_out, cq_out, ck_out, cv_out, co_out):
        ref[...] = rest_ref[:, at : at + ref.shape[1]]
        at += ref.shape[1]
    feed = gate_out.shape[1]
    for at in range(0, feed, tile):
        units = min(tile, feed - at)
        for n, ref in enumerate((gate_out, up_out, down_out)):
            start = 3 * at + n * units
            ref[:, at : at + units] = feed_ref[:, start : start + units]


def finish(in_sum, rest_sum, feed_sum, rows, layer_rows, table, gains):
    f32 = jnp.float32
    own = layer_rows.shape[1]
    layers, both, width = rows.shape

    def flat(x):
        return x.reshape(64, x.shape[-1])

    def out(*shape, dtype=f32):
        return jax.ShapeDtypeStruct(shape, dtype)

    wide, feed = in_sum.shape[-1] // 2, feed_sum.shape[-1] // 3
    gain = out(1, width)
    vmem = pl.BlockSpec(memory_space=pltpu.VMEM)
    return pl.pallas_call(
        finish_kernel,
        name="finish",
        out_shape=(
            out(*layer_rows.shape, dtype=layer_rows.dtype),
            out(layers, own, width),
            out(layers, both - own, width),
            out(*table.shape),
            gain,
            out(64, wide),
            out(64, wide // 2),
            out(64, wide // 2),
            out(64, wide),
            gain,
            out(64, wide),
            out(64, wide // 2),
            out(64, wide // 2),
            out(64, wide),
            gain,
            out(64, feed),
            out(64, feed),
            out(64, feed),
        ),
        in_specs=[vmem] * 7,
        out_specs=(vmem,) * 18,
        compiler_params=pltpu.CompilerParams(vmem_limit_bytes=67043328),
    )(flat(in_sum), flat(rest_sum), flat(feed_sum), rows, layer_rows, table, gains)

def sum_scratch(layers, cols):
    steps = 2 * layers
    bf16 = jnp.bfloat16
    return [
        pltpu.VMEM((layers, 2, 2, 2, 2, 16, cols), bf16),
        pltpu.VMEM((layers, 2, 2, 2, 16, cols), bf16),
        pltpu.VMEM((steps, 2, 16, cols), bf16),
        pltpu.VMEM((steps, 2, 16, cols), bf16),
        pltpu.VMEM((steps, 2, 16, cols), bf16),
        dma((3, layers)),
        dma((2, steps, 2, 2)),
        dma((2, steps, 2)),
        dma((2, steps)),
        dma((2, steps)),
    ]


def sum_steps(layers):
    return 2 * layers + layers + 3


class GradSum:
    def __init__(self, layers, cols, whole, got, out, own, first, second, below, above, load, s1, s2, su, sd):
        self.cols = cols
        self.got = got
        self.layers, self.whole, self.out, self.own = layers, whole, out, own
        self.first, self.second, self.below, self.above = first, second, below, above
        self.load, self.s1, self.s2, self.su, self.sd = load, s1, s2, su, sd
        self.rank, self.z, self.y, self.x = chip_place(layers)
        self.x_chip = self.rank + 1 - 2 * self.x
        self.y_chip = self.rank + 2 - 4 * self.y
        self.steps = 2 * layers

    def layer_of(self, n):
        turn = n // 2
        return jnp.where(turn % 2 == 1, turn // 2, self.layers - 1 - turn // 2)

    def loads(self, turn):
        layer = self.layer_of(2 * turn)
        copies = [
            pltpu.make_async_copy(
                self.whole.at[(layer, *[slice(None)] * 5, self.cols)],
                self.own.at[layer],
                self.load.at[0, turn],
            )
        ]
        for colour, came in enumerate(self.got):
            copies.append(
                pltpu.make_async_copy(
                    came.at[layer, :, :, :, self.cols],
                    self.first.at[layer, colour],
                    self.load.at[1 + colour, turn],
                )
            )
        return copies

    def hop_one(self, n, colour, which):
        layer, chunk = self.layer_of(n), n % 2
        if colour == 0:
            source, chip = self.own.at[layer, which, 1 - self.x, 0, chunk], self.x_chip
        else:
            source, chip = self.own.at[layer, 1 - self.y, which, 1, chunk], self.y_chip
        return pltpu.make_async_remote_copy(
            src_ref=source,
            dst_ref=self.first.at[layer, colour, which, chunk],
            send_sem=self.s1.at[0, n, colour, which],
            recv_sem=self.s1.at[1, n, colour, which],
            **to_chip(chip),
        )

    def hop_two(self, n, colour):
        layer, chunk = self.layer_of(n), n % 2
        if colour == 0:
            source, chip = self.own.at[layer, 1 - self.y, self.x, 0, chunk], self.y_chip
        else:
            source, chip = self.own.at[layer, self.y, 1 - self.x, 1, chunk], self.x_chip
        return pltpu.make_async_remote_copy(
            src_ref=source,
            dst_ref=self.second.at[n, colour],
            send_sem=self.s2.at[0, n, colour],
            recv_sem=self.s2.at[1, n, colour],
            **to_chip(chip),
        )

    def hop_z(self, n, up):
        layer, chunk = self.layer_of(n), n % 2
        sems = self.su if up else self.sd
        return pltpu.make_async_remote_copy(
            src_ref=self.own.at[layer, self.y, self.x, :, chunk],
            dst_ref=(self.below if up else self.above).at[n],
            send_sem=sems.at[0, n],
            recv_sem=sems.at[1, n],
            **to_chip(self.rank + (4 if up else -4)),
        )

    def start(self):
        for turn in range(self.layers):
            for copy in self.loads(turn):
                copy.start()

    def send_first(self, n):
        @pl.when(n < self.steps)
        def _():
            if self.whole is not None:

                @pl.when(n % 2 == 0)
                def _():
                    for copy in self.loads(n // 2):
                        copy.wait()

            if not self.got:
                for which in range(2):
                    for colour in range(2):
                        self.hop_one(n, colour, which).start()

    def advance(self, m):
        steps, layers = self.steps, self.layers
        n = m - 1

        @pl.when((n >= 0) & (n < steps))
        def _():
            layer, chunk = self.layer_of(n), n % 2
            for colour in range(2):
                for other in range(2):
                    if colour == 0:
                        which = (1 - self.y) if other == 0 else self.y
                        place = (layer, which, self.x, 0, chunk)
                    else:
                        which = (1 - self.x) if other == 0 else self.x
                        place = (layer, self.y, which, 1, chunk)
                    if not self.got:
                        self.hop_one(n, colour, which).wait_recv()
                    self.own[place] = self.own[place] + self.first[layer, colour, which, chunk]
                    if other == 0:
                        self.hop_two(n, colour).start()

        n2 = m - 2

        @pl.when((n2 >= 0) & (n2 < steps))
        def _():
            layer, chunk = self.layer_of(n2), n2 % 2
            for colour in range(2):
                self.hop_two(n2, colour).wait_recv()
                place = (layer, self.y, self.x, colour, chunk)
                self.own[place] = self.own[place] + self.second[n2, colour]

        for up in (True, False):
            chain = self.z if up else layers - 1 - self.z
            nz = m - 2 - chain
            layer = self.layer_of(nz)
            beyond = (layer > self.z) if up else (layer < self.z)

            @pl.when((nz >= 0) & (nz < steps) & beyond)
            def _():
                @pl.when(chain > 0)
                def _():
                    self.hop_z(nz, up).wait_recv()
                    came = self.below if up else self.above
                    for colour in range(2):
                        place = (layer, self.y, self.x, colour, nz % 2)
                        self.own[place] = self.own[place] + came[nz, colour]

                self.hop_z(nz, up).start()

        nf = m - 2 - layers

        @pl.when((nf >= 0) & (nf < steps) & (self.layer_of(nf) == self.z))
        def _():
            layer, chunk = self.layer_of(nf), nf % 2
            for colour in range(2):
                self.out[colour, chunk, :, self.cols] = self.own[layer, self.y, self.x, colour, chunk].astype(
                    jnp.float32
                )
            for up in (True, False):
                chain = self.z if up else layers - 1 - self.z

                @pl.when(chain > 0)
                def _():
                    self.hop_z(nf, up).wait_recv()
                    came = self.below if up else self.above
                    for colour in range(2):
                        self.out[colour, chunk, :, self.cols] += came[nf, colour].astype(jnp.float32)

    def finish(self):
        def one(n, carry):
            for colour in range(2):
                if not self.got:
                    for which in range(2):
                        self.hop_one(n, colour, which).wait_send()
                self.hop_two(n, colour).wait_send()
            layer = self.layer_of(n)
            for up in (True, False):

                @pl.when((layer > self.z) if up else (layer < self.z))
                def _():
                    self.hop_z(n, up).wait_send()

            return carry

        lax.fori_loop(0, self.steps, one, 0)

def gather_scratch(layers, cols):
    return [
        pltpu.VMEM((2, 2, 16, cols), jnp.bfloat16),
        dma((1,)),
        dma((2, 2, layers, 2)),
        dma((2, layers, 2)),
        dma((2, layers, 2)),
        dma((2, layers, 2)),
        dma((2, layers, 2)),
    ]


class RowGather:
    def __init__(self, layers, short, whole, here, local, sz, sx, sy, sfx, sfy):
        self.short = short
        self.layers, self.whole, self.here = layers, whole, here
        self.local, self.sz, self.sx, self.sy, self.sfx, self.sfy = local, sz, sx, sy, sfx, sfy
        self.rank, self.z, self.y, self.x = chip_place(layers)
        self.x_chip = self.rank + 1 - 2 * self.x
        self.y_chip = self.rank + 2 - 4 * self.y

    def put(self):
        place = self.whole.at[self.z, self.y, self.x]
        return pltpu.make_async_copy(self.here, place, self.local.at[0])

    def source(self, layer, chunk, own, colours=slice(None)):
        if own:
            return self.here.at[colours, chunk]
        return self.whole.at[layer, self.y, self.x, colours, chunk]

    def along_z(self, layer, chunk, up, own=False):
        return pltpu.make_async_remote_copy(
            src_ref=self.source(layer, chunk, own),
            dst_ref=self.whole.at[layer, self.y, self.x, :, chunk],
            send_sem=self.sz.at[0, int(up), layer, chunk],
            recv_sem=self.sz.at[1, int(up), layer, chunk],
            **to_chip(self.rank + (4 if up else -4)),
        )

    def in_plane(self, layer, chunk, along_x, own=False):
        sems = self.sx if along_x else self.sy
        colours = slice(None)
        if self.short:
            colours = 0 if along_x else 1
        return pltpu.make_async_remote_copy(
            src_ref=self.source(layer, chunk, own, colours),
            dst_ref=self.whole.at[layer, self.y, self.x, colours, chunk],
            send_sem=sems.at[0, layer, chunk],
            recv_sem=sems.at[1, layer, chunk],
            **to_chip(self.x_chip if along_x else self.y_chip),
        )

    def onward(self, layer, chunk, along_x):
        if along_x:
            place = (layer, 1 - self.y, self.x, 1, chunk)
            sems, chip = self.sfx, self.x_chip
        else:
            place = (layer, self.y, 1 - self.x, 0, chunk)
            sems, chip = self.sfy, self.y_chip
        return pltpu.make_async_remote_copy(
            src_ref=self.whole.at[place],
            dst_ref=self.whole.at[place],
            send_sem=sems.at[0, layer, chunk],
            recv_sem=sems.at[1, layer, chunk],
            **to_chip(chip),
        )

    def send_z(self):
        for chunk in range(2):

            @pl.when(self.z < self.layers - 1)
            def _():
                self.along_z(self.z, chunk, True, own=True).start()

            @pl.when(self.z > 0)
            def _():
                self.along_z(self.z, chunk, False, own=True).start()

    def send_plane(self):
        for chunk in range(2):
            for along_x in (True, False):
                self.in_plane(self.z, chunk, along_x, own=True).start()
        self.put().start()

    def pass_on(self, m):
        far, chunk = m // 2, m % 2
        for up in (True, False):
            layer = self.z - far if up else self.z + far
            near = (layer >= 0) if up else (layer < self.layers)

            @pl.when((far > 0) & near)
            def _():
                self.along_z(layer, chunk, up).wait_recv()

                @pl.when((self.z < self.layers - 1) if up else (self.z > 0))
                def _():
                    self.along_z(layer, chunk, up).start()

                for along_x in (True, False):
                    self.in_plane(layer, chunk, along_x).start()

    def turn(self, m):
        far, chunk = m // 2, m % 2
        for up in (True, False):
            layer = self.z - far if up else self.z + far
            near = (layer >= 0) if up else ((layer < self.layers) & (far > 0))

            @pl.when(near)
            def _():
                for along_x in (True, False):
                    self.in_plane(layer, chunk, along_x).wait_recv()
                    self.onward(layer, chunk, not along_x).start()

    def step(self, m):
        @pl.when(m + 2 < 2 * self.layers)
        def _():
            self.pass_on(m + 2)

        if not self.short:
            self.turn(m)

    def finish(self):
        self.put().wait()

        def one(n, carry):
            layer, chunk = n // 2, n % 2
            for along_x in (True, False):
                if self.short:
                    self.in_plane(layer, chunk, along_x).wait_recv()
                else:
                    self.onward(layer, chunk, along_x).wait()
                self.in_plane(layer, chunk, along_x).wait_send()

            @pl.when((self.z < self.layers - 1) & (layer <= self.z))
            def _():
                self.along_z(layer, chunk, True).wait_send()

            @pl.when((self.z > 0) & (layer >= self.z))
            def _():
                self.along_z(layer, chunk, False).wait_send()

            return carry

        lax.fori_loop(0, 2 * self.layers, one, 0)

def begin_kernel(
    score_scale,
    layers,
    rows_ref,
    enc_ref,
    cot_ref,
    gain_ref,
    bias_ref,
    query_ref,
    key_ref,
    value_ref,
    out_ref,
    cq_ref,
    ck_ref,
    cv_ref,
    co_ref,
    gate_ref,
    up_ref,
    down_ref,
    rows_out,
    enc_out,
    cot_out,
    kept_ref,
    low_ref,
    full_ref,
    total_ref,
    nt_out,
    win_out,
    whole_ref,
    feed_whole,
    rows_land,
    enc_land,
    enc_all,
    cot_land,
    win_s,
    norm_s,
    qkv_s,
    came,
    landed,
    low_s,
    q_s,
    k_s,
    v_s,
    bias_s,
    score_s,
    rows_z,
    rows_core,
    enc_z,
    plane_sem,
    plane_core,
    cot_z,
    cot_core,
    in_sem,
    out_send,
    out_recv,
    win_sem,
    *gather_refs,
):
    f32, bf16 = jnp.float32, jnp.bfloat16
    blocks = bias_s.shape[1]
    sources = qkv_s.shape[0]
    head = k_s.shape[1]
    third = len(gather_refs) // 3
    first = RowGather(layers, False, win_s, *gather_refs[:third])
    gathers = (
        RowGather(layers, True, feed_whole, *gather_refs[2 * third :]),
        RowGather(layers, False, whole_ref, *gather_refs[third : 2 * third]),
    )
    rank, z, y, x = chip_place(layers)
    spot = 2 * y + x
    peers = peers_of(rank, y, x)
    rows = Column(layers, rows_ref, rows_land, rows_z, rows_core)
    enc = Column(layers, enc_ref, enc_land, enc_z)
    plane = PlaneGather(layers, enc_land, enc_all, plane_sem, plane_core)
    cot = Column(layers, cot_ref, cot_land, cot_z, cot_core)
    heads = PlaneSwap(layers, qkv_s, came, in_sem)

    def shard(gather, parts):
        gather.here[...] = jnp.concatenate(parts, axis=1).reshape(gather.here.shape)

    parts = []
    for kv in range(sources):
        parts.append(query_ref[:, 2 * kv * head : 2 * (kv + 1) * head])
        parts.append(key_ref[:, kv * head : (kv + 1) * head])
        parts.append(value_ref[:, kv * head : (kv + 1) * head])
    shard(first, parts)
    greet(layers)
    first.send_z()
    first.send_plane()
    shard(
        gathers[1],
        [out_ref[...], cq_ref[...], ck_ref[...], cv_ref[...], co_ref[...]],
    )
    feed = gate_ref.shape[1]
    parts = []
    for at in range(0, feed, tile):
        end = min(at + tile, feed)
        parts += [gate_ref[:, at:end], up_ref[:, at:end], down_ref[:, at:end]]
    shard(gathers[0], parts)

    def one(m, carry):
        first.step(m)
        return carry

    lax.fori_loop(0, layers, one, 0)
    rows.start()
    enc.start()
    lax.fori_loop(layers, 2 * layers, one, 0)
    for gather in gathers:
        gather.send_z()
    for gather in gathers:
        gather.send_plane()

    def make_bias(n, carry):
        row = jnp.broadcast_to(bias_ref[pl.ds(n, 1), :], (tile, 2 * tile))
        turned = pltpu.roll(row, tile + 1, 1, stride=1, stride_axis=0)
        bias_s[n // blocks, n % blocks] = turned[:, :tile]
        return carry

    lax.fori_loop(0, 2 * blocks, make_bias, 0)
    rows.arrive()
    first.finish()
    keep = pltpu.make_async_copy(win_s, win_out, win_sem.at[0])
    keep.start()
    rows.finish()
    rows_out[...] = rows_land[...]
    width = rows_ref.shape[2]
    for layer in range(layers):
        v = rows_land[layer].reshape(-1, width).astype(f32)
        at = slice(layer * v.shape[0], (layer + 1) * v.shape[0])
        norm_s[at, :] = (v * norm_scale(v) * gain_ref[...]).astype(bf16)
    for kv in range(sources):
        columns = win_s[..., 4 * head * kv : 4 * head * (kv + 1)].reshape(-1, 4 * head)
        qkv_s[kv] = matmul(norm_s[...], columns).astype(bf16)
    heads.start()
    enc.arrive()
    plane.start()
    cot.start()
    nt_out[...] = jnp.transpose(norm_s[...])
    heads.arrive()
    unpack_pair(came, q_s, k_s, v_s, score_scale)
    kept_ref[...] = came[...]

    def row_block(turn, carry):
        i = blocks - 1 - turn
        at = pl.ds(pl.multiple_of(i * tile, tile), tile)
        query = [q_s[h, at, :] for h in range(2)]

        def score_step(j, tops):
            key = k_s[pl.ds(pl.multiple_of(j * tile, tile), tile), :]
            found = []
            for h in range(2):
                score = dot_t(query[h], key) + bias_s[h, i - j]
                score_s[h, j] = score
                found.append(jnp.maximum(tops[h], jnp.maximum(score[:, :128], score[:, 128:])))
            return tuple(found)

        start = jnp.full((tile, 128), masked_score, jnp.float32)
        tops = lax.fori_loop(0, i + 1, score_step, (start, start))
        tops = [jnp.max(top, axis=1, keepdims=True) for top in tops]

        def share_step(j, state):
            value = v_s[pl.ds(pl.multiple_of(j * tile, tile), tile), :]
            found = []
            for h in range(2):
                total, summed = state[h]
                share = jnp.exp(score_s[h, j] - tops[h])
                summed = summed + jnp.dot(
                    share.astype(jnp.bfloat16), value, preferred_element_type=jnp.float32
                )
                found.append((total + share[:, :128] + share[:, 128:], summed))
            return tuple(found)

        nothing = (jnp.zeros((tile, 128), jnp.float32), jnp.zeros((tile, head), jnp.float32))
        state = lax.fori_loop(0, i + 1, share_step, (nothing, nothing))
        found = []
        for h in range(2):
            total = jnp.sum(state[h][0], axis=1, keepdims=True)
            found.append(state[h][1] / total)
            log_total = jnp.broadcast_to(tops[h] + jnp.log(total), (tile, 128))
            total_ref[pl.ds(h * blocks + i, 1), :] = jnp.transpose(log_total)[0:1, :]
        both = jnp.concatenate(found, axis=1)
        full_ref[at, :] = both
        both = both.astype(jnp.bfloat16)
        for part in range(tile // 128):
            block = i * (tile // 128) + part
            low_s[block] = both[part * 128 : (part + 1) * 128]

        for gather in gathers:
            gather.step(turn)
        for part in range(tile // 128):
            block = i * (tile // 128) + part

            @pl.when(block % sources == spot)
            def _():
                landed[spot, block // sources] = low_s[block]

            @pl.when(block % sources != spot)
            def _():
                hand_back(block).start()

        return carry

    def hand_back(block):
        return pltpu.make_async_remote_copy(
            src_ref=low_s.at[block],
            dst_ref=landed.at[spot, block // sources],
            send_sem=out_send.at[block],
            recv_sem=out_recv.at[spot, block // sources],
            **to_chip(rank - spot + block % sources),
        )

    lax.fori_loop(0, blocks // 2, row_block, 0)
    plane.arrive()
    cot.arrive()
    lax.fori_loop(blocks // 2, blocks, row_block, 0)
    for o in range(3):
        chip, there = peers[o]
        for turn in range(layers):
            pltpu.make_async_remote_copy(
                src_ref=low_s.at[0],
                dst_ref=landed.at[there, turn],
                send_sem=out_send.at[0],
                recv_sem=out_recv.at[there, turn],
                **to_chip(chip),
            ).wait_recv()
    for source in range(sources):
        for turn in range(layers):
            low_ref[turn * 128 : (turn + 1) * 128, source * 128 : (source + 1) * 128] = landed[
                source, turn
            ]
    heads.finish()
    cot.finish()
    cot_out[...] = cot_land[...]
    enc.finish()
    plane.finish()
    enc_out[...] = enc_all[...]
    keep.wait()
    for block in range(sources * layers):

        @pl.when(block % sources != spot)
        def _():
            hand_back(block).wait_send()

    for gather in gathers:
        gather.finish()


def begin(scale, layers, inputs, encoder, cotangent, gain, bias, *shards):
    f32, bf16 = jnp.float32, jnp.bfloat16
    own, width = inputs.shape[1:]
    enc_own = encoder.shape[1]
    rows = 2 * layers * own
    head = round(scale**-2)
    sources = 4
    length = sources * rows
    blocks = length // tile
    cols = sum(shard.shape[1] for shard in shards[:3])
    rest_cols = 4 * shards[3].shape[1]
    feed_cols = 3 * shards[8].shape[1]
    rows_shape, enc_shape = (layers, 2, own, width), (4, 2, layers, enc_own, width)
    qkv_shape = (sources, rows, 4 * head)
    chips = (layers, 2, 2, 2, 2, 16)
    vmem, anywhere = pl.BlockSpec(memory_space=pltpu.VMEM), pl.BlockSpec(memory_space=pl.ANY)
    return pl.pallas_call(
        functools.partial(begin_kernel, scale, layers),
        name="begin",
        out_shape=(
            jax.ShapeDtypeStruct(rows_shape, bf16),
            jax.ShapeDtypeStruct(enc_shape, bf16),
            jax.ShapeDtypeStruct(rows_shape, bf16),
            jax.ShapeDtypeStruct(qkv_shape, bf16),
            jax.ShapeDtypeStruct((rows, sources * 2 * head), bf16),
            jax.ShapeDtypeStruct((length, 2 * head), f32),
            jax.ShapeDtypeStruct((2 * blocks, tile), f32),
            jax.ShapeDtypeStruct((width, rows), bf16),
            jax.ShapeDtypeStruct((*chips, cols), bf16),
            jax.ShapeDtypeStruct((*chips, rest_cols), bf16),
            jax.ShapeDtypeStruct((*chips, feed_cols), bf16),
        ),
        in_specs=[vmem] * 16,
        out_specs=(vmem,) * 8 + (anywhere,) * 3,
        scratch_shapes=[
            pltpu.VMEM(rows_shape, bf16),
            pltpu.VMEM((layers, enc_own, width), bf16),
            pltpu.VMEM(enc_shape, bf16),
            pltpu.VMEM(rows_shape, bf16),
            pltpu.VMEM((*chips, cols), bf16),
            pltpu.VMEM((rows, width), bf16),
            pltpu.VMEM(qkv_shape, bf16),
            pltpu.VMEM(qkv_shape, bf16),
            pltpu.VMEM((sources, layers, 128, 2 * head), bf16),
            pltpu.VMEM((length // 128, 128, 2 * head), bf16),
            pltpu.VMEM((2, length, head), bf16),
            pltpu.VMEM((length, head), bf16),
            pltpu.VMEM((length, head), bf16),
            pltpu.VMEM((2, blocks, tile, tile), f32),
            pltpu.VMEM((2, blocks, tile, tile), f32),
            dma((2, layers)),
            dma((2, layers)),
            dma((2, layers)),
            dma((2, 3)),
            dma((2, 4)),
            dma((2, layers)),
            dma((2, layers)),
            dma((2, 3)),
            dma((length // 128,)),
            dma((sources, layers)),
            dma((1,)),
            *gather_scratch(layers, cols),
            *gather_scratch(layers, rest_cols),
            *gather_scratch(layers, feed_cols),
        ],
        compiler_params=pltpu.CompilerParams(
            collective_id=6, has_side_effects=True, vmem_limit_bytes=56 << 20
        ),
    )(inputs, encoder, cotangent, gain, bias, *shards)

def feed_cut(cols):
    return (cols // 128 + 1) // 2 * 128


def attend_backward_kernel(
    score_scale,
    layers,
    kept_ref,
    ctx_ref,
    full_ref,
    total_ref,
    bias_ref,
    kv_ref,
    rows_ref,
    grads_ref,
    feed_ref,
    got_x,
    got_y,
    out_ref,
    sums_ref,
    kv_out,
    rows_out,
    sum_a,
    sum_b,
    ctx_land,
    kv_land,
    rows_land,
    out_s,
    out_land,
    q_s,
    k_s,
    v_s,
    g_s,
    bias_s,
    sum_s,
    delta_s,
    dq_s,
    dk_s,
    dv_s,
    ctx_sem,
    kv_sem,
    rows_z,
    out_sem,
    *sum_refs,
):
    blocks = bias_s.shape[1]
    sources, rows, _ = kept_ref.shape
    head = k_s.shape[1]
    each = len(sum_refs) // 3
    cut = feed_cut(feed_ref.shape[-1])
    sums = (
        GradSum(layers, pl.ds(0, cut), feed_ref, (got_x, got_y), sum_b, *sum_refs[:each]),
        GradSum(
            layers,
            pl.ds(cut, feed_ref.shape[-1] - cut),
            feed_ref,
            (got_x, got_y),
            sum_b,
            *sum_refs[each : 2 * each],
        ),
        GradSum(layers, slice(None), grads_ref, (), sum_a, *sum_refs[2 * each :]),
    )
    context = PlaneSwap(layers, ctx_ref, ctx_land, ctx_sem)
    cross = PlaneSwap(layers, kv_ref, kv_land, kv_sem)
    ended = Column(layers, rows_ref, rows_land, rows_z)
    back = PlaneSwap(layers, out_s, out_land, out_sem)
    for grads in sums:
        grads.start()
    greet(layers)
    context.start()
    for grads in sums:
        grads.send_first(0)
    cross.start()
    ended.start()
    unpack_pair(kept_ref, q_s, k_s, v_s, score_scale)

    def make_bias(n, carry):
        row = jnp.broadcast_to(bias_ref[pl.ds(n, 1), :], (tile, 2 * tile))
        turned = pltpu.roll(row, 0, 1, stride=1, stride_axis=0)
        bias_s[n // blocks, n % blocks] = turned[:, tile:]
        return carry

    lax.fori_loop(0, 2 * blocks, make_bias, 0)
    sum_s[...] = jnp.zeros_like(sum_s)
    dq_s[...] = jnp.zeros_like(dq_s)
    dk_s[...] = jnp.zeros_like(dk_s)
    dv_s[...] = jnp.zeros_like(dv_s)
    context.arrive()
    for block in range(rows // 128 * sources):
        source, turn = block % sources, block // sources
        part = ctx_land[source, turn * 128 : (turn + 1) * 128, :]
        at = slice(block * 128, (block + 1) * 128)
        g_s[0, at, :] = part[:, :head]
        g_s[1, at, :] = part[:, head:]

    def make_delta(i, carry):
        at = pl.ds(pl.multiple_of(i * tile, tile), tile)
        for h in range(2):
            product = g_s[h, at, :].astype(jnp.float32) * full_ref[at, h * head : (h + 1) * head]
            column = jnp.broadcast_to(jnp.sum(product, axis=1, keepdims=True), (tile, 128))
            delta_s[pl.ds(h * blocks + i, 1), :] = jnp.transpose(column)[0:1, :]
        return carry

    lax.fori_loop(0, blocks, make_delta, 0)

    def one_tile(n, carry):
        line, at = n // blocks, n % blocks
        first = at < blocks - line
        d = jnp.where(first, line, blocks - line)
        i = jnp.where(first, at + line, at)
        at_q = pl.ds(pl.multiple_of(i * tile, tile), tile)
        at_k = pl.ds(pl.multiple_of((i - d) * tile, tile), tile)
        key, value = k_s[at_k, :], v_s[at_k, :]
        for h in range(2):
            query, grad = q_s[h, at_q, :], g_s[h, at_q, :]
            score = dot_t(key, query) + bias_s[h, d]
            share = jnp.exp(score - total_ref[pl.ds(h * blocks + i, 1), :])
            pull = dot_t(value, grad)
            grad_score = share * (pull - delta_s[pl.ds(h * blocks + i, 1), :])
            sum_s[h, d] += grad_score
            share_low = share.astype(jnp.bfloat16)
            grad_low = grad_score.astype(jnp.bfloat16)
            dv_s[at_k, :] += jnp.dot(share_low, grad, preferred_element_type=jnp.float32)
            dk_s[at_k, :] += jnp.dot(grad_low, query, preferred_element_type=jnp.float32)
            dq_s[h, at_q, :] += dot_first(grad_low, key)
        return carry

    tiles = blocks * (blocks + 1) // 2
    busy = 2 * layers

    def work(m, carry):
        for grads in sums:
            grads.send_first(m)
        low = (m - 1) * tiles // busy
        lax.fori_loop(low, m * tiles // busy, one_tile, 0)
        for grads in sums:
            grads.advance(m)
        return carry

    lax.fori_loop(1, 1 + busy, work, 0)

    for block in range(rows // 128 * sources):
        source, turn = block % sources, block // sources
        at = slice(block * 128, (block + 1) * 128)
        out_s[source, turn * 128 : (turn + 1) * 128, :] = jnp.concatenate(
            [dq_s[0, at, :] * score_scale, dq_s[1, at, :] * score_scale, dk_s[at, :], dv_s[at, :]],
            axis=1,
        ).astype(jnp.bfloat16)
    back.start()

    row_at = lax.broadcasted_iota(jnp.int32, (tile, tile), 0)
    col_at = lax.broadcasted_iota(jnp.int32, (tile, tile), 1)
    turn_rows = (row_at + col_at == tile - 1).astype(jnp.float32)

    def make_sums(n, carry):
        turned = jnp.dot(
            turn_rows,
            sum_s[n // blocks, n % blocks],
            precision=highest,
            preferred_element_type=jnp.float32,
        )
        wide = jnp.concatenate([turned, jnp.zeros_like(turned)], axis=1)
        wide = pltpu.roll(wide, 0, 1, stride=1, stride_axis=0)
        sums_ref[pl.ds(n, 1), :] = jnp.sum(wide, axis=0, keepdims=True)
        return carry

    cross.arrive()
    both = kv_land[0].astype(jnp.float32)
    for source in range(1, sources):
        both = both + kv_land[source].astype(jnp.float32)
    kv_out[...] = both.astype(jnp.bfloat16)
    ended.arrive()
    rows_out[...] = rows_land[...]

    left = sum_steps(layers) - 1 - busy

    def rest(m, carry):
        for grads in sums:
            grads.send_first(m)
        for grads in sums:
            grads.advance(m)
        n = m - 1 - busy
        lax.fori_loop(n * 2 * blocks // left, (n + 1) * 2 * blocks // left, make_sums, 0)
        return carry

    lax.fori_loop(1 + busy, sum_steps(layers), rest, 0)
    back.arrive()
    wide = 4 * head
    for source in range(sources):
        out_ref[:, source * wide : (source + 1) * wide] = out_land[source]
    context.finish()
    cross.finish()
    ended.finish()
    back.finish()
    for grads in sums:
        grads.finish()


def attend_backward(
    scale, layers, kept, ctx_grad, full, total, bias, kv, layer_rows, grads, feed_grads, got
):
    f32, bf16 = jnp.float32, jnp.bfloat16
    sources, rows, wide = kept.shape
    head = wide // 4
    length = sources * rows
    blocks = length // tile
    cols, feed_cols = grads.shape[1], feed_grads.shape[1]
    chips = (layers, 2, 2, 2, 2, 16)
    vmem, anywhere = pl.BlockSpec(memory_space=pltpu.VMEM), pl.BlockSpec(memory_space=pl.ANY)
    return pl.pallas_call(
        functools.partial(attend_backward_kernel, scale, layers),
        name="attend_backward",
        out_shape=(
            jax.ShapeDtypeStruct((rows, sources * wide), bf16),
            jax.ShapeDtypeStruct((2 * blocks, 2 * tile), f32),
            jax.ShapeDtypeStruct(kv.shape[1:], bf16),
            jax.ShapeDtypeStruct(layer_rows.shape, bf16),
            jax.ShapeDtypeStruct((2, 2, 16, cols), f32),
            jax.ShapeDtypeStruct((2, 2, 16, feed_cols), f32),
        ),
        in_specs=[vmem] * 7 + [anywhere] * 4,
        out_specs=(vmem,) * 6,
        scratch_shapes=[
            pltpu.VMEM(ctx_grad.shape, bf16),
            pltpu.VMEM(kv.shape, bf16),
            pltpu.VMEM(layer_rows.shape, bf16),
            pltpu.VMEM(kept.shape, bf16),
            pltpu.VMEM(kept.shape, bf16),
            pltpu.VMEM((2, length, head), bf16),
            pltpu.VMEM((length, head), bf16),
            pltpu.VMEM((length, head), bf16),
            pltpu.VMEM((2, length, head), bf16),
            pltpu.VMEM((2, blocks, tile, tile), f32),
            pltpu.VMEM((2, blocks, tile, tile), f32),
            pltpu.VMEM((2 * blocks, tile), f32),
            pltpu.VMEM((2, length, head), f32),
            pltpu.VMEM((length, head), f32),
            pltpu.VMEM((length, head), f32),
            dma((2, 3)),
            dma((2, 3)),
            dma((2, layers)),
            dma((2, 3)),
            *sum_scratch(layers, feed_cut(feed_cols)),
            *sum_scratch(layers, feed_cols - feed_cut(feed_cols)),
            *sum_scratch(layers, cols),
        ],
        compiler_params=pltpu.CompilerParams(
            collective_id=8, has_side_effects=True, vmem_limit_bytes=62 << 20
        ),
    )(
        kept,
        ctx_grad,
        full,
        total,
        bias,
        kv,
        layer_rows,
        grads.reshape(*chips, cols),
        feed_grads.reshape(*chips, feed_cols),
        *got,
    )

def norm_scale(v):
    return lax.rsqrt(jnp.mean(v * v, axis=-1, keepdims=True) + norm_eps)


def norm_pull(v, gain, grad):
    scale = norm_scale(v)
    turned = v * scale
    pulled = grad * gain
    mean = jnp.mean(pulled * turned, axis=-1, keepdims=True)
    return scale * (pulled - turned * mean), jnp.sum(grad * turned, axis=0, keepdims=True)


def middle_kernel(
    score_scale,
    layers,
    feed,
    ctx_ref,
    x_ref,
    cot_ref,
    enc_ref,
    wa_ref,
    cross_gain_ref,
    feed_gain_ref,
    wf_ref,
    layer_out,
    grad_out,
    gctx_out,
    kv_out,
    ga_out,
    gain_out,
    gb_out,
    got_x,
    got_y,
    w_s,
    gb_s,
    after_self,
    after_cross,
    nc_s,
    nf_s,
    nft_s,
    cott_s,
    down_s,
    dx_s,
    send_s,
    land_s,
    half_s,
    q_s,
    k_s,
    v_s,
    g_s,
    pair_s,
    cc_s,
    dq_s,
    dk_s,
    low_s,
    w_load,
    w_send,
    w_recv,
    g_send,
    g_recv,
    g_store,
    swap_sem,
    z_sem,
):
    f32, bf16 = jnp.float32, jnp.bfloat16
    rank, z, y, x = chip_place(layers)
    core = lax.axis_index(tensor_axis)
    x_chip, y_chip = rank + 1 - 2 * x, rank + 2 - 4 * y
    rows, width = x_ref.shape
    heads, _, head = q_s.shape
    kv_heads = heads // 2
    wide = heads * head
    enc_rows = enc_ref.shape[0]
    block = send_s.shape[2]
    chunks = rows // block
    at_out, at_cq, at_ck = 0, wide, 2 * wide
    at_cv, at_co = at_ck + wide // 2, at_ck + wide
    row_chip = 64

    def row_of(layer, at_y, at_x, colour=0):
        return pl.multiple_of(((layer * 2 + at_y) * 2 + at_x) * row_chip + 32 * colour, 32)

    def loads(n, cols):
        copies = []
        for layer in range(layers):
            for start, count in (
                (row_of(layer, y, x), 64),
                (row_of(layer, y, 1 - x, 0), 32),
                (row_of(layer, 1 - y, x, 1), 32),
            ):
                at = (pl.ds(start, count), cols)
                copies.append(pltpu.make_async_copy(wf_ref.at[at], w_s.at[at], w_load.at[n]))
        return copies

    def weights_hop(n, cols, layer, along_y, which):
        spot = row_of(layer, y, which, 0) if along_y else row_of(layer, which, x, 1)
        at = (pl.ds(spot, 32), cols)
        return pltpu.make_async_remote_copy(
            src_ref=wf_ref.at[at],
            dst_ref=w_s.at[at],
            send_sem=w_send.at[int(along_y), n],
            recv_sem=w_recv.at[int(along_y), n],
            **to_chip(y_chip if along_y else x_chip),
        )

    def weights_all(n, cols, along_y):
        at = (pl.ds(0, 64 * layers), cols)
        return pltpu.make_async_remote_copy(
            src_ref=wf_ref.at[at],
            dst_ref=w_s.at[at],
            send_sem=w_send.at[int(along_y), n],
            recv_sem=w_recv.at[int(along_y), n],
            **to_chip(y_chip if along_y else x_chip),
        )

    def grads_hop(n, cols, layer, along_y, which):
        spot = row_of(layer, 1 - y, which, 1) if along_y else row_of(layer, which, 1 - x, 0)
        return pltpu.make_async_remote_copy(
            src_ref=gb_s.at[pl.ds(spot, 32), cols],
            dst_ref=(got_y if along_y else got_x).at[layer, which, :, cols],
            send_sem=g_send.at[int(along_y), n],
            recv_sem=g_recv.at[int(along_y), n],
            **to_chip(y_chip if along_y else x_chip),
        )

    def grads_all(n, cols, along_y):
        return pltpu.make_async_remote_copy(
            src_ref=gb_s.at[pl.ds(0, 64 * layers), cols],
            dst_ref=(got_y if along_y else got_x).at[:, :, :, cols],
            send_sem=g_send.at[int(along_y), n],
            recv_sem=g_recv.at[int(along_y), n],
            **to_chip(y_chip if along_y else x_chip),
        )

    hops = [(layer, a, w) for layer in range(layers) for w in range(2) for a in (True, False)]
    full_blocks, last = feed // tile, feed % tile

    def each_block(work, order=lambda n: n):
        def one(n, carry):
            n = order(n)
            work(n, pl.ds(pl.multiple_of(n * 3 * tile, 3 * tile), 3 * tile), tile)
            return carry

        lax.fori_loop(0, full_blocks, one, 0)
        if last:
            work(full_blocks, pl.ds(full_blocks * 3 * tile, 3 * last), last)

    near = min(2, full_blocks // 2)
    odd = z % 2

    def crosses(n):
        from_even, from_odd = n < near, (n >= near) & (n < 2 * near)
        return ((odd == 1) & from_even) | ((odd == 0) & from_odd)

    def bring(n, cols, units):
        @pl.when(jnp.logical_not(crosses(n)))
        def _():
            for hop in hops:
                weights_hop(n, cols, *hop).start()

        for copy in loads(n, cols):
            copy.start()

    def block_cols(n):
        return pl.ds(pl.multiple_of(n * 3 * tile, 3 * tile), 3 * tile)

    def over_z(n, spot):
        at = (pl.ds(spot, 32), block_cols(n))
        return pltpu.make_async_remote_copy(
            src_ref=w_s.at[at],
            dst_ref=w_s.at[at],
            send_sem=z_sem.at[0, n],
            recv_sem=z_sem.at[1, n],
            **to_chip(rank + 4 - 8 * odd),
        )

    def over_z_all(n):
        at = (pl.ds(0, 128 * layers), block_cols(n))
        return pltpu.make_async_remote_copy(
            src_ref=w_s.at[at],
            dst_ref=w_s.at[at],
            send_sem=z_sem.at[0, n],
            recv_sem=z_sem.at[1, n],
            **to_chip(rank + 4 - 8 * odd),
        )

    def hand_over(turn):
        n = near * odd + turn
        for along_y in (True, False):
            weights_all(n, block_cols(n), along_y).wait_recv()
        for layer in range(layers):
            for which in range(2):
                over_z(n, row_of(layer, 1 - y, which, 0)).start()
                over_z(n, row_of(layer, which, 1 - x, 1)).start()

    greet(layers)
    each_block(bring)

    def swap(n, chunk):
        half = n == 3
        return pltpu.make_async_remote_copy(
            src_ref=half_s.at[0] if half else send_s.at[slots[n], chunk],
            dst_ref=half_s.at[1] if half else land_s.at[slots[n], chunk],
            send_sem=swap_sem.at[0, n, chunk],
            recv_sem=swap_sem.at[1, n, chunk],
            **to_core(1 - core),
        )

    slots = (0, 1, 0, None, 1)

    def span(chunk):
        return pl.ds(pl.multiple_of(chunk * block, block), block)

    def send_parts(n, part_of):
        def one(chunk, carry):
            send_s[slots[n], chunk] = part_of(span(chunk)).astype(bf16)
            swap(n, chunk).start()
            return carry

        lax.fori_loop(0, chunks, one, 0)

    def take_parts(n, use):
        def one(chunk, carry):
            swap(n, chunk).wait()
            both = send_s[slots[n], chunk].astype(f32) + land_s[slots[n], chunk].astype(f32)
            use(span(chunk), both)
            return carry

        lax.fori_loop(0, chunks, one, 0)

    cross_gain, feed_gain = cross_gain_ref[...], feed_gain_ref[...]

    send_parts(0, lambda at: dot_t(ctx_ref[at, :], wa_ref[:, at_out : at_out + wide]))
    key_value = matmul(enc_ref[...], wa_ref[:, at_ck : at_ck + wide]).astype(bf16)
    for kv in range(kv_heads):
        k_s[kv] = key_value[:, kv * head : (kv + 1) * head]
        v_s[kv] = key_value[:, wide // 2 + kv * head : wide // 2 + (kv + 1) * head]
    cott_s[...] = jnp.transpose(cot_ref[...])

    def enter_cross(at, both):
        v = x_ref[at, :].astype(f32) + both
        after_self[at, :] = v
        nc_s[at, :] = (v * norm_scale(v) * cross_gain).astype(bf16)
        query = matmul(nc_s[at, :], wa_ref[:, at_cq : at_cq + wide]).astype(bf16)
        for h in range(heads):
            q_s[h, at, :] = (query[:, h * head : (h + 1) * head] * score_scale).astype(bf16)

    take_parts(0, enter_cross)
    if near > 0:
        hand_over(0)

    def attend(kv, carry):
        key, value = k_s[kv], v_s[kv]
        for chunk in range(chunks):
            at = slice(chunk * block, (chunk + 1) * block)
            found = []
            for h in range(2):
                score = dot_t(q_s[2 * kv + h, at, :], key)
                share = jnp.exp(score - jnp.max(score, axis=1, keepdims=True))
                total = jnp.sum(share, axis=1, keepdims=True)
                found.append(matmul(share.astype(bf16), value) / total)
            pair_s[kv, at, :] = jnp.concatenate(found, axis=1).astype(bf16)
        return carry

    lax.fori_loop(0, kv_heads, attend, 0)
    if near > 1:
        hand_over(1)
    for kv in range(kv_heads):
        cc_s[:, 2 * kv * head : 2 * (kv + 1) * head] = pair_s[kv]
    send_parts(1, lambda at: dot_t(cc_s[at, :], wa_ref[:, at_co : at_co + wide]))

    def enter_feed(at, both):
        v = after_self[at, :] + both
        after_cross[at, :] = v
        nf_s[at, :] = (v * norm_scale(v) * feed_gain).astype(bf16)

    take_parts(1, enter_feed)
    nft_s[...] = jnp.transpose(nf_s[...])

    down_s[...] = jnp.zeros_like(down_s)
    dx_s[...] = jnp.zeros_like(dx_s)
    slope = math.sqrt(2.0 / math.pi)

    def come_in_plane(n, cols):
        for along_y in (True, False):
            weights_all(n, cols, along_y).wait_recv()

    def in_turn(step):
        over = near * (1 - odd) + step - (full_blocks - near)
        shared = step + near
        return jnp.where(
            step < near, near * odd + step, jnp.where(step < full_blocks - near, shared, over)
        )

    def feed_block(n, cols, units):
        have = (pl.ds(0, 128 * layers), cols)
        pltpu.make_async_copy(wf_ref.at[have], w_s.at[have], w_load.at[n]).wait()
        if isinstance(n, int):
            come_in_plane(n, cols)
        else:
            own = (n >= near * odd) & (n < near * odd + near)

            @pl.when(crosses(n))
            def _():
                over_z_all(n).wait_recv()

            @pl.when(jnp.logical_not(crosses(n) | own))
            def _():
                come_in_plane(n, cols)

        pair = w_s[:, pl.ds(cols.start, 2 * units)]
        down = w_s[:, pl.ds(cols.start + 2 * units, units)]
        both = matmul(nf_s[...], pair)
        gate, up = both[:, :units], both[:, units:]
        square = gate * gate
        bend = jnp.tanh(slope * (gate + 0.044715 * square * gate))
        bent = 0.5 * gate * (1.0 + bend)
        pull = 0.5 * (1.0 + bend) + 0.5 * gate * (1.0 - bend * bend) * slope * (
            1.0 + 3.0 * 0.044715 * square
        )
        hidden = (bent * up).astype(bf16)
        down_s[...] += dot_t(hidden, down)
        grad = matmul(cot_ref[...], down)
        grads = jnp.concatenate([grad * up * pull, grad * bent], axis=1).astype(bf16)
        dx_s[...] += dot_t(grads, pair)
        gb_s[:, pl.ds(cols.start, 2 * units)] = matmul(nft_s[...], grads).astype(bf16)
        gb_s[:, pl.ds(cols.start + 2 * units, units)] = matmul(cott_s[...], hidden).astype(bf16)
        for hop in hops:
            grads_hop(n, cols, *hop).start()

    each_block(feed_block, in_turn)

    send_parts(2, lambda at: dx_s[at, :])
    store = pltpu.make_async_copy(gb_s, gb_out, g_store.at[0])
    store.start()
    own = rows // (2 * layers)

    def halves(ref, which):
        return [ref[pl.ds((2 * layer + which) * own, own), :] for layer in range(layers)]

    low = jnp.concatenate(halves(down_s, 1 - core), axis=0).astype(bf16)
    half_s[0] = low
    swap(3, 0).start()

    def leave_feed(at, both):
        grad, gain = norm_pull(after_cross[at, :], feed_gain, both)
        dx_s[at, :] = cot_ref[at, :].astype(f32) + grad
        low = dx_s[at, :].astype(bf16)
        low_s[at, :] = low
        gain_out[1:2, :] += gain
        context = matmul(low, wa_ref[:, at_co : at_co + wide]).astype(bf16)
        for h in range(heads):
            g_s[h, at, :] = context[:, h * head : (h + 1) * head]

    gain_out[...] = jnp.zeros_like(gain_out)
    take_parts(2, leave_feed)
    swap(3, 0).wait()
    mine = halves(after_cross, core)
    down = halves(down_s, core)
    for layer in range(layers):
        came = half_s[1, layer * own : (layer + 1) * own, :].astype(f32)
        layer_out[layer] = (mine[layer] + (down[layer].astype(bf16).astype(f32) + came)).astype(bf16)

    ga_out[:, at_co : at_co + wide] = dot_first(low_s[...], cc_s[...]).astype(bf16)

    def attend_back(kv, carry):
        key, value = k_s[kv], v_s[kv]
        key_grad = jnp.zeros((enc_rows, head), f32)
        value_grad = jnp.zeros((enc_rows, head), f32)
        for chunk in range(chunks):
            at = slice(chunk * block, (chunk + 1) * block)
            found = []
            for h in range(2):
                query, grad = q_s[2 * kv + h, at, :], g_s[2 * kv + h, at, :]
                score = dot_t(key, query)
                share = jnp.exp(score - jnp.max(score, axis=0, keepdims=True))
                share = share * (1.0 / jnp.sum(share, axis=0, keepdims=True))
                pull = dot_t(value, grad)
                delta = jnp.sum(share * pull, axis=0, keepdims=True)
                grad_low = (share * (pull - delta)).astype(bf16)
                found.append(dot_first(grad_low, key) * score_scale)
                key_grad = key_grad + matmul(grad_low, query)
                value_grad = value_grad + matmul(share.astype(bf16), grad)
            pair_s[kv, at, :] = jnp.concatenate(found, axis=1).astype(bf16)
        dk_s[0, kv] = key_grad.astype(bf16)
        dk_s[1, kv] = value_grad.astype(bf16)
        return carry

    lax.fori_loop(0, kv_heads, attend_back, 0)
    for kv in range(kv_heads):
        dq_s[:, 2 * kv * head : 2 * (kv + 1) * head] = pair_s[kv]
    send_parts(4, lambda at: dot_t(dq_s[at, :], wa_ref[:, at_cq : at_cq + wide]))
    for n in range(2):
        kv_out[:, n * wide // 2 : (n + 1) * wide // 2] = jnp.concatenate(
            [dk_s[n, kv] for kv in range(kv_heads)], axis=1
        )
    ga_out[:, at_cq : at_cq + wide] = dot_first(nc_s[...], dq_s[...]).astype(bf16)
    ga_out[:, at_ck : at_ck + wide] = dot_first(enc_ref[...], kv_out[...]).astype(bf16)

    def leave_cross(at, both):
        grad, gain = norm_pull(after_self[at, :], cross_gain, both)
        dx_s[at, :] += grad
        low = dx_s[at, :].astype(bf16)
        low_s[at, :] = low
        gain_out[0:1, :] += gain
        context = matmul(low, wa_ref[:, at_out : at_out + wide]).astype(bf16)
        for q in range(4):
            gctx_out[q, at, :] = context[:, q * wide // 4 : (q + 1) * wide // 4]

    take_parts(4, leave_cross)
    ga_out[:, at_out : at_out + wide] = dot_first(low_s[...], ctx_ref[...]).astype(bf16)
    mine = halves(dx_s, core)
    for layer in range(layers):
        grad_out[layer] = mine[layer]

    store.wait()

    def settle(n, cols, units):
        @pl.when(jnp.logical_not(crosses(n)))
        def _():
            for along_y in (True, False):
                weights_all(n, cols, along_y).wait_send()

        for along_y in (True, False):
            grads_all(n, cols, along_y).wait()

    each_block(settle)
    for turn in range(near):
        over_z_all(near * odd + turn).wait_send()


def middle(scale, layers, feed, context, x_low, cot, enc, weights, *gains_and_feed):
    f32, bf16 = jnp.float32, jnp.bfloat16
    rows, width = x_low.shape
    wide = context.shape[1]
    head = round(scale**-2)
    heads = wide // head
    own = rows // (2 * layers)
    cols = gains_and_feed[-1].shape[1]
    block = rows // 2
    vmem, anywhere = pl.BlockSpec(memory_space=pltpu.VMEM), pl.BlockSpec(memory_space=pl.ANY)
    got = jax.ShapeDtypeStruct((layers, 2, 32, cols), bf16)
    return pl.pallas_call(
        functools.partial(middle_kernel, scale, layers, feed),
        name="middle",
        out_shape=(
            jax.ShapeDtypeStruct((layers, own, width), bf16),
            jax.ShapeDtypeStruct((layers, own, width), f32),
            jax.ShapeDtypeStruct((4, rows, wide // 4), bf16),
            jax.ShapeDtypeStruct((enc.shape[0], wide), bf16),
            jax.ShapeDtypeStruct((width, weights.shape[1]), bf16),
            jax.ShapeDtypeStruct((2, width), f32),
            jax.ShapeDtypeStruct((width, cols), bf16),
            got,
            got,
        ),
        in_specs=[vmem] * 7 + [anywhere],
        out_specs=(vmem,) * 6 + (anywhere,) * 3,
        scratch_shapes=[
            pltpu.VMEM((width, cols), bf16),
            pltpu.VMEM((width, cols), bf16),
            pltpu.VMEM((rows, width), f32),
            pltpu.VMEM((rows, width), f32),
            pltpu.VMEM((rows, width), bf16),
            pltpu.VMEM((rows, width), bf16),
            pltpu.VMEM((width, rows), bf16),
            pltpu.VMEM((width, rows), bf16),
            pltpu.VMEM((rows, width), f32),
            pltpu.VMEM((rows, width), f32),
            pltpu.VMEM((2, 2, block, width), bf16),
            pltpu.VMEM((2, 2, block, width), bf16),
            pltpu.VMEM((2, rows // 2, width), bf16),
            pltpu.VMEM((heads, rows, head), bf16),
            pltpu.VMEM((heads // 2, enc.shape[0], head), bf16),
            pltpu.VMEM((heads // 2, enc.shape[0], head), bf16),
            pltpu.VMEM((heads, rows, head), bf16),
            pltpu.VMEM((heads // 2, rows, 2 * head), bf16),
            pltpu.VMEM((rows, wide), bf16),
            pltpu.VMEM((rows, wide), bf16),
            pltpu.VMEM((2, heads // 2, enc.shape[0], head), bf16),
            pltpu.VMEM((rows, width), bf16),
            dma((pl.cdiv(feed, tile),)),
            dma((2, pl.cdiv(feed, tile))),
            dma((2, pl.cdiv(feed, tile))),
            dma((2, pl.cdiv(feed, tile))),
            dma((2, pl.cdiv(feed, tile))),
            dma((1,)),
            dma((2, 5, 2)),
            dma((2, pl.cdiv(feed, tile))),
        ],
        compiler_params=pltpu.CompilerParams(
            collective_id=9, has_side_effects=True, vmem_limit_bytes=67043328
        ),
    )(context, x_low, cot, enc, weights, *gains_and_feed)

def dot_t(left, right):
    return lax.dot_general(
        left, right, (((1,), (1,)), ((), ())), preferred_element_type=jnp.float32
    )


def dot_first(left, right):
    return lax.dot_general(
        left, right, (((0,), (0,)), ((), ())), preferred_element_type=jnp.float32
    )


def unpack_pair(qkv_ref, q_s, k_s, v_s, score_scale):
    sources, rows, _ = qkv_ref.shape
    blocks = rows // 128 * sources
    head = k_s.shape[1]
    for block in range(blocks):
        source, turn = block % sources, block // sources
        tile = qkv_ref[source, turn * 128 : (turn + 1) * 128, :]
        at = slice(block * 128, (block + 1) * 128)
        q_s[0, at, :] = (tile[:, :head] * score_scale).astype(jnp.bfloat16)
        q_s[1, at, :] = (tile[:, head : 2 * head] * score_scale).astype(jnp.bfloat16)
        k_s[at, :] = tile[:, 2 * head : 3 * head]
        v_s[at, :] = tile[:, 3 * head :]


def by_heads(
    inputs,
    encoder_out,
    out_cotangent,
    bucket_ids,
    position_table,
    self_gain,
    self_query,
    self_key,
    self_value,
    self_output,
    cross_gain,
    cross_query,
    cross_key,
    cross_value,
    cross_output,
    feed_gain,
    gate_weight,
    up_weight,
    down_weight,
):
    f32, bf16 = jnp.float32, jnp.bfloat16
    batches, own, width = inputs.shape
    enc_own = encoder_out.shape[1]
    length = bucket_ids.shape[0]
    heads_all, buckets = position_table.shape
    fsdp = lax.axis_size(fsdp_axis)
    plane = fsdp // batches
    rank, core = lax.axis_index(fsdp_axis), lax.axis_index(tensor_axis)
    head = self_query.shape[1] // (heads_all // 2)
    kv_local = self_key.shape[1] // head
    scale = head ** (-0.5)
    blocks = length // tile
    rows = batches * 2 * own
    enc_rows = batches * 2 * enc_own
    feed = gate_weight.shape[1]
    kv_index = core * kv_local + rank % plane
    table_here = lax.dynamic_slice_in_dim(position_table, 2 * kv_index, 2, 0)
    bucket_range = jnp.arange(buckets, dtype=jnp.int32)
    lower = jnp.sum((bucket_ids[None, :] < bucket_range[:, None]).astype(jnp.int32), axis=1)
    upper = jnp.concatenate([lower[1:], jnp.full((1,), length, jnp.int32)])
    offsets = (
        tile * jnp.arange(blocks, dtype=jnp.int32)[:, None]
        + jnp.arange(2 * tile, dtype=jnp.int32)[None, :]
    ).reshape(-1)

    def bias_of(offset):
        hit = (offset[None] >= lower[:, None]) & (offset[None] < upper[:, None])
        value = jnp.dot(table_here, hit.astype(f32), precision=highest)
        return jnp.where(offset[None] >= 0, value, masked_score).reshape(2 * blocks, 2 * tile)

    down_steps = (
        tile * jnp.arange(blocks, dtype=jnp.int32)[:, None]
        + (tile - 1)
        - jnp.arange(2 * tile, dtype=jnp.int32)[None, :]
    ).reshape(-1)
    bias_down = bias_of(down_steps)
    bias_up = bias_of(offsets - tile)

    def swap_add(partial):
        low = partial.astype(bf16)
        return low.astype(f32) + swap_cores(low).astype(f32)

    x_low, enc_all, cot_low, qkv_here, context_low, context_full, log_total, norm_t, *wholes = begin(
        scale,
        batches,
        inputs,
        encoder_out,
        out_cotangent,
        self_gain[None],
        bias_down,
        self_query,
        self_key,
        self_value,
        self_output.T,
        cross_query,
        cross_key,
        cross_value,
        cross_output.T,
        gate_weight,
        up_weight,
        down_weight.T,
    )
    x_low, enc_all = x_low.reshape(rows, width), enc_all.reshape(-1, width)
    in_full, rest_full, feed_full = [whole.reshape(width, -1) for whole in wholes]
    layer_rows, grad_after_self, grad_context, cross_kv, grads, mid_gains, feed_grads, *feed_got = (
        middle(
            scale,
            batches,
            feed,
            context_low,
            x_low,
            cot_low.reshape(rows, width),
            enc_all,
            rest_full,
            cross_gain[None],
            feed_gain[None],
            feed_full,
        )
    )
    feed_got = [came.reshape(batches, 2, 2, 16, -1) for came in feed_got]

    grad_qkv, diagonal_sums, kv_sum, layer_out, *most_sums = attend_backward(
        scale,
        batches,
        qkv_here,
        grad_context,
        context_full,
        log_total,
        bias_up,
        cross_kv.reshape(plane, enc_rows, -1),
        layer_rows,
        grads,
        feed_grads,
        feed_got,
    )
    spread = offsets - (tile - 1)
    hit = ((spread[None] >= lower[:, None]) & (spread[None] < upper[:, None])).astype(f32)
    hit = jnp.transpose(hit.reshape(buckets, blocks, 2 * tile), (1, 0, 2))
    in_sum, ended, table_sum, gain_sums = close_rows(
        batches,
        heads_all,
        grad_qkv,
        x_low,
        in_full,
        grad_after_self,
        kv_sum,
        self_gain[None],
        mid_gains,
        diagonal_sums,
        hit,
        norm_t,
        rest_full,
    )
    results = finish(in_sum, *most_sums, ended, layer_out, table_sum, gain_sums)
    turned, gains = (8, 13, 17), (4, 9, 14)
    return tuple(
        result.T if n in turned else result.reshape(-1) if n in gains else result
        for n, result in enumerate(results)
    )


def on_either(*args):
    batches, kv_heads = args[0].shape[0], args[7].shape[1] * lax.axis_size(tensor_axis)
    head_size = args[6].shape[1] * lax.axis_size(tensor_axis) // args[4].shape[0]
    devices = lax.axis_size(fsdp_axis) * lax.axis_size(tensor_axis)
    if devices == batches * (kv_heads // head_size):
        return by_heads(*args)
    return on_device(*args)


def solution(mesh):
    placed = (
        P(None, (fsdp_axis, tensor_axis), None),
        P(None, (fsdp_axis, tensor_axis), None),
        P(None, (fsdp_axis, tensor_axis), None),
        P(),
        P(),
        P(),
        P(fsdp_axis, tensor_axis),
        P(fsdp_axis, tensor_axis),
        P(fsdp_axis, tensor_axis),
        P(tensor_axis, fsdp_axis),
        P(),
        P(fsdp_axis, tensor_axis),
        P(fsdp_axis, tensor_axis),
        P(fsdp_axis, tensor_axis),
        P(tensor_axis, fsdp_axis),
        P(),
        P(fsdp_axis, tensor_axis),
        P(fsdp_axis, tensor_axis),
        P(tensor_axis, fsdp_axis),
    )
    return jax.shard_map(
        on_either,
        mesh=mesh,
        in_specs=placed,
        out_specs=(
            P(None, (fsdp_axis, tensor_axis), None),
            P(None, (fsdp_axis, tensor_axis), None),
            P(None, (fsdp_axis, tensor_axis), None),
            P(),
            P(),
            P(fsdp_axis, tensor_axis),
            P(fsdp_axis, tensor_axis),
            P(fsdp_axis, tensor_axis),
            P(tensor_axis, fsdp_axis),
            P(),
            P(fsdp_axis, tensor_axis),
            P(fsdp_axis, tensor_axis),
            P(fsdp_axis, tensor_axis),
            P(tensor_axis, fsdp_axis),
            P(),
            P(fsdp_axis, tensor_axis),
            P(fsdp_axis, tensor_axis),
            P(tensor_axis, fsdp_axis),
        ),
        check_vma=False,
    )
```

```python
import functools
import math
import types

import jax
import jax.numpy as jnp
from jax import lax
from jax.experimental import pallas as pl
from jax.experimental.pallas import tpu as pltpu
from jax.sharding import PartitionSpec as P

norm_eps = 1e-06
masked_score = -1e30
highest = lax.Precision.HIGHEST
key_block_width = 256
tile = 256
fsdp_axis, tensor_axis = "fsdp", "tensor"


def matmul(left, right):
    return jnp.dot(left, right, preferred_element_type=jnp.float32)


def norm_rows(row_block, gain):
    return (
        row_block
        * lax.rsqrt(jnp.mean(row_block * row_block, axis=-1, keepdims=True) + norm_eps)
        * gain
    )


def gather_rows(row_block):
    return lax.all_gather(row_block, tensor_axis, axis=0, tiled=True)


def sum_rows(row_block):
    return lax.psum_scatter(
        row_block.astype(jnp.bfloat16), tensor_axis, scatter_dimension=0, tiled=True
    ).astype(jnp.float32)


def gather_weights(shards):
    (
        self_query,
        self_key,
        self_value,
        self_output,
        cross_query,
        cross_key,
        cross_value,
        cross_output,
        gate_weight,
        up_weight,
        down_weight,
    ) = shards
    inner = (
        lax.all_gather(self_query, fsdp_axis, axis=0, tiled=True),
        lax.all_gather(self_key, fsdp_axis, axis=0, tiled=True),
        lax.all_gather(self_value, fsdp_axis, axis=0, tiled=True),
        lax.all_gather(cross_query, fsdp_axis, axis=0, tiled=True),
        lax.all_gather(cross_key, fsdp_axis, axis=0, tiled=True),
        lax.all_gather(cross_value, fsdp_axis, axis=0, tiled=True),
        lax.all_gather(gate_weight, fsdp_axis, axis=0, tiled=True),
        lax.all_gather(up_weight, fsdp_axis, axis=0, tiled=True),
    )
    outer = (
        lax.all_gather(self_output, fsdp_axis, axis=1, tiled=True),
        lax.all_gather(cross_output, fsdp_axis, axis=1, tiled=True),
        lax.all_gather(down_weight, fsdp_axis, axis=1, tiled=True),
    )
    return (
        inner[0],
        inner[1],
        inner[2],
        outer[0],
        inner[3],
        inner[4],
        inner[5],
        outer[1],
        inner[6],
        inner[7],
        outer[2],
    )


def scatter_grads(grads_full):
    (
        self_query,
        self_key,
        self_value,
        self_output,
        cross_query,
        cross_key,
        cross_value,
        cross_output,
        gate_weight,
        up_weight,
        down_weight,
    ) = grads_full
    inner = (
        lax.psum_scatter(self_query, fsdp_axis, scatter_dimension=0, tiled=True),
        lax.psum_scatter(self_key, fsdp_axis, scatter_dimension=0, tiled=True),
        lax.psum_scatter(self_value, fsdp_axis, scatter_dimension=0, tiled=True),
        lax.psum_scatter(cross_query, fsdp_axis, scatter_dimension=0, tiled=True),
        lax.psum_scatter(cross_key, fsdp_axis, scatter_dimension=0, tiled=True),
        lax.psum_scatter(cross_value, fsdp_axis, scatter_dimension=0, tiled=True),
        lax.psum_scatter(gate_weight, fsdp_axis, scatter_dimension=0, tiled=True),
        lax.psum_scatter(up_weight, fsdp_axis, scatter_dimension=0, tiled=True),
    )
    outer = (
        lax.psum_scatter(self_output, fsdp_axis, scatter_dimension=1, tiled=True),
        lax.psum_scatter(cross_output, fsdp_axis, scatter_dimension=1, tiled=True),
        lax.psum_scatter(down_weight, fsdp_axis, scatter_dimension=1, tiled=True),
    )
    return (
        inner[0],
        inner[1],
        inner[2],
        outer[0],
        inner[3],
        inner[4],
        inner[5],
        outer[1],
        inner[6],
        inner[7],
        outer[2],
    )


def add_all(first, second):
    return tuple((left_item + right_item for left_item, right_item in zip(first, second)))


def fold_keys(key_rows, value_rows, step_fn, initial):
    return step_fn(
        initial,
        (
            lax.all_gather(key_rows, fsdp_axis, axis=0, tiled=True),
            lax.all_gather(value_rows, fsdp_axis, axis=0, tiled=True),
        ),
        jnp.int32(0),
    )


def on_device(
    inputs,
    encoder_out,
    out_cotangent,
    bucket_ids,
    position_table,
    self_gain,
    self_query,
    self_key,
    self_value,
    self_output,
    cross_gain,
    cross_query,
    cross_key,
    cross_value,
    cross_output,
    feed_gain,
    gate_weight,
    up_weight,
    down_weight,
):
    shards = (
        self_query,
        self_key,
        self_value,
        self_output,
        cross_query,
        cross_key,
        cross_value,
        cross_output,
        gate_weight,
        up_weight,
        down_weight,
    )
    batches = inputs.shape[0]
    tensor_size = lax.axis_size(tensor_axis)
    piece_rows = inputs.shape[1] * tensor_size
    length = bucket_ids.shape[0]
    heads_all = position_table.shape[0]
    buckets = position_table.shape[1]
    local_heads = heads_all // tensor_size
    head_size = self_query.shape[1] // local_heads
    kv_local = self_key.shape[1] // head_size
    group_size = local_heads // kv_local
    score_scale = head_size ** (-0.5)
    fsdp_rank = lax.axis_index(fsdp_axis)
    tensor_rank = lax.axis_index(tensor_axis)
    query_start = fsdp_rank * piece_rows
    encoder_rows = encoder_out.shape[1] * tensor_size
    table_local = lax.dynamic_slice_in_dim(
        position_table, tensor_rank * local_heads, local_heads, 0
    )
    bucket_range = jnp.arange(buckets, dtype=jnp.int32)
    lower_bounds = jnp.sum((bucket_ids[None, :] < bucket_range[:, None]).astype(jnp.int32), axis=1)
    upper_bounds = jnp.concatenate([lower_bounds[1:], jnp.full((1,), length, jnp.int32)])

    def position_bias(row_start, col_start, row_count, col_count):
        offsets = (
            row_start
            - col_start
            + jnp.arange(row_count, dtype=jnp.int32)[:, None]
            - jnp.arange(col_count, dtype=jnp.int32)[None, :]
        )
        indicator = (
            (offsets[None] >= lower_bounds[:, None, None])
            & (offsets[None] < upper_bounds[:, None, None])
        ).astype(jnp.float32)
        bias_values = jnp.einsum("hb,bij->hij", table_local, indicator, precision=highest).reshape(
            kv_local, group_size, row_count, col_count
        )
        return (bias_values, offsets >= 0, indicator)

    def split_heads(row_block):
        return row_block.reshape(row_block.shape[0], kv_local, group_size, head_size)

    def split_kv(row_block):
        return row_block.reshape(row_block.shape[0], kv_local, head_size)

    def backward(batch_index, saved_state, weights):
        (
            query_full,
            key_full,
            value_full,
            output_full,
            cross_query_full,
            cross_key_full,
            cross_value_full,
            cross_output_full,
            gate_full,
            up_full,
            down_full,
        ) = weights
        cotangent = out_cotangent[batch_index].astype(jnp.float32)
        grad_feed = gather_rows(out_cotangent[batch_index])
        hidden = saved_state.hidden
        normed_feed = saved_state.normed_feed
        down_grad = jnp.einsum("tf,td->fd", hidden, grad_feed, preferred_element_type=jnp.float32)
        grad_hidden = jnp.einsum(
            "td,fd->tf", grad_feed, down_full, preferred_element_type=jnp.float32
        )
        gelu_pull = jax.vjp(
            lambda gate_in, up_in: jax.nn.gelu(gate_in, approximate=True) * up_in,
            saved_state.gate_values,
            saved_state.up_values,
        )[1]
        grad_gate, grad_up = gelu_pull(grad_hidden)
        grad_gate = grad_gate.astype(jnp.bfloat16)
        grad_up = grad_up.astype(jnp.bfloat16)
        gate_grad = jnp.einsum(
            "td,tf->df", normed_feed, grad_gate, preferred_element_type=jnp.float32
        )
        up_grad = jnp.einsum("td,tf->df", normed_feed, grad_up, preferred_element_type=jnp.float32)
        feed_rows = sum_rows(
            jnp.einsum("tf,df->td", grad_gate, gate_full, preferred_element_type=jnp.float32)
            + jnp.einsum("tf,df->td", grad_up, up_full, preferred_element_type=jnp.float32)
        )
        grad_norm_feed, feed_gain_grad = jax.vjp(norm_rows, saved_state.after_cross, feed_gain)[
            1
        ](feed_rows)
        grad_after_cross = cotangent + grad_norm_feed
        cross_context = saved_state.cross_context
        cross_weights = saved_state.cross_weights
        encoded = saved_state.encoded
        grad_cross_branch = gather_rows(grad_after_cross.astype(jnp.bfloat16))
        cross_output_grad = jnp.einsum(
            "te,td->ed", cross_context, grad_cross_branch, preferred_element_type=jnp.float32
        )
        grad_cross_context = split_heads(
            jnp.einsum(
                "td,ed->te",
                grad_cross_branch,
                cross_output_full,
                preferred_element_type=jnp.float32,
            ).astype(jnp.bfloat16)
        )
        grad_cross_weights = jnp.einsum(
            "ikgd,jkd->kgij",
            grad_cross_context,
            split_kv(saved_state.cross_values),
            preferred_element_type=jnp.float32,
        )
        grad_cross_scores = (
            cross_weights
            * (
                grad_cross_weights
                - jnp.sum(cross_weights * grad_cross_weights, axis=-1, keepdims=True)
            )
        ).astype(jnp.bfloat16)
        grad_cross_queries = (
            (
                jnp.einsum(
                    "kgij,jkd->ikgd",
                    grad_cross_scores,
                    split_kv(saved_state.cross_keys),
                    preferred_element_type=jnp.float32,
                )
                * score_scale
            )
            .reshape(piece_rows, local_heads * head_size)
            .astype(jnp.bfloat16)
        )
        key_part = (
            jnp.einsum(
                "kgij,ikgd->jkd",
                grad_cross_scores,
                split_heads(saved_state.cross_queries),
                preferred_element_type=jnp.float32,
            )
            * score_scale
        ).reshape(encoded.shape[0], kv_local * head_size)
        value_part = jnp.einsum(
            "kgij,ikgd->jkd",
            saved_state.cross_low,
            grad_cross_context,
            preferred_element_type=jnp.float32,
        ).reshape(encoded.shape[0], kv_local * head_size)
        key_sum, value_sum = (
            lax.psum_scatter(key_part, fsdp_axis, scatter_dimension=0, tiled=True),
            lax.psum_scatter(value_part, fsdp_axis, scatter_dimension=0, tiled=True),
        )
        key_low = key_sum.astype(jnp.bfloat16)
        value_low = value_sum.astype(jnp.bfloat16)
        encoded_own = lax.dynamic_slice_in_dim(encoded, fsdp_rank * encoder_rows, encoder_rows, 0)
        cross_key_grad = jnp.einsum(
            "ed,ec->dc", encoded_own, key_low, preferred_element_type=jnp.float32
        )
        cross_value_grad = jnp.einsum(
            "ed,ec->dc", encoded_own, value_low, preferred_element_type=jnp.float32
        )
        encoder_grad = sum_rows(
            jnp.einsum("ec,dc->ed", key_low, cross_key_full, preferred_element_type=jnp.float32)
            + jnp.einsum(
                "ec,dc->ed", value_low, cross_value_full, preferred_element_type=jnp.float32
            )
        )
        cross_query_grad = jnp.einsum(
            "td,tc->dc",
            saved_state.normed_cross,
            grad_cross_queries,
            preferred_element_type=jnp.float32,
        )
        cross_rows = sum_rows(
            jnp.einsum(
                "tc,dc->td",
                grad_cross_queries,
                cross_query_full,
                preferred_element_type=jnp.float32,
            )
        )
        grad_norm_cross, cross_gain_grad = jax.vjp(
            norm_rows, saved_state.after_self, cross_gain
        )[1](cross_rows)
        grad_after_self = grad_after_cross + grad_norm_cross
        queries = saved_state.queries
        keys_own = saved_state.keys_own
        values_own = saved_state.values_own
        context = saved_state.context
        log_total = saved_state.log_total
        normed_self = saved_state.normed_self
        query_heads = split_heads(queries)
        grad_self_branch = gather_rows(grad_after_self.astype(jnp.bfloat16))
        self_output_grad = jnp.einsum(
            "te,td->ed",
            saved_state.context_low,
            grad_self_branch,
            preferred_element_type=jnp.float32,
        )
        grad_context = jnp.einsum(
            "td,ed->te", grad_self_branch, output_full, preferred_element_type=jnp.float32
        ).astype(jnp.bfloat16)
        grad_context_heads = split_heads(grad_context)
        row_delta = jnp.transpose(
            jnp.sum(grad_context_heads.astype(jnp.float32) * context, axis=-1), (1, 2, 0)
        )

        def query_step():

            def step(carried, pieces, piece_start):
                key_piece, value_piece = pieces
                piece_length = key_piece.shape[0]
                block_width = math.gcd(piece_length, key_block_width)
                block_count = piece_length // block_width
                key_blocks = key_piece.reshape(block_count, block_width, kv_local, head_size)
                value_blocks = value_piece.reshape(block_count, block_width, kv_local, head_size)
                block_starts = block_width * jnp.arange(block_count, dtype=jnp.int32)

                def step_one_block(current, block_data):
                    key_block, value_block, block_start = block_data
                    bias_values, allowed, indicator = position_bias(
                        query_start, block_start, piece_rows, block_width
                    )
                    scores = (
                        jnp.einsum(
                            "ikgd,jkd->kgij",
                            query_heads,
                            key_block,
                            preferred_element_type=jnp.float32,
                        )
                        * score_scale
                        + bias_values
                    )
                    shares = jnp.where(allowed, jnp.exp(scores - log_total[..., None]), 0.0)
                    grad_shares = jnp.einsum(
                        "ikgd,jkd->kgij",
                        grad_context_heads,
                        value_block,
                        preferred_element_type=jnp.float32,
                    )
                    grad_scores = shares * (grad_shares - row_delta[..., None])
                    bias_grad = current[1] + jnp.einsum(
                        "hij,bij->hb",
                        grad_scores.reshape(local_heads, piece_rows, block_width),
                        indicator,
                        precision=highest,
                    )
                    scores_low = grad_scores.astype(jnp.bfloat16)
                    query_grad = (
                        current[0]
                        + jnp.einsum(
                            "kgij,jkd->ikgd",
                            scores_low,
                            key_block,
                            preferred_element_type=jnp.float32,
                        )
                        * score_scale
                    )
                    key_block_grad = (
                        jnp.einsum(
                            "kgij,ikgd->jkd",
                            scores_low,
                            query_heads,
                            preferred_element_type=jnp.float32,
                        ).reshape(block_width, kv_local * head_size)
                        * score_scale
                    )
                    value_block_grad = jnp.einsum(
                        "kgij,ikgd->jkd",
                        shares.astype(jnp.bfloat16),
                        grad_context_heads,
                        preferred_element_type=jnp.float32,
                    ).reshape(block_width, kv_local * head_size)
                    keys_all = lax.dynamic_update_slice_in_dim(
                        current[2],
                        lax.dynamic_slice_in_dim(current[2], block_start, block_width, 0)
                        + key_block_grad,
                        block_start,
                        0,
                    )
                    values_all = lax.dynamic_update_slice_in_dim(
                        current[3],
                        lax.dynamic_slice_in_dim(current[3], block_start, block_width, 0)
                        + value_block_grad,
                        block_start,
                        0,
                    )
                    return ((query_grad, bias_grad, keys_all, values_all), None)

                carried, unused = lax.scan(
                    step_one_block, carried, (key_blocks, value_blocks, block_starts)
                )
                return carried

            return step

        query_zero = jnp.zeros((piece_rows, kv_local, group_size, head_size), jnp.float32)
        bias_zero = jnp.zeros((local_heads, buckets), jnp.float32)
        all_zero = jnp.zeros((length, kv_local * head_size), jnp.float32)
        query_grad, bias_grad, keys_all, values_all = fold_keys(
            keys_own, values_own, query_step(), (query_zero, bias_zero, all_zero, all_zero)
        )
        key_sum_self, value_sum_self = (
            lax.psum_scatter(keys_all, fsdp_axis, scatter_dimension=0, tiled=True),
            lax.psum_scatter(values_all, fsdp_axis, scatter_dimension=0, tiled=True),
        )
        key_grad_low = key_sum_self.astype(jnp.bfloat16)
        value_grad_low = value_sum_self.astype(jnp.bfloat16)
        query_grad_low = query_grad.reshape(piece_rows, local_heads * head_size).astype(
            jnp.bfloat16
        )
        self_query_grad = jnp.einsum(
            "td,tc->dc", normed_self, query_grad_low, preferred_element_type=jnp.float32
        )
        self_key_grad = jnp.einsum(
            "td,tc->dc", normed_self, key_grad_low, preferred_element_type=jnp.float32
        )
        self_value_grad = jnp.einsum(
            "td,tc->dc", normed_self, value_grad_low, preferred_element_type=jnp.float32
        )
        self_rows = sum_rows(
            jnp.einsum("tc,dc->td", query_grad_low, query_full, preferred_element_type=jnp.float32)
            + jnp.einsum("tc,dc->td", key_grad_low, key_full, preferred_element_type=jnp.float32)
            + jnp.einsum(
                "tc,dc->td", value_grad_low, value_full, preferred_element_type=jnp.float32
            )
        )
        grad_norm_self, self_gain_grad = jax.vjp(norm_rows, saved_state.own_rows, self_gain)[1](
            self_rows
        )
        input_grad = grad_after_self + grad_norm_self
        grads_full = (
            self_query_grad,
            self_key_grad,
            self_value_grad,
            self_output_grad,
            cross_query_grad,
            cross_key_grad,
            cross_value_grad,
            cross_output_grad,
            gate_grad,
            up_grad,
            down_grad,
        )
        extras = (bias_grad, self_gain_grad, cross_gain_grad, feed_gain_grad)
        return (grads_full, extras, input_grad, encoder_grad)

    layer_list = []
    input_list = []
    encoder_list = []
    small_sums = None
    shard_grads = None
    for batch_index in range(batches):
        weights_forward = gather_weights(shards)
        (
            forward_query_full,
            forward_key_full,
            forward_value_full,
            forward_output_full,
            forward_cross_query_full,
            forward_cross_key_full,
            forward_cross_value_full,
            forward_cross_output_full,
            forward_gate_full,
            forward_up_full,
            forward_down_full,
        ) = weights_forward
        own_rows = inputs[batch_index].astype(jnp.float32)
        forward_normed_self = gather_rows(norm_rows(own_rows, self_gain).astype(jnp.bfloat16))
        forward_queries = matmul(forward_normed_self, forward_query_full).astype(jnp.bfloat16)
        forward_keys_own = matmul(forward_normed_self, forward_key_full).astype(jnp.bfloat16)
        forward_values_own = matmul(forward_normed_self, forward_value_full).astype(jnp.bfloat16)
        forward_query_heads = split_heads(forward_queries)

        def forward_step(carried, pieces, piece_start):
            key_piece, value_piece = pieces
            piece_length = key_piece.shape[0]
            block_width = math.gcd(piece_length, key_block_width)
            block_count = piece_length // block_width
            key_blocks = key_piece.reshape(block_count, block_width, kv_local, head_size)
            value_blocks = value_piece.reshape(block_count, block_width, kv_local, head_size)
            block_starts = block_width * jnp.arange(block_count, dtype=jnp.int32)

            def forward_one_block(current, block_data):
                running_max, running_total, accumulated = current
                key_block, value_block, block_start = block_data
                bias_values, allowed, indicator = position_bias(
                    query_start, block_start, piece_rows, block_width
                )
                scores = (
                    jnp.einsum(
                        "ikgd,jkd->kgij",
                        forward_query_heads,
                        key_block,
                        preferred_element_type=jnp.float32,
                    )
                    * score_scale
                    + bias_values
                )
                scores = jnp.where(allowed, scores, masked_score)
                new_max = jnp.maximum(running_max, jnp.max(scores, axis=-1))
                factor = jnp.exp(running_max - new_max)
                shares = jnp.where(allowed, jnp.exp(scores - new_max[..., None]), 0.0)
                running_total = running_total * factor + jnp.sum(shares, axis=-1)
                update = jnp.einsum(
                    "kgij,jkd->ikgd",
                    shares.astype(jnp.bfloat16),
                    value_block,
                    preferred_element_type=jnp.float32,
                )
                accumulated = accumulated * jnp.transpose(factor, (2, 0, 1))[..., None] + update
                return ((new_max, running_total, accumulated), None)

            carried, unused = lax.scan(
                forward_one_block, carried, (key_blocks, value_blocks, block_starts)
            )
            return carried

        stat_shape = (kv_local, group_size, piece_rows)
        initial = (
            jnp.full(stat_shape, masked_score, jnp.float32),
            jnp.zeros(stat_shape, jnp.float32),
            jnp.zeros((piece_rows, kv_local, group_size, head_size), jnp.float32),
        )
        running_max, running_total, accumulated = fold_keys(
            forward_keys_own, forward_values_own, forward_step, initial
        )
        forward_context = accumulated / jnp.transpose(running_total, (2, 0, 1))[..., None]
        forward_log_total = running_max + jnp.log(running_total)
        context_low = forward_context.reshape(piece_rows, local_heads * head_size).astype(
            jnp.bfloat16
        )
        after_self = own_rows + sum_rows(matmul(context_low, forward_output_full))
        normed_cross = gather_rows(norm_rows(after_self, cross_gain).astype(jnp.bfloat16))
        cross_queries = matmul(normed_cross, forward_cross_query_full).astype(jnp.bfloat16)
        forward_encoded = lax.all_gather(
            encoder_out[batch_index], (fsdp_axis, tensor_axis), axis=0, tiled=True
        )
        cross_keys = matmul(forward_encoded, forward_cross_key_full).astype(jnp.bfloat16)
        cross_values = matmul(forward_encoded, forward_cross_value_full).astype(jnp.bfloat16)
        cross_scores = (
            jnp.einsum(
                "ikgd,jkd->kgij",
                split_heads(cross_queries),
                split_kv(cross_keys),
                preferred_element_type=jnp.float32,
            )
            * score_scale
        )
        forward_cross_weights = jax.nn.softmax(cross_scores, axis=-1)
        cross_low = forward_cross_weights.astype(jnp.bfloat16)
        forward_cross_context = (
            jnp.einsum(
                "kgij,jkd->ikgd",
                cross_low,
                split_kv(cross_values),
                preferred_element_type=jnp.float32,
            )
            .reshape(piece_rows, local_heads * head_size)
            .astype(jnp.bfloat16)
        )
        after_cross = after_self + sum_rows(
            matmul(forward_cross_context, forward_cross_output_full)
        )
        forward_normed_feed = gather_rows(norm_rows(after_cross, feed_gain).astype(jnp.bfloat16))
        gate_values = matmul(forward_normed_feed, forward_gate_full)
        up_values = matmul(forward_normed_feed, forward_up_full)
        forward_hidden = (jax.nn.gelu(gate_values, approximate=True) * up_values).astype(
            jnp.bfloat16
        )
        layer_rows = after_cross + sum_rows(matmul(forward_hidden, forward_down_full))
        forward_saved_state = types.SimpleNamespace(
            own_rows=own_rows,
            normed_self=forward_normed_self,
            queries=forward_queries,
            keys_own=forward_keys_own,
            values_own=forward_values_own,
            context=forward_context,
            log_total=forward_log_total,
            context_low=context_low,
            after_self=after_self,
            normed_cross=normed_cross,
            cross_queries=cross_queries,
            encoded=forward_encoded,
            cross_keys=cross_keys,
            cross_values=cross_values,
            cross_weights=forward_cross_weights,
            cross_low=cross_low,
            cross_context=forward_cross_context,
            after_cross=after_cross,
            normed_feed=forward_normed_feed,
            gate_values=gate_values,
            up_values=up_values,
            hidden=forward_hidden,
        )
        layer_rows, saved_state = (layer_rows.astype(jnp.bfloat16), forward_saved_state)
        weights_backward = gather_weights(shards)
        grads_full, extras, input_grad, encoder_grad = backward(
            batch_index, saved_state, weights_backward
        )
        reduced = scatter_grads(grads_full)
        shard_grads = reduced if shard_grads is None else add_all(shard_grads, reduced)
        small_sums = extras if small_sums is None else add_all(small_sums, extras)
        layer_list.append(layer_rows)
        input_list.append(input_grad)
        encoder_list.append(encoder_grad)
    table_full = lax.dynamic_update_slice_in_dim(
        jnp.zeros((heads_all, buckets), jnp.float32), small_sums[0], tensor_rank * local_heads, 0
    )
    table_sum, self_gain_sum, cross_gain_sum, feed_gain_sum = lax.psum(
        (table_full, small_sums[1], small_sums[2], small_sums[3]), (fsdp_axis, tensor_axis)
    )
    return (
        jnp.stack(layer_list),
        jnp.stack(input_list),
        jnp.stack(encoder_list),
        table_sum,
        self_gain_sum,
        shard_grads[0],
        shard_grads[1],
        shard_grads[2],
        shard_grads[3],
        cross_gain_sum,
        shard_grads[4],
        shard_grads[5],
        shard_grads[6],
        shard_grads[7],
        feed_gain_sum,
        shard_grads[8],
        shard_grads[9],
        shard_grads[10],
    )


def to_chip(fsdp):
    return dict(device_id={fsdp_axis: fsdp}, device_id_type=pl.DeviceIdType.MESH)


def to_core(core):
    return dict(device_id={tensor_axis: core}, device_id_type=pl.DeviceIdType.MESH)


def chip_place(layers):
    rank = lax.axis_index(fsdp_axis)
    return rank, rank // 4, rank // 2 % 2, rank % 2


def peers_of(rank, y, x):
    found = []
    for o in (1, 2, 3):
        other_y = 1 - y if o & 2 else y
        other_x = 1 - x if o & 1 else x
        spot = 2 * other_y + other_x
        found.append((rank - 2 * y - x + spot, spot))
    return found


def greet_all(layers):
    chips = 4 * layers
    rank = lax.axis_index(fsdp_axis)
    barrier = pltpu.get_barrier_semaphore()
    for o in range(1, chips):
        pl.semaphore_signal(barrier, inc=1, **to_chip((rank + o) % chips))
    pl.semaphore_signal(barrier, inc=1, **to_core(1 - lax.axis_index(tensor_axis)))
    pl.semaphore_wait(barrier, chips)


def greet(layers):
    rank, z, y, x = chip_place(layers)
    barrier = pltpu.get_barrier_semaphore()
    for chip, spot in peers_of(rank, y, x):
        pl.semaphore_signal(barrier, inc=1, **to_chip(chip))
    for o in range(1, layers):
        pl.semaphore_signal(barrier, inc=1, **to_chip(rank - 4 * z + 4 * ((z + o) % layers)))
    pl.semaphore_signal(barrier, inc=1, **to_core(1 - lax.axis_index(tensor_axis)))
    pl.semaphore_wait(barrier, 3 + layers)


dma = pltpu.SemaphoreType.DMA


class Column:
    def __init__(self, layers, source, land, z_sem, core_sem=None):
        self.layers, self.source, self.land = layers, source, land
        self.z_sem, self.core_sem = z_sem, core_sem
        self.rank, self.z, self.y, self.x = chip_place(layers)
        self.core = lax.axis_index(tensor_axis)

    def place(self, layer):
        return (layer,) if self.core_sem is None else (layer, self.core)

    def hop(self, o):
        there = (self.z + o) % self.layers
        return pltpu.make_async_remote_copy(
            src_ref=self.source.at[there],
            dst_ref=self.land.at[self.place(self.z)],
            send_sem=self.z_sem.at[0, o],
            recv_sem=self.z_sem.at[1, self.z],
            **to_chip(self.rank + 4 * (there - self.z)),
        )

    def arrival(self, layer):
        return pltpu.make_async_remote_copy(
            src_ref=self.source.at[0],
            dst_ref=self.land.at[self.place(layer)],
            send_sem=self.z_sem.at[0, 0],
            recv_sem=self.z_sem.at[1, layer],
            **to_chip(self.rank + 4 - 8 * (self.z // 2)),
        )

    def over(self, layer):
        return pltpu.make_async_remote_copy(
            src_ref=self.land.at[layer, self.core],
            dst_ref=self.land.at[layer, self.core],
            send_sem=self.core_sem.at[0, layer],
            recv_sem=self.core_sem.at[1, layer],
            **to_core(1 - self.core),
        )

    def piece(self, o, n):
        there = (self.z + o) % self.layers
        at = pl.ds(pl.multiple_of(16 * n, 16), 16)
        return pltpu.make_async_remote_copy(
            src_ref=self.source.at[there, at],
            dst_ref=self.land.at[self.z, at],
            send_sem=self.z_sem.at[0, o],
            recv_sem=self.z_sem.at[1, self.z],
            **to_chip(self.rank + 4 * (there - self.z)),
        )

    def start(self):
        for o in range(1, self.layers):
            self.hop(o).start()
        self.land[self.place(self.z)] = self.source[self.z]

    def arrive(self):
        for o in range(1, self.layers):
            self.arrival((self.z + o) % self.layers).wait_recv()
        if self.core_sem is not None:
            for layer in range(self.layers):
                self.over(layer).start()

    def finish(self):
        for o in range(1, self.layers):
            self.hop(o).wait_send()
        if self.core_sem is not None:
            for layer in range(self.layers):
                self.over(layer).wait()


class PlaneSwap:
    def __init__(self, layers, source, land, sem):
        self.source, self.land, self.sem = source, land, sem
        self.rank, self.z, self.y, self.x = chip_place(layers)
        self.spot = 2 * self.y + self.x
        self.peers = peers_of(self.rank, self.y, self.x)

    def hop(self, o):
        chip, there = self.peers[o]
        return pltpu.make_async_remote_copy(
            src_ref=self.source.at[there],
            dst_ref=self.land.at[self.spot],
            send_sem=self.sem.at[0, o],
            recv_sem=self.sem.at[1, o],
            **to_chip(chip),
        )

    def start(self):
        for o in range(3):
            self.hop(o).start()
        self.land[self.spot] = self.source[self.spot]

    def arrival(self, o):
        chip, there = self.peers[o]
        return pltpu.make_async_remote_copy(
            src_ref=self.source.at[there],
            dst_ref=self.land.at[there],
            send_sem=self.sem.at[0, o],
            recv_sem=self.sem.at[1, o],
            **to_chip(chip),
        )

    def arrive(self):
        for o in range(3):
            self.arrival(o).wait_recv()

    def finish(self):
        for o in range(3):
            self.hop(o).wait_send()


class PlaneGather:
    def __init__(self, layers, source, land, sem, core_sem):
        self.source, self.land, self.sem, self.core_sem = source, land, sem, core_sem
        self.rank, self.z, self.y, self.x = chip_place(layers)
        self.core = lax.axis_index(tensor_axis)
        self.spot = 2 * self.y + self.x
        self.peers = peers_of(self.rank, self.y, self.x)

    def hop(self, o, spot):
        return pltpu.make_async_remote_copy(
            src_ref=self.source,
            dst_ref=self.land.at[spot, self.core],
            send_sem=self.sem.at[0, o],
            recv_sem=self.sem.at[1, o],
            **to_chip(self.peers[o][0]),
        )

    def over(self, spot):
        return pltpu.make_async_remote_copy(
            src_ref=self.land.at[spot, self.core],
            dst_ref=self.land.at[spot, self.core],
            send_sem=self.core_sem.at[0, spot],
            recv_sem=self.core_sem.at[1, spot],
            **to_core(1 - self.core),
        )

    def start(self):
        for o in range(3):
            self.hop(o, self.spot).start()
        self.land[self.spot, self.core] = self.source[...]

    def arrive(self):
        for o in range(3):
            self.hop(o, self.peers[o][1]).wait_recv()
        for spot in range(4):
            self.over(spot).start()

    def finish(self):
        for o in range(3):
            self.hop(o, self.spot).wait_send()
        for spot in range(4):
            self.over(spot).wait()


def close_kernel(
    layers,
    heads,
    gq_ref,
    x_ref,
    win_ref,
    gas_ref,
    kvs_ref,
    gains_ref,
    mid_ref,
    sums_ref,
    hit_ref,
    nt_s,
    wa_ref,
    sum_s,
    rows_land,
    table_out,
    gain_out,
    wkv_s,
    mine_s,
    halves_s,
    enc_s,
    ended_s,
    small_s,
    small_z,
    load_sem,
    core_sem,
    rows_z,
    small_sem,
    z_sem,
    *sum_refs,
):
    f32, bf16 = jnp.float32, jnp.bfloat16
    grads = GradSum(layers, slice(None), None, (), sum_s, *sum_refs)
    rows = Column(layers, ended_s, rows_land, rows_z)
    rank, z, y, x = chip_place(layers)
    core = lax.axis_index(tensor_axis)
    own = gas_ref.shape[1]
    width = x_ref.shape[1]
    enc_own = kvs_ref.shape[0] // (2 * layers)
    wide = kvs_ref.shape[1]
    kv_local = 4
    blocks = sums_ref.shape[0] // 2
    buckets = hit_ref.shape[1]
    gain = gains_ref[...]
    loads = pltpu.make_async_copy(
        wa_ref.at[:, pl.ds(2 * wide, wide)], wkv_s, load_sem.at[0]
    )
    loads.start()
    greet_all(layers)

    per_layer = width // layers

    def weigh(turn, carry):
        layer = grads.layer_of(2 * turn)
        at = pl.ds(pl.multiple_of(layer * per_layer, per_layer), per_layer)
        part = matmul(nt_s[at, :], gq_ref[...]).astype(bf16)
        grads.own[layer] = part.reshape(grads.own.shape[1:])
        grads.send_first(2 * turn)
        grads.send_first(2 * turn + 1)
        return carry

    lax.fori_loop(0, layers, weigh, 0)

    def gather(which):
        return jnp.concatenate(
            [
                gq_ref[pl.ds(pl.multiple_of((2 * layer + which) * own, own), own), :]
                for layer in range(layers)
            ],
            axis=0,
        )

    def across(n, shape_at):
        return pltpu.make_async_remote_copy(
            src_ref=halves_s.at[0, shape_at],
            dst_ref=halves_s.at[1, shape_at],
            send_sem=core_sem.at[0, n],
            recv_sem=core_sem.at[1, n],
            **to_core(1 - core),
        )

    body, tail = pl.ds(0, layers * own), pl.ds(layers * own, layers * enc_own)
    halves_s[0, body, :] = dot_t(gather(1 - core), win_ref[...]).astype(bf16)
    across(0, body).start()
    loads.wait()
    enc_s[...] = dot_t(kvs_ref[...], wkv_s[...])
    other = pl.ds(pl.multiple_of((1 - core) * layers * enc_own, enc_own), layers * enc_own)
    halves_s[0, tail, :] = enc_s[other, :].astype(bf16)
    across(1, tail).start()
    mine_s[...] = dot_t(gather(core), win_ref[...])
    grads.advance(1)
    grads.advance(2)

    found = [jnp.zeros((1, buckets), f32) for _ in range(2)]
    for d in range(blocks):
        by_bucket = lax.dot_general(
            sums_ref[...],
            hit_ref[d],
            (((1,), (1,)), ((), ())),
            precision=highest,
            preferred_element_type=f32,
        )
        for h in range(2):
            found[h] = found[h] + by_bucket[h * blocks + d : h * blocks + d + 1, :]
    half = width // 2
    lane = lax.broadcasted_iota(jnp.int32, (buckets, half), 1)
    spread = (lane % buckets == lax.broadcasted_iota(jnp.int32, (buckets, half), 0)).astype(f32)
    lane = lax.broadcasted_iota(jnp.int32, (1, half), 1)
    first_head = 2 * (core * kv_local + rank % 4)
    table = jnp.zeros((1, half), f32)
    for h in range(2):
        row = jnp.dot(found[h], spread, precision=highest, preferred_element_type=f32)
        table = table + jnp.where(lane // buckets == first_head + h, row, 0.0)
    small = [table, jnp.zeros((1, half), f32)]
    for n in (1, 0):
        small = [mid_ref[n : n + 1, :half], mid_ref[n : n + 1, half:]] + small

    across(0, body).wait()
    across(1, tail).wait()
    mine_enc = pl.ds(pl.multiple_of(core * layers * enc_own, enc_own), layers * enc_own)
    enc_sum = enc_s[mine_enc, :].astype(bf16).astype(f32) + halves_s[1, tail, :].astype(f32)

    total = jnp.zeros((1, width), f32)
    for layer in range(layers):
        at = slice(layer * own, (layer + 1) * own)
        both = mine_s[at, :].astype(bf16).astype(f32) + halves_s[1, at, :].astype(f32)
        v = x_ref[pl.ds(pl.multiple_of((2 * layer + core) * own, own), own), :].astype(f32)
        grad, gain_grad = norm_pull(v, gain, both)
        total = total + gain_grad
        ended_s[layer, :own, :] = (gas_ref[layer] + grad).astype(bf16)
        ended_s[layer, own:, :] = enc_sum[layer * enc_own : (layer + 1) * enc_own].astype(bf16)
    small_s[0] = jnp.concatenate([total[:, :half], total[:, half:]] + small, axis=0)
    chips = 4 * layers

    def spread_to(o):
        there = (rank + o) % chips
        return pltpu.make_async_remote_copy(
            src_ref=small_s.at[0],
            dst_ref=small_z.at[rank],
            send_sem=small_sem.at[0, o],
            recv_sem=small_sem.at[1, rank],
            **to_chip(there),
        )

    def came_from(o):
        there = (rank + o) % chips
        return pltpu.make_async_remote_copy(
            src_ref=small_s.at[0],
            dst_ref=small_z.at[there],
            send_sem=small_sem.at[0, o],
            recv_sem=small_sem.at[1, there],
            **to_chip(there),
        )

    across_core = pltpu.make_async_remote_copy(
        src_ref=small_s.at[1],
        dst_ref=small_s.at[2],
        send_sem=z_sem.at[0],
        recv_sem=z_sem.at[1],
        **to_core(1 - core),
    )
    for o in range(1, chips):
        spread_to(o).start()
    small_z[rank] = small_s[0]
    rows_land[z] = ended_s[z]

    def one(m, carry):
        grads.advance(m)
        return carry

    def feed_links(m, carry):
        for o in range(1, layers):
            rows.piece(o, m - 3).start()
        grads.advance(m)
        return carry

    pieces = (own + enc_own) // 16
    lax.fori_loop(3, 3 + pieces, feed_links, 0)
    lax.fori_loop(3 + pieces, 9, one, 0)
    for o in range(1, chips):
        came_from(o).wait_recv()
    summed = small_z[0]
    for chip in range(1, chips):
        summed = summed + small_z[chip]
    small_s[1] = summed
    across_core.start()
    lax.fori_loop(9, sum_steps(layers), one, 0)
    across_core.wait()
    for o in range(1, chips):
        spread_to(o).wait_send()
    both = small_s[1] + small_s[2]
    low = jnp.where(core == 0, small_s[1], small_s[2])
    for n, part in enumerate((both, low, low)):
        gain_out[n : n + 1, :half] = part[2 * n : 2 * n + 1, :]
        gain_out[n : n + 1, half:] = part[2 * n + 1 : 2 * n + 2, :]
    for h in range(heads):
        table_out[h : h + 1, :] = both[6:7, h * buckets : (h + 1) * buckets]
    rows.arrive()
    rows.finish()
    grads.finish()


def close_rows(
    layers, heads, grad_qkv, x_low, win, grad_rows, kv_sum, self_gain, mid, sums, hit, nt, weights
):
    f32, bf16 = jnp.float32, jnp.bfloat16
    width, cols = win.shape
    own = grad_rows.shape[1]
    wide = kv_sum.shape[1]
    enc_own = kv_sum.shape[0] // (2 * layers)
    buckets = hit.shape[1]
    vmem, anywhere = pl.BlockSpec(memory_space=pltpu.VMEM), pl.BlockSpec(memory_space=pl.ANY)
    rows_shape = (layers, own + enc_own, width)
    return pl.pallas_call(
        functools.partial(close_kernel, layers, heads),
        name="close_rows",
        out_shape=(
            jax.ShapeDtypeStruct((2, 2, 16, cols), f32),
            jax.ShapeDtypeStruct(rows_shape, bf16),
            jax.ShapeDtypeStruct((heads, buckets), f32),
            jax.ShapeDtypeStruct((3, width), f32),
        ),
        in_specs=[vmem] * 10 + [anywhere],
        out_specs=(vmem,) * 4,
        scratch_shapes=[
            pltpu.VMEM((width, wide), bf16),
            pltpu.VMEM((layers * own, width), f32),
            pltpu.VMEM((2, layers * (own + enc_own), width), bf16),
            pltpu.VMEM((2 * layers * enc_own, width), f32),
            pltpu.VMEM(rows_shape, bf16),
            pltpu.VMEM((3, 8, width // 2), f32),
            pltpu.VMEM((4 * layers, 8, width // 2), f32),
            dma((1,)),
            dma((2, 2)),
            dma((2, layers)),
            dma((2, 4 * layers)),
            dma((2,)),
            *sum_scratch(layers, cols),
        ],
        compiler_params=pltpu.CompilerParams(
            collective_id=7, has_side_effects=True, vmem_limit_bytes=67043328
        ),
    )(grad_qkv, x_low, win, grad_rows, kv_sum, self_gain, mid, sums, hit, nt, weights)


def finish_kernel(
    in_ref,
    rest_ref,
    feed_ref,
    rows_ref,
    layer_ref,
    table_ref,
    gain_ref,
    layer_out,
    input_out,
    enc_out,
    table_out,
    self_gain,
    query_out,
    key_out,
    value_out,
    out_out,
    cross_gain,
    cq_out,
    ck_out,
    cv_out,
    co_out,
    feed_gain,
    gate_out,
    up_out,
    down_out,
):
    layer_out[...] = layer_ref[...]
    own = input_out.shape[1]
    input_out[...] = rows_ref[:, :own, :].astype(jnp.float32)
    enc_out[...] = rows_ref[:, own:, :].astype(jnp.float32)
    table_out[...] = table_ref[...]
    for n, ref in enumerate((self_gain, cross_gain, feed_gain)):
        ref[...] = gain_ref[n : n + 1, :]
    group = in_ref.shape[1] // 4
    half = group // 4
    pieces = [in_ref[:, n * group : (n + 1) * group] for n in range(4)]
    query_out[...] = jnp.concatenate([p[:, : 2 * half] for p in pieces], axis=1)
    key_out[...] = jnp.concatenate([p[:, 2 * half : 3 * half] for p in pieces], axis=1)
    value_out[...] = jnp.concatenate([p[:, 3 * half :] for p in pieces], axis=1)
    at = 0
    for ref in (out_out, cq_out, ck_out, cv_out, co_out):
        ref[...] = rest_ref[:, at : at + ref.shape[1]]
        at += ref.shape[1]
    feed = gate_out.shape[1]
    for at in range(0, feed, tile):
        units = min(tile, feed - at)
        for n, ref in enumerate((gate_out, up_out, down_out)):
            start = 3 * at + n * units
            ref[:, at : at + units] = feed_ref[:, start : start + units]


def finish(in_sum, rest_sum, feed_sum, rows, layer_rows, table, gains):
    f32 = jnp.float32
    own = layer_rows.shape[1]
    layers, both, width = rows.shape

    def flat(x):
        return x.reshape(64, x.shape[-1])

    def out(*shape, dtype=f32):
        return jax.ShapeDtypeStruct(shape, dtype)

    wide, feed = in_sum.shape[-1] // 2, feed_sum.shape[-1] // 3
    gain = out(1, width)
    vmem = pl.BlockSpec(memory_space=pltpu.VMEM)
    return pl.pallas_call(
        finish_kernel,
        name="finish",
        out_shape=(
            out(*layer_rows.shape, dtype=layer_rows.dtype),
            out(layers, own, width),
            out(layers, both - own, width),
            out(*table.shape),
            gain,
            out(64, wide),
            out(64, wide // 2),
            out(64, wide // 2),
            out(64, wide),
            gain,
            out(64, wide),
            out(64, wide // 2),
            out(64, wide // 2),
            out(64, wide),
            gain,
            out(64, feed),
            out(64, feed),
            out(64, feed),
        ),
        in_specs=[vmem] * 7,
        out_specs=(vmem,) * 18,
        compiler_params=pltpu.CompilerParams(vmem_limit_bytes=67043328),
    )(flat(in_sum), flat(rest_sum), flat(feed_sum), rows, layer_rows, table, gains)

def sum_scratch(layers, cols):
    steps = 2 * layers
    bf16 = jnp.bfloat16
    return [
        pltpu.VMEM((layers, 2, 2, 2, 2, 16, cols), bf16),
        pltpu.VMEM((layers, 2, 2, 2, 16, cols), bf16),
        pltpu.VMEM((steps, 2, 16, cols), bf16),
        pltpu.VMEM((steps, 2, 16, cols), bf16),
        pltpu.VMEM((steps, 2, 16, cols), bf16),
        dma((3, layers)),
        dma((2, steps, 2, 2)),
        dma((2, steps, 2)),
        dma((2, steps)),
        dma((2, steps)),
    ]


def sum_steps(layers):
    return 2 * layers + layers + 3


class GradSum:
    def __init__(self, layers, cols, whole, got, out, own, first, second, below, above, load, s1, s2, su, sd):
        self.cols = cols
        self.got = got
        self.layers, self.whole, self.out, self.own = layers, whole, out, own
        self.first, self.second, self.below, self.above = first, second, below, above
        self.load, self.s1, self.s2, self.su, self.sd = load, s1, s2, su, sd
        self.rank, self.z, self.y, self.x = chip_place(layers)
        self.x_chip = self.rank + 1 - 2 * self.x
        self.y_chip = self.rank + 2 - 4 * self.y
        self.steps = 2 * layers

    def layer_of(self, n):
        turn = n // 2
        return jnp.where(turn % 2 == 1, turn // 2, self.layers - 1 - turn // 2)

    def loads(self, turn):
        layer = self.layer_of(2 * turn)
        copies = [
            pltpu.make_async_copy(
                self.whole.at[(layer, *[slice(None)] * 5, self.cols)],
                self.own.at[layer],
                self.load.at[0, turn],
            )
        ]
        for colour, came in enumerate(self.got):
            copies.append(
                pltpu.make_async_copy(
                    came.at[layer, :, :, :, self.cols],
                    self.first.at[layer, colour],
                    self.load.at[1 + colour, turn],
                )
            )
        return copies

    def hop_one(self, n, colour, which):
        layer, chunk = self.layer_of(n), n % 2
        if colour == 0:
            source, chip = self.own.at[layer, which, 1 - self.x, 0, chunk], self.x_chip
        else:
            source, chip = self.own.at[layer, 1 - self.y, which, 1, chunk], self.y_chip
        return pltpu.make_async_remote_copy(
            src_ref=source,
            dst_ref=self.first.at[layer, colour, which, chunk],
            send_sem=self.s1.at[0, n, colour, which],
            recv_sem=self.s1.at[1, n, colour, which],
            **to_chip(chip),
        )

    def hop_two(self, n, colour):
        layer, chunk = self.layer_of(n), n % 2
        if colour == 0:
            source, chip = self.own.at[layer, 1 - self.y, self.x, 0, chunk], self.y_chip
        else:
            source, chip = self.own.at[layer, self.y, 1 - self.x, 1, chunk], self.x_chip
        return pltpu.make_async_remote_copy(
            src_ref=source,
            dst_ref=self.second.at[n, colour],
            send_sem=self.s2.at[0, n, colour],
            recv_sem=self.s2.at[1, n, colour],
            **to_chip(chip),
        )

    def hop_z(self, n, up):
        layer, chunk = self.layer_of(n), n % 2
        sems = self.su if up else self.sd
        return pltpu.make_async_remote_copy(
            src_ref=self.own.at[layer, self.y, self.x, :, chunk],
            dst_ref=(self.below if up else self.above).at[n],
            send_sem=sems.at[0, n],
            recv_sem=sems.at[1, n],
            **to_chip(self.rank + (4 if up else -4)),
        )

    def start(self):
        for turn in range(self.layers):
            for copy in self.loads(turn):
                copy.start()

    def send_first(self, n):
        @pl.when(n < self.steps)
        def _():
            if self.whole is not None:

                @pl.when(n % 2 == 0)
                def _():
                    for copy in self.loads(n // 2):
                        copy.wait()

            if not self.got:
                for which in range(2):
                    for colour in range(2):
                        self.hop_one(n, colour, which).start()

    def advance(self, m):
        steps, layers = self.steps, self.layers
        n = m - 1

        @pl.when((n >= 0) & (n < steps))
        def _():
            layer, chunk = self.layer_of(n), n % 2
            for colour in range(2):
                for other in range(2):
                    if colour == 0:
                        which = (1 - self.y) if other == 0 else self.y
                        place = (layer, which, self.x, 0, chunk)
                    else:
                        which = (1 - self.x) if other == 0 else self.x
                        place = (layer, self.y, which, 1, chunk)
                    if not self.got:
                        self.hop_one(n, colour, which).wait_recv()
                    self.own[place] = self.own[place] + self.first[layer, colour, which, chunk]
                    if other == 0:
                        self.hop_two(n, colour).start()

        n2 = m - 2

        @pl.when((n2 >= 0) & (n2 < steps))
        def _():
            layer, chunk = self.layer_of(n2), n2 % 2
            for colour in range(2):
                self.hop_two(n2, colour).wait_recv()
                place = (layer, self.y, self.x, colour, chunk)
                self.own[place] = self.own[place] + self.second[n2, colour]

        for up in (True, False):
            chain = self.z if up else layers - 1 - self.z
            nz = m - 2 - chain
            layer = self.layer_of(nz)
            beyond = (layer > self.z) if up else (layer < self.z)

            @pl.when((nz >= 0) & (nz < steps) & beyond)
            def _():
                @pl.when(chain > 0)
                def _():
                    self.hop_z(nz, up).wait_recv()
                    came = self.below if up else self.above
                    for colour in range(2):
                        place = (layer, self.y, self.x, colour, nz % 2)
                        self.own[place] = self.own[place] + came[nz, colour]

                self.hop_z(nz, up).start()

        nf = m - 2 - layers

        @pl.when((nf >= 0) & (nf < steps) & (self.layer_of(nf) == self.z))
        def _():
            layer, chunk = self.layer_of(nf), nf % 2
            for colour in range(2):
                self.out[colour, chunk, :, self.cols] = self.own[layer, self.y, self.x, colour, chunk].astype(
                    jnp.float32
                )
            for up in (True, False):
                chain = self.z if up else layers - 1 - self.z

                @pl.when(chain > 0)
                def _():
                    self.hop_z(nf, up).wait_recv()
                    came = self.below if up else self.above
                    for colour in range(2):
                        self.out[colour, chunk, :, self.cols] += came[nf, colour].astype(jnp.float32)

    def finish(self):
        def one(n, carry):
            for colour in range(2):
                if not self.got:
                    for which in range(2):
                        self.hop_one(n, colour, which).wait_send()
                self.hop_two(n, colour).wait_send()
            layer = self.layer_of(n)
            for up in (True, False):

                @pl.when((layer > self.z) if up else (layer < self.z))
                def _():
                    self.hop_z(n, up).wait_send()

            return carry

        lax.fori_loop(0, self.steps, one, 0)

def gather_scratch(layers, cols):
    return [
        pltpu.VMEM((2, 2, 16, cols), jnp.bfloat16),
        dma((1,)),
        dma((2, 2, layers, 2)),
        dma((2, layers, 2)),
        dma((2, layers, 2)),
        dma((2, layers, 2)),
        dma((2, layers, 2)),
    ]


class RowGather:
    def __init__(self, layers, short, whole, here, local, sz, sx, sy, sfx, sfy):
        self.short = short
        self.layers, self.whole, self.here = layers, whole, here
        self.local, self.sz, self.sx, self.sy, self.sfx, self.sfy = local, sz, sx, sy, sfx, sfy
        self.rank, self.z, self.y, self.x = chip_place(layers)
        self.x_chip = self.rank + 1 - 2 * self.x
        self.y_chip = self.rank + 2 - 4 * self.y

    def put(self):
        place = self.whole.at[self.z, self.y, self.x]
        return pltpu.make_async_copy(self.here, place, self.local.at[0])

    def source(self, layer, chunk, own, colours=slice(None)):
        if own:
            return self.here.at[colours, chunk]
        return self.whole.at[layer, self.y, self.x, colours, chunk]

    def along_z(self, layer, chunk, up, own=False):
        return pltpu.make_async_remote_copy(
            src_ref=self.source(layer, chunk, own),
            dst_ref=self.whole.at[layer, self.y, self.x, :, chunk],
            send_sem=self.sz.at[0, int(up), layer, chunk],
            recv_sem=self.sz.at[1, int(up), layer, chunk],
            **to_chip(self.rank + (4 if up else -4)),
        )

    def in_plane(self, layer, chunk, along_x, own=False):
        sems = self.sx if along_x else self.sy
        colours = slice(None)
        if self.short:
            colours = 0 if along_x else 1
        return pltpu.make_async_remote_copy(
            src_ref=self.source(layer, chunk, own, colours),
            dst_ref=self.whole.at[layer, self.y, self.x, colours, chunk],
            send_sem=sems.at[0, layer, chunk],
            recv_sem=sems.at[1, layer, chunk],
            **to_chip(self.x_chip if along_x else self.y_chip),
        )

    def onward(self, layer, chunk, along_x):
        if along_x:
            place = (layer, 1 - self.y, self.x, 1, chunk)
            sems, chip = self.sfx, self.x_chip
        else:
            place = (layer, self.y, 1 - self.x, 0, chunk)
            sems, chip = self.sfy, self.y_chip
        return pltpu.make_async_remote_copy(
            src_ref=self.whole.at[place],
            dst_ref=self.whole.at[place],
            send_sem=sems.at[0, layer, chunk],
            recv_sem=sems.at[1, layer, chunk],
            **to_chip(chip),
        )

    def send_z(self):
        for chunk in range(2):

            @pl.when(self.z < self.layers - 1)
            def _():
                self.along_z(self.z, chunk, True, own=True).start()

            @pl.when(self.z > 0)
            def _():
                self.along_z(self.z, chunk, False, own=True).start()

    def send_plane(self):
        for chunk in range(2):
            for along_x in (True, False):
                self.in_plane(self.z, chunk, along_x, own=True).start()
        self.put().start()

    def pass_on(self, m):
        far, chunk = m // 2, m % 2
        for up in (True, False):
            layer = self.z - far if up else self.z + far
            near = (layer >= 0) if up else (layer < self.layers)

            @pl.when((far > 0) & near)
            def _():
                self.along_z(layer, chunk, up).wait_recv()

                @pl.when((self.z < self.layers - 1) if up else (self.z > 0))
                def _():
                    self.along_z(layer, chunk, up).start()

                for along_x in (True, False):
                    self.in_plane(layer, chunk, along_x).start()

    def turn(self, m):
        far, chunk = m // 2, m % 2
        for up in (True, False):
            layer = self.z - far if up else self.z + far
            near = (layer >= 0) if up else ((layer < self.layers) & (far > 0))

            @pl.when(near)
            def _():
                for along_x in (True, False):
                    self.in_plane(layer, chunk, along_x).wait_recv()
                    self.onward(layer, chunk, not along_x).start()

    def step(self, m):
        @pl.when(m + 2 < 2 * self.layers)
        def _():
            self.pass_on(m + 2)

        if not self.short:
            self.turn(m)

    def finish(self):
        self.put().wait()

        def one(n, carry):
            layer, chunk = n // 2, n % 2
            for along_x in (True, False):
                if self.short:
                    self.in_plane(layer, chunk, along_x).wait_recv()
                else:
                    self.onward(layer, chunk, along_x).wait()
                self.in_plane(layer, chunk, along_x).wait_send()

            @pl.when((self.z < self.layers - 1) & (layer <= self.z))
            def _():
                self.along_z(layer, chunk, True).wait_send()

            @pl.when((self.z > 0) & (layer >= self.z))
            def _():
                self.along_z(layer, chunk, False).wait_send()

            return carry

        lax.fori_loop(0, 2 * self.layers, one, 0)

def begin_kernel(
    score_scale,
    layers,
    rows_ref,
    enc_ref,
    cot_ref,
    gain_ref,
    bias_ref,
    query_ref,
    key_ref,
    value_ref,
    out_ref,
    cq_ref,
    ck_ref,
    cv_ref,
    co_ref,
    gate_ref,
    up_ref,
    down_ref,
    rows_out,
    enc_out,
    cot_out,
    kept_ref,
    low_ref,
    full_ref,
    total_ref,
    nt_out,
    win_out,
    whole_ref,
    feed_whole,
    rows_land,
    enc_land,
    enc_all,
    cot_land,
    win_s,
    norm_s,
    qkv_s,
    came,
    landed,
    low_s,
    q_s,
    k_s,
    v_s,
    bias_s,
    score_s,
    rows_z,
    rows_core,
    enc_z,
    plane_sem,
    plane_core,
    cot_z,
    cot_core,
    in_sem,
    out_send,
    out_recv,
    win_sem,
    *gather_refs,
):
    f32, bf16 = jnp.float32, jnp.bfloat16
    blocks = bias_s.shape[1]
    sources = qkv_s.shape[0]
    head = k_s.shape[1]
    third = len(gather_refs) // 3
    first = RowGather(layers, False, win_s, *gather_refs[:third])
    gathers = (
        RowGather(layers, True, feed_whole, *gather_refs[2 * third :]),
        RowGather(layers, False, whole_ref, *gather_refs[third : 2 * third]),
    )
    rank, z, y, x = chip_place(layers)
    spot = 2 * y + x
    peers = peers_of(rank, y, x)
    rows = Column(layers, rows_ref, rows_land, rows_z, rows_core)
    enc = Column(layers, enc_ref, enc_land, enc_z)
    plane = PlaneGather(layers, enc_land, enc_all, plane_sem, plane_core)
    cot = Column(layers, cot_ref, cot_land, cot_z, cot_core)
    heads = PlaneSwap(layers, qkv_s, came, in_sem)

    def shard(gather, parts):
        gather.here[...] = jnp.concatenate(parts, axis=1).reshape(gather.here.shape)

    parts = []
    for kv in range(sources):
        parts.append(query_ref[:, 2 * kv * head : 2 * (kv + 1) * head])
        parts.append(key_ref[:, kv * head : (kv + 1) * head])
        parts.append(value_ref[:, kv * head : (kv + 1) * head])
    shard(first, parts)
    greet(layers)
    first.send_z()
    first.send_plane()
    shard(
        gathers[1],
        [out_ref[...], cq_ref[...], ck_ref[...], cv_ref[...], co_ref[...]],
    )
    feed = gate_ref.shape[1]
    parts = []
    for at in range(0, feed, tile):
        end = min(at + tile, feed)
        parts += [gate_ref[:, at:end], up_ref[:, at:end], down_ref[:, at:end]]
    shard(gathers[0], parts)

    def one(m, carry):
        first.step(m)
        return carry

    lax.fori_loop(0, layers, one, 0)
    rows.start()
    enc.start()
    lax.fori_loop(layers, 2 * layers, one, 0)
    for gather in gathers:
        gather.send_z()
    for gather in gathers:
        gather.send_plane()

    def make_bias(n, carry):
        row = jnp.broadcast_to(bias_ref[pl.ds(n, 1), :], (tile, 2 * tile))
        turned = pltpu.roll(row, tile + 1, 1, stride=1, stride_axis=0)
        bias_s[n // blocks, n % blocks] = turned[:, :tile]
        return carry

    lax.fori_loop(0, 2 * blocks, make_bias, 0)
    rows.arrive()
    first.finish()
    keep = pltpu.make_async_copy(win_s, win_out, win_sem.at[0])
    keep.start()
    rows.finish()
    rows_out[...] = rows_land[...]
    width = rows_ref.shape[2]
    for layer in range(layers):
        v = rows_land[layer].reshape(-1, width).astype(f32)
        at = slice(layer * v.shape[0], (layer + 1) * v.shape[0])
        norm_s[at, :] = (v * norm_scale(v) * gain_ref[...]).astype(bf16)
    for kv in range(sources):
        columns = win_s[..., 4 * head * kv : 4 * head * (kv + 1)].reshape(-1, 4 * head)
        qkv_s[kv] = matmul(norm_s[...], columns).astype(bf16)
    heads.start()
    enc.arrive()
    plane.start()
    cot.start()
    nt_out[...] = jnp.transpose(norm_s[...])
    heads.arrive()
    unpack_pair(came, q_s, k_s, v_s, score_scale)
    kept_ref[...] = came[...]

    def row_block(turn, carry):
        i = blocks - 1 - turn
        at = pl.ds(pl.multiple_of(i * tile, tile), tile)
        query = [q_s[h, at, :] for h in range(2)]

        def score_step(j, tops):
            key = k_s[pl.ds(pl.multiple_of(j * tile, tile), tile), :]
            found = []
            for h in range(2):
                score = dot_t(query[h], key) + bias_s[h, i - j]
                score_s[h, j] = score
                found.append(jnp.maximum(tops[h], jnp.maximum(score[:, :128], score[:, 128:])))
            return tuple(found)

        start = jnp.full((tile, 128), masked_score, jnp.float32)
        tops = lax.fori_loop(0, i + 1, score_step, (start, start))
        tops = [jnp.max(top, axis=1, keepdims=True) for top in tops]

        def share_step(j, state):
            value = v_s[pl.ds(pl.multiple_of(j * tile, tile), tile), :]
            found = []
            for h in range(2):
                total, summed = state[h]
                share = jnp.exp(score_s[h, j] - tops[h])
                summed = summed + jnp.dot(
                    share.astype(jnp.bfloat16), value, preferred_element_type=jnp.float32
                )
                found.append((total + share[:, :128] + share[:, 128:], summed))
            return tuple(found)

        nothing = (jnp.zeros((tile, 128), jnp.float32), jnp.zeros((tile, head), jnp.float32))
        state = lax.fori_loop(0, i + 1, share_step, (nothing, nothing))
        found = []
        for h in range(2):
            total = jnp.sum(state[h][0], axis=1, keepdims=True)
            found.append(state[h][1] / total)
            log_total = jnp.broadcast_to(tops[h] + jnp.log(total), (tile, 128))
            total_ref[pl.ds(h * blocks + i, 1), :] = jnp.transpose(log_total)[0:1, :]
        both = jnp.concatenate(found, axis=1)
        full_ref[at, :] = both
        both = both.astype(jnp.bfloat16)
        for part in range(tile // 128):
            block = i * (tile // 128) + part
            low_s[block] = both[part * 128 : (part + 1) * 128]

        for gather in gathers:
            gather.step(turn)
        for part in range(tile // 128):
            block = i * (tile // 128) + part

            @pl.when(block % sources == spot)
            def _():
                landed[spot, block // sources] = low_s[block]

            @pl.when(block % sources != spot)
            def _():
                hand_back(block).start()

        return carry

    def hand_back(block):
        return pltpu.make_async_remote_copy(
            src_ref=low_s.at[block],
            dst_ref=landed.at[spot, block // sources],
            send_sem=out_send.at[block],
            recv_sem=out_recv.at[spot, block // sources],
            **to_chip(rank - spot + block % sources),
        )

    lax.fori_loop(0, blocks // 2, row_block, 0)
    plane.arrive()
    cot.arrive()
    lax.fori_loop(blocks // 2, blocks, row_block, 0)
    for o in range(3):
        chip, there = peers[o]
        for turn in range(layers):
            pltpu.make_async_remote_copy(
                src_ref=low_s.at[0],
                dst_ref=landed.at[there, turn],
                send_sem=out_send.at[0],
                recv_sem=out_recv.at[there, turn],
                **to_chip(chip),
            ).wait_recv()
    for source in range(sources):
        for turn in range(layers):
            low_ref[turn * 128 : (turn + 1) * 128, source * 128 : (source + 1) * 128] = landed[
                source, turn
            ]
    heads.finish()
    cot.finish()
    cot_out[...] = cot_land[...]
    enc.finish()
    plane.finish()
    enc_out[...] = enc_all[...]
    keep.wait()
    for block in range(sources * layers):

        @pl.when(block % sources != spot)
        def _():
            hand_back(block).wait_send()

    for gather in gathers:
        gather.finish()


def begin(scale, layers, inputs, encoder, cotangent, gain, bias, *shards):
    f32, bf16 = jnp.float32, jnp.bfloat16
    own, width = inputs.shape[1:]
    enc_own = encoder.shape[1]
    rows = 2 * layers * own
    head = round(scale**-2)
    sources = 4
    length = sources * rows
    blocks = length // tile
    cols = sum(shard.shape[1] for shard in shards[:3])
    rest_cols = 4 * shards[3].shape[1]
    feed_cols = 3 * shards[8].shape[1]
    rows_shape, enc_shape = (layers, 2, own, width), (4, 2, layers, enc_own, width)
    qkv_shape = (sources, rows, 4 * head)
    chips = (layers, 2, 2, 2, 2, 16)
    vmem, anywhere = pl.BlockSpec(memory_space=pltpu.VMEM), pl.BlockSpec(memory_space=pl.ANY)
    return pl.pallas_call(
        functools.partial(begin_kernel, scale, layers),
        name="begin",
        out_shape=(
            jax.ShapeDtypeStruct(rows_shape, bf16),
            jax.ShapeDtypeStruct(enc_shape, bf16),
            jax.ShapeDtypeStruct(rows_shape, bf16),
            jax.ShapeDtypeStruct(qkv_shape, bf16),
            jax.ShapeDtypeStruct((rows, sources * 2 * head), bf16),
            jax.ShapeDtypeStruct((length, 2 * head), f32),
            jax.ShapeDtypeStruct((2 * blocks, tile), f32),
            jax.ShapeDtypeStruct((width, rows), bf16),
            jax.ShapeDtypeStruct((*chips, cols), bf16),
            jax.ShapeDtypeStruct((*chips, rest_cols), bf16),
            jax.ShapeDtypeStruct((*chips, feed_cols), bf16),
        ),
        in_specs=[vmem] * 16,
        out_specs=(vmem,) * 8 + (anywhere,) * 3,
        scratch_shapes=[
            pltpu.VMEM(rows_shape, bf16),
            pltpu.VMEM((layers, enc_own, width), bf16),
            pltpu.VMEM(enc_shape, bf16),
            pltpu.VMEM(rows_shape, bf16),
            pltpu.VMEM((*chips, cols), bf16),
            pltpu.VMEM((rows, width), bf16),
            pltpu.VMEM(qkv_shape, bf16),
            pltpu.VMEM(qkv_shape, bf16),
            pltpu.VMEM((sources, layers, 128, 2 * head), bf16),
            pltpu.VMEM((length // 128, 128, 2 * head), bf16),
            pltpu.VMEM((2, length, head), bf16),
            pltpu.VMEM((length, head), bf16),
            pltpu.VMEM((length, head), bf16),
            pltpu.VMEM((2, blocks, tile, tile), f32),
            pltpu.VMEM((2, blocks, tile, tile), f32),
            dma((2, layers)),
            dma((2, layers)),
            dma((2, layers)),
            dma((2, 3)),
            dma((2, 4)),
            dma((2, layers)),
            dma((2, layers)),
            dma((2, 3)),
            dma((length // 128,)),
            dma((sources, layers)),
            dma((1,)),
            *gather_scratch(layers, cols),
            *gather_scratch(layers, rest_cols),
            *gather_scratch(layers, feed_cols),
        ],
        compiler_params=pltpu.CompilerParams(
            collective_id=6, has_side_effects=True, vmem_limit_bytes=56 << 20
        ),
    )(inputs, encoder, cotangent, gain, bias, *shards)

def feed_cut(cols):
    return (cols // 128 + 1) // 2 * 128


def attend_backward_kernel(
    score_scale,
    layers,
    kept_ref,
    ctx_ref,
    full_ref,
    total_ref,
    bias_ref,
    kv_ref,
    rows_ref,
    grads_ref,
    feed_ref,
    got_x,
    got_y,
    out_ref,
    sums_ref,
    kv_out,
    rows_out,
    sum_a,
    sum_b,
    ctx_land,
    kv_land,
    rows_land,
    out_s,
    out_land,
    q_s,
    k_s,
    v_s,
    g_s,
    bias_s,
    sum_s,
    delta_s,
    dq_s,
    dk_s,
    dv_s,
    ctx_sem,
    kv_sem,
    rows_z,
    out_sem,
    *sum_refs,
):
    blocks = bias_s.shape[1]
    sources, rows, _ = kept_ref.shape
    head = k_s.shape[1]
    each = len(sum_refs) // 3
    cut = feed_cut(feed_ref.shape[-1])
    sums = (
        GradSum(layers, pl.ds(0, cut), feed_ref, (got_x, got_y), sum_b, *sum_refs[:each]),
        GradSum(
            layers,
            pl.ds(cut, feed_ref.shape[-1] - cut),
            feed_ref,
            (got_x, got_y),
            sum_b,
            *sum_refs[each : 2 * each],
        ),
        GradSum(layers, slice(None), grads_ref, (), sum_a, *sum_refs[2 * each :]),
    )
    context = PlaneSwap(layers, ctx_ref, ctx_land, ctx_sem)
    cross = PlaneSwap(layers, kv_ref, kv_land, kv_sem)
    ended = Column(layers, rows_ref, rows_land, rows_z)
    back = PlaneSwap(layers, out_s, out_land, out_sem)
    for grads in sums:
        grads.start()
    greet(layers)
    context.start()
    for grads in sums:
        grads.send_first(0)
    cross.start()
    ended.start()
    unpack_pair(kept_ref, q_s, k_s, v_s, score_scale)

    def make_bias(n, carry):
        row = jnp.broadcast_to(bias_ref[pl.ds(n, 1), :], (tile // 2, 2 * tile))
        turned = pltpu.roll(row, 0, 1, stride=1, stride_axis=0)
        bias_s[n // blocks, n % blocks, : tile // 2] = turned[:, tile:]
        bias_s[n // blocks, n % blocks, tile // 2 :] = turned[:, tile // 2 : tile + tile // 2]
        return carry

    lax.fori_loop(0, 2 * blocks, make_bias, 0)
    sum_s[...] = jnp.zeros_like(sum_s)
    dq_s[...] = jnp.zeros_like(dq_s)
    dk_s[...] = jnp.zeros_like(dk_s)
    dv_s[...] = jnp.zeros_like(dv_s)
    context.arrive()
    for block in range(rows // 128 * sources):
        source, turn = block % sources, block // sources
        part = ctx_land[source, turn * 128 : (turn + 1) * 128, :]
        at = slice(block * 128, (block + 1) * 128)
        g_s[0, at, :] = part[:, :head]
        g_s[1, at, :] = part[:, head:]

    def make_delta(i, carry):
        at = pl.ds(pl.multiple_of(i * tile, tile), tile)
        for h in range(2):
            product = g_s[h, at, :].astype(jnp.float32) * full_ref[at, h * head : (h + 1) * head]
            column = jnp.broadcast_to(jnp.sum(product, axis=1, keepdims=True), (tile, 128))
            delta_s[pl.ds(h * blocks + i, 1), :] = jnp.transpose(column)[0:1, :]
        return carry

    lax.fori_loop(0, blocks, make_delta, 0)

    def one_tile(n, carry):
        line, at = n // blocks, n % blocks
        first = at < blocks - line
        d = jnp.where(first, line, blocks - line)
        i = jnp.where(first, at + line, at)
        at_q = pl.ds(pl.multiple_of(i * tile, tile), tile)
        at_k = pl.ds(pl.multiple_of((i - d) * tile, tile), tile)
        key, value = k_s[at_k, :], v_s[at_k, :]
        for h in range(2):
            query, grad = q_s[h, at_q, :], g_s[h, at_q, :]
            score = dot_t(key, query) + bias_s[h, d]
            share = jnp.exp(score - total_ref[pl.ds(h * blocks + i, 1), :])
            pull = dot_t(value, grad)
            grad_score = share * (pull - delta_s[pl.ds(h * blocks + i, 1), :])
            sum_s[h, d] += grad_score
            share_low = share.astype(jnp.bfloat16)
            grad_low = grad_score.astype(jnp.bfloat16)
            dv_s[at_k, :] += jnp.dot(share_low, grad, preferred_element_type=jnp.float32)
            dk_s[at_k, :] += jnp.dot(grad_low, query, preferred_element_type=jnp.float32)
            dq_s[h, at_q, :] += dot_first(grad_low, key)
        return carry

    tiles = blocks * (blocks + 1) // 2
    busy = 2 * layers

    def work(m, carry):
        for grads in sums:
            grads.send_first(m)
        low = (m - 1) * tiles // busy
        lax.fori_loop(low, m * tiles // busy, one_tile, 0)
        for grads in sums:
            grads.advance(m)
        return carry

    lax.fori_loop(1, 1 + busy, work, 0)

    for block in range(rows // 128 * sources):
        source, turn = block % sources, block // sources
        at = slice(block * 128, (block + 1) * 128)
        out_s[source, turn * 128 : (turn + 1) * 128, :] = jnp.concatenate(
            [dq_s[0, at, :] * score_scale, dq_s[1, at, :] * score_scale, dk_s[at, :], dv_s[at, :]],
            axis=1,
        ).astype(jnp.bfloat16)
    back.start()

    edge = tile // 2
    row_at = lax.broadcasted_iota(jnp.int32, (edge, edge), 0)
    col_at = lax.broadcasted_iota(jnp.int32, (edge, edge), 1)
    turn_rows = (row_at + col_at == edge - 1).astype(jnp.float32)
    gap = jnp.zeros((edge, edge), jnp.float32)

    def make_sums(n, carry):
        upper = sum_s[n // blocks, n % blocks, :edge]
        lower = sum_s[n // blocks, n % blocks, edge:]
        folded = jnp.concatenate([lower, gap], axis=1) + jnp.concatenate([gap, upper], axis=1)
        turned = jnp.dot(
            turn_rows, folded, precision=highest, preferred_element_type=jnp.float32
        )
        wide = jnp.concatenate([turned, gap], axis=1)
        wide = pltpu.roll(wide, 0, 1, stride=1, stride_axis=0)
        sums_ref[pl.ds(n, 1), :] = jnp.sum(wide, axis=0, keepdims=True)
        return carry

    cross.arrive()
    both = kv_land[0].astype(jnp.float32)
    for source in range(1, sources):
        both = both + kv_land[source].astype(jnp.float32)
    kv_out[...] = both.astype(jnp.bfloat16)
    ended.arrive()
    rows_out[...] = rows_land[...]

    left = sum_steps(layers) - 1 - busy

    def rest(m, carry):
        for grads in sums:
            grads.send_first(m)
        for grads in sums:
            grads.advance(m)
        n = m - 1 - busy
        lax.fori_loop(n * 2 * blocks // left, (n + 1) * 2 * blocks // left, make_sums, 0)
        return carry

    lax.fori_loop(1 + busy, sum_steps(layers), rest, 0)
    back.arrive()
    wide = 4 * head
    for source in range(sources):
        out_ref[:, source * wide : (source + 1) * wide] = out_land[source]
    context.finish()
    cross.finish()
    ended.finish()
    back.finish()
    for grads in sums:
        grads.finish()


def attend_backward(
    scale, layers, kept, ctx_grad, full, total, bias, kv, layer_rows, grads, feed_grads, got
):
    f32, bf16 = jnp.float32, jnp.bfloat16
    sources, rows, wide = kept.shape
    head = wide // 4
    length = sources * rows
    blocks = length // tile
    cols, feed_cols = grads.shape[1], feed_grads.shape[1]
    chips = (layers, 2, 2, 2, 2, 16)
    vmem, anywhere = pl.BlockSpec(memory_space=pltpu.VMEM), pl.BlockSpec(memory_space=pl.ANY)
    return pl.pallas_call(
        functools.partial(attend_backward_kernel, scale, layers),
        name="attend_backward",
        out_shape=(
            jax.ShapeDtypeStruct((rows, sources * wide), bf16),
            jax.ShapeDtypeStruct((2 * blocks, 2 * tile), f32),
            jax.ShapeDtypeStruct(kv.shape[1:], bf16),
            jax.ShapeDtypeStruct(layer_rows.shape, bf16),
            jax.ShapeDtypeStruct((2, 2, 16, cols), f32),
            jax.ShapeDtypeStruct((2, 2, 16, feed_cols), f32),
        ),
        in_specs=[vmem] * 7 + [anywhere] * 4,
        out_specs=(vmem,) * 6,
        scratch_shapes=[
            pltpu.VMEM(ctx_grad.shape, bf16),
            pltpu.VMEM(kv.shape, bf16),
            pltpu.VMEM(layer_rows.shape, bf16),
            pltpu.VMEM(kept.shape, bf16),
            pltpu.VMEM(kept.shape, bf16),
            pltpu.VMEM((2, length, head), bf16),
            pltpu.VMEM((length, head), bf16),
            pltpu.VMEM((length, head), bf16),
            pltpu.VMEM((2, length, head), bf16),
            pltpu.VMEM((2, blocks, tile, tile), f32),
            pltpu.VMEM((2, blocks, tile, tile), f32),
            pltpu.VMEM((2 * blocks, tile), f32),
            pltpu.VMEM((2, length, head), f32),
            pltpu.VMEM((length, head), f32),
            pltpu.VMEM((length, head), f32),
            dma((2, 3)),
            dma((2, 3)),
            dma((2, layers)),
            dma((2, 3)),
            *sum_scratch(layers, feed_cut(feed_cols)),
            *sum_scratch(layers, feed_cols - feed_cut(feed_cols)),
            *sum_scratch(layers, cols),
        ],
        compiler_params=pltpu.CompilerParams(
            collective_id=8, has_side_effects=True, vmem_limit_bytes=62 << 20
        ),
    )(
        kept,
        ctx_grad,
        full,
        total,
        bias,
        kv,
        layer_rows,
        grads.reshape(*chips, cols),
        feed_grads.reshape(*chips, feed_cols),
        *got,
    )

def norm_scale(v):
    return lax.rsqrt(jnp.mean(v * v, axis=-1, keepdims=True) + norm_eps)


def norm_pull(v, gain, grad):
    scale = norm_scale(v)
    turned = v * scale
    pulled = grad * gain
    mean = jnp.mean(pulled * turned, axis=-1, keepdims=True)
    return scale * (pulled - turned * mean), jnp.sum(grad * turned, axis=0, keepdims=True)


def middle_kernel(
    score_scale,
    layers,
    feed,
    ctx_ref,
    x_ref,
    cot_ref,
    enc_ref,
    wa_ref,
    cross_gain_ref,
    feed_gain_ref,
    wf_ref,
    layer_out,
    grad_out,
    gctx_out,
    kv_out,
    ga_out,
    gain_out,
    gb_out,
    got_x,
    got_y,
    w_s,
    gb_s,
    after_self,
    after_cross,
    nc_s,
    nf_s,
    nft_s,
    cott_s,
    down_s,
    dx_s,
    send_s,
    land_s,
    half_s,
    q_s,
    k_s,
    v_s,
    g_s,
    pair_s,
    cc_s,
    dq_s,
    dk_s,
    low_s,
    w_load,
    w_send,
    w_recv,
    g_send,
    g_recv,
    g_store,
    swap_sem,
    z_sem,
):
    f32, bf16 = jnp.float32, jnp.bfloat16
    rank, z, y, x = chip_place(layers)
    core = lax.axis_index(tensor_axis)
    x_chip, y_chip = rank + 1 - 2 * x, rank + 2 - 4 * y
    rows, width = x_ref.shape
    heads, _, head = q_s.shape
    kv_heads = heads // 2
    wide = heads * head
    enc_rows = enc_ref.shape[0]
    block = send_s.shape[2]
    chunks = rows // block
    at_out, at_cq, at_ck = 0, wide, 2 * wide
    at_cv, at_co = at_ck + wide // 2, at_ck + wide
    row_chip = 64

    def row_of(layer, at_y, at_x, colour=0):
        return pl.multiple_of(((layer * 2 + at_y) * 2 + at_x) * row_chip + 32 * colour, 32)

    def loads(n, cols):
        copies = []
        for layer in range(layers):
            for start, count in (
                (row_of(layer, y, x), 64),
                (row_of(layer, y, 1 - x, 0), 32),
                (row_of(layer, 1 - y, x, 1), 32),
            ):
                at = (pl.ds(start, count), cols)
                copies.append(pltpu.make_async_copy(wf_ref.at[at], w_s.at[at], w_load.at[n]))
        return copies

    def weights_hop(n, cols, layer, along_y, which):
        spot = row_of(layer, y, which, 0) if along_y else row_of(layer, which, x, 1)
        at = (pl.ds(spot, 32), cols)
        return pltpu.make_async_remote_copy(
            src_ref=wf_ref.at[at],
            dst_ref=w_s.at[at],
            send_sem=w_send.at[int(along_y), n],
            recv_sem=w_recv.at[int(along_y), n],
            **to_chip(y_chip if along_y else x_chip),
        )

    def weights_all(n, cols, along_y):
        at = (pl.ds(0, 64 * layers), cols)
        return pltpu.make_async_remote_copy(
            src_ref=wf_ref.at[at],
            dst_ref=w_s.at[at],
            send_sem=w_send.at[int(along_y), n],
            recv_sem=w_recv.at[int(along_y), n],
            **to_chip(y_chip if along_y else x_chip),
        )

    def grads_hop(n, cols, layer, along_y, which):
        spot = row_of(layer, 1 - y, which, 1) if along_y else row_of(layer, which, 1 - x, 0)
        return pltpu.make_async_remote_copy(
            src_ref=gb_s.at[pl.ds(spot, 32), cols],
            dst_ref=(got_y if along_y else got_x).at[layer, which, :, cols],
            send_sem=g_send.at[int(along_y), n],
            recv_sem=g_recv.at[int(along_y), n],
            **to_chip(y_chip if along_y else x_chip),
        )

    def grads_all(n, cols, along_y):
        return pltpu.make_async_remote_copy(
            src_ref=gb_s.at[pl.ds(0, 64 * layers), cols],
            dst_ref=(got_y if along_y else got_x).at[:, :, :, cols],
            send_sem=g_send.at[int(along_y), n],
            recv_sem=g_recv.at[int(along_y), n],
            **to_chip(y_chip if along_y else x_chip),
        )

    hops = [(layer, a, w) for layer in range(layers) for w in range(2) for a in (True, False)]
    full_blocks, last = feed // tile, feed % tile

    def each_block(work, order=lambda n: n):
        def one(n, carry):
            n = order(n)
            work(n, pl.ds(pl.multiple_of(n * 3 * tile, 3 * tile), 3 * tile), tile)
            return carry

        lax.fori_loop(0, full_blocks, one, 0)
        if last:
            work(full_blocks, pl.ds(full_blocks * 3 * tile, 3 * last), last)

    near = min(2, full_blocks // 2)
    odd = z % 2

    def crosses(n):
        from_even, from_odd = n < near, (n >= near) & (n < 2 * near)
        return ((odd == 1) & from_even) | ((odd == 0) & from_odd)

    def bring(n, cols, units):
        @pl.when(jnp.logical_not(crosses(n)))
        def _():
            for hop in hops:
                weights_hop(n, cols, *hop).start()

        for copy in loads(n, cols):
            copy.start()

    def block_cols(n):
        return pl.ds(pl.multiple_of(n * 3 * tile, 3 * tile), 3 * tile)

    def over_z(n, spot):
        at = (pl.ds(spot, 32), block_cols(n))
        return pltpu.make_async_remote_copy(
            src_ref=w_s.at[at],
            dst_ref=w_s.at[at],
            send_sem=z_sem.at[0, n],
            recv_sem=z_sem.at[1, n],
            **to_chip(rank + 4 - 8 * odd),
        )

    def over_z_all(n):
        at = (pl.ds(0, 128 * layers), block_cols(n))
        return pltpu.make_async_remote_copy(
            src_ref=w_s.at[at],
            dst_ref=w_s.at[at],
            send_sem=z_sem.at[0, n],
            recv_sem=z_sem.at[1, n],
            **to_chip(rank + 4 - 8 * odd),
        )

    def hand_over(turn):
        n = near * odd + turn
        for along_y in (True, False):
            weights_all(n, block_cols(n), along_y).wait_recv()
        for layer in range(layers):
            for which in range(2):
                over_z(n, row_of(layer, 1 - y, which, 0)).start()
                over_z(n, row_of(layer, which, 1 - x, 1)).start()

    greet(layers)
    each_block(bring)

    def swap(n, chunk):
        half = n == 3
        return pltpu.make_async_remote_copy(
            src_ref=half_s.at[0] if half else send_s.at[slots[n], chunk],
            dst_ref=half_s.at[1] if half else land_s.at[slots[n], chunk],
            send_sem=swap_sem.at[0, n, chunk],
            recv_sem=swap_sem.at[1, n, chunk],
            **to_core(1 - core),
        )

    slots = (0, 1, 0, None, 1)

    def span(chunk):
        return pl.ds(pl.multiple_of(chunk * block, block), block)

    def send_parts(n, part_of):
        def one(chunk, carry):
            send_s[slots[n], chunk] = part_of(span(chunk)).astype(bf16)
            swap(n, chunk).start()
            return carry

        lax.fori_loop(0, chunks, one, 0)

    def take_parts(n, use):
        def one(chunk, carry):
            swap(n, chunk).wait()
            both = send_s[slots[n], chunk].astype(f32) + land_s[slots[n], chunk].astype(f32)
            use(span(chunk), both)
            return carry

        lax.fori_loop(0, chunks, one, 0)

    cross_gain, feed_gain = cross_gain_ref[...], feed_gain_ref[...]

    send_parts(0, lambda at: dot_t(ctx_ref[at, :], wa_ref[:, at_out : at_out + wide]))
    key_value = matmul(enc_ref[...], wa_ref[:, at_ck : at_ck + wide]).astype(bf16)
    for kv in range(kv_heads):
        k_s[kv] = key_value[:, kv * head : (kv + 1) * head]
        v_s[kv] = key_value[:, wide // 2 + kv * head : wide // 2 + (kv + 1) * head]
    cott_s[...] = jnp.transpose(cot_ref[...])

    def enter_cross(at, both):
        v = x_ref[at, :].astype(f32) + both
        after_self[at, :] = v
        nc_s[at, :] = (v * norm_scale(v) * cross_gain).astype(bf16)
        query = matmul(nc_s[at, :], wa_ref[:, at_cq : at_cq + wide]).astype(bf16)
        for h in range(heads):
            q_s[h, at, :] = (query[:, h * head : (h + 1) * head] * score_scale).astype(bf16)

    take_parts(0, enter_cross)
    if near > 0:
        hand_over(0)

    def attend(kv, carry):
        key, value = k_s[kv], v_s[kv]
        for chunk in range(chunks):
            at = slice(chunk * block, (chunk + 1) * block)
            found = []
            for h in range(2):
                score = dot_t(q_s[2 * kv + h, at, :], key)
                share = jnp.exp(score - jnp.max(score, axis=1, keepdims=True))
                total = jnp.sum(share, axis=1, keepdims=True)
                found.append(matmul(share.astype(bf16), value) / total)
            pair_s[kv, at, :] = jnp.concatenate(found, axis=1).astype(bf16)
        return carry

    lax.fori_loop(0, kv_heads, attend, 0)
    if near > 1:
        hand_over(1)
    for kv in range(kv_heads):
        cc_s[:, 2 * kv * head : 2 * (kv + 1) * head] = pair_s[kv]
    send_parts(1, lambda at: dot_t(cc_s[at, :], wa_ref[:, at_co : at_co + wide]))

    def enter_feed(at, both):
        v = after_self[at, :] + both
        after_cross[at, :] = v
        nf_s[at, :] = (v * norm_scale(v) * feed_gain).astype(bf16)

    take_parts(1, enter_feed)
    nft_s[...] = jnp.transpose(nf_s[...])

    down_s[...] = jnp.zeros_like(down_s)
    dx_s[...] = jnp.zeros_like(dx_s)
    slope = math.sqrt(2.0 / math.pi)

    def come_in_plane(n, cols):
        for along_y in (True, False):
            weights_all(n, cols, along_y).wait_recv()

    def in_turn(step):
        over = near * (1 - odd) + step - (full_blocks - near)
        shared = step + near
        return jnp.where(
            step < near, near * odd + step, jnp.where(step < full_blocks - near, shared, over)
        )

    def feed_block(n, cols, units):
        have = (pl.ds(0, 128 * layers), cols)
        pltpu.make_async_copy(wf_ref.at[have], w_s.at[have], w_load.at[n]).wait()
        if isinstance(n, int):
            come_in_plane(n, cols)
        else:
            own = (n >= near * odd) & (n < near * odd + near)

            @pl.when(crosses(n))
            def _():
                over_z_all(n).wait_recv()

            @pl.when(jnp.logical_not(crosses(n) | own))
            def _():
                come_in_plane(n, cols)

        pair = w_s[:, pl.ds(cols.start, 2 * units)]
        down = w_s[:, pl.ds(cols.start + 2 * units, units)]
        both = matmul(nf_s[...], pair)
        gate, up = both[:, :units], both[:, units:]
        square = gate * gate
        bend = jnp.tanh(slope * (gate + 0.044715 * square * gate))
        bent = 0.5 * gate * (1.0 + bend)
        pull = 0.5 * (1.0 + bend) + 0.5 * gate * (1.0 - bend * bend) * slope * (
            1.0 + 3.0 * 0.044715 * square
        )
        hidden = (bent * up).astype(bf16)
        down_s[...] += dot_t(hidden, down)
        grad = matmul(cot_ref[...], down)
        grads = jnp.concatenate([grad * up * pull, grad * bent], axis=1).astype(bf16)
        dx_s[...] += dot_t(grads, pair)
        gb_s[:, pl.ds(cols.start, 2 * units)] = matmul(nft_s[...], grads).astype(bf16)
        gb_s[:, pl.ds(cols.start + 2 * units, units)] = matmul(cott_s[...], hidden).astype(bf16)
        for hop in hops:
            grads_hop(n, cols, *hop).start()

    each_block(feed_block, in_turn)

    send_parts(2, lambda at: dx_s[at, :])
    store = pltpu.make_async_copy(gb_s, gb_out, g_store.at[0])
    store.start()
    own = rows // (2 * layers)

    def halves(ref, which):
        return [ref[pl.ds((2 * layer + which) * own, own), :] for layer in range(layers)]

    low = jnp.concatenate(halves(down_s, 1 - core), axis=0).astype(bf16)
    half_s[0] = low
    swap(3, 0).start()

    def leave_feed(at, both):
        grad, gain = norm_pull(after_cross[at, :], feed_gain, both)
        dx_s[at, :] = cot_ref[at, :].astype(f32) + grad
        low = dx_s[at, :].astype(bf16)
        low_s[at, :] = low
        gain_out[1:2, :] += gain
        context = matmul(low, wa_ref[:, at_co : at_co + wide]).astype(bf16)
        for h in range(heads):
            g_s[h, at, :] = context[:, h * head : (h + 1) * head]

    gain_out[...] = jnp.zeros_like(gain_out)
    take_parts(2, leave_feed)
    swap(3, 0).wait()
    mine = halves(after_cross, core)
    down = halves(down_s, core)
    for layer in range(layers):
        came = half_s[1, layer * own : (layer + 1) * own, :].astype(f32)
        layer_out[layer] = (mine[layer] + (down[layer].astype(bf16).astype(f32) + came)).astype(bf16)

    ga_out[:, at_co : at_co + wide] = dot_first(low_s[...], cc_s[...]).astype(bf16)

    def attend_back(kv, carry):
        key, value = k_s[kv], v_s[kv]
        key_grad = jnp.zeros((enc_rows, head), f32)
        value_grad = jnp.zeros((enc_rows, head), f32)
        for chunk in range(chunks):
            at = slice(chunk * block, (chunk + 1) * block)
            found = []
            for h in range(2):
                query, grad = q_s[2 * kv + h, at, :], g_s[2 * kv + h, at, :]
                score = dot_t(key, query)
                share = jnp.exp(score - jnp.max(score, axis=0, keepdims=True))
                share = share * (1.0 / jnp.sum(share, axis=0, keepdims=True))
                pull = dot_t(value, grad)
                delta = jnp.sum(share * pull, axis=0, keepdims=True)
                grad_low = (share * (pull - delta)).astype(bf16)
                found.append(dot_first(grad_low, key) * score_scale)
                key_grad = key_grad + matmul(grad_low, query)
                value_grad = value_grad + matmul(share.astype(bf16), grad)
            pair_s[kv, at, :] = jnp.concatenate(found, axis=1).astype(bf16)
        dk_s[0, kv] = key_grad.astype(bf16)
        dk_s[1, kv] = value_grad.astype(bf16)
        return carry

    lax.fori_loop(0, kv_heads, attend_back, 0)
    for kv in range(kv_heads):
        dq_s[:, 2 * kv * head : 2 * (kv + 1) * head] = pair_s[kv]
    send_parts(4, lambda at: dot_t(dq_s[at, :], wa_ref[:, at_cq : at_cq + wide]))
    for n in range(2):
        kv_out[:, n * wide // 2 : (n + 1) * wide // 2] = jnp.concatenate(
            [dk_s[n, kv] for kv in range(kv_heads)], axis=1
        )
    ga_out[:, at_cq : at_cq + wide] = dot_first(nc_s[...], dq_s[...]).astype(bf16)
    ga_out[:, at_ck : at_ck + wide] = dot_first(enc_ref[...], kv_out[...]).astype(bf16)

    def leave_cross(at, both):
        grad, gain = norm_pull(after_self[at, :], cross_gain, both)
        dx_s[at, :] += grad
        low = dx_s[at, :].astype(bf16)
        low_s[at, :] = low
        gain_out[0:1, :] += gain
        context = matmul(low, wa_ref[:, at_out : at_out + wide]).astype(bf16)
        for q in range(4):
            gctx_out[q, at, :] = context[:, q * wide // 4 : (q + 1) * wide // 4]

    take_parts(4, leave_cross)
    ga_out[:, at_out : at_out + wide] = dot_first(low_s[...], ctx_ref[...]).astype(bf16)
    mine = halves(dx_s, core)
    for layer in range(layers):
        grad_out[layer] = mine[layer]

    store.wait()

    def settle(n, cols, units):
        @pl.when(jnp.logical_not(crosses(n)))
        def _():
            for along_y in (True, False):
                weights_all(n, cols, along_y).wait_send()

        for along_y in (True, False):
            grads_all(n, cols, along_y).wait()

    each_block(settle)
    for turn in range(near):
        over_z_all(near * odd + turn).wait_send()


def middle(scale, layers, feed, context, x_low, cot, enc, weights, *gains_and_feed):
    f32, bf16 = jnp.float32, jnp.bfloat16
    rows, width = x_low.shape
    wide = context.shape[1]
    head = round(scale**-2)
    heads = wide // head
    own = rows // (2 * layers)
    cols = gains_and_feed[-1].shape[1]
    block = rows // 2
    vmem, anywhere = pl.BlockSpec(memory_space=pltpu.VMEM), pl.BlockSpec(memory_space=pl.ANY)
    got = jax.ShapeDtypeStruct((layers, 2, 32, cols), bf16)
    return pl.pallas_call(
        functools.partial(middle_kernel, scale, layers, feed),
        name="middle",
        out_shape=(
            jax.ShapeDtypeStruct((layers, own, width), bf16),
            jax.ShapeDtypeStruct((layers, own, width), f32),
            jax.ShapeDtypeStruct((4, rows, wide // 4), bf16),
            jax.ShapeDtypeStruct((enc.shape[0], wide), bf16),
            jax.ShapeDtypeStruct((width, weights.shape[1]), bf16),
            jax.ShapeDtypeStruct((2, width), f32),
            jax.ShapeDtypeStruct((width, cols), bf16),
            got,
            got,
        ),
        in_specs=[vmem] * 7 + [anywhere],
        out_specs=(vmem,) * 6 + (anywhere,) * 3,
        scratch_shapes=[
            pltpu.VMEM((width, cols), bf16),
            pltpu.VMEM((width, cols), bf16),
            pltpu.VMEM((rows, width), f32),
            pltpu.VMEM((rows, width), f32),
            pltpu.VMEM((rows, width), bf16),
            pltpu.VMEM((rows, width), bf16),
            pltpu.VMEM((width, rows), bf16),
            pltpu.VMEM((width, rows), bf16),
            pltpu.VMEM((rows, width), f32),
            pltpu.VMEM((rows, width), f32),
            pltpu.VMEM((2, 2, block, width), bf16),
            pltpu.VMEM((2, 2, block, width), bf16),
            pltpu.VMEM((2, rows // 2, width), bf16),
            pltpu.VMEM((heads, rows, head), bf16),
            pltpu.VMEM((heads // 2, enc.shape[0], head), bf16),
            pltpu.VMEM((heads // 2, enc.shape[0], head), bf16),
            pltpu.VMEM((heads, rows, head), bf16),
            pltpu.VMEM((heads // 2, rows, 2 * head), bf16),
            pltpu.VMEM((rows, wide), bf16),
            pltpu.VMEM((rows, wide), bf16),
            pltpu.VMEM((2, heads // 2, enc.shape[0], head), bf16),
            pltpu.VMEM((rows, width), bf16),
            dma((pl.cdiv(feed, tile),)),
            dma((2, pl.cdiv(feed, tile))),
            dma((2, pl.cdiv(feed, tile))),
            dma((2, pl.cdiv(feed, tile))),
            dma((2, pl.cdiv(feed, tile))),
            dma((1,)),
            dma((2, 5, 2)),
            dma((2, pl.cdiv(feed, tile))),
        ],
        compiler_params=pltpu.CompilerParams(
            collective_id=9, has_side_effects=True, vmem_limit_bytes=67043328
        ),
    )(context, x_low, cot, enc, weights, *gains_and_feed)

def dot_t(left, right):
    return lax.dot_general(
        left, right, (((1,), (1,)), ((), ())), preferred_element_type=jnp.float32
    )


def dot_first(left, right):
    return lax.dot_general(
        left, right, (((0,), (0,)), ((), ())), preferred_element_type=jnp.float32
    )


def unpack_pair(qkv_ref, q_s, k_s, v_s, score_scale):
    sources, rows, _ = qkv_ref.shape
    blocks = rows // 128 * sources
    head = k_s.shape[1]
    for block in range(blocks):
        source, turn = block % sources, block // sources
        tile = qkv_ref[source, turn * 128 : (turn + 1) * 128, :]
        at = slice(block * 128, (block + 1) * 128)
        q_s[0, at, :] = (tile[:, :head] * score_scale).astype(jnp.bfloat16)
        q_s[1, at, :] = (tile[:, head : 2 * head] * score_scale).astype(jnp.bfloat16)
        k_s[at, :] = tile[:, 2 * head : 3 * head]
        v_s[at, :] = tile[:, 3 * head :]


def by_heads(
    inputs,
    encoder_out,
    out_cotangent,
    bucket_ids,
    position_table,
    self_gain,
    self_query,
    self_key,
    self_value,
    self_output,
    cross_gain,
    cross_query,
    cross_key,
    cross_value,
    cross_output,
    feed_gain,
    gate_weight,
    up_weight,
    down_weight,
):
    f32, bf16 = jnp.float32, jnp.bfloat16
    batches, own, width = inputs.shape
    enc_own = encoder_out.shape[1]
    length = bucket_ids.shape[0]
    heads_all, buckets = position_table.shape
    fsdp = lax.axis_size(fsdp_axis)
    plane = fsdp // batches
    rank, core = lax.axis_index(fsdp_axis), lax.axis_index(tensor_axis)
    head = self_query.shape[1] // (heads_all // 2)
    kv_local = self_key.shape[1] // head
    scale = head ** (-0.5)
    blocks = length // tile
    rows = batches * 2 * own
    enc_rows = batches * 2 * enc_own
    feed = gate_weight.shape[1]
    kv_index = core * kv_local + rank % plane
    table_here = lax.dynamic_slice_in_dim(position_table, 2 * kv_index, 2, 0)
    bucket_range = jnp.arange(buckets, dtype=jnp.int32)
    lower = jnp.sum((bucket_ids[None, :] < bucket_range[:, None]).astype(jnp.int32), axis=1)
    upper = jnp.concatenate([lower[1:], jnp.full((1,), length, jnp.int32)])
    offsets = (
        tile * jnp.arange(blocks, dtype=jnp.int32)[:, None]
        + jnp.arange(2 * tile, dtype=jnp.int32)[None, :]
    ).reshape(-1)

    def bias_of(offset):
        hit = (offset[None] >= lower[:, None]) & (offset[None] < upper[:, None])
        value = jnp.dot(table_here, hit.astype(f32), precision=highest)
        return jnp.where(offset[None] >= 0, value, masked_score).reshape(2 * blocks, 2 * tile)

    down_steps = (
        tile * jnp.arange(blocks, dtype=jnp.int32)[:, None]
        + (tile - 1)
        - jnp.arange(2 * tile, dtype=jnp.int32)[None, :]
    ).reshape(-1)
    bias_down = bias_of(down_steps)
    bias_up = bias_of(offsets - tile)

    def swap_add(partial):
        low = partial.astype(bf16)
        return low.astype(f32) + swap_cores(low).astype(f32)

    x_low, enc_all, cot_low, qkv_here, context_low, context_full, log_total, norm_t, *wholes = begin(
        scale,
        batches,
        inputs,
        encoder_out,
        out_cotangent,
        self_gain[None],
        bias_down,
        self_query,
        self_key,
        self_value,
        self_output.T,
        cross_query,
        cross_key,
        cross_value,
        cross_output.T,
        gate_weight,
        up_weight,
        down_weight.T,
    )
    x_low, enc_all = x_low.reshape(rows, width), enc_all.reshape(-1, width)
    in_full, rest_full, feed_full = [whole.reshape(width, -1) for whole in wholes]
    layer_rows, grad_after_self, grad_context, cross_kv, grads, mid_gains, feed_grads, *feed_got = (
        middle(
            scale,
            batches,
            feed,
            context_low,
            x_low,
            cot_low.reshape(rows, width),
            enc_all,
            rest_full,
            cross_gain[None],
            feed_gain[None],
            feed_full,
        )
    )
    feed_got = [came.reshape(batches, 2, 2, 16, -1) for came in feed_got]

    grad_qkv, diagonal_sums, kv_sum, layer_out, *most_sums = attend_backward(
        scale,
        batches,
        qkv_here,
        grad_context,
        context_full,
        log_total,
        bias_up,
        cross_kv.reshape(plane, enc_rows, -1),
        layer_rows,
        grads,
        feed_grads,
        feed_got,
    )
    spread = offsets - (tile - 1)
    hit = ((spread[None] >= lower[:, None]) & (spread[None] < upper[:, None])).astype(f32)
    hit = jnp.transpose(hit.reshape(buckets, blocks, 2 * tile), (1, 0, 2))
    in_sum, ended, table_sum, gain_sums = close_rows(
        batches,
        heads_all,
        grad_qkv,
        x_low,
        in_full,
        grad_after_self,
        kv_sum,
        self_gain[None],
        mid_gains,
        diagonal_sums,
        hit,
        norm_t,
        rest_full,
    )
    results = finish(in_sum, *most_sums, ended, layer_out, table_sum, gain_sums)
    turned, gains = (8, 13, 17), (4, 9, 14)
    return tuple(
        result.T if n in turned else result.reshape(-1) if n in gains else result
        for n, result in enumerate(results)
    )


def on_either(*args):
    batches, kv_heads = args[0].shape[0], args[7].shape[1] * lax.axis_size(tensor_axis)
    head_size = args[6].shape[1] * lax.axis_size(tensor_axis) // args[4].shape[0]
    devices = lax.axis_size(fsdp_axis) * lax.axis_size(tensor_axis)
    held = args[0].shape[1], args[6].shape[0], lax.axis_size(fsdp_axis)
    if held == (64, 64, 16) and devices == batches * (kv_heads // head_size):
        return by_heads(*args)
    return on_device(*args)


def solution(mesh):
    placed = (
        P(None, (fsdp_axis, tensor_axis), None),
        P(None, (fsdp_axis, tensor_axis), None),
        P(None, (fsdp_axis, tensor_axis), None),
        P(),
        P(),
        P(),
        P(fsdp_axis, tensor_axis),
        P(fsdp_axis, tensor_axis),
        P(fsdp_axis, tensor_axis),
        P(tensor_axis, fsdp_axis),
        P(),
        P(fsdp_axis, tensor_axis),
        P(fsdp_axis, tensor_axis),
        P(fsdp_axis, tensor_axis),
        P(tensor_axis, fsdp_axis),
        P(),
        P(fsdp_axis, tensor_axis),
        P(fsdp_axis, tensor_axis),
        P(tensor_axis, fsdp_axis),
    )
    return jax.shard_map(
        on_either,
        mesh=mesh,
        in_specs=placed,
        out_specs=(
            P(None, (fsdp_axis, tensor_axis), None),
            P(None, (fsdp_axis, tensor_axis), None),
            P(None, (fsdp_axis, tensor_axis), None),
            P(),
            P(),
            P(fsdp_axis, tensor_axis),
            P(fsdp_axis, tensor_axis),
            P(fsdp_axis, tensor_axis),
            P(tensor_axis, fsdp_axis),
            P(),
            P(fsdp_axis, tensor_axis),
            P(fsdp_axis, tensor_axis),
            P(fsdp_axis, tensor_axis),
            P(tensor_axis, fsdp_axis),
            P(),
            P(fsdp_axis, tensor_axis),
            P(fsdp_axis, tensor_axis),
            P(tensor_axis, fsdp_axis),
        ),
        check_vma=False,
    )
```
